32 devices in a mesh: dp: 8 (over z, y), tensor: 4 (over x, core).
Axes of the slice: x: 2, y: 2, z: 4, core: 2. Of those that a mesh axis runs over, the one named last changes fastest.
Arguments:
- block_input: bfloat16 [16384, 1024], P(('dp', 'tensor')), may hold values from -6 to 6
- value_first: bfloat16 [16384, 1024], P('dp', 'tensor'), may hold values from -6 to 6
- segment_ids: int32 [16384], P('dp'), may hold values from 0 to 4, as said below
- positions: int32 [16384], P('dp'), may hold values from 0 to 2046, as said below
- gain_attn: bfloat16 [1024], replicated, may hold values from 0.25 to 1.75
- query_weight: bfloat16 [1024, 1024], P('dp', 'tensor'), may hold values from -0.1875 to 0.1875
- key_weight: bfloat16 [1024, 1024], P('dp', 'tensor'), may hold values from -0.1875 to 0.1875
- value_weight: bfloat16 [1024, 1024], P('dp', 'tensor'), may hold values from -0.1875 to 0.1875
- out_weight: bfloat16 [1024, 1024], P('tensor', 'dp'), may hold values from -2 to 2
- gain_mlp: bfloat16 [1024], replicated, may hold values from 0.25 to 1.75
- gate_weight: bfloat16 [1024, 2816], P('dp', 'tensor'), may hold values from -0.1875 to 0.1875
- up_weight: bfloat16 [1024, 2816], P('dp', 'tensor'), may hold values from -0.1875 to 0.1875
- down_weight: bfloat16 [2816, 1024], P('tensor', 'dp'), may hold values from -0.109375 to 0.109375
- output_grad: bfloat16 [16384, 1024], P(('dp', 'tensor')), may hold values from -6 to 6
Outputs:
- block_output: bfloat16 [16384, 1024], P(('dp', 'tensor'))
- input_grad: float32 [16384, 1024], P(('dp', 'tensor'))
- value_first_grad: float32 [16384, 1024], P('dp', 'tensor')
- gain_attn_grad: float32 [1024], replicated
- query_weight_grad: float32 [1024, 1024], P('dp', 'tensor')
- key_weight_grad: float32 [1024, 1024], P('dp', 'tensor')
- value_weight_grad: float32 [1024, 1024], P('dp', 'tensor')
- out_weight_grad: float32 [1024, 1024], P('tensor', 'dp')
- gain_mlp_grad: float32 [1024], replicated
- gate_weight_grad: float32 [1024, 2816], P('dp', 'tensor')
- up_weight_grad: float32 [1024, 2816], P('dp', 'tensor')
- down_weight_grad: float32 [2816, 1024], P('tensor', 'dp')
The draws below stay inside these ranges and needn't reach their ends.
Inputs may be any that keep to these rules, and one draw needn't show every extreme that they name: `segment_ids`: within each sequence of 1024 tokens the ids are constant on aligned pieces of 256 tokens; a piece is text (0) or a picture piece whose id is its index within the sequence plus one. The last piece of the first sequence is a picture piece. `positions`: they are 0 at each sequence's first token and rise by 1 or 2 from token to token; in the first sequence they rise by 2 at every token.
All inputs are finite; a program needn't handle non-finite values.
Results may differ from the reference program's by a relative error of at most 0.018.
Values may be sent and summed in bfloat16 or wider, within the bound.
A program may use at most 128 MiB of HBM per device.

```python
import jax
import jax.numpy as jnp
from jax import lax

D = 1024
HEADS = 16
HEAD_DIM = 64
FF = 2816
SEQ_LEN = 1024
PIECE = 256
QBLOCK = 512
SEQS = 2
TOKENS = 16384


def draw_segment_ids(key, part):
    seq_count = TOKENS // SEQ_LEN
    piece_count = SEQ_LEN // PIECE
    picture = jax.random.randint(key, (seq_count, piece_count), 0, 2).astype(jnp.int32)
    picture = picture.at[0, piece_count - 1].set(1)
    piece_ids = picture * (jnp.arange(piece_count, dtype=jnp.int32) + 1)[None, :]
    return jnp.repeat(piece_ids, PIECE, axis=1).reshape(TOKENS).astype(jnp.int32)


def draw_positions(key, part):
    seq_count = TOKENS // SEQ_LEN
    stride = jax.random.randint(key, (seq_count, SEQ_LEN), 1, 3).astype(jnp.int32)
    stride = stride.at[0].set(2)
    running = jnp.cumsum(stride, axis=1) - stride[:, :1]
    return running.reshape(TOKENS).astype(jnp.int32)


def shard_levels(stream_key, extent, split, least, top_value):
    def one(axis_at, shards_of):
        heights = jax.random.uniform(jax.random.fold_in(jax.random.fold_in(stream_key, 6), axis_at), (shards_of,), jnp.float32, least / len(split), top_value / len(split))
        return jnp.repeat(jnp.exp(heights), extent[axis_at] // shards_of).reshape((-1,) + (1,) * (len(extent) - axis_at - 1))

    factor_of = one(*split[0])
    for cut in split[1:]:
        factor_of = factor_of * one(*cut)
    return factor_of


def bell_draw(stream_key, extent, width, bound, cuts=(), kind=jnp.bfloat16):
    result = jax.random.normal(stream_key, extent, jnp.float32) * width
    if len(cuts) > 0:
        result = shard_levels(stream_key, extent, cuts, -0.22, 0.18) * result
    return jnp.clip(result, min=-bound, max=bound).astype(kind)


def setup_inputs(seed: int = 0) -> dict:
    arg_keys = jax.random.split(jax.random.key(seed), 15)
    block_input = bell_draw(arg_keys[0], (TOKENS, D), 1.0, 6.0, ((0, 32),))
    value_first = bell_draw(arg_keys[1], (TOKENS, D), 1.0, 6.0, ((0, 8), (1, 4)))
    segment_ids = draw_segment_ids(jax.random.fold_in(arg_keys[14], 71), 0)
    positions = draw_positions(jax.random.fold_in(arg_keys[14], 71), 0)
    gain_attn = jnp.clip(1.0 + 0.15 * jax.random.normal(arg_keys[4], (D,), jnp.float32), 0.25, 1.75).astype(jnp.bfloat16)
    query_weight = bell_draw(arg_keys[5], (D, D), D ** -0.5, 0.1875, ((0, 8), (1, 4)))
    key_weight = bell_draw(arg_keys[6], (D, D), D ** -0.5, 0.1875, ((0, 8), (1, 4)))
    value_weight = bell_draw(arg_keys[7], (D, D), D ** -0.5, 0.1875, ((0, 8), (1, 4)))
    out_weight = bell_draw(arg_keys[8], (D, D), (max(D // 128, 1)) ** -0.5, 2.0, ((0, 4), (1, 8)))
    gain_mlp = jnp.clip(1.0 + 0.15 * jax.random.normal(arg_keys[9], (D,), jnp.float32), 0.25, 1.75).astype(jnp.bfloat16)
    gate_weight = bell_draw(arg_keys[10], (D, FF), D ** -0.5, 0.1875, ((0, 8), (1, 4)))
    up_weight = bell_draw(arg_keys[11], (D, FF), D ** -0.5, 0.1875, ((0, 8), (1, 4)))
    down_weight = bell_draw(arg_keys[12], (FF, D), FF ** -0.5, 0.109375, ((0, 4), (1, 8)))
    output_grad = bell_draw(arg_keys[13], (TOKENS, D), 1.0, 6.0, ((0, 32),))
    return {"block_input": block_input, "value_first": value_first, "segment_ids": segment_ids, "positions": positions, "gain_attn": gain_attn, "query_weight": query_weight, "key_weight": key_weight, "value_weight": value_weight, "out_weight": out_weight, "gain_mlp": gain_mlp, "gate_weight": gate_weight, "up_weight": up_weight, "down_weight": down_weight, "output_grad": output_grad}


@jax.custom_vjp
def low(v):
    return lax.optimization_barrier(v.astype(jnp.bfloat16)).astype(jnp.float32)

@jax.custom_vjp
def low_back(v):
    return v

def low_keep(v):
    return (low(v), None)

def low_pass(kept, grad):
    return (grad,)

def back_keep(v):
    return (v, None)

def back_low(kept, grad):
    return (low(grad),)
low.defvjp(low_keep, low_pass)
low_back.defvjp(back_keep, back_low)
EPSILON = 1e-06
ROPE_BASE = 10000.0
MASKED = -1e+30

def matmul(left, right):
    return jnp.dot(left, right, precision=lax.Precision.HIGHEST)

def rms_scale(values, gain):
    factor = lax.rsqrt(lax.optimization_barrier(jnp.mean(values * values, axis=-1, keepdims=True)) + EPSILON)
    return values * factor * gain

def rope_angles(position_ids, head_size):
    half_dim = head_size // 2
    frequency = ROPE_BASE ** (-(2.0 * jnp.arange(half_dim).astype(jnp.float32)) / head_size)
    return position_ids.astype(jnp.float32)[:, None] * frequency[None, :]

def rotate(values, angles):
    half_dim = values.shape[-1] // 2
    cosine = jnp.cos(angles)[:, None, :]
    sine_part = jnp.sin(angles)[:, None, :]
    first_half = values[..., :half_dim]
    second_half = values[..., half_dim:]
    return jnp.concatenate([first_half * cosine - second_half * sine_part, second_half * cosine + first_half * sine_part], axis=-1)

def attend_sequence(pieces):
    queries, key_rows, values, seq_ids = pieces
    scale = HEAD_DIM ** (-0.5)

    def one_block(number):
        block_start = number * QBLOCK
        query_block = lax.dynamic_slice_in_dim(queries, block_start, QBLOCK, 0)
        seg_query = lax.dynamic_slice_in_dim(seq_ids, block_start, QBLOCK, 0)
        scores = jnp.einsum('qhd,khd->hqk', query_block, key_rows, precision=lax.Precision.HIGHEST) * scale
        scores = low_back(scores)
        query_pos = block_start + jnp.arange(QBLOCK, dtype=jnp.int32)
        key_pos = jnp.arange(SEQ_LEN, dtype=jnp.int32)
        same_piece = (seg_query[:, None] == seq_ids[None, :]) & (seg_query[:, None] > 0)
        visible = (key_pos[None, :] <= query_pos[:, None]) | same_piece
        scores = jnp.where(visible[None], scores, MASKED)
        row_max = lax.optimization_barrier(jnp.max(scores, axis=-1, keepdims=True))
        exponent = jnp.exp(scores - row_max)
        probabilities = exponent / lax.optimization_barrier(jnp.sum(exponent, axis=-1, keepdims=True))
        return jnp.einsum('hqk,khd->qhd', low(probabilities), values, precision=lax.Precision.HIGHEST)
    blocks = lax.map(jax.checkpoint(one_block), jnp.arange(SEQ_LEN // QBLOCK, dtype=jnp.int32))
    return blocks.reshape(SEQ_LEN, HEADS, HEAD_DIM)

def forward(segment_ids, positions, inputs, first_value, gain_attn, query_weight, key_weight, value_weight, out_weight, gain_mlp, gate_weight, up_weight, down_weight):
    group_rows = inputs.shape[0]
    seq_count = group_rows // SEQ_LEN
    angles = rope_angles(positions, HEAD_DIM)
    normed = low(rms_scale(inputs, gain_attn))
    queries = low(rotate(low_back(matmul(normed, query_weight)).reshape(group_rows, HEADS, HEAD_DIM), angles))
    key_rows = low(rotate(low_back(matmul(normed, key_weight)).reshape(group_rows, HEADS, HEAD_DIM), angles))
    value_mixed = low(0.5 * low_back(matmul(normed, value_weight)) + 0.5 * first_value)
    value_mixed = value_mixed.reshape(group_rows, HEADS, HEAD_DIM)
    attended = lax.map(attend_sequence, (queries.reshape(seq_count, SEQ_LEN, HEADS, HEAD_DIM), key_rows.reshape(seq_count, SEQ_LEN, HEADS, HEAD_DIM), value_mixed.reshape(seq_count, SEQ_LEN, HEADS, HEAD_DIM), segment_ids.reshape(seq_count, SEQ_LEN)))
    attended = low(low_back(attended.reshape(group_rows, HEADS * HEAD_DIM)))
    hidden_state = inputs + low_back(matmul(attended, out_weight))
    normed_mlp = low(rms_scale(hidden_state, gain_mlp))
    gate_value = low_back(matmul(normed_mlp, gate_weight))
    upward = low_back(matmul(normed_mlp, up_weight))
    activated = low(gate_value * jax.nn.sigmoid(gate_value) * upward)
    return hidden_state + low_back(matmul(activated, down_weight))

def reference(block_input, value_first, segment_ids, positions, gain_attn, query_weight, key_weight, value_weight, out_weight, gain_mlp, gate_weight, up_weight, down_weight, output_grad):
    group_rows = SEQS * SEQ_LEN
    group_count = block_input.shape[0] // group_rows
    params = tuple((weight.astype(jnp.float32) for weight in (gain_attn, query_weight, key_weight, value_weight, out_weight, gain_mlp, gate_weight, up_weight, down_weight)))

    def group_step(running, pieces):
        rows_in, first_in, seg_in, pos_in, grad_in = pieces

        def local_forward(inputs, first_value, *weights):
            return forward(seg_in, pos_in, inputs, first_value, *weights)
        output, pullback = jax.vjp(local_forward, rows_in, first_in, *params)
        gradients = pullback(grad_in)
        running = tuple((total + piece for total, piece in zip(running, gradients[2:])))
        return (running, (output.astype(jnp.bfloat16), gradients[0], gradients[1]))
    zero_init = tuple((jnp.zeros_like(weight) for weight in params))
    totals, (outputs, input_grads, first_grads) = lax.scan(group_step, zero_init, (block_input.astype(jnp.float32).reshape(group_count, group_rows, D), value_first.astype(jnp.float32).reshape(group_count, group_rows, D), segment_ids.reshape(group_count, group_rows), positions.reshape(group_count, group_rows), output_grad.astype(jnp.float32).reshape(group_count, group_rows, D)))
    return (outputs.reshape(-1, D), input_grads.reshape(-1, D), first_grads.reshape(-1, D), totals[0], totals[1], totals[2], totals[3], totals[4], totals[5], totals[6], totals[7], totals[8])
```

```python
import functools

import jax
import jax.numpy as jnp
from jax import lax
from jax.experimental import pallas as pl
from jax.experimental.pallas import tpu as pltpu
from jax.sharding import PartitionSpec as P

HEAD_DIM = 64
SEQ_LEN = 1024
PIECE = 256
HALF = 512
TILE = 256
EPSILON = 1e-06
ROPE_BASE = 10000.0
MASKED = -1e30
MESH = pl.DeviceIdType.MESH
F32 = jnp.float32
BF16 = jnp.bfloat16
VMEM_LIMIT = 62 * 2**20


def dot_nn(a, b):
    return lax.dot_general(a, b, (((1,), (0,)), ((), ())), preferred_element_type=F32)


def dot_nt(a, b):
    return lax.dot_general(a, b, (((1,), (1,)), ((), ())), preferred_element_type=F32)


def dot_tn(a, b):
    return lax.dot_general(a, b, (((0,), (0,)), ((), ())), preferred_element_type=F32)


def rows_at(start, size):
    return pl.ds(pl.multiple_of(start, size), size)


class Place:
    def __init__(self, dp):
        self.d = lax.axis_index("dp")
        self.t = lax.axis_index("tensor")
        self.core = lax.rem(self.t, 2)
        self.chip = self.t // 2
        self.line = dp // 2
        self.y = lax.rem(self.d, 2)
        self.z = self.d // 2
        self.sibling = (self.d, self.t + 1 - 2 * self.core)
        self.across = (self.d, lax.rem(self.t + 2, 4))
        self.pair = (self.d + 1 - 2 * self.y, self.t)

    def ahead(self, k):
        return (2 * lax.rem(self.z + k, self.line) + self.y, self.t)

    def behind_z(self, k):
        return lax.rem(self.z + self.line - k, self.line)

    def greet(self):
        barrier = pltpu.get_barrier_semaphore()
        partners = [self.sibling, self.across, self.pair]
        for k in range(1, self.line):
            partners.append(self.ahead(k))
        for who in partners:
            pl.semaphore_signal(barrier, inc=1, device_id=who, device_id_type=MESH)
        pl.semaphore_wait(barrier, len(partners))


def send(src, dst, sems, k, who):
    return pltpu.make_async_remote_copy(
        src_ref=src,
        dst_ref=dst,
        send_sem=sems[0].at[k],
        recv_sem=sems[1].at[k],
        device_id=who,
        device_id_type=MESH,
    )


class Gather:
    def __init__(self, place, shard, full, line_sems, pair_sems):
        self.p, self.shard, self.full = place, shard, full
        self.line_sems, self.pair_sems = line_sems, pair_sems
        self.r = shard.shape[0]

    def slot(self, z, y):
        return self.full.at[rows_at((2 * z + y) * self.r, self.r)]

    def start(self):
        p = self.p
        self.out = [send(self.shard, self.slot(p.z, p.y), self.pair_sems, 0, p.pair)]
        for k in range(1, p.line):
            self.out.append(
                send(self.shard, self.slot(p.z, p.y), self.line_sems, k - 1, p.ahead(k))
            )
        for copy in self.out:
            copy.start()
        self.full[rows_at((2 * p.z + p.y) * self.r, self.r), :] = self.shard[...]

    def relay(self, k):
        p = self.p
        here = self.slot(p.behind_z(k), p.y)
        send(here, here, self.line_sems, k - 1, p.pair).wait_recv()
        copy = send(here, here, self.pair_sems, k, p.pair)
        copy.start()
        self.out.append(copy)

    def finish(self):
        p = self.p
        for k in range(p.line):
            there = self.slot(p.behind_z(k), 1 - p.y)
            send(there, there, self.pair_sems, k, p.pair).wait_recv()

    def drain(self):
        for copy in self.out:
            copy.wait_send()


def swap_halves(u):
    lane = lax.broadcasted_iota(jnp.int32, u.shape, 1)
    low = lax.rem(lane, HEAD_DIM) < HEAD_DIM // 2
    return jnp.where(low, pltpu.roll(u, 96, 1), pltpu.roll(u, 32, 1))


def norm_factor(u):
    return lax.rsqrt(jnp.mean(u * u, axis=-1, keepdims=True) + EPSILON)


def attention_rows(seq, pair_of_heads, i, q, k, vt, limits, attended, lse):
    lane = lax.broadcasted_iota(jnp.int32, (TILE, 128), 1)
    key_in_piece = lax.broadcasted_iota(jnp.int32, (TILE, TILE), 0)
    lanes = pl.ds(pair_of_heads * 128, 128)
    rows = pl.ds(seq * SEQ_LEN + i * TILE, TILE)
    q2 = q[rows, lanes]
    shown = key_in_piece <= limits[:, rows]
    sides = []
    for a in range(2):
        qa = jnp.where((lane < HEAD_DIM) == (a == 0), q2, jnp.zeros_like(q2))
        vta = pl.ds(pair_of_heads * 128 + a * HEAD_DIM, HEAD_DIM)
        score = jnp.where(shown, dot_nt(k[rows, lanes], qa), MASKED)
        top = jnp.max(score, axis=0, keepdims=True)
        if i > 0:
            before = dot_nt(k[pl.ds(seq * SEQ_LEN, i * TILE), lanes], qa)
            top = jnp.maximum(top, jnp.max(before, axis=0, keepdims=True))
        weight = jnp.exp(score - top)
        total = jnp.sum(weight, axis=0, keepdims=True)
        out = dot_nn(vt[vta, pl.ds(i * TILE, TILE)], weight.astype(BF16))
        if i > 0:
            weight = jnp.exp(before - top)
            total = total + jnp.sum(weight, axis=0, keepdims=True)
            out = out + dot_nn(vt[vta, pl.ds(0, i * TILE)], weight.astype(BF16))
        sides.append(out * (1.0 / total))
        lse[pl.ds(seq * 4 + pair_of_heads * 2 + a, 1), pl.ds(i * TILE, TILE)] = top + jnp.log(total)
    attended[rows, lanes] = jnp.concatenate(sides, axis=0).T.astype(BF16)


def first_kernel(
    dp,
    x_own,
    og_own,
    value_first,
    qkv_shard,
    out_shard,
    ff_shard,
    gains,
    cosine,
    sine,
    limits,
    qkv_w,
    out_w,
    ff_w,
    normed,
    q,
    k,
    v,
    attended,
    lse,
    og,
    hidden,
    normed_mlp,
    xb,
    vt,
    half_out,
    half_in,
    sum_out,
    sum_in,
    group_sems_out,
    group_sems_in,
    core_sems_out,
    core_sems_in,
    line_out,
    line_in,
    pair_out,
    pair_in,
):
    p = Place(dp)
    group = (group_sems_out, group_sems_in)
    cores = (core_sems_out, core_sems_in)
    sent = []

    def go(copy):
        copy.start()
        sent.append(copy)

    def block(b):
        return rows_at(b * HALF, HALF)

    p.greet()
    gathers = []
    for n, (shard, full) in enumerate(((qkv_shard, qkv_w), (out_shard, out_w), (ff_shard, ff_w))):
        gathers.append(
            Gather(p, shard, full, (line_out.at[n], line_in.at[n]), (pair_out.at[n], pair_in.at[n]))
        )
    go(send(x_own, xb.at[p.chip], group, 0, p.across))
    gathers[0].start()
    gain_attn = gains[0:1, :]
    gain_mlp = gains[1:2, :]
    other = lax.rem(p.t + 2, 4)

    def norm_block(b, source):
        @pl.loop(0, HALF // TILE)
        def _(j):
            u = source[rows_at(j * TILE, TILE), :].astype(F32)
            normed[rows_at(b * HALF + j * TILE, TILE), :] = (
                u * norm_factor(u) * gain_attn
            ).astype(BF16)

    xb[p.chip] = x_own[...]
    norm_block(p.t, x_own)
    go(send(normed.at[block(p.t)], normed.at[block(p.t)], cores, 0, p.sibling))
    for n in range(1, p.line):
        gathers[0].relay(n)
    for g in gathers[1:]:
        g.start()
    there = xb.at[1 - p.chip]
    send(there, there, group, 0, p.across).wait_recv()
    own_rows = og.at[block(p.t)]
    go(send(og_own, own_rows, group, 1, p.across))
    go(send(og_own, own_rows, cores, 2, p.sibling))
    og[block(p.t), :] = og_own[...]
    norm_block(other, there)
    go(send(normed.at[block(other)], normed.at[block(other)], cores, 1, p.sibling))
    gathers[0].finish()
    sib = p.t + 1 - 2 * p.core
    for n, b in ((0, sib), (1, lax.rem(sib + 2, 4))):
        there = normed.at[block(b)]
        send(there, there, cores, n, p.sibling).wait_recv()

    def project(seq):
        @pl.loop(0, SEQ_LEN // TILE)
        def _(j):
            rows = rows_at(seq * SEQ_LEN + j * TILE, TILE)
            made = dot_nn(normed[rows, :], qkv_w[...])
            cos, sin = cosine[rows, :], sine[rows, :]
            for n in range(2):
                lanes = slice(n * 128, (n + 1) * 128)
                u = made[:, n * 128 : (n + 1) * 128]
                q[rows, lanes] = ((u * cos + swap_halves(u) * sin) * HEAD_DIM**-0.5).astype(BF16)
                u = made[:, 256 + n * 128 : 256 + (n + 1) * 128]
                k[rows, lanes] = (u * cos + swap_halves(u) * sin).astype(BF16)
            mixed = 0.5 * made[:, 512:768] + 0.5 * value_first[rows, :].astype(F32)
            v[rows, :] = mixed.astype(BF16)
            vt[:, rows_at(j * TILE, TILE)] = mixed.T.astype(BF16)

    def branch(seq):
        for h, add in ((1 - p.core, False), (p.core, True)):
            if add:
                there = half_in.at[seq]
                send(there, there, cores, 4 + seq, p.sibling).wait_recv()

            @pl.loop(0, HALF // TILE)
            def _(j):
                rows = rows_at(seq * SEQ_LEN + h * HALF + j * TILE, TILE)
                part = dot_nt(attended[rows, :], out_w[...])
                tile = rows_at(j * TILE, TILE)
                if add:
                    sum_out[seq, tile, :] = (part + half_in[seq, tile, :].astype(F32)).astype(BF16)
                else:
                    half_out[seq, tile, :] = part.astype(BF16)

            if add:
                go(send(sum_out.at[seq], sum_in.at[seq], group, 2 + seq, p.across))
            else:
                go(send(half_out.at[seq], half_in.at[seq], cores, 4 + seq, p.sibling))

    def finish_branch(seq):
        there = sum_in.at[seq]
        send(there, there, group, 2 + seq, p.across).wait_recv()

        @pl.loop(0, HALF // TILE)
        def _(j):
            tile = rows_at(j * TILE, TILE)
            both = sum_out[seq, tile, :].astype(F32) + sum_in[seq, tile, :].astype(F32)
            u = xb[seq, tile, :].astype(F32) + both
            hidden[seq, tile, :] = u
            normed_mlp[rows_at((2 * seq + p.core) * HALF + j * TILE, TILE), :] = (
                u * norm_factor(u) * gain_mlp
            ).astype(BF16)

        mine = normed_mlp.at[block(2 * seq + p.core)]
        go(send(mine, mine, cores, 6 + seq, p.sibling))

    for seq in range(2):
        project(seq)
        for heads in range(2):
            for i in range(SEQ_LEN // TILE):
                attention_rows(seq, heads, i, q, k, vt, limits, attended, lse)
            if seq == 0 and heads == 0:
                for n in range(1, p.line):
                    gathers[1].relay(n)
                gathers[1].finish()
        branch(seq)
        if seq == 0:
            for n in range(1, p.line):
                gathers[2].relay(n)
            there = og.at[block(other)]
            send(there, there, group, 1, p.across).wait_recv()
            go(send(there, there, cores, 3, p.sibling))
    for seq in range(2):
        finish_branch(seq)
    for n, b in ((2, sib), (3, lax.rem(sib + 2, 4))):
        there = og.at[block(b)]
        send(there, there, cores, n, p.sibling).wait_recv()
    for seq in range(2):
        there = normed_mlp.at[block(2 * seq + 1 - p.core)]
        send(there, there, cores, 6 + seq, p.sibling).wait_recv()
    gathers[2].finish()
    for copy in sent:
        copy.wait_send()
    for g in gathers:
        g.drain()


def first_stage(dp, x, og, vf, qkv_shard, out_shard, ff_shard, gains, cosine, sine, limits):
    rows = 4 * x.shape[0]
    width = x.shape[1]
    heads_width = vf.shape[1]
    line = dp // 2
    vmem = pl.BlockSpec(memory_space=pltpu.VMEM)
    shapes = [
        ((width, qkv_shard.shape[1]), BF16),
        ((width, out_shard.shape[1]), BF16),
        ((width, ff_shard.shape[1]), BF16),
        ((rows, width), BF16),
        ((rows, heads_width), BF16),
        ((rows, heads_width), BF16),
        ((rows, heads_width), BF16),
        ((rows, heads_width), BF16),
        ((8, SEQ_LEN), F32),
        ((rows, width), BF16),
        ((2, HALF, width), F32),
        ((rows, width), BF16),
    ]
    dma = pltpu.SemaphoreType.DMA
    return pl.pallas_call(
        functools.partial(first_kernel, dp),
        out_shape=[jax.ShapeDtypeStruct(s, t) for s, t in shapes],
        in_specs=[vmem] * 10,
        out_specs=[vmem] * len(shapes),
        scratch_shapes=[
            pltpu.VMEM((2, HALF, width), BF16),
            pltpu.VMEM((heads_width, SEQ_LEN), BF16),
            pltpu.VMEM((2, HALF, width), BF16),
            pltpu.VMEM((2, HALF, width), BF16),
            pltpu.VMEM((2, HALF, width), BF16),
            pltpu.VMEM((2, HALF, width), BF16),
            dma((4,)),
            dma((4,)),
            dma((8,)),
            dma((8,)),
            dma((3, max(line - 1, 1))),
            dma((3, max(line - 1, 1))),
            dma((3, line)),
            dma((3, line)),
        ],
        compiler_params=pltpu.CompilerParams(
            collective_id=0, has_side_effects=True, vmem_limit_bytes=VMEM_LIMIT
        ),
        name="attention_forward",
    )(x, og, vf, qkv_shard, out_shard, ff_shard, gains, cosine, sine, limits)


def cut_along(shard, dim, peers):
    before, after = (shard.shape[:dim], shard.shape[dim + 1 :])
    return jnp.moveaxis(shard.reshape(*before, peers, -1, *after), dim, 0)


def summed_on_arrival(shard, axis, dim):
    peers = lax.axis_size(axis)
    pieces = lax.all_to_all(cut_along(shard, dim, peers), axis, 0, 0, tiled=True)
    return jnp.sum(pieces.astype(jnp.float32), axis=0)


def norm_back(grad_normed, values, factor, gain):
    scaled = grad_normed * gain
    input_part = factor * scaled - values * factor * factor * factor * jnp.mean(
        scaled * values, axis=-1, keepdims=True
    )
    return (input_part, jnp.sum(grad_normed * values * factor, axis=0))


def rope_tables(positions):
    half = HEAD_DIM // 2
    frequency = ROPE_BASE ** (-(2.0 * jnp.arange(half).astype(F32)) / HEAD_DIM)
    angles = positions.astype(F32)[:, None] * frequency[None, :]
    cos, sin = jnp.cos(angles), jnp.sin(angles)
    return (
        jnp.concatenate([cos, cos, cos, cos], axis=1),
        jnp.concatenate([-sin, sin, -sin, sin], axis=1),
    )


def widen(weight, width):
    return jnp.pad(weight, ((0, 0), (0, width - weight.shape[1])))


def unrotate(grad, cos, sin):
    n = grad.shape[1] // 128
    g = grad.reshape(-1, n, 4, 32)
    sw = jnp.concatenate([g[:, :, 1:2], g[:, :, 0:1], g[:, :, 3:4], g[:, :, 2:3]], axis=2)
    c = cos.reshape(-1, 1, 4, 32)
    s = sin.reshape(-1, 1, 4, 32)
    return (g * c - sw * s).reshape(grad.shape)


def attention_backward_xla(q, k, v, seg, lse, go):
    rows = q.shape[0]
    qs = q.reshape(2, 1024, 4, 64); ks = k.reshape(2, 1024, 4, 64); vs = v.reshape(2, 1024, 4, 64)
    gs = go.reshape(2, 1024, 4, 64)
    sg = seg.reshape(2, 1024)
    outs = []
    for s in range(2):
        sc = jnp.einsum("qhd,khd->hqk", qs[s], ks[s], preferred_element_type=F32)
        pos = jnp.arange(1024)
        vis = (pos[None, :] <= pos[:, None]) | ((sg[s][:, None] == sg[s][None, :]) & (sg[s][:, None] > 0))
        sc = jnp.where(vis[None], sc, MASKED)
        pr = jnp.exp(sc - lse[s * 4 : s * 4 + 4][:, :, None])
        gp = jnp.einsum("qhd,khd->hqk", gs[s], vs[s], preferred_element_type=F32)
        delta = jnp.sum(gp * pr, axis=-1, keepdims=True)
        ds = (pr * (gp - delta)).astype(BF16)
        dq = jnp.einsum("hqk,khd->qhd", ds, ks[s], preferred_element_type=F32) * HEAD_DIM**-0.5
        dk = jnp.einsum("hqk,qhd->khd", ds, qs[s], preferred_element_type=F32)
        dv = jnp.einsum("hqk,qhd->khd", pr.astype(BF16), gs[s], preferred_element_type=F32)
        outs.append([u.reshape(1024, 256) for u in (dq, dk, dv)])
    return tuple(jnp.concatenate([outs[0][n], outs[1][n]], axis=0) for n in range(3))


def on_device(
    dp,
    block_input,
    value_first,
    segment_ids,
    positions,
    gain_attn,
    query_weight,
    key_weight,
    value_weight,
    out_weight,
    gain_mlp,
    gate_weight,
    up_weight,
    down_weight,
    output_grad,
):
    ff = gate_weight.shape[1]
    wide = -(-ff // 256) * 256
    inputs = block_input.astype(F32)
    gains = jnp.stack([gain_attn, gain_mlp]).astype(F32)
    attn_gain, mlp_gain = gains[0], gains[1]
    cos, sin = rope_tables(positions)
    place_in = jnp.arange(segment_ids.shape[0], dtype=jnp.int32) % PIECE
    limits = jnp.where(segment_ids > 0, PIECE - 1, place_in)[None, :]
    qkv_shard = jnp.concatenate([query_weight, key_weight, value_weight], axis=1)
    ff_shard = jnp.concatenate(
        [widen(gate_weight, wide), widen(up_weight, wide), widen(down_weight.T, wide)], axis=1
    )
    (qkv_w, out_w, ff_w, normed_attn, q, k, v, attended, lse, grad_rows, hidden, normed_mlp) = first_stage(
        dp, block_input, output_grad, value_first, qkv_shard, out_weight.T, ff_shard, gains, cos, sin, limits
    )
    chip = lax.axis_index("tensor") // 2
    hidden_state = jnp.where(chip == 0, hidden[0], hidden[1])
    gate_full, up_full, down_t = ff_w[:, :ff], ff_w[:, wide : wide + ff], ff_w[:, 2 * wide : 2 * wide + ff]
    mlp_factor = lax.rsqrt(jnp.mean(hidden_state * hidden_state, axis=-1, keepdims=True) + EPSILON)
    attn_factor = lax.rsqrt(jnp.mean(inputs * inputs, axis=-1, keepdims=True) + EPSILON)
    gate_value = jnp.dot(normed_mlp, gate_full, preferred_element_type=jnp.float32)
    upward = jnp.dot(normed_mlp, up_full, preferred_element_type=jnp.float32)
    sigmoid_gate = jax.nn.sigmoid(gate_value)
    activated = (gate_value * sigmoid_gate * upward).astype(jnp.bfloat16)
    mlp_branch = lax.psum_scatter(
        dot_nt(activated, down_t).astype(jnp.bfloat16), "tensor", scatter_dimension=0, tiled=True
    ).astype(jnp.float32)
    block_output = (hidden_state + mlp_branch).astype(jnp.bfloat16)
    down_grad = jnp.dot(activated.T, grad_rows, preferred_element_type=jnp.float32)
    grad_act = jnp.dot(grad_rows, down_t, preferred_element_type=jnp.float32)
    grad_gate = (
        grad_act * upward * sigmoid_gate * (1.0 + gate_value * (1.0 - sigmoid_gate))
    ).astype(jnp.bfloat16)
    grad_up = (grad_act * gate_value * sigmoid_gate).astype(jnp.bfloat16)
    gate_grad = jnp.dot(normed_mlp.T, grad_gate, preferred_element_type=jnp.float32)
    up_grad = jnp.dot(normed_mlp.T, grad_up, preferred_element_type=jnp.float32)
    mlp_partial = dot_nt(grad_gate, gate_full) + dot_nt(grad_up, up_full)
    grad_normed_mlp = lax.psum_scatter(
        mlp_partial.astype(jnp.bfloat16), "tensor", scatter_dimension=0, tiled=True
    ).astype(jnp.float32)
    gate_sum, up_sum, down_sum = (
        lax.psum_scatter(gate_grad, "dp", scatter_dimension=0, tiled=True),
        lax.psum_scatter(up_grad, "dp", scatter_dimension=0, tiled=True),
        lax.psum_scatter(down_grad, "dp", scatter_dimension=1, tiled=True),
    )
    hidden_part, mlp_gain_part = norm_back(grad_normed_mlp, hidden_state, mlp_factor, mlp_gain)
    grad_hidden = output_grad.astype(jnp.float32) + hidden_part
    hidden_low = grad_hidden.astype(jnp.bfloat16)
    grad_hidden_rows = lax.all_gather(hidden_low, "tensor", axis=0, tiled=True)
    out_grad_part = jnp.dot(attended.T, grad_hidden_rows, preferred_element_type=jnp.float32)
    grad_attended = dot_nn(grad_hidden_rows, out_w).astype(jnp.bfloat16)
    dq, dk, dv = attention_backward_xla(q, k, v, segment_ids, lse, grad_attended)
    grad_query = unrotate(dq, cos, sin).astype(BF16)
    grad_key = unrotate(dk, cos, sin).astype(BF16)
    grad_value = (0.5 * dv).astype(BF16)
    value_first_grad = 0.5 * dv
    dqkv = jnp.concatenate([grad_query, grad_key, grad_value], axis=1)
    qkv_grad = jnp.dot(normed_attn.T, dqkv, preferred_element_type=jnp.float32)
    attn_partial = dot_nt(dqkv, qkv_w)
    grad_normed_attn = lax.psum_scatter(
        attn_partial.astype(jnp.bfloat16), "tensor", scatter_dimension=0, tiled=True
    ).astype(jnp.float32)
    qkv_sum = summed_on_arrival(qkv_grad.astype(BF16), "dp", 0)
    hw = value_first.shape[1]
    query_sum, key_sum, value_sum = (qkv_sum[:, n * hw : (n + 1) * hw] for n in range(3))
    out_sum = summed_on_arrival(out_grad_part.astype(BF16), "dp", 1)
    input_part, attn_gain_part = norm_back(grad_normed_attn, inputs, attn_factor, attn_gain)
    input_grad = grad_hidden + input_part
    gain_attn_grad, gain_mlp_grad = lax.psum((attn_gain_part, mlp_gain_part), ("dp", "tensor"))
    return (
        block_output,
        input_grad,
        value_first_grad,
        gain_attn_grad,
        query_sum,
        key_sum,
        value_sum,
        out_sum,
        gain_mlp_grad,
        gate_sum,
        up_sum,
        down_sum,
    )


def solution(mesh):
    rows = P(("dp", "tensor"), None)
    weight = P("dp", "tensor")
    across = P("tensor", "dp")
    return jax.shard_map(
        functools.partial(on_device, mesh.shape["dp"]),
        mesh=mesh,
        in_specs=(
            rows,
            weight,
            P("dp"),
            P("dp"),
            P(),
            weight,
            weight,
            weight,
            across,
            P(),
            weight,
            weight,
            across,
            rows,
        ),
        out_specs=(
            rows,
            rows,
            weight,
            P(),
            weight,
            weight,
            weight,
            across,
            P(),
            weight,
            weight,
            across,
        ),
        check_vma=False,
    )
```

```python
import functools

import jax
import jax.numpy as jnp
from jax import lax
from jax.experimental import pallas as pl
from jax.experimental.pallas import tpu as pltpu
from jax.sharding import PartitionSpec as P

HEAD_DIM = 64
SEQ_LEN = 1024
PIECE = 256
HALF = 512
TILE = 256
EPSILON = 1e-06
ROPE_BASE = 10000.0
MASKED = -1e30
MESH = pl.DeviceIdType.MESH
F32 = jnp.float32
BF16 = jnp.bfloat16
VMEM_LIMIT = 62 * 2**20


def dot_nn(a, b):
    return lax.dot_general(a, b, (((1,), (0,)), ((), ())), preferred_element_type=F32)


def dot_nt(a, b):
    return lax.dot_general(a, b, (((1,), (1,)), ((), ())), preferred_element_type=F32)


def dot_tn(a, b):
    return lax.dot_general(a, b, (((0,), (0,)), ((), ())), preferred_element_type=F32)


def rows_at(start, size):
    return pl.ds(pl.multiple_of(start, size), size)


class Place:
    def __init__(self, dp):
        self.d = lax.axis_index("dp")
        self.t = lax.axis_index("tensor")
        self.core = lax.rem(self.t, 2)
        self.chip = self.t // 2
        self.line = dp // 2
        self.y = lax.rem(self.d, 2)
        self.z = self.d // 2
        self.sibling = (self.d, self.t + 1 - 2 * self.core)
        self.across = (self.d, lax.rem(self.t + 2, 4))
        self.pair = (self.d + 1 - 2 * self.y, self.t)

    def ahead(self, k):
        return (2 * lax.rem(self.z + k, self.line) + self.y, self.t)

    def behind_z(self, k):
        return lax.rem(self.z + self.line - k, self.line)

    def greet(self, everyone=True):
        barrier = pltpu.get_barrier_semaphore()
        partners = [self.sibling, self.across]
        if everyone:
            partners.append(self.pair)
            partners.extend(self.ahead(k) for k in range(1, self.line))
        for who in partners:
            pl.semaphore_signal(barrier, inc=1, device_id=who, device_id_type=MESH)
        pl.semaphore_wait(barrier, len(partners))


def send(src, dst, sems, k, who):
    return pltpu.make_async_remote_copy(
        src_ref=src,
        dst_ref=dst,
        send_sem=sems[0].at[k],
        recv_sem=sems[1].at[k],
        device_id=who,
        device_id_type=MESH,
    )


class Gather:
    def __init__(self, place, shard, full, line_sems, pair_sems):
        self.p, self.shard, self.full = place, shard, full
        self.line_sems, self.pair_sems = line_sems, pair_sems
        self.r = shard.shape[0]

    def slot(self, z, y):
        return self.full.at[rows_at((2 * z + y) * self.r, self.r)]

    def start(self):
        p = self.p
        self.out = [send(self.shard, self.slot(p.z, p.y), self.pair_sems, 0, p.pair)]
        for k in range(1, p.line):
            self.out.append(
                send(self.shard, self.slot(p.z, p.y), self.line_sems, k - 1, p.ahead(k))
            )
        for copy in self.out:
            copy.start()
        self.full[rows_at((2 * p.z + p.y) * self.r, self.r), :] = self.shard[...]

    def relay(self, k):
        p = self.p
        here = self.slot(p.behind_z(k), p.y)
        send(here, here, self.line_sems, k - 1, p.pair).wait_recv()
        copy = send(here, here, self.pair_sems, k, p.pair)
        copy.start()
        self.out.append(copy)

    def finish(self):
        p = self.p
        for k in range(p.line):
            there = self.slot(p.behind_z(k), 1 - p.y)
            send(there, there, self.pair_sems, k, p.pair).wait_recv()

    def drain(self):
        for copy in self.out:
            copy.wait_send()


def swap_halves(u):
    lane = lax.broadcasted_iota(jnp.int32, u.shape, 1)
    low = lax.rem(lane, HEAD_DIM) < HEAD_DIM // 2
    return jnp.where(low, pltpu.roll(u, 96, 1), pltpu.roll(u, 32, 1))


def norm_factor(u):
    return lax.rsqrt(jnp.mean(u * u, axis=-1, keepdims=True) + EPSILON)


def attention_rows(seq, pair_of_heads, i, q, k, vt, limits, attended, lse):
    lane = lax.broadcasted_iota(jnp.int32, (TILE, 128), 1)
    key_in_piece = lax.broadcasted_iota(jnp.int32, (TILE, TILE), 0)
    lanes = pl.ds(pair_of_heads * 128, 128)
    rows = pl.ds(seq * SEQ_LEN + i * TILE, TILE)
    q2 = q[rows, lanes]
    shown = key_in_piece <= limits[:, rows]
    sides = []
    for a in range(2):
        qa = jnp.where((lane < HEAD_DIM) == (a == 0), q2, jnp.zeros_like(q2))
        vta = pl.ds(pair_of_heads * 128 + a * HEAD_DIM, HEAD_DIM)
        score = jnp.where(shown, dot_nt(k[rows, lanes], qa), MASKED)
        top = jnp.max(score, axis=0, keepdims=True)
        if i > 0:
            before = dot_nt(k[pl.ds(seq * SEQ_LEN, i * TILE), lanes], qa)
            top = jnp.maximum(top, jnp.max(before, axis=0, keepdims=True))
        weight = jnp.exp(score - top)
        total = jnp.sum(weight, axis=0, keepdims=True)
        out = dot_nn(vt[vta, pl.ds(i * TILE, TILE)], weight.astype(BF16))
        if i > 0:
            weight = jnp.exp(before - top)
            total = total + jnp.sum(weight, axis=0, keepdims=True)
            out = out + dot_nn(vt[vta, pl.ds(0, i * TILE)], weight.astype(BF16))
        sides.append(out * (1.0 / total))
        lse[pl.ds(seq * 4 + pair_of_heads * 2 + a, 1), pl.ds(i * TILE, TILE)] = top + jnp.log(total)
    attended[rows, lanes] = jnp.concatenate(sides, axis=0).T.astype(BF16)


def first_kernel(
    dp,
    x_own,
    og_own,
    value_first,
    qkv_shard,
    out_shard,
    ff_shard,
    gains,
    cosine,
    sine,
    limits,
    qkv_w,
    out_w,
    ff_w,
    normed,
    q,
    k,
    v,
    attended,
    lse,
    og,
    hidden,
    normed_mlp,
    xb,
    vt,
    half_out,
    half_in,
    sum_out,
    sum_in,
    group_sems_out,
    group_sems_in,
    core_sems_out,
    core_sems_in,
    line_out,
    line_in,
    pair_out,
    pair_in,
):
    p = Place(dp)
    group = (group_sems_out, group_sems_in)
    cores = (core_sems_out, core_sems_in)
    sent = []

    def go(copy):
        copy.start()
        sent.append(copy)

    def block(b):
        return rows_at(b * HALF, HALF)

    p.greet()
    gathers = []
    for n, (shard, full) in enumerate(((qkv_shard, qkv_w), (out_shard, out_w), (ff_shard, ff_w))):
        gathers.append(
            Gather(p, shard, full, (line_out.at[n], line_in.at[n]), (pair_out.at[n], pair_in.at[n]))
        )
    go(send(x_own, xb.at[p.chip], group, 0, p.across))
    gathers[0].start()
    gain_attn = gains[0:1, :]
    gain_mlp = gains[1:2, :]
    other = lax.rem(p.t + 2, 4)

    def norm_block(b, source):
        @pl.loop(0, HALF // TILE)
        def _(j):
            u = source[rows_at(j * TILE, TILE), :].astype(F32)
            normed[rows_at(b * HALF + j * TILE, TILE), :] = (
                u * norm_factor(u) * gain_attn
            ).astype(BF16)

    xb[p.chip] = x_own[...]
    norm_block(p.t, x_own)
    go(send(normed.at[block(p.t)], normed.at[block(p.t)], cores, 0, p.sibling))
    for n in range(1, p.line):
        gathers[0].relay(n)
    for g in gathers[1:]:
        g.start()
    there = xb.at[1 - p.chip]
    send(there, there, group, 0, p.across).wait_recv()
    own_rows = og.at[block(p.t)]
    go(send(og_own, own_rows, group, 1, p.across))
    go(send(og_own, own_rows, cores, 2, p.sibling))
    og[block(p.t), :] = og_own[...]
    norm_block(other, there)
    go(send(normed.at[block(other)], normed.at[block(other)], cores, 1, p.sibling))
    gathers[0].finish()
    sib = p.t + 1 - 2 * p.core
    for n, b in ((0, sib), (1, lax.rem(sib + 2, 4))):
        there = normed.at[block(b)]
        send(there, there, cores, n, p.sibling).wait_recv()

    def project(seq):
        @pl.loop(0, SEQ_LEN // TILE)
        def _(j):
            rows = rows_at(seq * SEQ_LEN + j * TILE, TILE)
            made = dot_nn(normed[rows, :], qkv_w[...])
            cos, sin = cosine[rows, :], sine[rows, :]
            for n in range(2):
                lanes = slice(n * 128, (n + 1) * 128)
                u = made[:, n * 128 : (n + 1) * 128]
                q[rows, lanes] = ((u * cos + swap_halves(u) * sin) * HEAD_DIM**-0.5).astype(BF16)
                u = made[:, 256 + n * 128 : 256 + (n + 1) * 128]
                k[rows, lanes] = (u * cos + swap_halves(u) * sin).astype(BF16)
            mixed = 0.5 * made[:, 512:768] + 0.5 * value_first[rows, :].astype(F32)
            v[rows, :] = mixed.astype(BF16)
            vt[:, rows_at(j * TILE, TILE)] = mixed.T.astype(BF16)

    def branch(seq):
        for h, add in ((1 - p.core, False), (p.core, True)):
            if add:
                there = half_in.at[seq]
                send(there, there, cores, 4 + seq, p.sibling).wait_recv()

            @pl.loop(0, HALF // TILE)
            def _(j):
                rows = rows_at(seq * SEQ_LEN + h * HALF + j * TILE, TILE)
                part = dot_nt(attended[rows, :], out_w[...])
                tile = rows_at(j * TILE, TILE)
                if add:
                    sum_out[seq, tile, :] = (part + half_in[seq, tile, :].astype(F32)).astype(BF16)
                else:
                    half_out[seq, tile, :] = part.astype(BF16)

            if add:
                go(send(sum_out.at[seq], sum_in.at[seq], group, 2 + seq, p.across))
            else:
                go(send(half_out.at[seq], half_in.at[seq], cores, 4 + seq, p.sibling))

    def finish_branch(seq):
        there = sum_in.at[seq]
        send(there, there, group, 2 + seq, p.across).wait_recv()

        @pl.loop(0, HALF // TILE)
        def _(j):
            tile = rows_at(j * TILE, TILE)
            both = sum_out[seq, tile, :].astype(F32) + sum_in[seq, tile, :].astype(F32)
            u = xb[seq, tile, :].astype(F32) + both
            hidden[seq, tile, :] = u
            normed_mlp[rows_at((2 * seq + p.core) * HALF + j * TILE, TILE), :] = (
                u * norm_factor(u) * gain_mlp
            ).astype(BF16)

        mine = normed_mlp.at[block(2 * seq + p.core)]
        go(send(mine, mine, cores, 6 + seq, p.sibling))

    for seq in range(2):
        project(seq)
        for heads in range(2):
            for i in range(SEQ_LEN // TILE):
                attention_rows(seq, heads, i, q, k, vt, limits, attended, lse)
            if seq == 0 and heads == 0:
                for n in range(1, p.line):
                    gathers[1].relay(n)
                gathers[1].finish()
        branch(seq)
        if seq == 0:
            for n in range(1, p.line):
                gathers[2].relay(n)
            there = og.at[block(other)]
            send(there, there, group, 1, p.across).wait_recv()
            go(send(there, there, cores, 3, p.sibling))
    for seq in range(2):
        finish_branch(seq)
    for n, b in ((2, sib), (3, lax.rem(sib + 2, 4))):
        there = og.at[block(b)]
        send(there, there, cores, n, p.sibling).wait_recv()
    for seq in range(2):
        there = normed_mlp.at[block(2 * seq + 1 - p.core)]
        send(there, there, cores, 6 + seq, p.sibling).wait_recv()
    gathers[2].finish()
    for copy in sent:
        copy.wait_send()
    for g in gathers:
        g.drain()


def first_stage(dp, x, og, vf, qkv_shard, out_shard, ff_shard, gains, cosine, sine, limits):
    rows = 4 * x.shape[0]
    width = x.shape[1]
    heads_width = vf.shape[1]
    line = dp // 2
    vmem = pl.BlockSpec(memory_space=pltpu.VMEM)
    shapes = [
        ((width, qkv_shard.shape[1]), BF16),
        ((width, out_shard.shape[1]), BF16),
        ((width, ff_shard.shape[1]), BF16),
        ((rows, width), BF16),
        ((rows, heads_width), BF16),
        ((rows, heads_width), BF16),
        ((rows, heads_width), BF16),
        ((rows, heads_width), BF16),
        ((8, SEQ_LEN), F32),
        ((rows, width), BF16),
        ((2, HALF, width), F32),
        ((rows, width), BF16),
    ]
    dma = pltpu.SemaphoreType.DMA
    return pl.pallas_call(
        functools.partial(first_kernel, dp),
        out_shape=[jax.ShapeDtypeStruct(s, t) for s, t in shapes],
        in_specs=[vmem] * 10,
        out_specs=[vmem] * len(shapes),
        scratch_shapes=[
            pltpu.VMEM((2, HALF, width), BF16),
            pltpu.VMEM((heads_width, SEQ_LEN), BF16),
            pltpu.VMEM((2, HALF, width), BF16),
            pltpu.VMEM((2, HALF, width), BF16),
            pltpu.VMEM((2, HALF, width), BF16),
            pltpu.VMEM((2, HALF, width), BF16),
            dma((4,)),
            dma((4,)),
            dma((8,)),
            dma((8,)),
            dma((3, max(line - 1, 1))),
            dma((3, max(line - 1, 1))),
            dma((3, line)),
            dma((3, line)),
        ],
        compiler_params=pltpu.CompilerParams(
            collective_id=0, has_side_effects=True, vmem_limit_bytes=VMEM_LIMIT
        ),
        name="attention_forward",
    )(x, og, vf, qkv_shard, out_shard, ff_shard, gains, cosine, sine, limits)


class Scatter:
    def __init__(self, place, full, pair_in, line_in, pair_sems, line_sems):
        self.p, self.full = place, full
        self.pair_in, self.line_in = pair_in, line_in
        self.pair_sems, self.line_sems = pair_sems, line_sems
        self.r = pair_in.shape[1]
        self.out = []

    def rows(self, k, y):
        z = lax.rem(self.p.z + k, self.p.line)
        return rows_at((2 * z + y) * self.r, self.r)

    def start(self):
        p = self.p
        for k in [*range(1, p.line), 0]:
            copy = send(
                self.full.at[self.rows(k, 1 - p.y)],
                self.pair_in.at[k],
                self.pair_sems,
                k,
                p.pair,
            )
            copy.start()
            self.out.append(copy)

    def relay(self, k):
        p = self.p
        there = self.pair_in.at[k]
        send(there, there, self.pair_sems, k, p.pair).wait_recv()
        mine = self.rows(k, p.y)
        self.full[mine, :] = (self.full[mine, :].astype(F32) + there[...].astype(F32)).astype(BF16)
        copy = send(
            self.full.at[mine], self.line_in.at[k - 1], self.line_sems, k - 1, p.ahead(k)
        )
        copy.start()
        self.out.append(copy)

    def finish(self, total):
        p = self.p
        there = self.pair_in.at[0]
        send(there, there, self.pair_sems, 0, p.pair).wait_recv()
        whole = self.full[self.rows(0, p.y), :].astype(F32) + there[...].astype(F32)
        for k in range(p.line - 1):
            there = self.line_in.at[k]
            send(there, there, self.line_sems, k, p.pair).wait_recv()
            whole = whole + there[...].astype(F32)
        total[...] = whole

    def drain(self):
        for copy in self.out:
            copy.wait_send()


def norm_pull(grad, u, gain):
    r = norm_factor(u)
    scaled = grad * gain
    back = r * scaled - u * (r * r * r) * jnp.mean(scaled * u, axis=-1, keepdims=True)
    return back, grad * u * r


def second_kernel(
    dp,
    normed_mlp,
    og,
    ff_w,
    hidden,
    gains,
    block_output,
    hidden_low,
    grad_hidden,
    ff_grad,
    gain_part,
    units,
    g_half_out,
    g_half_in,
    g_sum_out,
    g_sum_in,
    m_half_out,
    m_half_in,
    m_sum,
    m_in,
    group_sems_out,
    group_sems_in,
    core_sems_out,
    core_sems_in,
):
    p = Place(dp)
    group = (group_sems_out, group_sems_in)
    cores = (core_sems_out, core_sems_in)
    wide = ff_w.shape[1] // 3
    sent = []

    def go(copy):
        copy.start()
        sent.append(copy)

    def block(b):
        return rows_at(b * HALF, HALF)

    p.greet(everyone=False)
    gain_mlp = gains[1:2, :]

    def feed(seq):
        for h, add in ((1 - p.core, False), (p.core, True)):
            if add:
                for there, n in ((g_half_in.at[seq], seq), (m_half_in.at[seq], 2 + seq)):
                    send(there, there, cores, n, p.sibling).wait_recv()

            @pl.loop(0, HALF // TILE)
            def _(j):
                rows = rows_at(seq * SEQ_LEN + h * HALF + j * TILE, TILE)
                tile = rows_at(j * TILE, TILE)
                made = dot_nn(normed_mlp[rows, :], ff_w[:, : 2 * wide])
                grad_act = dot_nn(og[rows, :], ff_w[:, 2 * wide :])
                gate, up = made[:, :wide], made[:, wide:]
                sig = 1.0 / (1.0 + jnp.exp(-gate))
                swish = gate * sig
                act = (swish * up).astype(BF16)
                units[rows, :wide] = (grad_act * up * sig * (1.0 + gate * (1.0 - sig))).astype(BF16)
                units[rows, wide : 2 * wide] = (grad_act * swish).astype(BF16)
                units[rows, 2 * wide :] = act
                down = dot_nt(act, ff_w[:, 2 * wide :])
                back = dot_nt(units[rows, : 2 * wide], ff_w[:, : 2 * wide])
                if add:
                    g_sum_out[seq, tile, :] = (back + g_half_in[seq, tile, :].astype(F32)).astype(
                        BF16
                    )
                    m_sum[seq, tile, :] = (down + m_half_in[seq, tile, :].astype(F32)).astype(BF16)
                else:
                    g_half_out[seq, tile, :] = back.astype(BF16)
                    m_half_out[seq, tile, :] = down.astype(BF16)

            if add:
                go(send(g_sum_out.at[seq], g_sum_in.at[seq], group, seq, p.across))

                @pl.when(p.chip != seq)
                def _():
                    send(m_sum.at[seq], m_in, group, 2, p.across).start()
            else:
                go(send(g_half_out.at[seq], g_half_in.at[seq], cores, seq, p.sibling))
                go(send(m_half_out.at[seq], m_half_in.at[seq], cores, 2 + seq, p.sibling))

    def pull(seq):
        there = g_sum_in.at[seq]
        send(there, there, group, seq, p.across).wait_recv()

        @pl.loop(0, HALF // TILE)
        def _(j):
            tile = rows_at(j * TILE, TILE)
            rows = rows_at((2 * seq + p.core) * HALF + j * TILE, TILE)
            grad = g_sum_out[seq, tile, :].astype(F32) + g_sum_in[seq, tile, :].astype(F32)
            back, gain_rows = norm_pull(grad, hidden[seq, tile, :], gain_mlp)
            whole = og[rows, :].astype(F32) + back
            hidden_low[rows, :] = whole.astype(BF16)

            @pl.when(p.chip == seq)
            def _():
                grad_hidden[tile, :] = whole
                gain_part[...] += jnp.sum(gain_rows, axis=0, keepdims=True)

        mine = hidden_low.at[block(2 * seq + p.core)]
        go(send(mine, mine, cores, 4 + seq, p.sibling))

    gain_part[...] = jnp.zeros_like(gain_part)
    feed(0)
    feed(1)
    pull(0)

    @pl.loop(0, ff_w.shape[0] // TILE)
    def _(j):
        cols = rows_at(j * TILE, TILE)
        for n, left in ((0, normed_mlp), (1, normed_mlp), (2, og)):
            ff_grad[cols, n * wide : (n + 1) * wide] = dot_tn(
                left[:, cols], units[:, n * wide : (n + 1) * wide]
            ).astype(BF16)

    pull(1)
    send(m_in, m_in, group, 2, p.across).wait_recv()

    @pl.loop(0, HALF // TILE)
    def _(j):
        tile = rows_at(j * TILE, TILE)
        both = m_sum[p.chip, tile, :].astype(F32) + m_in[tile, :].astype(F32)
        block_output[tile, :] = (hidden[p.chip, tile, :] + both).astype(BF16)

    for seq in range(2):
        there = hidden_low.at[block(2 * seq + 1 - p.core)]
        send(there, there, cores, 4 + seq, p.sibling).wait_recv()
    send(m_sum.at[1 - p.chip], m_in, group, 2, p.across).wait_send()
    for copy in sent:
        copy.wait_send()


def second_stage(dp, normed_mlp, og, ff_w, hidden, gains):
    rows, width = normed_mlp.shape
    vmem = pl.BlockSpec(memory_space=pltpu.VMEM)
    shapes = [
        ((HALF, width), BF16),
        ((rows, width), BF16),
        ((HALF, width), F32),
        (ff_w.shape, BF16),
        ((1, width), F32),
    ]
    dma = pltpu.SemaphoreType.DMA
    two = pltpu.VMEM((2, HALF, width), BF16)
    return pl.pallas_call(
        functools.partial(second_kernel, dp),
        out_shape=[jax.ShapeDtypeStruct(s, t) for s, t in shapes],
        in_specs=[vmem] * 5,
        out_specs=[vmem] * len(shapes),
        scratch_shapes=[
            pltpu.VMEM((rows, ff_w.shape[1]), BF16),
            two,
            two,
            two,
            two,
            two,
            two,
            two,
            pltpu.VMEM((HALF, width), BF16),
            dma((3,)),
            dma((3,)),
            dma((6,)),
            dma((6,)),
        ],
        compiler_params=pltpu.CompilerParams(
            collective_id=1, has_side_effects=True, vmem_limit_bytes=VMEM_LIMIT
        ),
        name="feed_forward",
    )(normed_mlp, og, ff_w, hidden, gains)


def attention_rows_back(seq, heads, i, q, k, v, kt, limits, lse, attended, grad_att, dk, dv, cos, sin, dqkv):
    lane = lax.broadcasted_iota(jnp.int32, (TILE, 128), 1)
    key_in_piece = lax.broadcasted_iota(jnp.int32, (TILE, TILE), 0)
    lanes = pl.ds(heads * 128, 128)
    local = pl.ds(i * TILE, TILE)
    rows = pl.ds(seq * SEQ_LEN + i * TILE, TILE)
    first = i == SEQ_LEN // TILE - 1
    q2, g2 = q[rows, lanes], grad_att[local, lanes]
    shown = key_in_piece <= limits[:, rows]
    products = (g2.astype(F32) * attended[rows, lanes].astype(F32)).T
    parts = [(i * TILE, TILE, True)]
    if i > 0:
        parts.append((0, i * TILE, False))
    sides = [None, None]
    for start, size, diagonal in parts:
        keys = pl.ds(seq * SEQ_LEN + start, size)
        here = pl.ds(start, size)
        dk_part, dv_part = 0.0, 0.0
        for a in range(2):
            mine = (lane < HEAD_DIM) == (a == 0)
            qa = jnp.where(mine, q2, jnp.zeros_like(q2))
            ga = jnp.where(mine, g2, jnp.zeros_like(g2))
            delta = jnp.sum(products[a * HEAD_DIM : (a + 1) * HEAD_DIM], axis=0, keepdims=True)
            stat = lse[pl.ds(seq * 4 + heads * 2 + a, 1), local]
            score = dot_nt(k[keys, lanes], qa)
            if diagonal:
                score = jnp.where(shown, score, MASKED)
            prob = jnp.exp(score - stat)
            grad_prob = dot_nt(v[keys, lanes], ga)
            grad_score = (prob * (grad_prob - delta)).astype(BF16)
            dv_part = dv_part + dot_nn(prob.astype(BF16), ga)
            dk_part = dk_part + dot_nn(grad_score, qa)
            side = dot_nn(kt[pl.ds(heads * 128 + a * HEAD_DIM, HEAD_DIM), here], grad_score)
            sides[a] = side if sides[a] is None else sides[a] + side
        if first:
            dk[here, :] = dk_part
            dv[here, :] = dv_part
        else:
            dk[here, :] += dk_part
            dv[here, :] += dv_part
    dq = jnp.concatenate(sides, axis=0).T * HEAD_DIM**-0.5
    dqkv[rows, lanes] = (dq * cos[rows, :] - swap_halves(dq) * sin[rows, :]).astype(BF16)


def third_kernel(
    dp,
    hidden_low,
    attended,
    q,
    k,
    v,
    lse,
    out_w,
    qkv_w,
    normed,
    ff_grad_in,
    x_own,
    grad_hidden,
    cos,
    sin,
    limits,
    gains,
    gain_mlp_part,
    input_grad,
    value_first_grad,
    attn_sum,
    ff_sum,
    gain_grads,
    ff_grad,
    attn_grad,
    kt,
    grad_att,
    dk,
    dv,
    dqkv,
    half_out,
    half_in,
    sums,
    sum_in,
    ff_pair_in,
    ff_line_in,
    attn_pair_in,
    attn_line_in,
    gain_acc,
    gain_in,
    group_sems_out,
    group_sems_in,
    core_sems_out,
    core_sems_in,
    line_out,
    line_in,
    pair_out,
    pair_in,
    gain_sems_out,
    gain_sems_in,
):
    p = Place(dp)
    group = (group_sems_out, group_sems_in)
    cores = (core_sems_out, core_sems_in)
    hw = q.shape[1]
    sent = []

    def go(copy):
        copy.start()
        sent.append(copy)

    p.greet()
    ff_grad[...] = ff_grad_in[...]
    ff = Scatter(
        p,
        ff_grad,
        ff_pair_in,
        ff_line_in,
        (pair_out.at[0], pair_in.at[0]),
        (line_out.at[0], line_in.at[0]),
    )
    attn = Scatter(
        p,
        attn_grad,
        attn_pair_in,
        attn_line_in,
        (pair_out.at[1], pair_in.at[1]),
        (line_out.at[1], line_in.at[1]),
    )
    ff.start()

    @pl.loop(0, normed.shape[1] // TILE)
    def _(j):
        cols = rows_at(j * TILE, TILE)
        attn_grad[cols, 3 * hw :] = dot_tn(hidden_low[:, cols], attended[...]).astype(BF16)

    def heads_back(seq, heads):
        for i in reversed(range(SEQ_LEN // TILE)):
            attention_rows_back(
                seq, heads, i, q, k, v, kt, limits, lse, attended, grad_att, dk, dv, cos, sin, dqkv
            )

        @pl.loop(0, SEQ_LEN // TILE)
        def _(j):
            local = rows_at(j * TILE, TILE)
            rows = rows_at(seq * SEQ_LEN + j * TILE, TILE)
            u = dk[local, :]
            dqkv[rows, hw + heads * 128 : hw + (heads + 1) * 128] = (
                u * cos[rows, :] - swap_halves(u) * sin[rows, :]
            ).astype(BF16)
            half = 0.5 * dv[local, :]
            dqkv[rows, 2 * hw + heads * 128 : 2 * hw + (heads + 1) * 128] = half.astype(BF16)
            value_first_grad[rows, heads * 128 : (heads + 1) * 128] = half

    def prepare(seq):
        @pl.loop(0, SEQ_LEN // TILE)
        def _(j):
            local = rows_at(j * TILE, TILE)
            rows = rows_at(seq * SEQ_LEN + j * TILE, TILE)
            grad_att[local, :] = dot_nn(hidden_low[rows, :], out_w[...]).astype(BF16)
            kt[:, local] = k[rows, :].astype(F32).T.astype(BF16)

    def branch_back(seq):
        for h, add in ((1 - p.core, False), (p.core, True)):
            if add:
                there = half_in.at[seq]
                send(there, there, cores, seq, p.sibling).wait_recv()

            @pl.loop(0, HALF // TILE)
            def _(j):
                rows = rows_at(seq * SEQ_LEN + h * HALF + j * TILE, TILE)
                tile = rows_at(j * TILE, TILE)
                part = dot_nt(dqkv[rows, :], qkv_w[...])
                if add:
                    sums[seq, tile, :] = (part + half_in[seq, tile, :].astype(F32)).astype(BF16)
                else:
                    half_out[seq, tile, :] = part.astype(BF16)

            if add:

                @pl.when(p.chip != seq)
                def _():
                    send(sums.at[seq], sum_in, group, 0, p.across).start()
            else:
                go(send(half_out.at[seq], half_in.at[seq], cores, seq, p.sibling))

    relays = list(range(1, p.line))
    for seq in range(2):
        prepare(seq)
        for heads in range(2):
            heads_back(seq, heads)
            if relays and (seq, heads) != (0, 0):
                ff.relay(relays.pop(0))
        if seq == 0:
            branch_back(0)
    while relays:
        ff.relay(relays.pop(0))

    @pl.loop(0, normed.shape[1] // TILE)
    def _(j):
        cols = rows_at(j * TILE, TILE)
        attn_grad[cols, : 3 * hw] = dot_tn(normed[:, cols], dqkv[...]).astype(BF16)

    attn.start()
    branch_back(1)
    for n in range(1, p.line):
        attn.relay(n)
    send(sum_in, sum_in, group, 0, p.across).wait_recv()
    gain_attn = gains[0:1, :]
    gain_acc[0:1, :] = jnp.zeros_like(gain_acc[0:1, :])
    gain_acc[1:2, :] = gain_mlp_part[...]

    @pl.loop(0, HALF // TILE)
    def _(j):
        tile = rows_at(j * TILE, TILE)
        grad = sums[p.chip, tile, :].astype(F32) + sum_in[tile, :].astype(F32)
        back, gain_rows = norm_pull(grad, x_own[tile, :].astype(F32), gain_attn)
        input_grad[tile, :] = grad_hidden[tile, :] + back
        gain_acc[0:1, :] += jnp.sum(gain_rows, axis=0, keepdims=True)

    gain_sems = (gain_sems_out, gain_sems_in)

    def exchange(partners, first):
        copies = []
        for n, who in enumerate(partners):
            copy = send(gain_acc, gain_in.at[first + n], gain_sems, first + n, who)
            copy.start()
            copies.append(copy)
        for copy in copies:
            copy.wait()
        whole = gain_acc[...]
        for n in range(len(partners)):
            whole = whole + gain_in[first + n]
        gain_acc[...] = whole

    exchange([p.sibling], 0)
    exchange([p.across], 1)
    exchange([p.pair], 2)
    if p.line > 1:
        exchange([p.ahead(n) for n in range(1, p.line)], 3)
    gain_grads[...] = gain_acc[...]
    ff.finish(ff_sum)
    attn.finish(attn_sum)
    send(sums.at[1 - p.chip], sum_in, group, 0, p.across).wait_send()
    for copy in sent:
        copy.wait_send()
    ff.drain()
    attn.drain()


def third_stage(dp, hidden_low, attended, q, k, v, lse, out_w, qkv_w, normed, ff_grad, x, *rest):
    rows, width = normed.shape
    hw = q.shape[1]
    line = dp // 2
    r = width // dp
    vmem = pl.BlockSpec(memory_space=pltpu.VMEM)
    shapes = [
        ((HALF, width), F32),
        ((rows, hw), F32),
        ((r, 4 * hw), F32),
        ((r, ff_grad.shape[1]), F32),
        ((2, width), F32),
    ]
    dma = pltpu.SemaphoreType.DMA
    two = pltpu.VMEM((2, HALF, width), BF16)
    hops = max(line - 1, 1)
    return pl.pallas_call(
        functools.partial(third_kernel, dp),
        out_shape=[jax.ShapeDtypeStruct(s, t) for s, t in shapes],
        in_specs=[vmem] * (11 + len(rest)),
        out_specs=[vmem] * len(shapes),
        scratch_shapes=[
            pltpu.VMEM(ff_grad.shape, BF16),
            pltpu.VMEM((width, 4 * hw), BF16),
            pltpu.VMEM((hw, SEQ_LEN), BF16),
            pltpu.VMEM((SEQ_LEN, hw), BF16),
            pltpu.VMEM((SEQ_LEN, 128), F32),
            pltpu.VMEM((SEQ_LEN, 128), F32),
            pltpu.VMEM((rows, 3 * hw), BF16),
            two,
            two,
            two,
            pltpu.VMEM((HALF, width), BF16),
            pltpu.VMEM((line, r, ff_grad.shape[1]), BF16),
            pltpu.VMEM((hops, r, ff_grad.shape[1]), BF16),
            pltpu.VMEM((line, r, 4 * hw), BF16),
            pltpu.VMEM((hops, r, 4 * hw), BF16),
            pltpu.VMEM((2, width), F32),
            pltpu.VMEM((2 + line, 2, width), F32),
            dma((1,)),
            dma((1,)),
            dma((2,)),
            dma((2,)),
            dma((2, hops)),
            dma((2, hops)),
            dma((2, line)),
            dma((2, line)),
            dma((2 + line,)),
            dma((2 + line,)),
        ],
        compiler_params=pltpu.CompilerParams(
            collective_id=2, has_side_effects=True, vmem_limit_bytes=VMEM_LIMIT
        ),
        name="attention_backward",
    )(hidden_low, attended, q, k, v, lse, out_w, qkv_w, normed, ff_grad, x, *rest)


def rope_tables(positions):
    half = HEAD_DIM // 2
    frequency = ROPE_BASE ** (-(2.0 * jnp.arange(half).astype(F32)) / HEAD_DIM)
    angles = positions.astype(F32)[:, None] * frequency[None, :]
    cos, sin = jnp.cos(angles), jnp.sin(angles)
    return (
        jnp.concatenate([cos, cos, cos, cos], axis=1),
        jnp.concatenate([-sin, sin, -sin, sin], axis=1),
    )


def widen(weight, width):
    return jnp.pad(weight, ((0, 0), (0, width - weight.shape[1])))


def on_device(
    dp,
    block_input,
    value_first,
    segment_ids,
    positions,
    gain_attn,
    query_weight,
    key_weight,
    value_weight,
    out_weight,
    gain_mlp,
    gate_weight,
    up_weight,
    down_weight,
    output_grad,
):
    ff = gate_weight.shape[1]
    wide = -(-ff // 256) * 256
    gains = jnp.stack([gain_attn, gain_mlp]).astype(F32)
    cos, sin = rope_tables(positions)
    place_in = jnp.arange(segment_ids.shape[0], dtype=jnp.int32) % PIECE
    limits = jnp.where(segment_ids > 0, PIECE - 1, place_in)[None, :]
    qkv_shard = jnp.concatenate([query_weight, key_weight, value_weight], axis=1)
    ff_shard = jnp.concatenate(
        [widen(gate_weight, wide), widen(up_weight, wide), widen(down_weight.T, wide)], axis=1
    )
    (qkv_w, out_w, ff_w, normed, q, k, v, attended, lse, og, hidden, normed_mlp) = first_stage(
        dp,
        block_input,
        output_grad,
        value_first,
        qkv_shard,
        out_weight.T,
        ff_shard,
        gains,
        cos,
        sin,
        limits,
    )
    block_output, hidden_low, grad_hidden, ff_grad, gain_part = second_stage(
        dp, normed_mlp, og, ff_w, hidden, gains
    )
    input_grad, value_first_grad, attn_sum, ff_sum, gain_grads = third_stage(
        dp,
        hidden_low,
        attended,
        q,
        k,
        v,
        lse,
        out_w,
        qkv_w,
        normed,
        ff_grad,
        block_input,
        grad_hidden,
        cos,
        sin,
        limits,
        gains,
        gain_part,
    )
    hw = value_first.shape[1]
    query_sum, key_sum, value_sum = (attn_sum[:, n * hw : (n + 1) * hw] for n in range(3))
    out_sum = attn_sum[:, 3 * hw :].T
    gate_sum, up_sum = ff_sum[:, :ff], ff_sum[:, wide : wide + ff]
    down_sum = ff_sum[:, 2 * wide : 2 * wide + ff].T
    gain_attn_grad, gain_mlp_grad = gain_grads[0], gain_grads[1]
    return (
        block_output,
        input_grad,
        value_first_grad,
        gain_attn_grad,
        query_sum,
        key_sum,
        value_sum,
        out_sum,
        gain_mlp_grad,
        gate_sum,
        up_sum,
        down_sum,
    )


def solution(mesh):
    rows = P(("dp", "tensor"), None)
    weight = P("dp", "tensor")
    across = P("tensor", "dp")
    return jax.shard_map(
        functools.partial(on_device, mesh.shape["dp"]),
        mesh=mesh,
        in_specs=(
            rows,
            weight,
            P("dp"),
            P("dp"),
            P(),
            weight,
            weight,
            weight,
            across,
            P(),
            weight,
            weight,
            across,
            rows,
        ),
        out_specs=(
            rows,
            rows,
            weight,
            P(),
            weight,
            weight,
            weight,
            across,
            P(),
            weight,
            weight,
            across,
        ),
        check_vma=False,
    )
```

```python
import functools

import jax
import jax.numpy as jnp
from jax import lax
from jax.experimental import pallas as pl
from jax.experimental.pallas import tpu as pltpu
from jax.sharding import PartitionSpec as P

HEAD_DIM = 64
SEQ_LEN = 1024
SEQS = 2
PIECE = 256
HALF = 512
TILE = 256
EPSILON = 1e-06
ROPE_BASE = 10000.0
MASKED = -1e30
MESH = pl.DeviceIdType.MESH
F32 = jnp.float32
BF16 = jnp.bfloat16
VMEM_LIMIT = 639 * 2**20 // 10


def dot_nn(a, b):
    return lax.dot_general(a, b, (((1,), (0,)), ((), ())), preferred_element_type=F32)


def dot_nt(a, b):
    return lax.dot_general(a, b, (((1,), (1,)), ((), ())), preferred_element_type=F32)


def dot_tn(a, b):
    return lax.dot_general(a, b, (((0,), (0,)), ((), ())), preferred_element_type=F32)


def rows_at(start, size):
    return pl.ds(pl.multiple_of(start, size), size)


def block(b):
    return rows_at(b * HALF, HALF)


class Place:
    def __init__(self, dp):
        self.d = lax.axis_index("dp")
        self.t = lax.axis_index("tensor")
        self.core = lax.rem(self.t, 2)
        self.chip = self.t // 2
        self.line = dp // 2
        self.y = lax.rem(self.d, 2)
        self.z = self.d // 2
        self.sibling = (self.d, self.t + 1 - 2 * self.core)
        self.across = (self.d, lax.rem(self.t + 2, 4))
        self.diagonal = (self.d, lax.rem(self.t + 3 - 2 * self.core, 4))
        self.pair = (self.d + 1 - 2 * self.y, self.t)
        self.up = (self.d + 2, self.t)
        self.down = (self.d - 2, self.t)

    def ahead(self, k):
        return (2 * lax.rem(self.z + k, self.line) + self.y, self.t)

    def behind(self, k):
        return (2 * lax.rem(self.z + self.line - k, self.line) + self.y, self.t)

    def greet(self):
        barrier = pltpu.get_barrier_semaphore()
        partners = [self.sibling, self.across, self.diagonal, self.pair]
        partners.extend(self.ahead(k) for k in range(1, self.line))
        for who in partners:
            tell(barrier, who)
        pl.semaphore_wait(barrier, len(partners))


def tell(sem, who):
    pl.semaphore_signal(sem, inc=1, device_id=who, device_id_type=MESH)


def send(src, dst, sems, k, who):
    return pltpu.make_async_remote_copy(
        src_ref=src,
        dst_ref=dst,
        send_sem=sems[0].at[k],
        recv_sem=sems[1].at[k],
        device_id=who,
        device_id_type=MESH,
    )


class Gather:
    def __init__(self, place, full, rows, up_sems, down_sems, pair_sems):
        self.p, self.full, self.r = place, full, rows
        self.up_sems, self.down_sems, self.pair_sems = up_sems, down_sems, pair_sems

    def slot(self, z, y):
        return self.full.at[rows_at((2 * z + y) * self.r, self.r)]

    def copies(self, k):
        p = self.p
        found = []
        for z, exists, sems, onward, to in (
            (p.z - k, p.z >= k, self.up_sems, p.z + 1 < p.line, p.up),
            (p.z + k, p.z + k < p.line, self.down_sems, p.z >= 1, p.down),
        ):
            found.append((z, exists, sems, onward, to))
        return found

    def start_line(self):
        p = self.p
        here = self.slot(p.z, p.y)
        for z, exists, sems, onward, to in self.copies(0):

            @pl.when(onward)
            def _():
                send(here, here, sems, 0, to).start()

    def start_pair(self):
        here = self.slot(self.p.z, self.p.y)
        send(here, here, self.pair_sems, self.p.z, self.p.pair).start()

    def relay(self, k):
        p = self.p
        for z, exists, sems, onward, to in self.copies(k):

            @pl.when(exists)
            def _():
                here = self.slot(z, p.y)
                send(here, here, sems, k - 1, to).wait_recv()

                @pl.when(onward)
                def _():
                    send(here, here, sems, k, to).start()

                send(here, here, self.pair_sems, z, p.pair).start()

    def finish(self):
        p = self.p
        for z in range(p.line):
            there = self.slot(z, 1 - p.y)
            send(there, there, self.pair_sems, z, p.pair).wait_recv()

    def drain(self):
        p = self.p
        for z in range(p.line):
            here = self.slot(z, p.y)
            send(here, here, self.pair_sems, z, p.pair).wait_send()
        for k in range(p.line - 1):
            for z, exists, sems, onward, to in self.copies(k):

                @pl.when(jnp.logical_and(exists, onward))
                def _():
                    here = self.slot(z, p.y)
                    send(here, here, sems, k, to).wait_send()


class Scatter:
    def __init__(self, place, full, pair_in, line_in, pair_sems, line_sems, free=None):
        self.p, self.full = place, full
        self.pair_in, self.line_in = pair_in, line_in
        self.pair_sems, self.line_sems = pair_sems, line_sems
        self.free = free
        self.r = full.shape[0] // (2 * place.line)
        self.out = []

    def rows(self, k, y):
        z = lax.rem(self.p.z + k, self.p.line)
        return rows_at((2 * z + y) * self.r, self.r)

    def start(self):
        p = self.p
        if self.free is not None:
            pl.semaphore_wait(self.free.at[0], 1)
        for k in [*range(1, p.line), 0]:
            copy = send(
                self.full.at[self.rows(k, 1 - p.y)], self.pair_in(k), self.pair_sems, k, p.pair
            )
            copy.start()
            self.out.append(copy)

    def relay(self, k):
        p = self.p
        there = self.pair_in(k)
        send(there, there, self.pair_sems, k, p.pair).wait_recv()
        mine = self.rows(k, p.y)
        self.full[mine, :] = (self.full[mine, :].astype(F32) + there[...].astype(F32)).astype(BF16)
        if self.free is not None:
            pl.semaphore_wait(self.free.at[k], 1)
        copy = send(self.full.at[mine], self.line_in(k), self.line_sems, k - 1, p.ahead(k))
        copy.start()
        self.out.append(copy)

    def finish(self):
        p = self.p
        there = self.pair_in(0)
        send(there, there, self.pair_sems, 0, p.pair).wait_recv()
        for k in range(1, p.line):
            there = self.line_in(k)
            send(there, there, self.line_sems, k - 1, p.pair).wait_recv()

    def total(self, lanes):
        mine = self.rows(0, self.p.y)
        whole = self.full[mine, lanes].astype(F32) + self.pair_in(0)[:, lanes].astype(F32)
        for k in range(1, self.p.line):
            whole = whole + self.line_in(k)[:, lanes].astype(F32)
        return whole

    def drain(self):
        for copy in self.out:
            copy.wait_send()


def swap_halves(u):
    lane = lax.broadcasted_iota(jnp.int32, u.shape, 1)
    low = lax.rem(lane, HEAD_DIM) < HEAD_DIM // 2
    return jnp.where(low, pltpu.roll(u, 96, 1), pltpu.roll(u, 32, 1))


def norm_factor(u):
    return lax.rsqrt(jnp.mean(u * u, axis=-1, keepdims=True) + EPSILON)


def norm_pull(grad, u, gain):
    r = norm_factor(u)
    scaled = grad * gain
    back = r * scaled - u * (r * r * r) * jnp.mean(scaled * u, axis=-1, keepdims=True)
    return back, grad * u * r


def visible(segments):
    key = lax.broadcasted_iota(jnp.int32, (TILE, TILE), 0)
    query = lax.broadcasted_iota(jnp.int32, (TILE, TILE), 1)
    return jnp.logical_or(key <= query, segments > 0)


def attention_rows(seq, heads, i, q, k, vt, segments, attended, lse):
    lane = lax.broadcasted_iota(jnp.int32, (TILE, 128), 1)
    lanes = pl.ds(heads * 128, 128)
    rows = pl.ds(seq * SEQ_LEN + i * TILE, TILE)
    q2 = q[rows, lanes]
    shown = visible(segments[:, rows])
    sides = []
    for a in range(2):
        qa = jnp.where((lane < HEAD_DIM) == (a == 0), q2, jnp.zeros_like(q2))
        vta = pl.ds(heads * 128 + a * HEAD_DIM, HEAD_DIM)
        score = jnp.where(shown, dot_nt(k[rows, lanes], qa), MASKED)
        top = jnp.max(score, axis=0, keepdims=True)
        if i > 0:
            before = dot_nt(k[pl.ds(seq * SEQ_LEN, i * TILE), lanes], qa)
            top = jnp.maximum(top, jnp.max(before, axis=0, keepdims=True))
        weight = jnp.exp(score - top)
        total = jnp.sum(weight, axis=0, keepdims=True)
        out = dot_nn(vt[vta, pl.ds(i * TILE, TILE)], weight.astype(BF16))
        if i > 0:
            weight = jnp.exp(before - top)
            total = total + jnp.sum(weight, axis=0, keepdims=True)
            out = out + dot_nn(vt[vta, pl.ds(0, i * TILE)], weight.astype(BF16))
        sides.append(out * (1.0 / total))
        lse[pl.ds(seq * 4 + heads * 2 + a, 1), pl.ds(i * TILE, TILE)] = top + jnp.log(total)
    attended[rows, lanes] = jnp.concatenate(sides, axis=0).T.astype(BF16)


def attention_rows_back(
    seq, heads, i, q, k, v, kt, segments, lse, attended, grad_att, dk, dv, cos, sin, dqkv
):
    lane = lax.broadcasted_iota(jnp.int32, (TILE, 128), 1)
    lanes = pl.ds(heads * 128, 128)
    local = pl.ds(i * TILE, TILE)
    rows = pl.ds(seq * SEQ_LEN + i * TILE, TILE)
    first = i == SEQ_LEN // TILE - 1
    q2, g2 = q[rows, lanes], grad_att(i, heads)
    shown = visible(segments[:, rows])
    products = (g2.astype(F32) * attended[rows, lanes].astype(F32)).T
    parts = [(i * TILE, TILE, True)]
    if i > 0:
        parts.append((0, i * TILE, False))
    sides = [None, None]
    for start, size, diagonal in parts:
        keys = pl.ds(seq * SEQ_LEN + start, size)
        here = pl.ds(start, size)
        dk_part, dv_part = 0.0, 0.0
        for a in range(2):
            mine = (lane < HEAD_DIM) == (a == 0)
            qa = jnp.where(mine, q2, jnp.zeros_like(q2))
            ga = jnp.where(mine, g2, jnp.zeros_like(g2))
            delta = jnp.sum(products[a * HEAD_DIM : (a + 1) * HEAD_DIM], axis=0, keepdims=True)
            stat = lse[pl.ds(seq * 4 + heads * 2 + a, 1), local]
            score = dot_nt(k[keys, lanes], qa)
            if diagonal:
                score = jnp.where(shown, score, MASKED)
            prob = jnp.exp(score - stat)
            grad_prob = dot_nt(v[keys, lanes], ga)
            grad_score = (prob * (grad_prob - delta)).astype(BF16)
            dv_part = dv_part + dot_nn(prob.astype(BF16), ga)
            dk_part = dk_part + dot_nn(grad_score, qa)
            side = dot_nn(kt[pl.ds(heads * 128 + a * HEAD_DIM, HEAD_DIM), here], grad_score)
            sides[a] = side if sides[a] is None else sides[a] + side
        if first:
            dk[here, :] = dk_part
            dv[here, :] = dv_part
        else:
            dk[here, :] += dk_part
            dv[here, :] += dv_part
    dq = jnp.concatenate(sides, axis=0).T * HEAD_DIM**-0.5
    dqkv[local, lanes] = (dq * cos[rows, :] - swap_halves(dq) * sin[rows, :]).astype(BF16)


def layer_kernel(
    dp,
    x_in,
    og_in,
    value_first,
    segments,
    positions,
    frequency,
    gain_attn_in,
    gain_mlp_in,
    query_shard,
    key_shard,
    value_shard,
    out_shard,
    gate_shard,
    up_shard,
    down_shard,
    block_output,
    input_grad,
    value_first_grad,
    gain_attn_grad,
    query_sum,
    key_sum,
    value_sum,
    out_sum,
    gain_mlp_grad,
    gate_sum,
    up_sum,
    down_sum,
    xb,
    normed,
    normed_mlp,
    og,
    qkv_w,
    out_w,
    ff_w,
    q,
    k,
    v,
    attended,
    lse,
    hidden,
    grad_hidden,
    units,
    ff_grad,
    attn_grad,
    half_out,
    half_in,
    sum_out,
    sum_in,
    m_sum,
    turned,
    dk,
    dv,
    cos,
    sin,
    gain_acc,
    gain_in,
    local_sems,
    group_out,
    group_in,
    core_out,
    core_in,
    up_out,
    up_in,
    down_out,
    down_in,
    pair_out,
    pair_in,
    line_out,
    line_in,
    gain_out_sems,
    gain_in_sems,
    credits,
    ff_free,
    attn_free,
):
    p = Place(dp)
    group, cores = (group_out, group_in), (core_out, core_in)
    rows_r, hw = query_shard.shape
    ff = gate_shard.shape[0]
    wide = ff_w.shape[1] // 3
    width = x_in.shape[1]
    tiles = SEQ_LEN // TILE
    slot = rows_at(p.d * rows_r, rows_r)
    sent = {}

    def go(name, copy):
        copy.start()
        sent[name] = copy

    def gone(name):
        sent.pop(name).wait_send()

    def arrived(there, sems, n, who):
        send(there, there, sems, n, who).wait_recv()

    def fetch(n, src, dst):
        copy = pltpu.make_async_copy(src, dst, local_sems.at[n])
        copy.start()
        return copy

    x_copy = fetch(0, x_in, xb.at[p.chip])
    qkv_copies = [
        fetch(1 + n, shard, qkv_w.at[slot, pl.ds(n * hw, hw)])
        for n, shard in enumerate((query_shard, key_shard, value_shard))
    ]
    og_copy = fetch(4, og_in, og.at[block(p.t)])
    vf_copy = fetch(5, value_first, attended)
    p.greet()
    gathers = [
        Gather(
            p,
            full,
            rows_r,
            (up_out.at[n], up_in.at[n]),
            (down_out.at[n], down_in.at[n]),
            (pair_out.at[n], pair_in.at[n]),
        )
        for n, full in enumerate((qkv_w, out_w, ff_w))
    ]
    for copy in qkv_copies:
        copy.wait()
    gathers[0].start_line()
    gathers[0].start_pair()
    x_copy.wait()
    go("x", send(xb.at[p.chip], xb.at[p.chip], group, 0, p.across))
    gain_attn = gain_attn_in[...].astype(F32)
    gain_mlp = gain_mlp_in[...].astype(F32)
    other = lax.rem(p.t + 2, 4)
    sib = p.t + 1 - 2 * p.core
    sib_other = lax.rem(sib + 2, 4)

    def norm_block(b, chip):
        @pl.loop(0, HALF // TILE)
        def _(j):
            u = xb[chip, rows_at(j * TILE, TILE), :].astype(F32)
            normed[rows_at(b * HALF + j * TILE, TILE), :] = (
                u * norm_factor(u) * gain_attn
            ).astype(BF16)

        here = normed.at[block(b)]
        n = 0 if chip is p.chip else 1
        go(("normed", n), send(here, here, cores, n, p.sibling))

    norm_block(p.t, p.chip)
    out_w[slot, :] = out_shard[...].astype(F32).T.astype(BF16)
    for n, shard in enumerate((gate_shard, up_shard, down_shard)):
        flat = shard[...].astype(F32)
        if wide > ff:
            flat = jnp.concatenate([flat, jnp.zeros((wide - ff, rows_r), F32)], axis=0)
        ff_w[slot, n * wide : (n + 1) * wide] = flat.T.astype(BF16)
    if p.line > 1:
        gathers[0].relay(1)

    @pl.loop(0, SEQS * tiles)
    def _(j):
        rows = rows_at(j * TILE, TILE)
        place = jnp.broadcast_to(positions[:, rows].astype(F32), (128, TILE)).T
        angle = place * frequency[...]
        lane = lax.broadcasted_iota(jnp.int32, (TILE, 128), 1)
        cos[rows, :] = jnp.cos(angle)
        sine = jnp.sin(angle)
        sin[rows, :] = jnp.where(lax.rem(lane, HEAD_DIM) < HEAD_DIM // 2, -sine, sine)

    for n in range(2, p.line):
        gathers[0].relay(n)
    gathers[1].start_line()
    gathers[2].start_line()
    arrived(xb.at[1 - p.chip], group, 0, p.across)
    og_copy.wait()
    own_rows = og.at[block(p.t)]
    go("og_x", send(own_rows, own_rows, group, 1, p.across))
    norm_block(other, 1 - p.chip)
    go("og_c", send(own_rows, own_rows, cores, 2, p.sibling))
    gathers[0].finish()
    gathers[1].start_pair()
    gathers[2].start_pair()
    arrived(normed.at[block(sib)], cores, 0, p.sibling)
    arrived(normed.at[block(sib_other)], cores, 1, p.sibling)
    vf_copy.wait()

    def project(seq):
        @pl.loop(0, tiles)
        def _(j):
            rows = rows_at(seq * SEQ_LEN + j * TILE, TILE)
            made = dot_nn(normed[rows, :], qkv_w[...])
            c, s = cos[rows, :], sin[rows, :]
            for n in range(hw // 128):
                lanes = slice(n * 128, (n + 1) * 128)
                u = made[:, n * 128 : (n + 1) * 128]
                q[rows, lanes] = ((u * c + swap_halves(u) * s) * HEAD_DIM**-0.5).astype(BF16)
                u = made[:, hw + n * 128 : hw + (n + 1) * 128]
                k[rows, lanes] = (u * c + swap_halves(u) * s).astype(BF16)
            mixed = 0.5 * made[:, 2 * hw :] + 0.5 * attended[rows, :].astype(F32)
            v[rows, :] = mixed.astype(BF16)
            turned[:, rows_at(j * TILE, TILE)] = mixed.T.astype(BF16)

    def branch(seq):
        for h, add in ((1 - p.core, False), (p.core, True)):
            if add:
                arrived(half_in.at[seq], cores, 4 + seq, p.sibling)

            @pl.loop(0, HALF // TILE)
            def _(j):
                rows = rows_at(seq * SEQ_LEN + h * HALF + j * TILE, TILE)
                part = dot_nt(attended[rows, :], out_w[...])
                tile = rows_at(j * TILE, TILE)
                if add:
                    sum_out[seq, tile, :] = (part + half_in[seq, tile, :].astype(F32)).astype(BF16)
                else:
                    half_out[seq, tile, :] = part.astype(BF16)

            if add:
                go(("sum", seq), send(sum_out.at[seq], sum_in.at[seq], group, 2 + seq, p.across))
            else:
                go(
                    ("half", seq),
                    send(half_out.at[seq], half_in.at[seq], cores, 4 + seq, p.sibling),
                )

    def finish_branch(seq):
        arrived(sum_in.at[seq], group, 2 + seq, p.across)

        @pl.loop(0, HALF // TILE)
        def _(j):
            tile = rows_at(j * TILE, TILE)
            both = sum_out[seq, tile, :].astype(F32) + sum_in[seq, tile, :].astype(F32)
            u = xb[seq, tile, :].astype(F32) + both
            hidden[seq, tile, :] = u
            normed_mlp[rows_at((2 * seq + p.core) * HALF + j * TILE, TILE), :] = (
                u * norm_factor(u) * gain_mlp
            ).astype(BF16)

        mine = normed_mlp.at[block(2 * seq + p.core)]
        go(("mlp", seq), send(mine, mine, cores, 6 + seq, p.sibling))
        tell(credits.at[seq], p.across)

    later = [(gathers[1], n) for n in range(1, p.line)]
    later_ff = list(range(1, p.line))

    def relay_ff():
        if later_ff:
            gathers[2].relay(later_ff.pop(0))

    for seq in range(SEQS):
        project(seq)
        for heads in range(hw // 128):
            for i in range(tiles):
                attention_rows(seq, heads, i, q, k, turned, segments, attended, lse)
            if seq == 0 and heads == 0:
                for g, n in later:
                    g.relay(n)
                gathers[1].finish()
                relay_ff()
            elif seq == 1:
                relay_ff()
        branch(seq)
        if seq == 0:
            arrived(og.at[block(other)], group, 1, p.across)
            there = og.at[block(other)]
            go("og_f", send(there, there, cores, 3, p.sibling))
    while later_ff:
        relay_ff()
    finish_branch(0)
    arrived(og.at[block(sib)], cores, 2, p.sibling)
    arrived(og.at[block(sib_other)], cores, 3, p.sibling)
    gathers[2].finish()

    def feed(seq):
        arrived(normed_mlp.at[block(2 * seq + 1 - p.core)], cores, 6 + seq, p.sibling)
        for n in range(2):
            gone(("half", n))
        gone(("sum", seq))
        for h, add in ((1 - p.core, False), (p.core, True)):
            if add:
                for n in range(2):
                    arrived(half_in.at[n], cores, 8 + 2 * seq + n, p.sibling)

            @pl.loop(0, HALF // TILE)
            def _(j):
                local = rows_at(h * HALF + j * TILE, TILE)
                rows = rows_at(seq * SEQ_LEN + h * HALF + j * TILE, TILE)
                tile = rows_at(j * TILE, TILE)
                for n in range(wide // 256):
                    lanes = [slice(m * wide + n * 256, m * wide + (n + 1) * 256) for m in range(3)]
                    gate = dot_nn(normed_mlp[rows, :], ff_w[:, lanes[0]])
                    up = dot_nn(normed_mlp[rows, :], ff_w[:, lanes[1]])
                    grad_act = dot_nn(og[rows, :], ff_w[:, lanes[2]])
                    sig = 1.0 / (1.0 + jnp.exp(-gate))
                    swish = gate * sig
                    units[local, lanes[0]] = (
                        grad_act * up * sig * (1.0 + gate * (1.0 - sig))
                    ).astype(BF16)
                    units[local, lanes[1]] = (grad_act * swish).astype(BF16)
                    units[local, lanes[2]] = (swish * up).astype(BF16)
                down = dot_nt(units[local, 2 * wide :], ff_w[:, 2 * wide :])
                back = dot_nt(units[local, : 2 * wide], ff_w[:, : 2 * wide])
                if add:
                    sum_out[seq, tile, :] = (back + half_in[0, tile, :].astype(F32)).astype(BF16)
                    m_sum[seq, tile, :] = (down + half_in[1, tile, :].astype(F32)).astype(BF16)
                else:
                    half_out[0, tile, :] = back.astype(BF16)
                    half_out[1, tile, :] = down.astype(BF16)

            if add:
                pl.semaphore_wait(credits.at[seq], 1)
                go(("sum", seq), send(sum_out.at[seq], sum_in.at[seq], group, 4 + seq, p.across))
            else:
                for n in range(2):
                    go(
                        ("half", n),
                        send(half_out.at[n], half_in.at[n], cores, 8 + 2 * seq + n, p.sibling),
                    )

    def ff_weights(seq):
        rows = pl.ds(seq * SEQ_LEN, SEQ_LEN)

        @pl.loop(0, width // TILE)
        def _(j):
            cols = rows_at(j * TILE, TILE)
            for n, left in ((0, normed_mlp), (1, normed_mlp), (2, og)):
                lanes = slice(n * wide, (n + 1) * wide)
                part = dot_tn(left[rows, cols], units[:, lanes])
                if seq > 0:
                    part = part + ff_grad[cols, lanes].astype(F32)
                ff_grad[cols, lanes] = part.astype(BF16)

    def pull(seq):
        arrived(sum_in.at[seq], group, 4 + seq, p.across)

        @pl.loop(0, HALF // TILE)
        def _(j):
            tile = rows_at(j * TILE, TILE)
            rows = rows_at((2 * seq + p.core) * HALF + j * TILE, TILE)
            grad = sum_out[seq, tile, :].astype(F32) + sum_in[seq, tile, :].astype(F32)
            back, gain_rows = norm_pull(grad, hidden[seq, tile, :], gain_mlp)
            whole = og[rows, :].astype(F32) + back
            normed_mlp[rows, :] = whole.astype(BF16)

            @pl.when(p.chip == seq)
            def _():
                grad_hidden[tile, :] = whole
                gain_acc[1:2, :] += jnp.sum(gain_rows, axis=0, keepdims=True)

        mine = normed_mlp.at[block(2 * seq + p.core)]
        go(("low", seq), send(mine, mine, cores, 12 + seq, p.sibling))

        @pl.when(p.chip == seq)
        def _():
            tell(credits.at[3], p.across)

    def release(sems):
        for who, n in [(p.pair, 0)] + [(p.behind(n), n) for n in range(1, p.line)]:
            tell(sems.at[n], who)

    feed(0)
    ff_weights(0)
    finish_branch(1)
    feed(1)
    gathers[2].drain()
    release(ff_free)
    gain_acc[...] = jnp.zeros_like(gain_acc)
    ff_weights(1)
    for n in range(2):
        gone(("mlp", n))
    tell(credits.at[2], p.sibling)
    scatter_ff = Scatter(
        p,
        ff_grad,
        lambda n: ff_w.at[pl.ds(n * rows_r, rows_r)],
        lambda n: ff_w.at[pl.ds((p.line + n - 1) * rows_r, rows_r)],
        (pair_out.at[3], pair_in.at[3]),
        (line_out.at[0], line_in.at[0]),
        ff_free,
    )
    scatter_attn = Scatter(
        p,
        attn_grad,
        lambda n: og.at[pl.ds(n * rows_r, rows_r)],
        lambda n: og.at[pl.ds((p.line + n - 1) * rows_r, rows_r)],
        (pair_out.at[4], pair_in.at[4]),
        (line_out.at[1], line_in.at[1]),
        attn_free,
    )
    scatter_ff.start()
    pl.semaphore_wait(credits.at[2], 1)

    dqkv = units

    def grad_att(i, heads):
        return units[pl.ds(i * TILE, TILE), pl.ds(3 * hw + heads * 128, 128)]

    def prepare(seq):
        arrived(normed_mlp.at[block(2 * seq + 1 - p.core)], cores, 12 + seq, p.sibling)

        @pl.loop(0, tiles)
        def _(j):
            local = rows_at(j * TILE, TILE)
            rows = rows_at(seq * SEQ_LEN + j * TILE, TILE)
            units[local, 3 * hw : 4 * hw] = dot_nn(normed_mlp[rows, :], out_w[...]).astype(BF16)
            turned[:, local] = k[rows, :].astype(F32).T.astype(BF16)

    def heads_back(seq, heads):
        if (seq, heads) != (0, 0):
            sent.pop("dv").wait()
        for i in reversed(range(tiles)):
            attention_rows_back(
                seq,
                heads,
                i,
                q,
                k,
                v,
                turned,
                segments,
                lse,
                attended,
                grad_att,
                dk,
                dv,
                cos,
                sin,
                dqkv,
            )

        @pl.loop(0, tiles)
        def _(j):
            local = rows_at(j * TILE, TILE)
            rows = rows_at(seq * SEQ_LEN + j * TILE, TILE)
            u = dk[local, :]
            lanes = slice(hw + heads * 128, hw + (heads + 1) * 128)
            dqkv[local, lanes] = (u * cos[rows, :] - swap_halves(u) * sin[rows, :]).astype(BF16)
            half = 0.5 * dv[local, :]
            lanes = slice(2 * hw + heads * 128, 2 * hw + (heads + 1) * 128)
            dqkv[local, lanes] = half.astype(BF16)
            dv[local, :] = half

        sent["dv"] = fetch(
            6,
            dv,
            value_first_grad.at[pl.ds(seq * SEQ_LEN, SEQ_LEN), pl.ds(heads * 128, 128)],
        )

    def attn_weights(seq):
        rows = pl.ds(seq * SEQ_LEN, SEQ_LEN)

        @pl.loop(0, width // TILE)
        def _(j):
            cols = rows_at(j * TILE, TILE)
            for left, right, lanes in (
                (normed, units[:, : 3 * hw], slice(0, 3 * hw)),
                (normed_mlp, attended[rows, :], slice(3 * hw, 4 * hw)),
            ):
                part = dot_tn(left[rows, cols], right)
                if seq > 0:
                    part = part + attn_grad[cols, lanes].astype(F32)
                attn_grad[cols, lanes] = part.astype(BF16)

    def branch_back(seq):
        gone(("half", seq))
        gone(("sum", seq))
        for h, add in ((1 - p.core, False), (p.core, True)):
            if add:
                arrived(half_in.at[seq], cores, 14 + seq, p.sibling)

            @pl.loop(0, HALF // TILE)
            def _(j):
                local = rows_at(h * HALF + j * TILE, TILE)
                tile = rows_at(j * TILE, TILE)
                part = dot_nt(dqkv[local, : 3 * hw], qkv_w[...])
                if add:
                    sum_out[seq, tile, :] = (part + half_in[seq, tile, :].astype(F32)).astype(BF16)
                else:
                    half_out[seq, tile, :] = part.astype(BF16)

            if add:

                @pl.when(p.chip != seq)
                def _():
                    pl.semaphore_wait(credits.at[3], 1)
                    send(sum_out.at[seq], sum_in.at[seq], group, 7, p.across).start()
            else:
                go(
                    ("half", seq),
                    send(half_out.at[seq], half_in.at[seq], cores, 14 + seq, p.sibling),
                )

    relays = list(range(1, p.line))

    def relay_grad():
        if relays:
            scatter_ff.relay(relays.pop(0))

    for seq in range(SEQS):
        pull(seq)
        if seq == 1:
            for name in ("og_x", "og_c", "og_f"):
                gone(name)
            release(attn_free)
            go("m", send(m_sum.at[1 - p.chip], xb.at[p.chip], group, 6, p.across))
        prepare(seq)
        for heads in range(hw // 128):
            heads_back(seq, heads)
            if (seq, heads) != (0, 0):
                relay_grad()
        attn_weights(seq)
        if seq == 1:
            scatter_attn.start()
        branch_back(seq)
    while relays:
        relay_grad()

    arrived(xb.at[1 - p.chip], group, 6, p.across)

    @pl.loop(0, HALF // TILE)
    def _(j):
        tile = rows_at(j * TILE, TILE)
        both = m_sum[p.chip, tile, :].astype(F32) + xb[1 - p.chip, tile, :].astype(F32)
        m_sum[p.chip, tile, :] = (hidden[p.chip, tile, :] + both).astype(BF16)

    stores = [fetch(8, m_sum.at[p.chip], block_output)]
    arrived(sum_in.at[p.chip], group, 7, p.across)

    @pl.loop(0, HALF // TILE)
    def _(j):
        tile = rows_at(j * TILE, TILE)
        grad = sum_out[p.chip, tile, :].astype(F32) + sum_in[p.chip, tile, :].astype(F32)
        back, gain_rows = norm_pull(grad, xb[p.chip, tile, :].astype(F32), gain_attn)
        grad_hidden[tile, :] = grad_hidden[tile, :] + back
        gain_acc[0:1, :] += jnp.sum(gain_rows, axis=0, keepdims=True)

    stores.append(fetch(9, grad_hidden, input_grad))
    gain_sems = (gain_out_sems, gain_in_sems)

    def exchange(partners, first):
        copies = []
        for n, who in enumerate(partners):
            copy = send(gain_acc, gain_in.at[first + n], gain_sems, first + n, who)
            copy.start()
            copies.append(copy)

        def rest():
            for copy in copies:
                copy.wait()
            whole = gain_acc[...]
            for n in range(len(partners)):
                whole = whole + gain_in[first + n]
            gain_acc[...] = whole

        return rest

    todo = list(range(1, p.line))

    def relay_attn():
        if todo:
            scatter_attn.relay(todo.pop(0))

    rest = exchange([p.sibling, p.across, p.diagonal], 0)
    relay_attn()
    rest()
    rest = exchange([p.pair], 3)
    relay_attn()
    rest()
    rest = exchange([p.ahead(n) for n in range(1, p.line)], 4)
    while todo:
        relay_attn()
    rest()
    gain_attn_grad[...] = gain_acc[0:1, :]
    gain_mlp_grad[...] = gain_acc[1:2, :]
    scatter_ff.finish()
    for n, out in enumerate((gate_sum, up_sum, down_sum)):
        out[...] = scatter_ff.total(slice(n * wide, (n + 1) * wide)).T[:ff, :]
    scatter_attn.finish()
    for n, out in enumerate((query_sum, key_sum, value_sum)):
        out[...] = scatter_attn.total(slice(n * hw, (n + 1) * hw))
    out_sum[...] = scatter_attn.total(slice(3 * hw, 4 * hw)).T
    send(sum_out.at[1 - p.chip], sum_in.at[1 - p.chip], group, 7, p.across).wait_send()
    sent.pop("dv").wait()
    for name in list(sent):
        gone(name)
    for g in gathers[:2]:
        g.drain()
    scatter_ff.drain()
    scatter_attn.drain()
    for copy in stores:
        copy.wait()


def layer(dp, x, og, vf, segments, positions, frequency, gain_a, gain_m, wq, wk, wv, wo, wg, wu, wd):
    rows, width = 4 * x.shape[0], x.shape[1]
    hw, ff, r = vf.shape[1], wg.shape[0], wq.shape[0]
    wide = -(-ff // 256) * 256
    line = dp // 2
    hops = max(line - 1, 1)
    vmem = pl.BlockSpec(memory_space=pltpu.VMEM)
    far = pl.BlockSpec(memory_space=pl.ANY)
    shapes = [
        ((HALF, width), BF16, far),
        ((HALF, width), F32, far),
        ((rows, hw), F32, far),
        ((1, width), F32, vmem),
        ((r, hw), F32, vmem),
        ((r, hw), F32, vmem),
        ((r, hw), F32, vmem),
        ((hw, r), F32, vmem),
        ((1, width), F32, vmem),
        ((ff, r), F32, vmem),
        ((ff, r), F32, vmem),
        ((ff, r), F32, vmem),
    ]
    dma = pltpu.SemaphoreType.DMA
    bf = lambda *shape: pltpu.VMEM(shape, BF16)
    fl = lambda *shape: pltpu.VMEM(shape, F32)
    scratch = [
        bf(2, HALF, width),
        bf(rows, width),
        bf(rows, width),
        bf(rows, width),
        bf(width, 3 * hw),
        bf(width, hw),
        bf(width, 3 * wide),
        bf(rows, hw),
        bf(rows, hw),
        bf(rows, hw),
        bf(rows, hw),
        fl(8, SEQ_LEN),
        fl(2, HALF, width),
        fl(HALF, width),
        bf(SEQ_LEN, 3 * wide),
        bf(width, 3 * wide),
        bf(width, 4 * hw),
        bf(2, HALF, width),
        bf(2, HALF, width),
        bf(2, HALF, width),
        bf(2, HALF, width),
        bf(2, HALF, width),
        bf(hw, SEQ_LEN),
        fl(SEQ_LEN, 128),
        fl(SEQ_LEN, 128),
        fl(rows, 128),
        fl(rows, 128),
        fl(2, width),
        fl(4 + hops, 2, width),
        dma((10,)),
        dma((8,)),
        dma((8,)),
        dma((16,)),
        dma((16,)),
        dma((3, hops)),
        dma((3, hops)),
        dma((3, hops)),
        dma((3, hops)),
        dma((5, line)),
        dma((5, line)),
        dma((2, hops)),
        dma((2, hops)),
        dma((4 + hops,)),
        dma((4 + hops,)),
        pltpu.SemaphoreType.REGULAR((4,)),
        pltpu.SemaphoreType.REGULAR((line,)),
        pltpu.SemaphoreType.REGULAR((line,)),
    ]
    in_specs = [far] * 3 + [vmem] * 5 + [far] * 3 + [vmem] * 4
    return pl.pallas_call(
        functools.partial(layer_kernel, dp),
        out_shape=[jax.ShapeDtypeStruct(s, t) for s, t, _ in shapes],
        in_specs=in_specs,
        out_specs=[space for _, _, space in shapes],
        scratch_shapes=scratch,
        compiler_params=pltpu.CompilerParams(
            collective_id=0, has_side_effects=True, vmem_limit_bytes=VMEM_LIMIT
        ),
        name="layer",
    )(x, og, vf, segments, positions, frequency, gain_a, gain_m, wq, wk, wv, wo, wg, wu, wd)


def on_device(
    dp,
    block_input,
    value_first,
    segment_ids,
    positions,
    gain_attn,
    query_weight,
    key_weight,
    value_weight,
    out_weight,
    gain_mlp,
    gate_weight,
    up_weight,
    down_weight,
    output_grad,
):
    half = HEAD_DIM // 2
    frequency = ROPE_BASE ** (-(2.0 * jnp.arange(half).astype(F32)) / HEAD_DIM)
    outs = layer(
        dp,
        block_input,
        output_grad,
        value_first,
        segment_ids[None, :],
        positions[None, :],
        jnp.tile(frequency, 128 // half)[None, :],
        gain_attn[None, :],
        gain_mlp[None, :],
        query_weight,
        key_weight,
        value_weight,
        out_weight,
        gate_weight.T,
        up_weight.T,
        down_weight,
    )
    (
        block_output,
        input_grad,
        value_first_grad,
        gain_attn_grad,
        query_sum,
        key_sum,
        value_sum,
        out_sum,
        gain_mlp_grad,
        gate_sum,
        up_sum,
        down_sum,
    ) = outs
    return (
        block_output,
        input_grad,
        value_first_grad,
        gain_attn_grad[0],
        query_sum,
        key_sum,
        value_sum,
        out_sum,
        gain_mlp_grad[0],
        gate_sum.T,
        up_sum.T,
        down_sum,
    )


def solution(mesh):
    rows = P(("dp", "tensor"), None)
    weight = P("dp", "tensor")
    across = P("tensor", "dp")
    return jax.shard_map(
        functools.partial(on_device, mesh.shape["dp"]),
        mesh=mesh,
        in_specs=(
            rows,
            weight,
            P("dp"),
            P("dp"),
            P(),
            weight,
            weight,
            weight,
            across,
            P(),
            weight,
            weight,
            across,
            rows,
        ),
        out_specs=(
            rows,
            rows,
            weight,
            P(),
            weight,
            weight,
            weight,
            across,
            P(),
            weight,
            weight,
            across,
        ),
        check_vma=False,
    )
```

```python
import functools
import math

import jax
import jax.numpy as jnp
from jax import lax
from jax.experimental import pallas as pl
from jax.experimental.pallas import tpu as pltpu
from jax.sharding import PartitionSpec as P

HEAD_DIM = 64
SEQ_LEN = 1024
SEQS = 2
PIECE = 256
HALF = 512
TILE = 256
EPSILON = 1e-06
ROPE_BASE = 10000.0
MASKED = -1e30
MESH = pl.DeviceIdType.MESH
F32 = jnp.float32
BF16 = jnp.bfloat16
VMEM_LIMIT = 639 * 2**20 // 10


def dot_nn(a, b):
    return lax.dot_general(a, b, (((1,), (0,)), ((), ())), preferred_element_type=F32)


def dot_nt(a, b):
    return lax.dot_general(a, b, (((1,), (1,)), ((), ())), preferred_element_type=F32)


def dot_tn(a, b):
    return lax.dot_general(a, b, (((0,), (0,)), ((), ())), preferred_element_type=F32)


def rows_at(start, size):
    return pl.ds(pl.multiple_of(start, size), size)


def block(b):
    return rows_at(b * HALF, HALF)


class Place:
    def __init__(self, dp):
        self.d = lax.axis_index("dp")
        self.t = lax.axis_index("tensor")
        self.core = lax.rem(self.t, 2)
        self.chip = self.t // 2
        self.line = dp // 2
        self.y = lax.rem(self.d, 2)
        self.z = self.d // 2
        self.sibling = (self.d, self.t + 1 - 2 * self.core)
        self.across = (self.d, lax.rem(self.t + 2, 4))
        self.diagonal = (self.d, lax.rem(self.t + 3 - 2 * self.core, 4))
        self.pair = (self.d + 1 - 2 * self.y, self.t)
        self.up = (self.d + 2, self.t)
        self.down = (self.d - 2, self.t)

    def ahead(self, k):
        return (2 * lax.rem(self.z + k, self.line) + self.y, self.t)

    def behind(self, k):
        return (2 * lax.rem(self.z + self.line - k, self.line) + self.y, self.t)

    def greet(self):
        barrier = pltpu.get_barrier_semaphore()
        partners = [self.sibling, self.across, self.diagonal, self.pair]
        partners.extend(self.ahead(k) for k in range(1, self.line))
        for who in partners:
            tell(barrier, who)
        self.greeted = len(partners)

    def met(self):
        pl.semaphore_wait(pltpu.get_barrier_semaphore(), self.greeted)


def tell(sem, who):
    pl.semaphore_signal(sem, inc=1, device_id=who, device_id_type=MESH)


def send(src, dst, sems, k, who):
    return pltpu.make_async_remote_copy(
        src_ref=src,
        dst_ref=dst,
        send_sem=sems[0].at[k],
        recv_sem=sems[1].at[k],
        device_id=who,
        device_id_type=MESH,
    )


class Gather:
    def __init__(self, place, full, lanes, rows, spread, up_sems, down_sems, pair_sems):
        self.p, self.full, self.lanes, self.r, self.spread = place, full, lanes, rows, spread
        self.up_sems, self.down_sems, self.pair_sems = up_sems, down_sems, pair_sems

    def shard(self, z, y):
        return self.full.at[rows_at((2 * z + y) * self.r, self.r), self.lanes]

    def load(self, z):
        if self.spread:
            return self.shard(z, self.p.y)
        return self.full.at[rows_at(2 * z * self.r, 2 * self.r), self.lanes]

    def sides(self, k):
        p = self.p
        return (
            (p.z - k, p.z >= k, self.up_sems, p.z + 1 < p.line, p.up),
            (p.z + k, p.z + k < p.line, self.down_sems, p.z >= 1, p.down),
        )

    def start_pair(self):
        p = self.p
        here = self.shard(p.z, p.y)
        send(here, here, self.pair_sems, p.z, p.pair).start()

    def start_line(self):
        p = self.p
        if not self.spread:
            there = self.shard(p.z, 1 - p.y)
            send(there, there, self.pair_sems, p.z, p.pair).wait_recv()
        here = self.load(p.z)
        for _, _, sems, onward, to in self.sides(0):

            @pl.when(onward)
            def _():
                send(here, here, sems, 0, to).start()

    def relay(self, k):
        p = self.p
        for z, exists, sems, onward, to in self.sides(k):

            @pl.when(exists)
            def _():
                here = self.load(z)
                send(here, here, sems, k - 1, to).wait_recv()

                @pl.when(onward)
                def _():
                    send(here, here, sems, k, to).start()

                if self.spread:
                    send(here, here, self.pair_sems, z, p.pair).start()

    def finish(self):
        p = self.p
        if self.spread:
            for z in range(p.line):
                there = self.shard(z, 1 - p.y)
                send(there, there, self.pair_sems, z, p.pair).wait_recv()

    def drain(self):
        p = self.p
        for z in range(p.line) if self.spread else (p.z,):
            here = self.shard(z, p.y)
            send(here, here, self.pair_sems, z, p.pair).wait_send()
        for k in range(p.line - 1):
            for z, exists, sems, onward, to in self.sides(k):

                @pl.when(jnp.logical_and(exists, onward))
                def _():
                    here = self.load(z)
                    send(here, here, sems, k, to).wait_send()


class Scatter:
    def __init__(self, place, full, pair_in, line_in, pair_sems, line_sems, free):
        self.p, self.full = place, full
        self.pair_in, self.line_in = pair_in, line_in
        self.pair_sems, self.line_sems = pair_sems, line_sems
        self.free = free
        self.r = full.shape[0] // (2 * place.line)
        self.out = []

    def rows(self, k, y):
        z = lax.rem(self.p.z + k, self.p.line)
        return rows_at((2 * z + y) * self.r, self.r)

    def start(self, steps):
        p = self.p
        if steps[0] == 1 or p.line == 1:
            pl.semaphore_wait(self.free.at[0], 1)
        for k in steps:
            copy = send(
                self.full.at[self.rows(k, 1 - p.y)], self.pair_in(k), self.pair_sems, k, p.pair
            )
            copy.start()
            self.out.append(copy)

    def relay(self, k):
        p = self.p
        there = self.pair_in(k)
        send(there, there, self.pair_sems, k, p.pair).wait_recv()
        mine = self.rows(k, p.y)
        self.full[mine, :] = (self.full[mine, :].astype(F32) + there[...].astype(F32)).astype(BF16)
        pl.semaphore_wait(self.free.at[k], 1)
        copy = send(self.full.at[mine], self.line_in(k), self.line_sems, k - 1, p.ahead(k))
        copy.start()
        self.out.append(copy)

    def finish(self):
        p = self.p
        there = self.pair_in(0)
        send(there, there, self.pair_sems, 0, p.pair).wait_recv()
        for k in range(1, p.line):
            there = self.line_in(k)
            send(there, there, self.line_sems, k - 1, p.pair).wait_recv()

    def total(self, lanes):
        mine = self.rows(0, self.p.y)
        whole = self.full[mine, lanes].astype(F32) + self.pair_in(0)[:, lanes].astype(F32)
        for k in range(1, self.p.line):
            whole = whole + self.line_in(k)[:, lanes].astype(F32)
        return whole

    def drain(self):
        for copy in self.out:
            copy.wait_send()


def swap_halves(u):
    lane = lax.broadcasted_iota(jnp.int32, u.shape, 1)
    low = lax.rem(lane, HEAD_DIM) < HEAD_DIM // 2
    return jnp.where(low, pltpu.roll(u, 96, 1), pltpu.roll(u, 32, 1))


def norm_factor(u):
    return lax.rsqrt(jnp.mean(u * u, axis=-1, keepdims=True) + EPSILON)


def norm_pull(grad, u, gain):
    r = norm_factor(u)
    scaled = grad * gain
    back = r * scaled - u * (r * r * r) * jnp.mean(scaled * u, axis=-1, keepdims=True)
    return back, grad * u * r


def visible(segments):
    key = lax.broadcasted_iota(jnp.int32, (TILE, TILE), 0)
    query = lax.broadcasted_iota(jnp.int32, (TILE, TILE), 1)
    return jnp.logical_or(key <= query, segments > 0)


def attention_rows(seq, heads, i, q, k, vt, segments, attended, lse):
    lane = lax.broadcasted_iota(jnp.int32, (TILE, 128), 1)
    lanes = rows_at(heads * 128, 128)
    rows = pl.ds(seq * SEQ_LEN + i * TILE, TILE)
    q2 = q[rows, lanes]
    shown = visible(segments[:, rows])
    sides = []
    for a in range(2):
        qa = jnp.where((lane < HEAD_DIM) == (a == 0), q2, jnp.zeros_like(q2))
        vta = rows_at((heads * 2 + a) * HEAD_DIM, HEAD_DIM)
        score = jnp.where(shown, dot_nt(k[rows, lanes], qa), MASKED)
        top = jnp.max(score, axis=0, keepdims=True)
        if i > 0:
            before = dot_nt(k[pl.ds(seq * SEQ_LEN, i * TILE), lanes], qa)
            top = jnp.maximum(top, jnp.max(before, axis=0, keepdims=True))
        weight = jnp.exp(score - top)
        total = jnp.sum(weight, axis=0, keepdims=True)
        out = dot_nn(vt[vta, pl.ds(i * TILE, TILE)], weight.astype(BF16))
        if i > 0:
            weight = jnp.exp(before - top)
            total = total + jnp.sum(weight, axis=0, keepdims=True)
            out = out + dot_nn(vt[vta, pl.ds(0, i * TILE)], weight.astype(BF16))
        sides.append(out * (1.0 / total))
        lse[seq * 4 + heads * 2 + a, :, pl.ds(i * TILE, TILE)] = top + jnp.log(total)
    attended[rows, lanes] = jnp.concatenate(sides, axis=0).T.astype(BF16)


def attention_rows_back(
    seq, heads, i, q, k, v, kt, segments, lse, attended, grad_att, dk, dv, cos, sin, dqkv
):
    lane = lax.broadcasted_iota(jnp.int32, (TILE, 128), 1)
    lanes = rows_at(heads * 128, 128)
    local = pl.ds(i * TILE, TILE)
    rows = pl.ds(seq * SEQ_LEN + i * TILE, TILE)
    first = i == SEQ_LEN // TILE - 1
    q2, g2 = q[rows, lanes], grad_att(i, heads)
    shown = visible(segments[:, rows])
    products = (g2.astype(F32) * attended[rows, lanes].astype(F32)).T
    parts = [(i * TILE, TILE, True)]
    if i > 0:
        parts.append((0, i * TILE, False))
    sides = [None, None]
    for start, size, diagonal in parts:
        keys = pl.ds(seq * SEQ_LEN + start, size)
        here = pl.ds(start, size)
        dk_part, dv_part = 0.0, 0.0
        for a in range(2):
            mine = (lane < HEAD_DIM) == (a == 0)
            qa = jnp.where(mine, q2, jnp.zeros_like(q2))
            ga = jnp.where(mine, g2, jnp.zeros_like(g2))
            delta = jnp.sum(products[a * HEAD_DIM : (a + 1) * HEAD_DIM], axis=0, keepdims=True)
            stat = lse[seq * 4 + heads * 2 + a, :, local]
            score = dot_nt(k[keys, lanes], qa)
            if diagonal:
                score = jnp.where(shown, score, MASKED)
            prob = jnp.exp(score - stat)
            grad_prob = dot_nt(v[keys, lanes], ga)
            grad_score = (prob * (grad_prob - delta)).astype(BF16)
            dv_part = dv_part + dot_nn(prob.astype(BF16), ga)
            dk_part = dk_part + dot_nn(grad_score, qa)
            side = dot_nn(kt[rows_at((heads * 2 + a) * HEAD_DIM, HEAD_DIM), here], grad_score)
            sides[a] = side if sides[a] is None else sides[a] + side
        if first:
            dk[here, :] = dk_part
            dv[here, :] = dv_part
        else:
            dk[here, :] += dk_part
            dv[here, :] += dv_part
    dq = jnp.concatenate(sides, axis=0).T * HEAD_DIM**-0.5
    dqkv[local, lanes] = (dq * cos[rows, :] - swap_halves(dq) * sin[rows, :]).astype(BF16)


def layer_kernel(
    dp,
    x_in,
    og_in,
    value_first,
    segments,
    positions,
    gains,
    query_shard,
    key_shard,
    value_shard,
    out_shard,
    gate_shard,
    up_shard,
    down_shard,
    block_output,
    input_grad,
    value_first_grad,
    gain_attn_grad,
    query_sum,
    key_sum,
    value_sum,
    out_sum,
    gain_mlp_grad,
    gate_sum,
    up_sum,
    down_sum,
    xb,
    normed,
    normed_mlp,
    og,
    attn_w,
    ff_w,
    q,
    k,
    v,
    attended,
    lse,
    hidden,
    grad_hidden,
    units,
    ff_grad,
    attn_grad,
    half_out,
    half_in,
    sum_out,
    sum_in,
    m_sum,
    turned,
    dk,
    dv,
    cos,
    sin,
    gain_acc,
    gain_in,
    local_sems,
    group_out,
    group_in,
    core_out,
    core_in,
    up_out,
    up_in,
    down_out,
    down_in,
    pair_out,
    pair_in,
    line_out,
    line_in,
    gain_out_sems,
    gain_in_sems,
    credits,
    ff_free,
    attn_free,
):
    p = Place(dp)
    group, cores = (group_out, group_in), (core_out, core_in)
    rows_r, hw = query_shard.shape
    ff = gate_shard.shape[0]
    wide = ff_w.shape[1] // 3
    width = x_in.shape[1]
    tiles = SEQ_LEN // TILE
    slot = rows_at(p.d * rows_r, rows_r)
    qkv, out_lanes = slice(0, 3 * hw), slice(3 * hw, 4 * hw)
    sent = {}

    def go(name, copy):
        copy.start()
        sent[name] = copy

    def gone(name):
        sent.pop(name).wait_send()

    def arrived(there, sems, n, who):
        send(there, there, sems, n, who).wait_recv()

    def local(n, src, dst):
        return pltpu.make_async_copy(src, dst, local_sems.at[n])

    def fetch(n, src, dst):
        copy = local(n, src, dst)
        copy.start()
        return copy

    p.greet()
    x_copy = fetch(0, x_in, xb.at[p.chip])
    qkv_copies = [
        fetch(1 + n, shard, attn_w.at[slot, pl.ds(n * hw, hw)])
        for n, shard in enumerate((query_shard, key_shard, value_shard))
    ]
    og_copy = fetch(4, og_in, og.at[block(p.t)])
    vf_copy = fetch(5, value_first, attended)
    attn_w[slot, out_lanes] = out_shard[...].astype(F32).T.astype(BF16)
    p.met()
    x_copy.wait()
    go("x", send(xb.at[p.chip], xb.at[p.chip], group, 0, p.across))
    gathers = [
        Gather(
            p,
            full,
            pl.ds(first, lanes),
            rows_r,
            spread,
            (up_out.at[n], up_in.at[n]),
            (down_out.at[n], down_in.at[n]),
            (pair_out.at[n], pair_in.at[n]),
        )
        for n, (full, first, lanes, spread) in enumerate(
            (
                (attn_w, 0, 4 * hw, True),
                (ff_w, wide, 2 * wide, True),
                (ff_w, 0, wide, False),
            )
        )
    ]
    of_attn, of_ff, of_gate = gathers
    for copy in qkv_copies:
        copy.wait()
    of_attn.start_line()
    of_attn.start_pair()
    gain_attn, gain_mlp = gains[0:1, :], gains[1:2, :]
    other = lax.rem(p.t + 2, 4)
    sib = p.t + 1 - 2 * p.core
    sib_other = lax.rem(sib + 2, 4)

    def norm_block(b, chip, n):
        @pl.loop(0, HALF // TILE)
        def _(j):
            u = xb[chip, rows_at(j * TILE, TILE), :].astype(F32)
            normed[rows_at(b * HALF + j * TILE, TILE), :] = (
                u * norm_factor(u) * gain_attn
            ).astype(BF16)

        here = normed.at[block(b)]
        go(("normed", n), send(here, here, cores, n, p.sibling))

    norm_block(p.t, p.chip, 0)
    for n, shard in enumerate((gate_shard, up_shard, down_shard)):
        flat = shard[...].astype(F32)
        if wide > ff:
            flat = jnp.concatenate([flat, jnp.zeros((wide - ff, rows_r), F32)], axis=0)
        ff_w[slot, n * wide : (n + 1) * wide] = flat.T.astype(BF16)
    if p.line > 1:
        of_attn.relay(1)

    @pl.loop(0, SEQS * tiles)
    def _(j):
        rows = rows_at(j * TILE, TILE)
        lane = lax.broadcasted_iota(jnp.int32, (TILE, 128), 1)
        half = HEAD_DIM // 2
        power = lax.rem(lane[0:1, :], half).astype(F32) * (-2.0 / HEAD_DIM)
        frequency = jnp.exp(power * math.log(ROPE_BASE))
        place = jnp.broadcast_to(positions[:, rows].astype(F32), (128, TILE)).T
        angle = place * frequency
        cos[rows, :] = jnp.cos(angle)
        sine = jnp.sin(angle)
        sin[rows, :] = jnp.where(lax.rem(lane, HEAD_DIM) < half, -sine, sine)

    for n in range(2, p.line):
        of_attn.relay(n)
    of_ff.start_line()
    of_gate.start_pair()
    of_ff.start_pair()
    arrived(xb.at[1 - p.chip], group, 0, p.across)
    norm_block(other, 1 - p.chip, 1)
    og_copy.wait()
    own_rows = og.at[block(p.t)]
    go("og_x", send(own_rows, own_rows, group, 1, p.across))
    go("og_c", send(own_rows, own_rows, cores, 2, p.sibling))
    of_attn.finish()
    arrived(normed.at[block(sib)], cores, 0, p.sibling)
    arrived(normed.at[block(sib_other)], cores, 1, p.sibling)
    vf_copy.wait()

    def project(seq):
        @pl.loop(0, tiles)
        def _(j):
            rows = rows_at(seq * SEQ_LEN + j * TILE, TILE)
            made = dot_nn(normed[rows, :], attn_w[:, qkv])
            c, s = cos[rows, :], sin[rows, :]
            for n in range(hw // 128):
                lanes = slice(n * 128, (n + 1) * 128)
                u = made[:, n * 128 : (n + 1) * 128]
                q[rows, lanes] = ((u * c + swap_halves(u) * s) * HEAD_DIM**-0.5).astype(BF16)
                u = made[:, hw + n * 128 : hw + (n + 1) * 128]
                k[rows, lanes] = (u * c + swap_halves(u) * s).astype(BF16)
            mixed = 0.5 * made[:, 2 * hw :] + 0.5 * attended[rows, :].astype(F32)
            v[rows, :] = mixed.astype(BF16)
            turned[:, rows_at(j * TILE, TILE)] = mixed.T.astype(BF16)

    def attend(seq):
        @pl.loop(0, hw // 128)
        def _(heads):
            for i in range(tiles):
                attention_rows(seq, heads, i, q, k, turned, segments, attended, lse)

    def branch_other(seq):
        @pl.loop(0, HALF // TILE)
        def _(j):
            rows = rows_at(seq * SEQ_LEN + (1 - p.core) * HALF + j * TILE, TILE)
            half_out[seq, rows_at(j * TILE, TILE), :] = dot_nt(
                attended[rows, :], attn_w[:, out_lanes]
            ).astype(BF16)

        go(("half", seq), send(half_out.at[seq], half_in.at[seq], cores, 4 + seq, p.sibling))

    def branch_own(seq):
        arrived(half_in.at[seq], cores, 4 + seq, p.sibling)

        @pl.loop(0, HALF // TILE)
        def _(j):
            rows = rows_at(seq * SEQ_LEN + p.core * HALF + j * TILE, TILE)
            tile = rows_at(j * TILE, TILE)
            part = dot_nt(attended[rows, :], attn_w[:, out_lanes])
            sum_out[seq, tile, :] = (part + half_in[seq, tile, :].astype(F32)).astype(BF16)

        go(("sum", seq), send(sum_out.at[seq], sum_in.at[seq], group, 2 + seq, p.across))

    def finish_branch(seq):
        arrived(sum_in.at[seq], group, 2 + seq, p.across)

        @pl.loop(0, HALF // TILE)
        def _(j):
            tile = rows_at(j * TILE, TILE)
            both = sum_out[seq, tile, :].astype(F32) + sum_in[seq, tile, :].astype(F32)
            u = xb[seq, tile, :].astype(F32) + both
            hidden[seq, tile, :] = u
            normed_mlp[rows_at((2 * seq + p.core) * HALF + j * TILE, TILE), :] = (
                u * norm_factor(u) * gain_mlp
            ).astype(BF16)

        mine = normed_mlp.at[block(2 * seq + p.core)]
        go(("mlp", seq), send(mine, mine, cores, 6 + seq, p.sibling))
        tell(credits.at[seq], p.across)

    steps_ff, steps_gate = list(range(1, p.line)), list(range(1, p.line))

    def relay_ff():
        if steps_ff:
            of_ff.relay(steps_ff.pop(0))

    def relay_gate():
        if steps_gate:
            of_gate.relay(steps_gate.pop(0))

    project(0)
    relay_ff()
    of_gate.start_line()
    attend(0)
    branch_other(0)
    relay_ff()
    project(1)
    branch_own(0)
    relay_gate()
    attend(1)
    branch_other(1)
    relay_ff()
    arrived(og.at[block(other)], group, 1, p.across)
    there = og.at[block(other)]
    go("og_f", send(there, there, cores, 3, p.sibling))
    branch_own(1)
    while steps_ff:
        relay_ff()
    while steps_gate:
        relay_gate()
    finish_branch(0)
    arrived(og.at[block(sib)], cores, 2, p.sibling)
    arrived(og.at[block(sib_other)], cores, 3, p.sibling)
    of_ff.finish()

    def feed_copy(seq, n, j):
        tile = rows_at(j * TILE, TILE)
        there = half_in.at[n, tile]
        return send(half_out.at[n, tile], there, cores, 8 + seq * 4 + n * 2 + j, p.sibling)

    def feed_sum(seq, j):
        tile = rows_at(j * TILE, TILE)
        return send(sum_out.at[seq, tile], sum_in.at[seq, tile], group, 6 + seq * 2 + j, p.across)

    def feed_gone(seq):
        for n in range(2):
            for j in range(HALF // TILE):
                feed_copy(seq, n, j).wait_send()

    def feed(seq):
        arrived(normed_mlp.at[block(2 * seq + 1 - p.core)], cores, 6 + seq, p.sibling)
        if seq == 0:
            for n in range(2):
                gone(("half", n))
        else:
            feed_gone(0)
        gone(("sum", seq))
        pl.semaphore_wait(credits.at[seq], 1)

        @pl.loop(0, tiles)
        def _(step):
            j = lax.rem(step, HALF // TILE)
            others = step < HALF // TILE
            h = jnp.where(others, 1 - p.core, p.core)
            here = rows_at(h * HALF + j * TILE, TILE)
            rows = rows_at(seq * SEQ_LEN + h * HALF + j * TILE, TILE)
            tile = rows_at(j * TILE, TILE)
            for n in range(wide // 256):
                lanes = [slice(m * wide + n * 256, m * wide + (n + 1) * 256) for m in range(3)]
                gate = dot_nn(normed_mlp[rows, :], ff_w[:, lanes[0]])
                up = dot_nn(normed_mlp[rows, :], ff_w[:, lanes[1]])
                grad_act = dot_nn(og[rows, :], ff_w[:, lanes[2]])
                sig = 1.0 / (1.0 + jnp.exp(-gate))
                swish = gate * sig
                units[here, lanes[0]] = (
                    grad_act * up * sig * (1.0 + gate * (1.0 - sig))
                ).astype(BF16)
                units[here, lanes[1]] = (grad_act * swish).astype(BF16)
                units[here, lanes[2]] = (swish * up).astype(BF16)
            down = dot_nt(units[here, 2 * wide :], ff_w[:, 2 * wide :])
            back = dot_nt(units[here, : 2 * wide], ff_w[:, : 2 * wide])

            @pl.when(others)
            def _():
                half_out[0, tile, :] = back.astype(BF16)
                half_out[1, tile, :] = down.astype(BF16)
                for n in range(2):
                    feed_copy(seq, n, j).start()

            @pl.when(jnp.logical_not(others))
            def _():
                for n in range(2):
                    feed_copy(seq, n, j).wait_recv()
                sum_out[seq, tile, :] = (back + half_in[0, tile, :].astype(F32)).astype(BF16)
                m_sum[seq, tile, :] = (down + half_in[1, tile, :].astype(F32)).astype(BF16)
                feed_sum(seq, j).start()

    def ff_weights(seq, first, last):
        rows = pl.ds(seq * SEQ_LEN, SEQ_LEN)

        @pl.loop(first, last)
        def _(j):
            cols = rows_at(j * TILE, TILE)
            for n, left in ((0, normed_mlp), (1, normed_mlp), (2, og)):
                lanes = slice(n * wide, (n + 1) * wide)
                part = dot_tn(left[rows, cols], units[:, lanes])
                if seq > 0:
                    part = part + ff_grad[cols, lanes].astype(F32)
                ff_grad[cols, lanes] = part.astype(BF16)

    def pull(seq):
        for j in range(HALF // TILE):
            feed_sum(seq, j).wait_recv()

        @pl.loop(0, HALF // TILE)
        def _(j):
            tile = rows_at(j * TILE, TILE)
            rows = rows_at((2 * seq + p.core) * HALF + j * TILE, TILE)
            grad = sum_out[seq, tile, :].astype(F32) + sum_in[seq, tile, :].astype(F32)
            back, gain_rows = norm_pull(grad, hidden[seq, tile, :], gain_mlp)
            whole = og[rows, :].astype(F32) + back
            normed_mlp[rows, :] = whole.astype(BF16)

            @pl.when(p.chip == seq)
            def _():
                grad_hidden[tile, :] = whole
                gain_acc[1:2, :] += jnp.sum(gain_rows, axis=0, keepdims=True)

        mine = normed_mlp.at[block(2 * seq + p.core)]
        pl.semaphore_wait(credits.at[2 + seq], 1)
        go(("low", seq), send(mine, mine, cores, 16 + seq, p.sibling))

        @pl.when(p.chip == seq)
        def _():
            tell(credits.at[4], p.across)

    def release(sems):
        for who, n in [(p.pair, 0)] + [(p.behind(n), n) for n in range(1, p.line)]:
            tell(sems.at[n], who)

    def free_rows(seq):
        gone(("mlp", seq))
        tell(credits.at[2 + seq], p.sibling)

    halfway = width // TILE // 2
    feed(0)
    ff_weights(0, 0, halfway)
    finish_branch(1)
    ff_weights(0, halfway, width // TILE)
    free_rows(0)
    feed(1)
    of_ff.drain()
    of_gate.drain()
    release(ff_free)
    gain_acc[...] = jnp.zeros_like(gain_acc)
    pull(0)
    ff_weights(1, 0, width // TILE)
    free_rows(1)
    scatter_ff = Scatter(
        p,
        ff_grad,
        lambda n: ff_w.at[pl.ds(n * rows_r, rows_r)],
        lambda n: ff_w.at[pl.ds((p.line + n - 1) * rows_r, rows_r)],
        (pair_out.at[3], pair_in.at[3]),
        (line_out.at[0], line_in.at[0]),
        ff_free,
    )
    scatter_attn = Scatter(
        p,
        attn_grad,
        lambda n: og.at[pl.ds(n * rows_r, rows_r)],
        lambda n: og.at[pl.ds((p.line + n - 1) * rows_r, rows_r)],
        (pair_out.at[4], pair_in.at[4]),
        (line_out.at[1], line_in.at[1]),
        attn_free,
    )
    away = list(range(1, p.line))
    if away:
        scatter_ff.start(away)

    dqkv = units

    def grad_att(i, heads):
        return units[pl.ds(i * TILE, TILE), rows_at(3 * hw + heads * 128, 128)]

    def prepare(seq):
        arrived(normed_mlp.at[block(2 * seq + 1 - p.core)], cores, 16 + seq, p.sibling)

        @pl.loop(0, tiles)
        def _(j):
            here = rows_at(j * TILE, TILE)
            rows = rows_at(seq * SEQ_LEN + j * TILE, TILE)
            units[here, out_lanes] = dot_nn(normed_mlp[rows, :], attn_w[:, out_lanes]).astype(BF16)
            turned[:, here] = k[rows, :].astype(F32).T.astype(BF16)

    def grad_store(seq, heads):
        rows = pl.ds(seq * SEQ_LEN, SEQ_LEN)
        return local(6, dv, value_first_grad.at[rows, rows_at(heads * 128, 128)])

    def attend_back(seq):
        if seq > 0:
            grad_store(0, hw // 128 - 1).wait()

        @pl.loop(0, hw // 128)
        def _(heads):
            @pl.when(heads > 0)
            def _():
                grad_store(seq, heads - 1).wait()

            for i in reversed(range(tiles)):
                attention_rows_back(
                    seq,
                    heads,
                    i,
                    q,
                    k,
                    v,
                    turned,
                    segments,
                    lse,
                    attended,
                    grad_att,
                    dk,
                    dv,
                    cos,
                    sin,
                    dqkv,
                )

            @pl.loop(0, tiles)
            def _(j):
                here = rows_at(j * TILE, TILE)
                rows = rows_at(seq * SEQ_LEN + j * TILE, TILE)
                u = dk[here, :]
                dqkv[here, rows_at(hw + heads * 128, 128)] = (
                    u * cos[rows, :] - swap_halves(u) * sin[rows, :]
                ).astype(BF16)
                half = 0.5 * dv[here, :]
                dqkv[here, rows_at(2 * hw + heads * 128, 128)] = half.astype(BF16)
                dv[here, :] = half

            grad_store(seq, heads).start()

    def attn_weights(seq):
        rows = pl.ds(seq * SEQ_LEN, SEQ_LEN)

        @pl.loop(0, width // TILE)
        def _(j):
            cols = rows_at(j * TILE, TILE)
            for left, right, lanes in (
                (normed, units[:, qkv], qkv),
                (normed_mlp, attended[rows, :], out_lanes),
            ):
                part = dot_tn(left[rows, cols], right)
                if seq > 0:
                    part = part + attn_grad[cols, lanes].astype(F32)
                attn_grad[cols, lanes] = part.astype(BF16)

    def back_other(seq):
        if seq == 0:
            feed_gone(1)

        @pl.loop(0, HALF // TILE)
        def _(j):
            here = rows_at((1 - p.core) * HALF + j * TILE, TILE)
            half_out[seq, rows_at(j * TILE, TILE), :] = dot_nt(
                dqkv[here, qkv], attn_w[:, qkv]
            ).astype(BF16)

        go(("half", seq), send(half_out.at[seq], half_in.at[seq], cores, 18 + seq, p.sibling))

    def back_own(seq):
        arrived(half_in.at[seq], cores, 18 + seq, p.sibling)
        for j in range(HALF // TILE):
            feed_sum(seq, j).wait_send()

        @pl.loop(0, HALF // TILE)
        def _(j):
            here = rows_at(p.core * HALF + j * TILE, TILE)
            tile = rows_at(j * TILE, TILE)
            part = dot_nt(dqkv[here, qkv], attn_w[:, qkv])
            sum_out[seq, tile, :] = (part + half_in[seq, tile, :].astype(F32)).astype(BF16)

        @pl.when(p.chip != seq)
        def _():
            pl.semaphore_wait(credits.at[4], 1)
            send(sum_out.at[seq], sum_in.at[seq], group, 5, p.across).start()

    relays = list(range(1, p.line))

    def relay_grad():
        if relays:
            scatter_ff.relay(relays.pop(0))

    prepare(0)
    attend_back(0)
    pull(1)
    for name in ("og_x", "og_c", "og_f"):
        gone(name)
    release(attn_free)
    relay_grad()
    back_other(0)
    attn_weights(0)
    back_own(0)
    go("m", send(m_sum.at[1 - p.chip], xb.at[p.chip], group, 4, p.across))
    prepare(1)
    relay_grad()
    attend_back(1)
    back_other(1)
    attn_weights(1)
    if away:
        scatter_attn.start(away)
    scatter_attn.start([0])
    scatter_ff.start([0])
    back_own(1)
    while relays:
        relay_grad()

    for n in range(1, p.line):
        scatter_attn.relay(n)
    arrived(sum_in.at[p.chip], group, 5, p.across)

    @pl.loop(0, HALF // TILE)
    def _(j):
        tile = rows_at(j * TILE, TILE)
        grad = sum_out[p.chip, tile, :].astype(F32) + sum_in[p.chip, tile, :].astype(F32)
        back, gain_rows = norm_pull(grad, xb[p.chip, tile, :].astype(F32), gain_attn)
        grad_hidden[tile, :] = grad_hidden[tile, :] + back
        gain_acc[0:1, :] += jnp.sum(gain_rows, axis=0, keepdims=True)

    stores = [fetch(9, grad_hidden, input_grad)]
    gain_sems = (gain_out_sems, gain_in_sems)

    def exchange(partners, first):
        copies = []
        for n, who in enumerate(partners):
            copy = send(gain_acc, gain_in.at[first + n], gain_sems, first + n, who)
            copy.start()
            copies.append(copy)

        def rest():
            for copy in copies:
                copy.wait()
            whole = gain_acc[...]
            for n in range(len(partners)):
                whole = whole + gain_in[first + n]
            gain_acc[...] = whole

        return rest

    rest = exchange([p.sibling, p.across, p.diagonal], 0)
    arrived(xb.at[1 - p.chip], group, 4, p.across)

    @pl.loop(0, HALF // TILE)
    def _(j):
        tile = rows_at(j * TILE, TILE)
        both = m_sum[p.chip, tile, :].astype(F32) + xb[1 - p.chip, tile, :].astype(F32)
        m_sum[p.chip, tile, :] = (hidden[p.chip, tile, :] + both).astype(BF16)

    stores.append(fetch(8, m_sum.at[p.chip], block_output))
    rest()
    rest = exchange([p.pair], 3)
    rest()
    rest = exchange([p.ahead(n) for n in range(1, p.line)], 4)
    scatter_attn.finish()
    for n, out in enumerate((query_sum, key_sum, value_sum)):
        out[...] = scatter_attn.total(slice(n * hw, (n + 1) * hw))
    out_sum[...] = scatter_attn.total(out_lanes).T
    rest()
    gain_attn_grad[...] = gain_acc[0:1, :]
    gain_mlp_grad[...] = gain_acc[1:2, :]
    scatter_ff.finish()
    for n, out in enumerate((gate_sum, up_sum, down_sum)):
        out[...] = scatter_ff.total(slice(n * wide, (n + 1) * wide)).T[:ff, :]
    send(sum_out.at[1 - p.chip], sum_in.at[1 - p.chip], group, 5, p.across).wait_send()
    grad_store(SEQS - 1, hw // 128 - 1).wait()
    for name in list(sent):
        gone(name)
    of_attn.drain()
    scatter_ff.drain()
    scatter_attn.drain()
    for copy in stores:
        copy.wait()


def layer(dp, x, og, vf, segments, positions, gains, wq, wk, wv, wo, wg, wu, wd):
    rows, width = 4 * x.shape[0], x.shape[1]
    hw, ff, r = vf.shape[1], wg.shape[0], wq.shape[0]
    wide = -(-ff // 256) * 256
    line = dp // 2
    hops = max(line - 1, 1)
    vmem = pl.BlockSpec(memory_space=pltpu.VMEM)
    far = pl.BlockSpec(memory_space=pl.ANY)
    shapes = [
        ((HALF, width), BF16, far),
        ((HALF, width), F32, far),
        ((rows, hw), F32, far),
        ((1, width), F32, vmem),
        ((r, hw), F32, vmem),
        ((r, hw), F32, vmem),
        ((r, hw), F32, vmem),
        ((hw, r), F32, vmem),
        ((1, width), F32, vmem),
        ((ff, r), F32, vmem),
        ((ff, r), F32, vmem),
        ((ff, r), F32, vmem),
    ]
    dma = pltpu.SemaphoreType.DMA
    flag = pltpu.SemaphoreType.REGULAR

    def bf(*shape):
        return pltpu.VMEM(shape, BF16)

    def fl(*shape):
        return pltpu.VMEM(shape, F32)

    scratch = [
        bf(2, HALF, width),
        bf(rows, width),
        bf(rows, width),
        bf(rows, width),
        bf(width, 4 * hw),
        bf(width, 3 * wide),
        bf(rows, hw),
        bf(rows, hw),
        bf(rows, hw),
        bf(rows, hw),
        fl(8, 1, SEQ_LEN),
        fl(2, HALF, width),
        fl(HALF, width),
        bf(SEQ_LEN, 3 * wide),
        bf(width, 3 * wide),
        bf(width, 4 * hw),
        bf(2, HALF, width),
        bf(2, HALF, width),
        bf(2, HALF, width),
        bf(2, HALF, width),
        bf(2, HALF, width),
        bf(hw, SEQ_LEN),
        fl(SEQ_LEN, 128),
        fl(SEQ_LEN, 128),
        fl(rows, 128),
        fl(rows, 128),
        fl(2, width),
        fl(4 + hops, 2, width),
        dma((10,)),
        dma((10,)),
        dma((10,)),
        dma((20,)),
        dma((20,)),
        dma((3, hops)),
        dma((3, hops)),
        dma((3, hops)),
        dma((3, hops)),
        dma((5, line)),
        dma((5, line)),
        dma((2, hops)),
        dma((2, hops)),
        dma((4 + hops,)),
        dma((4 + hops,)),
        flag((5,)),
        flag((line,)),
        flag((line,)),
    ]
    in_specs = [far] * 3 + [vmem] * 3 + [far] * 3 + [vmem] * 4
    return pl.pallas_call(
        functools.partial(layer_kernel, dp),
        out_shape=[jax.ShapeDtypeStruct(s, t) for s, t, _ in shapes],
        in_specs=in_specs,
        out_specs=[space for _, _, space in shapes],
        scratch_shapes=scratch,
        compiler_params=pltpu.CompilerParams(
            collective_id=0, has_side_effects=True, vmem_limit_bytes=VMEM_LIMIT
        ),
        name="layer",
    )(x, og, vf, segments, positions, gains, wq, wk, wv, wo, wg, wu, wd)


def settle_kernel(count, *refs):
    ins, outs, held, sems = refs[:count], refs[count : 2 * count], refs[2 * count : -1], refs[-1]
    first = [pltpu.make_async_copy(ins[n], held[n], sems.at[n]) for n in range(count)]
    second = [pltpu.make_async_copy(held[n], outs[n], sems.at[count + n]) for n in range(count)]
    for copy in first:
        copy.start()
    for n in range(count):
        first[n].wait()
        second[n].start()
    for copy in second:
        copy.wait()


def settle(arrays):
    count = len(arrays)
    far = pl.BlockSpec(memory_space=pl.ANY)
    return pl.pallas_call(
        functools.partial(settle_kernel, count),
        out_shape=[jax.ShapeDtypeStruct(a.shape, a.dtype) for a in arrays],
        in_specs=[far] * count,
        out_specs=[far] * count,
        scratch_shapes=[pltpu.VMEM(a.shape, a.dtype) for a in arrays]
        + [pltpu.SemaphoreType.DMA((2 * count,))],
        compiler_params=pltpu.CompilerParams(vmem_limit_bytes=16 * 2**20),
        name="settle",
    )(*arrays)


def on_device(
    dp,
    block_input,
    value_first,
    segment_ids,
    positions,
    gain_attn,
    query_weight,
    key_weight,
    value_weight,
    out_weight,
    gain_mlp,
    gate_weight,
    up_weight,
    down_weight,
    output_grad,
):
    outs = layer(
        dp,
        block_input,
        output_grad,
        value_first,
        segment_ids[None, :],
        positions[None, :],
        jnp.stack([gain_attn, gain_mlp]).astype(F32),
        query_weight,
        key_weight,
        value_weight,
        out_weight,
        gate_weight.T,
        up_weight.T,
        down_weight,
    )
    (
        block_output,
        input_grad,
        value_first_grad,
        gain_attn_grad,
        query_sum,
        key_sum,
        value_sum,
        out_sum,
        gain_mlp_grad,
        gate_sum,
        up_sum,
        down_sum,
    ) = settle(outs)
    return (
        block_output,
        input_grad,
        value_first_grad,
        gain_attn_grad[0],
        query_sum,
        key_sum,
        value_sum,
        out_sum,
        gain_mlp_grad[0],
        gate_sum.T,
        up_sum.T,
        down_sum,
    )


def solution(mesh):
    rows = P(("dp", "tensor"), None)
    weight = P("dp", "tensor")
    across = P("tensor", "dp")
    return jax.shard_map(
        functools.partial(on_device, mesh.shape["dp"]),
        mesh=mesh,
        in_specs=(
            rows,
            weight,
            P("dp"),
            P("dp"),
            P(),
            weight,
            weight,
            weight,
            across,
            P(),
            weight,
            weight,
            across,
            rows,
        ),
        out_specs=(
            rows,
            rows,
            weight,
            P(),
            weight,
            weight,
            weight,
            across,
            P(),
            weight,
            weight,
            across,
        ),
        check_vma=False,
    )
```

```python
import functools
import math

import jax
import jax.numpy as jnp
from jax import lax
from jax.experimental import pallas as pl
from jax.experimental.pallas import tpu as pltpu
from jax.sharding import PartitionSpec as P

HEAD_DIM = 64
SEQ_LEN = 1024
SEQS = 2
PIECE = 256
HALF = 512
TILE = 256
EPSILON = 1e-06
ROPE_BASE = 10000.0
MASKED = -1e30
MESH = pl.DeviceIdType.MESH
F32 = jnp.float32
BF16 = jnp.bfloat16
VMEM_LIMIT = 639 * 2**20 // 10


def dot_nn(a, b):
    return lax.dot_general(a, b, (((1,), (0,)), ((), ())), preferred_element_type=F32)


def dot_nt(a, b):
    return lax.dot_general(a, b, (((1,), (1,)), ((), ())), preferred_element_type=F32)


def dot_tn(a, b):
    return lax.dot_general(a, b, (((0,), (0,)), ((), ())), preferred_element_type=F32)


def rows_at(start, size):
    return pl.ds(pl.multiple_of(start, size), size)


def block(b):
    return rows_at(b * HALF, HALF)


class Place:
    def __init__(self, dp):
        self.d = lax.axis_index("dp")
        self.t = lax.axis_index("tensor")
        self.core = lax.rem(self.t, 2)
        self.chip = self.t // 2
        self.line = dp // 2
        self.y = lax.rem(self.d, 2)
        self.z = self.d // 2
        self.sibling = (self.d, self.t + 1 - 2 * self.core)
        self.across = (self.d, lax.rem(self.t + 2, 4))
        self.diagonal = (self.d, lax.rem(self.t + 3 - 2 * self.core, 4))
        self.pair = (self.d + 1 - 2 * self.y, self.t)
        self.up = (self.d + 2, self.t)
        self.down = (self.d - 2, self.t)

    def ahead(self, k):
        return (2 * lax.rem(self.z + k, self.line) + self.y, self.t)

    def beyond(self, k):
        return (2 * lax.rem(self.z + k, self.line) + 1 - self.y, self.t)

    def behind(self, k):
        return (2 * lax.rem(self.z + self.line - k, self.line) + self.y, self.t)

    def greet(self):
        barrier = pltpu.get_barrier_semaphore()
        partners = [self.sibling, self.across, self.diagonal, self.pair]
        partners.extend(self.ahead(k) for k in range(1, self.line))
        partners.extend(self.beyond(k) for k in range(1, self.line))
        for who in partners:
            tell(barrier, who)
        self.greeted = len(partners)

    def met(self):
        pl.semaphore_wait(pltpu.get_barrier_semaphore(), self.greeted)


def tell(sem, who):
    pl.semaphore_signal(sem, inc=1, device_id=who, device_id_type=MESH)


def send(src, dst, sems, k, who):
    return pltpu.make_async_remote_copy(
        src_ref=src,
        dst_ref=dst,
        send_sem=sems[0].at[k],
        recv_sem=sems[1].at[k],
        device_id=who,
        device_id_type=MESH,
    )


class Gather:
    def __init__(self, place, full, lanes, rows, spread, up_sems, down_sems, pair_sems):
        self.p, self.full, self.lanes, self.r, self.spread = place, full, lanes, rows, spread
        self.up_sems, self.down_sems, self.pair_sems = up_sems, down_sems, pair_sems

    def shard(self, z, y):
        return self.full.at[rows_at((2 * z + y) * self.r, self.r), self.lanes]

    def load(self, z):
        if self.spread:
            return self.shard(z, self.p.y)
        return self.full.at[rows_at(2 * z * self.r, 2 * self.r), self.lanes]

    def sides(self, k):
        p = self.p
        return (
            (p.z - k, p.z >= k, self.up_sems, p.z + 1 < p.line, p.up),
            (p.z + k, p.z + k < p.line, self.down_sems, p.z >= 1, p.down),
        )

    def start_pair(self):
        p = self.p
        here = self.shard(p.z, p.y)
        send(here, here, self.pair_sems, p.z, p.pair).start()

    def start_line(self):
        p = self.p
        if not self.spread:
            there = self.shard(p.z, 1 - p.y)
            send(there, there, self.pair_sems, p.z, p.pair).wait_recv()
        here = self.load(p.z)
        for _, _, sems, onward, to in self.sides(0):

            @pl.when(onward)
            def _():
                send(here, here, sems, 0, to).start()

    def relay(self, k):
        p = self.p
        for z, exists, sems, onward, to in self.sides(k):

            @pl.when(exists)
            def _():
                here = self.load(z)
                send(here, here, sems, k - 1, to).wait_recv()

                @pl.when(onward)
                def _():
                    send(here, here, sems, k, to).start()

                if self.spread:
                    send(here, here, self.pair_sems, z, p.pair).start()

    def finish(self):
        p = self.p
        if self.spread:
            for z in range(p.line):
                there = self.shard(z, 1 - p.y)
                send(there, there, self.pair_sems, z, p.pair).wait_recv()

    def drain(self):
        p = self.p
        for z in range(p.line) if self.spread else (p.z,):
            here = self.shard(z, p.y)
            send(here, here, self.pair_sems, z, p.pair).wait_send()
        for k in range(p.line - 1):
            for z, exists, sems, onward, to in self.sides(k):

                @pl.when(jnp.logical_and(exists, onward))
                def _():
                    here = self.load(z)
                    send(here, here, sems, k, to).wait_send()


class Scatter:
    def __init__(self, place, full, into, lanes, pair_sems, line_sems, free):
        self.p, self.full, self.into, self.lanes = place, full, into, lanes
        self.pair_sems, self.line_sems = pair_sems, line_sems
        self.free = free
        self.r = full.shape[0] // (2 * place.line)
        self.out = []

    def rows(self, k, y):
        z = lax.rem(self.p.z + k, self.p.line)
        return rows_at((2 * z + y) * self.r, self.r)

    def pair_in(self, k):
        return self.into.at[pl.ds(k * self.r, self.r), self.lanes]

    def line_in(self, k):
        return self.into.at[pl.ds((self.p.line + k - 1) * self.r, self.r), self.lanes]

    def start(self, steps):
        p = self.p
        if self.free is not None and not self.out:
            pl.semaphore_wait(self.free.at[0], 1)
        for k in steps:
            theirs = self.full.at[self.rows(k, 1 - p.y), self.lanes]
            copy = send(theirs, self.pair_in(k), self.pair_sems, k, p.pair)
            copy.start()
            self.out.append(copy)

    def relay(self, k):
        p = self.p
        there = self.pair_in(k)
        send(there, there, self.pair_sems, k, p.pair).wait_recv()
        mine = self.rows(k, p.y)
        self.full[mine, self.lanes] = (
            self.full[mine, self.lanes].astype(F32) + there[...].astype(F32)
        ).astype(BF16)
        if self.free is not None:
            pl.semaphore_wait(self.free.at[k], 1)
        self.onward(k).start()

    def onward(self, k):
        p = self.p
        mine = self.full.at[self.rows(k, p.y), self.lanes]
        return send(mine, self.line_in(k), self.line_sems, k - 1, p.ahead(k))

    def finish(self):
        p = self.p
        there = self.pair_in(0)
        send(there, there, self.pair_sems, 0, p.pair).wait_recv()
        for k in range(1, p.line):
            there = self.line_in(k)
            send(there, there, self.line_sems, k - 1, p.pair).wait_recv()

    def total(self):
        whole = self.full[self.rows(0, self.p.y), self.lanes].astype(F32)
        whole = whole + self.pair_in(0)[...].astype(F32)
        for k in range(1, self.p.line):
            whole = whole + self.line_in(k)[...].astype(F32)
        return whole

    def drain(self):
        for copy in self.out:
            copy.wait_send()
        for k in range(1, self.p.line):
            self.onward(k).wait_send()


def swap_halves(u):
    lane = lax.broadcasted_iota(jnp.int32, u.shape, 1)
    low = lax.rem(lane, HEAD_DIM) < HEAD_DIM // 2
    return jnp.where(low, pltpu.roll(u, 96, 1), pltpu.roll(u, 32, 1))


def norm_factor(u):
    return lax.rsqrt(jnp.mean(u * u, axis=-1, keepdims=True) + EPSILON)


def norm_pull(grad, u, gain):
    r = norm_factor(u)
    scaled = grad * gain
    back = r * scaled - u * (r * r * r) * jnp.mean(scaled * u, axis=-1, keepdims=True)
    return back, grad * u * r


def visible(segments):
    key = lax.broadcasted_iota(jnp.int32, (TILE, TILE), 0)
    query = lax.broadcasted_iota(jnp.int32, (TILE, TILE), 1)
    return jnp.logical_or(key <= query, segments > 0)


def attention_rows(seq, heads, i, q, k, vt, segments, attended, lse):
    lane = lax.broadcasted_iota(jnp.int32, (TILE, 128), 1)
    lanes = rows_at(heads * 128, 128)
    rows = pl.ds(seq * SEQ_LEN + i * TILE, TILE)
    q2 = q[rows, lanes]
    shown = visible(segments[:, rows])
    sides = []
    for a in range(2):
        qa = jnp.where((lane < HEAD_DIM) == (a == 0), q2, jnp.zeros_like(q2))
        vta = rows_at((heads * 2 + a) * HEAD_DIM, HEAD_DIM)
        score = jnp.where(shown, dot_nt(k[rows, lanes], qa), MASKED)
        top = jnp.max(score, axis=0, keepdims=True)
        if i > 0:
            before = dot_nt(k[pl.ds(seq * SEQ_LEN, i * TILE), lanes], qa)
            top = jnp.maximum(top, jnp.max(before, axis=0, keepdims=True))
        weight = jnp.exp(score - top)
        total = jnp.sum(weight, axis=0, keepdims=True)
        out = dot_nn(vt[vta, pl.ds(i * TILE, TILE)], weight.astype(BF16))
        if i > 0:
            weight = jnp.exp(before - top)
            total = total + jnp.sum(weight, axis=0, keepdims=True)
            out = out + dot_nn(vt[vta, pl.ds(0, i * TILE)], weight.astype(BF16))
        sides.append(out * (1.0 / total))
        lse[seq * 4 + heads * 2 + a, :, pl.ds(i * TILE, TILE)] = top + jnp.log(total)
    attended[rows, lanes] = jnp.concatenate(sides, axis=0).T.astype(BF16)


def attention_rows_back(
    seq, heads, i, q, k, v, kt, segments, lse, attended, grad_att, dk, dv, cos, sin, dqkv
):
    lane = lax.broadcasted_iota(jnp.int32, (TILE, 128), 1)
    lanes = rows_at(heads * 128, 128)
    local = pl.ds(i * TILE, TILE)
    rows = pl.ds(seq * SEQ_LEN + i * TILE, TILE)
    first = i == SEQ_LEN // TILE - 1
    q2, g2 = q[rows, lanes], grad_att(i, heads)
    shown = visible(segments[:, rows])
    products = (g2.astype(F32) * attended[rows, lanes].astype(F32)).T
    parts = [(i * TILE, TILE, True)]
    if i > 0:
        parts.append((0, i * TILE, False))
    sides = [None, None]
    for start, size, diagonal in parts:
        keys = pl.ds(seq * SEQ_LEN + start, size)
        here = pl.ds(start, size)
        dk_part, dv_part = 0.0, 0.0
        for a in range(2):
            mine = (lane < HEAD_DIM) == (a == 0)
            qa = jnp.where(mine, q2, jnp.zeros_like(q2))
            ga = jnp.where(mine, g2, jnp.zeros_like(g2))
            delta = jnp.sum(products[a * HEAD_DIM : (a + 1) * HEAD_DIM], axis=0, keepdims=True)
            stat = lse[seq * 4 + heads * 2 + a, :, local]
            score = dot_nt(k[keys, lanes], qa)
            if diagonal:
                score = jnp.where(shown, score, MASKED)
            prob = jnp.exp(score - stat)
            grad_prob = dot_nt(v[keys, lanes], ga)
            grad_score = (prob * (grad_prob - delta)).astype(BF16)
            dv_part = dv_part + dot_nn(prob.astype(BF16), ga)
            dk_part = dk_part + dot_nn(grad_score, qa)
            side = dot_nn(kt[rows_at((heads * 2 + a) * HEAD_DIM, HEAD_DIM), here], grad_score)
            sides[a] = side if sides[a] is None else sides[a] + side
        if first:
            dk[here, :] = dk_part
            dv[here, :] = dv_part
        else:
            dk[here, :] += dk_part
            dv[here, :] += dv_part
    dq = jnp.concatenate(sides, axis=0).T * HEAD_DIM**-0.5
    dqkv[local, lanes] = (dq * cos[rows, :] - swap_halves(dq) * sin[rows, :]).astype(BF16)


def layer_kernel(
    dp,
    x_in,
    og_in,
    value_first,
    segments,
    positions,
    gains,
    query_shard,
    key_shard,
    value_shard,
    out_shard,
    gate_shard,
    up_shard,
    down_shard,
    block_output,
    input_grad,
    value_first_grad,
    gain_attn_grad,
    query_sum,
    key_sum,
    value_sum,
    out_sum,
    gain_mlp_grad,
    gate_sum,
    up_sum,
    down_sum,
    xb,
    normed,
    normed_mlp,
    og,
    attn_w,
    ff_w,
    q,
    k,
    v,
    attended,
    lse,
    hidden,
    grad_hidden,
    units,
    ff_grad,
    attn_grad,
    half_out,
    half_in,
    sum_out,
    sum_in,
    m_sum,
    turned,
    dk,
    dv,
    cos,
    sin,
    gain_acc,
    gain_in,
    local_sems,
    group_out,
    group_in,
    core_out,
    core_in,
    up_out,
    up_in,
    down_out,
    down_in,
    pair_out,
    pair_in,
    line_out,
    line_in,
    gain_out_sems,
    gain_in_sems,
    credits,
    ff_free,
    attn_free,
):
    p = Place(dp)
    group, cores = (group_out, group_in), (core_out, core_in)
    rows_r, hw = query_shard.shape
    ff = gate_shard.shape[0]
    wide = ff_w.shape[1] // 3
    width = x_in.shape[1]
    tiles = SEQ_LEN // TILE
    slot = rows_at(p.d * rows_r, rows_r)
    qkv, out_lanes = slice(0, 3 * hw), slice(3 * hw, 4 * hw)
    sent = {}

    def go(name, copy):
        copy.start()
        sent[name] = copy

    def gone(name):
        sent.pop(name).wait_send()

    def arrived(there, sems, n, who):
        send(there, there, sems, n, who).wait_recv()

    def local(n, src, dst):
        return pltpu.make_async_copy(src, dst, local_sems.at[n])

    def fetch(n, src, dst):
        copy = local(n, src, dst)
        copy.start()
        return copy

    p.greet()
    x_copy = fetch(0, x_in, xb.at[p.chip])
    qkv_copies = [
        fetch(1 + n, shard, attn_w.at[slot, pl.ds(n * hw, hw)])
        for n, shard in enumerate((query_shard, key_shard, value_shard))
    ]
    og_copy = fetch(4, og_in, og.at[block(p.t)])
    vf_copy = fetch(5, value_first, attended)
    attn_w[slot, out_lanes] = out_shard[...].astype(F32).T.astype(BF16)
    p.met()
    x_copy.wait()
    go("x", send(xb.at[p.chip], xb.at[p.chip], group, 0, p.across))
    gathers = [
        Gather(
            p,
            full,
            pl.ds(first, lanes),
            rows_r,
            spread,
            (up_out.at[n], up_in.at[n]),
            (down_out.at[n], down_in.at[n]),
            (pair_out.at[n], pair_in.at[n]),
        )
        for n, (full, first, lanes, spread) in enumerate(
            (
                (attn_w, 0, 3 * hw, True),
                (attn_w, 3 * hw, hw, True),
                (ff_w, wide // 2, 3 * wide - wide // 2, True),
                (ff_w, 0, wide // 2, False),
            )
        )
    ]
    of_attn, of_out, of_ff, of_gate = gathers
    for copy in qkv_copies:
        copy.wait()
    of_attn.start_line()
    of_attn.start_pair()
    of_out.start_line()
    of_out.start_pair()
    gain_attn, gain_mlp = gains[0:1, :], gains[1:2, :]
    other = lax.rem(p.t + 2, 4)
    sib = p.t + 1 - 2 * p.core
    sib_other = lax.rem(sib + 2, 4)

    def norm_block(b, chip, n):
        @pl.loop(0, HALF // TILE)
        def _(j):
            u = xb[chip, rows_at(j * TILE, TILE), :].astype(F32)
            normed[rows_at(b * HALF + j * TILE, TILE), :] = (
                u * norm_factor(u) * gain_attn
            ).astype(BF16)

        here = normed.at[block(b)]
        go(("normed", n), send(here, here, cores, n, p.sibling))

    norm_block(p.t, p.chip, 0)
    for n, shard in enumerate((gate_shard, up_shard, down_shard)):
        flat = shard[...].astype(F32)
        if wide > ff:
            flat = jnp.concatenate([flat, jnp.zeros((wide - ff, rows_r), F32)], axis=0)
        ff_w[slot, n * wide : (n + 1) * wide] = flat.T.astype(BF16)
    of_gate.start_pair()
    if p.line > 1:
        of_attn.relay(1)
        of_out.relay(1)

    @pl.loop(0, SEQS * tiles)
    def _(j):
        rows = rows_at(j * TILE, TILE)
        lane = lax.broadcasted_iota(jnp.int32, (TILE, 128), 1)
        half = HEAD_DIM // 2
        power = lax.rem(lane[0:1, :], half).astype(F32) * (-2.0 / HEAD_DIM)
        frequency = jnp.exp(power * math.log(ROPE_BASE))
        place = jnp.broadcast_to(positions[:, rows].astype(F32), (128, TILE)).T
        angle = place * frequency
        cos[rows, :] = jnp.cos(angle)
        sine = jnp.sin(angle)
        sin[rows, :] = jnp.where(lax.rem(lane, HEAD_DIM) < half, -sine, sine)

    og_copy.wait()
    own_rows = og.at[block(p.t)]
    go("og_c", send(own_rows, own_rows, cores, 2, p.sibling))
    for n in range(2, p.line):
        of_attn.relay(n)
        of_out.relay(n)
        if n == 2:
            go("og_x", send(own_rows, own_rows, group, 1, p.across))
    if p.line < 3:
        go("og_x", send(own_rows, own_rows, group, 1, p.across))
    of_ff.start_line()
    of_gate.start_line()
    arrived(xb.at[1 - p.chip], group, 0, p.across)
    norm_block(other, 1 - p.chip, 1)
    of_ff.start_pair()
    of_attn.finish()
    arrived(normed.at[block(sib)], cores, 0, p.sibling)
    arrived(normed.at[block(sib_other)], cores, 1, p.sibling)
    vf_copy.wait()

    def project(seq):
        @pl.loop(0, tiles)
        def _(j):
            rows = rows_at(seq * SEQ_LEN + j * TILE, TILE)
            made = dot_nn(normed[rows, :], attn_w[:, qkv])
            c, s = cos[rows, :], sin[rows, :]
            for n in range(hw // 128):
                lanes = slice(n * 128, (n + 1) * 128)
                u = made[:, n * 128 : (n + 1) * 128]
                q[rows, lanes] = ((u * c + swap_halves(u) * s) * HEAD_DIM**-0.5).astype(BF16)
                u = made[:, hw + n * 128 : hw + (n + 1) * 128]
                k[rows, lanes] = (u * c + swap_halves(u) * s).astype(BF16)
            mixed = 0.5 * made[:, 2 * hw :] + 0.5 * attended[rows, :].astype(F32)
            v[rows, :] = mixed.astype(BF16)
            turned[:, rows_at(j * TILE, TILE)] = mixed.T.astype(BF16)

    def attend(seq):
        @pl.loop(0, hw // 128)
        def _(heads):
            for i in range(tiles):
                attention_rows(seq, heads, i, q, k, turned, segments, attended, lse)

    def branch_other(seq):
        @pl.loop(0, HALF // TILE)
        def _(j):
            rows = rows_at(seq * SEQ_LEN + (1 - p.core) * HALF + j * TILE, TILE)
            half_out[seq, rows_at(j * TILE, TILE), :] = dot_nt(
                attended[rows, :], attn_w[:, out_lanes]
            ).astype(BF16)

        go(("half", seq), send(half_out.at[seq], half_in.at[seq], cores, 4 + seq, p.sibling))

    def branch_own(seq):
        arrived(half_in.at[seq], cores, 4 + seq, p.sibling)

        @pl.loop(0, HALF // TILE)
        def _(j):
            rows = rows_at(seq * SEQ_LEN + p.core * HALF + j * TILE, TILE)
            tile = rows_at(j * TILE, TILE)
            part = dot_nt(attended[rows, :], attn_w[:, out_lanes])
            sum_out[seq, tile, :] = (part + half_in[seq, tile, :].astype(F32)).astype(BF16)

        go(("sum", seq), send(sum_out.at[seq], sum_in.at[seq], group, 2 + seq, p.across))

    def finish_branch(seq):
        arrived(sum_in.at[seq], group, 2 + seq, p.across)

        @pl.loop(0, HALF // TILE)
        def _(j):
            tile = rows_at(j * TILE, TILE)
            both = sum_out[seq, tile, :].astype(F32) + sum_in[seq, tile, :].astype(F32)
            u = xb[seq, tile, :].astype(F32) + both
            hidden[seq, tile, :] = u
            normed_mlp[rows_at((2 * seq + p.core) * HALF + j * TILE, TILE), :] = (
                u * norm_factor(u) * gain_mlp
            ).astype(BF16)

        mine = normed_mlp.at[block(2 * seq + p.core)]
        go(("mlp", seq), send(mine, mine, cores, 6 + seq, p.sibling))
        tell(credits.at[seq], p.across)

    steps_ff, steps_gate = list(range(1, p.line)), list(range(1, p.line))

    def relay_ff():
        if steps_ff:
            of_ff.relay(steps_ff.pop(0))

    def relay_gate():
        if steps_gate:
            of_gate.relay(steps_gate.pop(0))

    project(0)
    attend(0)
    of_out.finish()
    branch_other(0)
    relay_ff()
    project(1)
    branch_own(0)
    relay_gate()
    attend(1)
    branch_other(1)
    branch_own(1)
    relay_ff()
    relay_gate()
    arrived(og.at[block(other)], group, 1, p.across)
    there = og.at[block(other)]
    go("og_f", send(there, there, cores, 3, p.sibling))
    while steps_ff:
        relay_ff()
        relay_gate()
    finish_branch(0)
    arrived(og.at[block(sib)], cores, 2, p.sibling)
    arrived(og.at[block(sib_other)], cores, 3, p.sibling)
    of_ff.finish()

    def feed_copy(seq, n, j):
        tile = rows_at(j * TILE, TILE)
        there = half_in.at[n, tile]
        return send(half_out.at[n, tile], there, cores, 8 + seq * 4 + n * 2 + j, p.sibling)

    def feed_sum(seq, j):
        tile = rows_at(j * TILE, TILE)
        return send(sum_out.at[seq, tile], sum_in.at[seq, tile], group, 6 + seq * 2 + j, p.across)

    def feed_gone(seq):
        for n in range(2):
            for j in range(HALF // TILE):
                feed_copy(seq, n, j).wait_send()

    def feed(seq):
        arrived(normed_mlp.at[block(2 * seq + 1 - p.core)], cores, 6 + seq, p.sibling)
        if seq == 0:
            for n in range(2):
                gone(("half", n))
        else:
            feed_gone(0)
        gone(("sum", seq))
        pl.semaphore_wait(credits.at[seq], 1)

        @pl.loop(0, tiles)
        def _(step):
            j = lax.rem(step, HALF // TILE)
            others = step < HALF // TILE
            h = jnp.where(others, 1 - p.core, p.core)
            here = rows_at(h * HALF + j * TILE, TILE)
            rows = rows_at(seq * SEQ_LEN + h * HALF + j * TILE, TILE)
            tile = rows_at(j * TILE, TILE)
            for n in range(wide // 256):
                lanes = [slice(m * wide + n * 256, m * wide + (n + 1) * 256) for m in range(3)]
                gate = dot_nn(normed_mlp[rows, :], ff_w[:, lanes[0]])
                up = dot_nn(normed_mlp[rows, :], ff_w[:, lanes[1]])
                grad_act = dot_nn(og[rows, :], ff_w[:, lanes[2]])
                sig = 1.0 / (1.0 + jnp.exp(-gate))
                swish = gate * sig
                units[here, lanes[0]] = (
                    grad_act * up * sig * (1.0 + gate * (1.0 - sig))
                ).astype(BF16)
                units[here, lanes[1]] = (grad_act * swish).astype(BF16)
                units[here, lanes[2]] = (swish * up).astype(BF16)
            down = dot_nt(units[here, 2 * wide :], ff_w[:, 2 * wide :])
            back = dot_nt(units[here, : 2 * wide], ff_w[:, : 2 * wide])

            @pl.when(others)
            def _():
                half_out[0, tile, :] = back.astype(BF16)
                half_out[1, tile, :] = down.astype(BF16)
                for n in range(2):
                    feed_copy(seq, n, j).start()

            @pl.when(jnp.logical_not(others))
            def _():
                for n in range(2):
                    feed_copy(seq, n, j).wait_recv()
                sum_out[seq, tile, :] = (back + half_in[0, tile, :].astype(F32)).astype(BF16)
                m_sum[seq, tile, :] = (down + half_in[1, tile, :].astype(F32)).astype(BF16)
                feed_sum(seq, j).start()

    def ff_weights(seq, n):
        rows = pl.ds(seq * SEQ_LEN, SEQ_LEN)
        left = og if n == 2 else normed_mlp
        lanes = slice(n * wide, (n + 1) * wide)

        @pl.loop(0, width // TILE)
        def _(j):
            cols = rows_at(j * TILE, TILE)
            part = dot_tn(left[rows, cols], units[:, lanes])
            if seq > 0:
                part = part + ff_grad[cols, lanes].astype(F32)
            ff_grad[cols, lanes] = part.astype(BF16)

    def pull(seq):
        for j in range(HALF // TILE):
            feed_sum(seq, j).wait_recv()

        @pl.loop(0, HALF // TILE)
        def _(j):
            tile = rows_at(j * TILE, TILE)
            rows = rows_at((2 * seq + p.core) * HALF + j * TILE, TILE)
            grad = sum_out[seq, tile, :].astype(F32) + sum_in[seq, tile, :].astype(F32)
            back, gain_rows = norm_pull(grad, hidden[seq, tile, :], gain_mlp)
            whole = og[rows, :].astype(F32) + back
            normed_mlp[rows, :] = whole.astype(BF16)

            @pl.when(p.chip == seq)
            def _():
                grad_hidden[tile, :] = whole
                gain_acc[1:2, :] += jnp.sum(gain_rows, axis=0, keepdims=True)

        mine = normed_mlp.at[block(2 * seq + p.core)]
        pl.semaphore_wait(credits.at[2 + seq], 1)
        go(("low", seq), send(mine, mine, cores, 16 + seq, p.sibling))

        @pl.when(p.chip == seq)
        def _():
            tell(credits.at[4], p.across)

    def release(sems):
        for who, n in [(p.pair, 0)] + [(p.behind(n), n) for n in range(1, p.line)]:
            tell(sems.at[n], who)

    def free_rows(seq):
        gone(("mlp", seq))
        tell(credits.at[2 + seq], p.sibling)

    feed(0)
    ff_weights(0, 0)
    ff_weights(0, 1)
    finish_branch(1)
    ff_weights(0, 2)
    free_rows(0)
    feed(1)
    of_ff.drain()
    of_gate.drain()
    release(ff_free)
    gain_acc[...] = jnp.zeros_like(gain_acc)
    scatters = [
        Scatter(
            p,
            ff_grad,
            ff_w,
            pl.ds(n * wide, wide),
            (pair_out.at[4 + n], pair_in.at[4 + n]),
            (line_out.at[n], line_in.at[n]),
            ff_free if n == 0 else None,
        )
        for n in range(3)
    ]
    scatter_attn = Scatter(
        p,
        attn_grad,
        og,
        pl.ds(0, 4 * hw),
        (pair_out.at[7], pair_in.at[7]),
        (line_out.at[3], line_in.at[3]),
        attn_free,
    )
    away = list(range(1, p.line))
    for n in range(3):
        ff_weights(1, n)
        scatters[n].start(away or [0])
    if away:
        for n in range(3):
            scatters[n].start([0])
    relays = [(scatters[n], k) for n in range(3) for k in away]

    def relay_grad():
        if relays:
            scatter, k = relays.pop(0)
            scatter.relay(k)

    pull(0)
    free_rows(1)

    dqkv = units

    def grad_att(i, heads):
        return units[pl.ds(i * TILE, TILE), rows_at(3 * hw + heads * 128, 128)]

    def turn(seq):
        @pl.loop(0, tiles)
        def _(j):
            rows = rows_at(seq * SEQ_LEN + j * TILE, TILE)
            turned[:, rows_at(j * TILE, TILE)] = k[rows, :].astype(F32).T.astype(BF16)

    def prepare(seq):
        arrived(normed_mlp.at[block(2 * seq + 1 - p.core)], cores, 16 + seq, p.sibling)

        @pl.loop(0, tiles)
        def _(j):
            here = rows_at(j * TILE, TILE)
            rows = rows_at(seq * SEQ_LEN + j * TILE, TILE)
            units[here, out_lanes] = dot_nn(normed_mlp[rows, :], attn_w[:, out_lanes]).astype(BF16)

    def grad_store(seq, heads):
        rows = pl.ds(seq * SEQ_LEN, SEQ_LEN)
        return local(6, dv, value_first_grad.at[rows, rows_at(heads * 128, 128)])

    def attend_back(seq):
        if seq > 0:
            grad_store(0, hw // 128 - 1).wait()

        @pl.loop(0, hw // 128)
        def _(heads):
            @pl.when(heads > 0)
            def _():
                grad_store(seq, heads - 1).wait()

            @pl.when(heads > 0)
            def _():
                for _ in range(2):
                    relay_grad()

            for i in reversed(range(tiles)):
                attention_rows_back(
                    seq,
                    heads,
                    i,
                    q,
                    k,
                    v,
                    turned,
                    segments,
                    lse,
                    attended,
                    grad_att,
                    dk,
                    dv,
                    cos,
                    sin,
                    dqkv,
                )

            @pl.loop(0, tiles)
            def _(j):
                here = rows_at(j * TILE, TILE)
                rows = rows_at(seq * SEQ_LEN + j * TILE, TILE)
                u = dk[here, :]
                dqkv[here, rows_at(hw + heads * 128, 128)] = (
                    u * cos[rows, :] - swap_halves(u) * sin[rows, :]
                ).astype(BF16)
                half = 0.5 * dv[here, :]
                dqkv[here, rows_at(2 * hw + heads * 128, 128)] = half.astype(BF16)
                dv[here, :] = half

            grad_store(seq, heads).start()

    def attn_weights(seq):
        rows = pl.ds(seq * SEQ_LEN, SEQ_LEN)

        @pl.loop(0, width // TILE)
        def _(j):
            cols = rows_at(j * TILE, TILE)
            for left, right, lanes in (
                (normed, units[:, qkv], qkv),
                (normed_mlp, attended[rows, :], out_lanes),
            ):
                part = dot_tn(left[rows, cols], right)
                if seq > 0:
                    part = part + attn_grad[cols, lanes].astype(F32)
                attn_grad[cols, lanes] = part.astype(BF16)

    def back_other(seq):
        if seq == 0:
            feed_gone(1)

        @pl.loop(0, HALF // TILE)
        def _(j):
            here = rows_at((1 - p.core) * HALF + j * TILE, TILE)
            half_out[seq, rows_at(j * TILE, TILE), :] = dot_nt(
                dqkv[here, qkv], attn_w[:, qkv]
            ).astype(BF16)

        go(("half", seq), send(half_out.at[seq], half_in.at[seq], cores, 18 + seq, p.sibling))

    def back_own(seq):
        arrived(half_in.at[seq], cores, 18 + seq, p.sibling)
        for j in range(HALF // TILE):
            feed_sum(seq, j).wait_send()

        @pl.loop(0, HALF // TILE)
        def _(j):
            here = rows_at(p.core * HALF + j * TILE, TILE)
            tile = rows_at(j * TILE, TILE)
            part = dot_nt(dqkv[here, qkv], attn_w[:, qkv])
            sum_out[seq, tile, :] = (part + half_in[seq, tile, :].astype(F32)).astype(BF16)

        @pl.when(p.chip != seq)
        def _():
            pl.semaphore_wait(credits.at[4], 1)
            send(sum_out.at[seq], sum_in.at[seq], group, 5, p.across).start()

    turn(0)
    relay_grad()
    prepare(0)
    attend_back(0)
    relay_grad()
    back_other(0)
    turn(1)
    attn_weights(0)
    pull(1)
    go("m", send(m_sum.at[1 - p.chip], xb.at[p.chip], group, 4, p.across))
    for name in ("og_x", "og_c", "og_f"):
        gone(name)
    release(attn_free)
    back_own(0)
    relay_grad()
    prepare(1)
    attend_back(1)
    back_other(1)
    relay_grad()
    back_own(1)
    attn_weights(1)
    scatter_attn.start(away or [0])
    if away:
        scatter_attn.start([0])
    while relays:
        relay_grad()

    for n in range(1, p.line):
        scatter_attn.relay(n)
    arrived(sum_in.at[p.chip], group, 5, p.across)

    @pl.loop(0, HALF // TILE)
    def _(j):
        tile = rows_at(j * TILE, TILE)
        grad = sum_out[p.chip, tile, :].astype(F32) + sum_in[p.chip, tile, :].astype(F32)
        back, gain_rows = norm_pull(grad, xb[p.chip, tile, :].astype(F32), gain_attn)
        grad_hidden[tile, :] = grad_hidden[tile, :] + back
        gain_acc[0:1, :] += jnp.sum(gain_rows, axis=0, keepdims=True)

    stores = [fetch(9, grad_hidden, input_grad)]
    gain_sems = (gain_out_sems, gain_in_sems)

    def exchange(partners, first):
        copies = []
        for n, who in enumerate(partners):
            copy = send(gain_acc, gain_in.at[first + n], gain_sems, first + n, who)
            copy.start()
            copies.append(copy)

        def rest():
            for copy in copies:
                copy.wait()
            whole = gain_acc[...]
            for n in range(len(partners)):
                whole = whole + gain_in[first + n]
            gain_acc[...] = whole

        return rest

    rest = exchange([p.sibling, p.across, p.diagonal], 0)
    arrived(xb.at[1 - p.chip], group, 4, p.across)

    @pl.loop(0, HALF // TILE)
    def _(j):
        tile = rows_at(j * TILE, TILE)
        both = m_sum[p.chip, tile, :].astype(F32) + xb[1 - p.chip, tile, :].astype(F32)
        m_sum[p.chip, tile, :] = (hidden[p.chip, tile, :] + both).astype(BF16)

    stores.append(fetch(8, m_sum.at[p.chip], block_output))
    rest()
    far = [p.ahead(n) for n in range(1, p.line)] + [p.beyond(n) for n in range(1, p.line)]
    rest = exchange([p.pair] + far, 3)
    for n, out in enumerate((gate_sum, up_sum, down_sum)):
        scatters[n].finish()
        out[...] = scatters[n].total().T[:ff, :]
    scatter_attn.finish()
    whole = scatter_attn.total()
    for n, out in enumerate((query_sum, key_sum, value_sum)):
        out[...] = whole[:, n * hw : (n + 1) * hw]
    out_sum[...] = whole[:, out_lanes].T
    rest()
    gain_attn_grad[...] = gain_acc[0:1, :]
    gain_mlp_grad[...] = gain_acc[1:2, :]
    send(sum_out.at[1 - p.chip], sum_in.at[1 - p.chip], group, 5, p.across).wait_send()
    grad_store(SEQS - 1, hw // 128 - 1).wait()
    for name in list(sent):
        gone(name)
    of_attn.drain()
    of_out.drain()
    for scatter in (*scatters, scatter_attn):
        scatter.drain()
    for copy in stores:
        copy.wait()


def layer(dp, x, og, vf, segments, positions, gains, wq, wk, wv, wo, wg, wu, wd):
    rows, width = 4 * x.shape[0], x.shape[1]
    hw, ff, r = vf.shape[1], wg.shape[0], wq.shape[0]
    wide = -(-ff // 256) * 256
    line = dp // 2
    hops = max(line - 1, 1)
    vmem = pl.BlockSpec(memory_space=pltpu.VMEM)
    far = pl.BlockSpec(memory_space=pl.ANY)
    shapes = [
        ((HALF, width), BF16, far),
        ((HALF, width), F32, far),
        ((rows, hw), F32, far),
        ((1, width), F32, vmem),
        ((r, hw), F32, vmem),
        ((r, hw), F32, vmem),
        ((r, hw), F32, vmem),
        ((hw, r), F32, vmem),
        ((1, width), F32, vmem),
        ((ff, r), F32, vmem),
        ((ff, r), F32, vmem),
        ((ff, r), F32, vmem),
    ]
    dma = pltpu.SemaphoreType.DMA
    flag = pltpu.SemaphoreType.REGULAR

    def bf(*shape):
        return pltpu.VMEM(shape, BF16)

    def fl(*shape):
        return pltpu.VMEM(shape, F32)

    scratch = [
        bf(2, HALF, width),
        bf(rows, width),
        bf(rows, width),
        bf(rows, width),
        bf(width, 4 * hw),
        bf(width, 3 * wide),
        bf(rows, hw),
        bf(rows, hw),
        bf(rows, hw),
        bf(rows, hw),
        fl(8, 1, SEQ_LEN),
        fl(2, HALF, width),
        fl(HALF, width),
        bf(SEQ_LEN, 3 * wide),
        bf(width, 3 * wide),
        bf(width, 4 * hw),
        bf(2, HALF, width),
        bf(2, HALF, width),
        bf(2, HALF, width),
        bf(2, HALF, width),
        bf(2, HALF, width),
        bf(hw, SEQ_LEN),
        fl(SEQ_LEN, 128),
        fl(SEQ_LEN, 128),
        fl(rows, 128),
        fl(rows, 128),
        fl(2, width),
        fl(4 + 2 * hops, 2, width),
        dma((10,)),
        dma((10,)),
        dma((10,)),
        dma((20,)),
        dma((20,)),
        dma((4, hops)),
        dma((4, hops)),
        dma((4, hops)),
        dma((4, hops)),
        dma((8, line)),
        dma((8, line)),
        dma((4, hops)),
        dma((4, hops)),
        dma((4 + 2 * hops,)),
        dma((4 + 2 * hops,)),
        flag((5,)),
        flag((line,)),
        flag((line,)),
    ]
    in_specs = [far] * 3 + [vmem] * 3 + [far] * 3 + [vmem] * 4
    return pl.pallas_call(
        functools.partial(layer_kernel, dp),
        out_shape=[jax.ShapeDtypeStruct(s, t) for s, t, _ in shapes],
        in_specs=in_specs,
        out_specs=[space for _, _, space in shapes],
        scratch_shapes=scratch,
        compiler_params=pltpu.CompilerParams(
            collective_id=0, has_side_effects=True, vmem_limit_bytes=VMEM_LIMIT
        ),
        name="layer",
    )(x, og, vf, segments, positions, gains, wq, wk, wv, wo, wg, wu, wd)


def settle_kernel(count, *refs):
    ins, outs, held, sems = refs[:count], refs[count : 2 * count], refs[2 * count : -1], refs[-1]
    first = [pltpu.make_async_copy(ins[n], held[n], sems.at[n]) for n in range(count)]
    second = [pltpu.make_async_copy(held[n], outs[n], sems.at[count + n]) for n in range(count)]
    for copy in first:
        copy.start()
    for n in range(count):
        first[n].wait()
        second[n].start()
    for copy in second:
        copy.wait()


def settle(arrays):
    count = len(arrays)
    far = pl.BlockSpec(memory_space=pl.ANY)
    return pl.pallas_call(
        functools.partial(settle_kernel, count),
        out_shape=[jax.ShapeDtypeStruct(a.shape, a.dtype) for a in arrays],
        in_specs=[far] * count,
        out_specs=[far] * count,
        scratch_shapes=[pltpu.VMEM(a.shape, a.dtype) for a in arrays]
        + [pltpu.SemaphoreType.DMA((2 * count,))],
        compiler_params=pltpu.CompilerParams(vmem_limit_bytes=VMEM_LIMIT),
        name="settle",
    )(*arrays)


def on_device(
    dp,
    block_input,
    value_first,
    segment_ids,
    positions,
    gain_attn,
    query_weight,
    key_weight,
    value_weight,
    out_weight,
    gain_mlp,
    gate_weight,
    up_weight,
    down_weight,
    output_grad,
):
    outs = layer(
        dp,
        block_input,
        output_grad,
        value_first,
        segment_ids[None, :],
        positions[None, :],
        jnp.stack([gain_attn, gain_mlp]).astype(F32),
        query_weight,
        key_weight,
        value_weight,
        out_weight,
        gate_weight.T,
        up_weight.T,
        down_weight,
    )
    (
        block_output,
        input_grad,
        value_first_grad,
        gain_attn_grad,
        query_sum,
        key_sum,
        value_sum,
        out_sum,
        gain_mlp_grad,
        gate_sum,
        up_sum,
        down_sum,
    ) = settle(outs)
    return (
        block_output,
        input_grad,
        value_first_grad,
        gain_attn_grad[0],
        query_sum,
        key_sum,
        value_sum,
        out_sum,
        gain_mlp_grad[0],
        gate_sum.T,
        up_sum.T,
        down_sum,
    )


def solution(mesh):
    rows = P(("dp", "tensor"), None)
    weight = P("dp", "tensor")
    across = P("tensor", "dp")
    return jax.shard_map(
        functools.partial(on_device, mesh.shape["dp"]),
        mesh=mesh,
        in_specs=(
            rows,
            weight,
            P("dp"),
            P("dp"),
            P(),
            weight,
            weight,
            weight,
            across,
            P(),
            weight,
            weight,
            across,
            rows,
        ),
        out_specs=(
            rows,
            rows,
            weight,
            P(),
            weight,
            weight,
            weight,
            across,
            P(),
            weight,
            weight,
            across,
        ),
        check_vma=False,
    )
```

```python
import functools
import math

import jax
import jax.numpy as jnp
from jax import lax
from jax.experimental import pallas as pl
from jax.experimental.pallas import tpu as pltpu
from jax.sharding import PartitionSpec as P

HEAD_DIM = 64
SEQ_LEN = 1024
SEQS = 2
PIECE = 256
HALF = 512
TILE = 256
EPSILON = 1e-06
ROPE_BASE = 10000.0
MASKED = -1e30
MESH = pl.DeviceIdType.MESH
F32 = jnp.float32
BF16 = jnp.bfloat16
VMEM_LIMIT = 639 * 2**20 // 10


def dot_nn(a, b):
    return lax.dot_general(a, b, (((1,), (0,)), ((), ())), preferred_element_type=F32)


def dot_nt(a, b):
    return lax.dot_general(a, b, (((1,), (1,)), ((), ())), preferred_element_type=F32)


def dot_tn(a, b):
    return lax.dot_general(a, b, (((0,), (0,)), ((), ())), preferred_element_type=F32)


def rows_at(start, size):
    return pl.ds(pl.multiple_of(start, size), size)


def block(b):
    return rows_at(b * HALF, HALF)


class Place:
    def __init__(self, dp):
        self.d = lax.axis_index("dp")
        self.t = lax.axis_index("tensor")
        self.core = lax.rem(self.t, 2)
        self.chip = self.t // 2
        self.line = dp // 2
        self.y = lax.rem(self.d, 2)
        self.z = self.d // 2
        self.sibling = (self.d, self.t + 1 - 2 * self.core)
        self.across = (self.d, lax.rem(self.t + 2, 4))
        self.pair = (self.d + 1 - 2 * self.y, self.t)
        self.up = (self.d + 2, self.t)
        self.down = (self.d - 2, self.t)

    def ahead(self, k):
        return (2 * lax.rem(self.z + k, self.line) + self.y, self.t)

    def beyond(self, k):
        return (2 * lax.rem(self.z + k, self.line) + 1 - self.y, self.t)

    def behind(self, k):
        return (2 * lax.rem(self.z + self.line - k, self.line) + self.y, self.t)

    def greet(self):
        barrier = pltpu.get_barrier_semaphore()
        partners = [self.sibling, self.across, self.pair]
        partners.extend(self.ahead(k) for k in range(1, self.line))
        partners.extend(self.beyond(k) for k in range(1, self.line))
        for who in partners:
            tell(barrier, who)
        self.greeted = len(partners)

    def met(self):
        pl.semaphore_wait(pltpu.get_barrier_semaphore(), self.greeted)


def tell(sem, who):
    pl.semaphore_signal(sem, inc=1, device_id=who, device_id_type=MESH)


def send(src, dst, sems, k, who):
    return pltpu.make_async_remote_copy(
        src_ref=src,
        dst_ref=dst,
        send_sem=sems[0].at[k],
        recv_sem=sems[1].at[k],
        device_id=who,
        device_id_type=MESH,
    )


class Gather:
    def __init__(self, place, full, lanes, rows, spread, up_sems, down_sems, pair_sems):
        self.p, self.full, self.lanes, self.r, self.spread = place, full, lanes, rows, spread
        self.up_sems, self.down_sems, self.pair_sems = up_sems, down_sems, pair_sems

    def shard(self, z, y):
        return self.full.at[rows_at((2 * z + y) * self.r, self.r), self.lanes]

    def load(self, z):
        if self.spread:
            return self.shard(z, self.p.y)
        return self.full.at[rows_at(2 * z * self.r, 2 * self.r), self.lanes]

    def sides(self, k):
        p = self.p
        return (
            (p.z - k, p.z >= k, self.up_sems, p.z + 1 < p.line, p.up),
            (p.z + k, p.z + k < p.line, self.down_sems, p.z >= 1, p.down),
        )

    def start_pair(self):
        p = self.p
        here = self.shard(p.z, p.y)
        send(here, here, self.pair_sems, p.z, p.pair).start()

    def start_line(self):
        p = self.p
        if not self.spread:
            there = self.shard(p.z, 1 - p.y)
            send(there, there, self.pair_sems, p.z, p.pair).wait_recv()
        here = self.load(p.z)
        for _, _, sems, onward, to in self.sides(0):

            @pl.when(onward)
            def _():
                send(here, here, sems, 0, to).start()

    def relay(self, k):
        p = self.p
        for z, exists, sems, onward, to in self.sides(k):

            @pl.when(exists)
            def _():
                here = self.load(z)
                send(here, here, sems, k - 1, to).wait_recv()

                @pl.when(onward)
                def _():
                    send(here, here, sems, k, to).start()

                if self.spread:
                    send(here, here, self.pair_sems, z, p.pair).start()

    def finish(self):
        p = self.p
        if self.spread:
            for z in range(p.line):
                there = self.shard(z, 1 - p.y)
                send(there, there, self.pair_sems, z, p.pair).wait_recv()

    def drain(self):
        p = self.p
        for z in range(p.line) if self.spread else (p.z,):
            here = self.shard(z, p.y)
            send(here, here, self.pair_sems, z, p.pair).wait_send()
        for k in range(p.line - 1):
            for z, exists, sems, onward, to in self.sides(k):

                @pl.when(jnp.logical_and(exists, onward))
                def _():
                    here = self.load(z)
                    send(here, here, sems, k, to).wait_send()


def far_first(n):
    if n < 4:
        return list(range(1, n))
    last = [2, n - 2] if n > 4 else [2]
    return [1, n - 1, *range(3, n - 2), *last]


class Scatter:
    def __init__(self, place, full, into, lanes, pair_sems, line_sems, free):
        self.p, self.full, self.into, self.lanes = place, full, into, lanes
        self.pair_sems, self.line_sems = pair_sems, line_sems
        self.free = free
        self.r = full.shape[0] // (2 * place.line)
        self.out = []

    def rows(self, k, y):
        z = lax.rem(self.p.z + k, self.p.line)
        return rows_at((2 * z + y) * self.r, self.r)

    def pair_in(self, k):
        return self.into.at[pl.ds(k * self.r, self.r), self.lanes]

    def line_in(self, k):
        return self.into.at[pl.ds((self.p.line + k - 1) * self.r, self.r), self.lanes]

    def start(self, steps):
        p = self.p
        if self.free is not None and not self.out:
            pl.semaphore_wait(self.free.at[0], 1)
        for k in steps:
            theirs = self.full.at[self.rows(k, 1 - p.y), self.lanes]
            copy = send(theirs, self.pair_in(k), self.pair_sems, k, p.pair)
            copy.start()
            self.out.append(copy)

    def relay(self, k):
        p = self.p
        n = p.line
        there = self.pair_in(k)
        send(there, there, self.pair_sems, k, p.pair).wait_recv()
        mine = self.rows(k, p.y)
        self.full[mine, self.lanes] = (
            self.full[mine, self.lanes].astype(F32) + there[...].astype(F32)
        ).astype(BF16)
        if self.free is not None and k == 1:
            for m in range(1, n):
                pl.semaphore_wait(self.free.at[m], 1)
        if n >= 4 and k in (2, n - 2):
            helping = jnp.logical_or(
                jnp.logical_and(p.z == 1, k == n - 2), jnp.logical_and(p.z == n - 2, k == 2)
            )

            @pl.when(helping)
            def _():
                self.helped().wait_recv()
                self.full[mine, self.lanes] = (
                    self.full[mine, self.lanes].astype(F32) + self.line_in(n)[...].astype(F32)
                ).astype(BF16)

        if n >= 4 and k in (1, n - 1):
            from_end = p.z == (0 if k == n - 1 else n - 1)

            @pl.when(from_end)
            def _():
                self.helped(k).start()

            @pl.when(jnp.logical_not(from_end))
            def _():
                self.onward(k).start()
        else:
            self.onward(k).start()

    def helped(self, k=1):
        p = self.p
        near = jnp.where(p.z == 0, 1, p.line - 2)
        mine = self.full.at[self.rows(k, p.y), self.lanes]
        return pltpu.make_async_remote_copy(
            src_ref=mine,
            dst_ref=self.line_in(p.line),
            send_sem=self.line_sems[0].at[k - 1],
            recv_sem=self.line_sems[1].at[p.line - 1],
            device_id=(2 * near + p.y, p.t),
            device_id_type=MESH,
        )

    def onward(self, k):
        p = self.p
        mine = self.full.at[self.rows(k, p.y), self.lanes]
        return send(mine, self.line_in(k), self.line_sems, k - 1, p.ahead(k))

    def merged(self, k):
        n = self.p.line
        if n < 4 or k not in (1, n - 1):
            return None
        return self.p.z == (n - 1 if k == n - 1 else 0)

    def finish(self):
        p = self.p
        there = self.pair_in(0)
        send(there, there, self.pair_sems, 0, p.pair).wait_recv()
        for k in range(1, p.line):
            there = self.line_in(k)
            merged = self.merged(k)
            if merged is None:
                send(there, there, self.line_sems, k - 1, p.pair).wait_recv()
            else:

                @pl.when(jnp.logical_not(merged))
                def _():
                    send(there, there, self.line_sems, k - 1, p.pair).wait_recv()

    def total(self):
        whole = self.full[self.rows(0, self.p.y), self.lanes].astype(F32)
        whole = whole + self.pair_in(0)[...].astype(F32)
        for k in range(1, self.p.line):
            came = self.line_in(k)[...].astype(F32)
            merged = self.merged(k)
            if merged is not None:
                came = jnp.where(merged, jnp.zeros_like(came), came)
            whole = whole + came
        return whole

    def drain(self):
        for copy in self.out:
            copy.wait_send()
        for k in range(1, self.p.line):
            self.onward(k).wait_send()


def swap_halves(u):
    lane = lax.broadcasted_iota(jnp.int32, u.shape, 1)
    low = lax.rem(lane, HEAD_DIM) < HEAD_DIM // 2
    return jnp.where(low, pltpu.roll(u, 96, 1), pltpu.roll(u, 32, 1))


def norm_factor(u):
    return lax.rsqrt(jnp.mean(u * u, axis=-1, keepdims=True) + EPSILON)


def norm_pull(grad, u, gain):
    r = norm_factor(u)
    scaled = grad * gain
    back = r * scaled - u * (r * r * r) * jnp.mean(scaled * u, axis=-1, keepdims=True)
    return back, grad * u * r


def visible(segments):
    key = lax.broadcasted_iota(jnp.int32, (TILE, TILE), 0)
    query = lax.broadcasted_iota(jnp.int32, (TILE, TILE), 1)
    return jnp.logical_or(key <= query, segments > 0)


def attention_rows(seq, heads, i, q, k, vt, segments, attended, lse):
    lane = lax.broadcasted_iota(jnp.int32, (TILE, 128), 1)
    lanes = rows_at(heads * 128, 128)
    rows = pl.ds(seq * SEQ_LEN + i * TILE, TILE)
    q2 = q[rows, lanes]
    shown = visible(segments[:, rows])
    sides = []
    for a in range(2):
        qa = jnp.where((lane < HEAD_DIM) == (a == 0), q2, jnp.zeros_like(q2))
        vta = rows_at((heads * 2 + a) * HEAD_DIM, HEAD_DIM)
        score = jnp.where(shown, dot_nt(k[rows, lanes], qa), MASKED)
        top = jnp.max(score, axis=0, keepdims=True)
        if i > 0:
            before = dot_nt(k[pl.ds(seq * SEQ_LEN, i * TILE), lanes], qa)
            top = jnp.maximum(top, jnp.max(before, axis=0, keepdims=True))
        weight = jnp.exp(score - top)
        total = jnp.sum(weight, axis=0, keepdims=True)
        out = dot_nn(vt[vta, pl.ds(i * TILE, TILE)], weight.astype(BF16))
        if i > 0:
            weight = jnp.exp(before - top)
            total = total + jnp.sum(weight, axis=0, keepdims=True)
            out = out + dot_nn(vt[vta, pl.ds(0, i * TILE)], weight.astype(BF16))
        sides.append(out * (1.0 / total))
        lse[seq * 4 + heads * 2 + a, :, pl.ds(i * TILE, TILE)] = top + jnp.log(total)
    attended[rows, lanes] = jnp.concatenate(sides, axis=0).T.astype(BF16)


def attention_rows_back(
    seq, heads, i, q, k, v, kt, segments, lse, attended, grad_att, dk, dv, cos, sin, dqkv
):
    lane = lax.broadcasted_iota(jnp.int32, (TILE, 128), 1)
    lanes = rows_at(heads * 128, 128)
    local = pl.ds(i * TILE, TILE)
    rows = pl.ds(seq * SEQ_LEN + i * TILE, TILE)
    first = i == SEQ_LEN // TILE - 1
    q2, g2 = q[rows, lanes], grad_att(i, heads)
    shown = visible(segments[:, rows])
    products = (g2.astype(F32) * attended[rows, lanes].astype(F32)).T
    parts = [(i * TILE, TILE, True)]
    if i > 0:
        parts.append((0, i * TILE, False))
    sides = [None, None]
    for start, size, diagonal in parts:
        keys = pl.ds(seq * SEQ_LEN + start, size)
        here = pl.ds(start, size)
        dk_part, dv_part = 0.0, 0.0
        for a in range(2):
            mine = (lane < HEAD_DIM) == (a == 0)
            qa = jnp.where(mine, q2, jnp.zeros_like(q2))
            ga = jnp.where(mine, g2, jnp.zeros_like(g2))
            delta = jnp.sum(products[a * HEAD_DIM : (a + 1) * HEAD_DIM], axis=0, keepdims=True)
            stat = lse[seq * 4 + heads * 2 + a, :, local]
            score = dot_nt(k[keys, lanes], qa)
            if diagonal:
                score = jnp.where(shown, score, MASKED)
            prob = jnp.exp(score - stat)
            grad_prob = dot_nt(v[keys, lanes], ga)
            grad_score = (prob * (grad_prob - delta)).astype(BF16)
            dv_part = dv_part + dot_nn(prob.astype(BF16), ga)
            dk_part = dk_part + dot_nn(grad_score, qa)
            side = dot_nn(kt[rows_at((heads * 2 + a) * HEAD_DIM, HEAD_DIM), here], grad_score)
            sides[a] = side if sides[a] is None else sides[a] + side
        if first:
            dk[here, :] = dk_part
            dv[here, :] = dv_part
        else:
            dk[here, :] += dk_part
            dv[here, :] += dv_part
    dq = jnp.concatenate(sides, axis=0).T * HEAD_DIM**-0.5
    dqkv[local, lanes] = (dq * cos[rows, :] - swap_halves(dq) * sin[rows, :]).astype(BF16)


def layer_kernel(
    dp,
    x_in,
    og_in,
    value_first,
    segments,
    positions,
    gains,
    query_shard,
    key_shard,
    value_shard,
    out_shard,
    gate_shard,
    up_shard,
    down_shard,
    block_output,
    input_grad,
    value_first_grad,
    gain_attn_grad,
    query_sum,
    key_sum,
    value_sum,
    out_sum,
    gain_mlp_grad,
    gate_sum,
    up_sum,
    down_sum,
    xb,
    normed,
    normed_mlp,
    og,
    attn_w,
    ff_w,
    q,
    k,
    v,
    attended,
    lse,
    hidden,
    grad_hidden,
    units,
    ff_grad,
    attn_grad,
    half_out,
    half_in,
    sum_out,
    sum_in,
    m_sum,
    turned,
    dk,
    dv,
    cos,
    sin,
    gain_acc,
    gain_in,
    local_sems,
    group_out,
    group_in,
    core_out,
    core_in,
    up_out,
    up_in,
    down_out,
    down_in,
    pair_out,
    pair_in,
    line_out,
    line_in,
    gain_out_sems,
    gain_in_sems,
    credits,
    ff_free,
    attn_free,
):
    p = Place(dp)
    group, cores = (group_out, group_in), (core_out, core_in)
    rows_r, hw = query_shard.shape
    ff = gate_shard.shape[0]
    wide = ff_w.shape[1] // 3
    width = x_in.shape[1]
    tiles = SEQ_LEN // TILE
    slot = rows_at(p.d * rows_r, rows_r)
    qkv, out_lanes = slice(0, 3 * hw), slice(3 * hw, 4 * hw)
    middle = wide + 5 * wide // 6 // 128 * 128
    sent = {}

    def go(name, copy):
        copy.start()
        sent[name] = copy

    def gone(name):
        sent.pop(name).wait_send()

    def arrived(there, sems, n, who):
        send(there, there, sems, n, who).wait_recv()

    def local(n, src, dst):
        return pltpu.make_async_copy(src, dst, local_sems.at[n])

    def fetch(n, src, dst):
        copy = local(n, src, dst)
        copy.start()
        return copy

    p.greet()
    x_copy = fetch(0, x_in, xb.at[p.chip])
    qkv_copies = [
        fetch(1 + n, shard, attn_w.at[slot, pl.ds(n * hw, hw)])
        for n, shard in enumerate((query_shard, key_shard, value_shard))
    ]
    og_copy = fetch(4, og_in, og.at[block(p.t)])
    vf_copy = fetch(5, value_first, attended)
    attn_w[slot, out_lanes] = out_shard[...].astype(F32).T.astype(BF16)
    p.met()
    x_copy.wait()
    go("x", send(xb.at[p.chip], xb.at[p.chip], group, 0, p.across))
    gathers = [
        Gather(
            p,
            full,
            pl.ds(first, lanes),
            rows_r,
            spread,
            (up_out.at[n], up_in.at[n]),
            (down_out.at[n], down_in.at[n]),
            (pair_out.at[n], pair_in.at[n]),
        )
        for n, (full, first, lanes, spread) in enumerate(
            (
                (attn_w, 0, 3 * hw, True),
                (attn_w, 3 * hw, hw, True),
                (ff_w, wide // 2, middle - wide // 2, True),
                (ff_w, middle, 3 * wide - middle, True),
                (ff_w, 0, wide // 2, False),
            )
        )
    ]
    of_attn, of_out, of_ff, of_rest, of_gate = gathers
    for copy in qkv_copies:
        copy.wait()
    of_attn.start_line()
    of_attn.start_pair()
    of_out.start_line()
    of_out.start_pair()
    gain_attn, gain_mlp = gains[0:1, :], gains[1:2, :]
    other = lax.rem(p.t + 2, 4)
    sib = p.t + 1 - 2 * p.core
    sib_other = lax.rem(sib + 2, 4)

    def norm_block(b, chip, n):
        @pl.loop(0, HALF // TILE)
        def _(j):
            u = xb[chip, rows_at(j * TILE, TILE), :].astype(F32)
            normed[rows_at(b * HALF + j * TILE, TILE), :] = (
                u * norm_factor(u) * gain_attn
            ).astype(BF16)

        here = normed.at[block(b)]
        go(("normed", n), send(here, here, cores, n, p.sibling))

    norm_block(p.t, p.chip, 0)
    for n, shard in enumerate((gate_shard, up_shard, down_shard)):
        flat = shard[...].astype(F32)
        if wide > ff:
            flat = jnp.concatenate([flat, jnp.zeros((wide - ff, rows_r), F32)], axis=0)
        ff_w[slot, n * wide : (n + 1) * wide] = flat.T.astype(BF16)
    of_gate.start_pair()
    if p.line > 1:
        of_attn.relay(1)
        of_out.relay(1)

    @pl.loop(0, SEQS * tiles)
    def _(j):
        rows = rows_at(j * TILE, TILE)
        lane = lax.broadcasted_iota(jnp.int32, (TILE, 128), 1)
        half = HEAD_DIM // 2
        power = lax.rem(lane[0:1, :], half).astype(F32) * (-2.0 / HEAD_DIM)
        frequency = jnp.exp(power * math.log(ROPE_BASE))
        place = jnp.broadcast_to(positions[:, rows].astype(F32), (128, TILE)).T
        angle = place * frequency
        cos[rows, :] = jnp.cos(angle)
        sine = jnp.sin(angle)
        sin[rows, :] = jnp.where(lax.rem(lane, HEAD_DIM) < half, -sine, sine)

    og_copy.wait()
    own_rows = og.at[block(p.t)]
    go("og_c", send(own_rows, own_rows, cores, 2, p.sibling))
    for n in range(2, p.line):
        of_attn.relay(n)
        of_out.relay(n)
        if n == 2:
            go("og_x", send(own_rows, own_rows, group, 1, p.across))
    if p.line < 3:
        go("og_x", send(own_rows, own_rows, group, 1, p.across))
    of_ff.start_line()
    of_rest.start_line()
    of_gate.start_line()
    arrived(xb.at[1 - p.chip], group, 0, p.across)
    norm_block(other, 1 - p.chip, 1)
    of_ff.start_pair()
    of_rest.start_pair()
    of_attn.finish()
    arrived(normed.at[block(sib)], cores, 0, p.sibling)
    arrived(normed.at[block(sib_other)], cores, 1, p.sibling)
    vf_copy.wait()

    def project(seq):
        @pl.loop(0, tiles)
        def _(j):
            rows = rows_at(seq * SEQ_LEN + j * TILE, TILE)
            made = dot_nn(normed[rows, :], attn_w[:, qkv])
            c, s = cos[rows, :], sin[rows, :]
            for n in range(hw // 128):
                lanes = slice(n * 128, (n + 1) * 128)
                u = made[:, n * 128 : (n + 1) * 128]
                q[rows, lanes] = ((u * c + swap_halves(u) * s) * HEAD_DIM**-0.5).astype(BF16)
                u = made[:, hw + n * 128 : hw + (n + 1) * 128]
                k[rows, lanes] = (u * c + swap_halves(u) * s).astype(BF16)
            mixed = 0.5 * made[:, 2 * hw :] + 0.5 * attended[rows, :].astype(F32)
            v[rows, :] = mixed.astype(BF16)
            turned[:, rows_at(j * TILE, TILE)] = mixed.T.astype(BF16)

    def attend(seq, between):
        @pl.loop(0, hw // 128)
        def _(heads):
            @pl.when(heads == hw // 128 - 1)
            def _():
                for relay in between:
                    relay()

            for i in range(tiles):
                attention_rows(seq, heads, i, q, k, turned, segments, attended, lse)

    def branch_other(seq):
        @pl.loop(0, HALF // TILE)
        def _(j):
            rows = rows_at(seq * SEQ_LEN + (1 - p.core) * HALF + j * TILE, TILE)
            half_out[seq, rows_at(j * TILE, TILE), :] = dot_nt(
                attended[rows, :], attn_w[:, out_lanes]
            ).astype(BF16)

        go(("half", seq), send(half_out.at[seq], half_in.at[seq], cores, 4 + seq, p.sibling))

    def branch_own(seq):
        arrived(half_in.at[seq], cores, 4 + seq, p.sibling)

        @pl.loop(0, HALF // TILE)
        def _(j):
            rows = rows_at(seq * SEQ_LEN + p.core * HALF + j * TILE, TILE)
            tile = rows_at(j * TILE, TILE)
            part = dot_nt(attended[rows, :], attn_w[:, out_lanes])
            sum_out[seq, tile, :] = (part + half_in[seq, tile, :].astype(F32)).astype(BF16)

        go(("sum", seq), send(sum_out.at[seq], sum_in.at[seq], group, 2 + seq, p.across))

    def finish_branch(seq):
        arrived(sum_in.at[seq], group, 2 + seq, p.across)

        @pl.loop(0, HALF // TILE)
        def _(j):
            tile = rows_at(j * TILE, TILE)
            both = sum_out[seq, tile, :].astype(F32) + sum_in[seq, tile, :].astype(F32)
            u = xb[seq, tile, :].astype(F32) + both
            hidden[seq, tile, :] = u
            normed_mlp[rows_at((2 * seq + p.core) * HALF + j * TILE, TILE), :] = (
                u * norm_factor(u) * gain_mlp
            ).astype(BF16)

        mine = normed_mlp.at[block(2 * seq + p.core)]
        go(("mlp", seq), send(mine, mine, cores, 6 + seq, p.sibling))
        tell(credits.at[seq], p.across)

    def in_steps(gather):
        steps = list(range(1, p.line))

        def relay():
            if steps:
                gather.relay(steps.pop(0))

        return relay, steps

    relay_ff, steps = in_steps(of_ff)
    relay_rest, _ = in_steps(of_rest)
    relay_gate, left = in_steps(of_gate)
    project(0)
    attend(0, [relay_ff])
    relay_rest()
    of_out.finish()
    branch_other(0)
    project(1)
    branch_own(0)
    relay_gate()
    relay_ff()
    attend(1, [relay_rest])
    relay_gate()
    branch_other(1)
    branch_own(1)
    relay_ff()
    relay_rest()
    arrived(og.at[block(other)], group, 1, p.across)
    there = og.at[block(other)]
    go("og_f", send(there, there, cores, 3, p.sibling))
    while steps or left:
        relay_ff()
        relay_rest()
        relay_gate()
    finish_branch(0)
    arrived(og.at[block(sib)], cores, 2, p.sibling)
    arrived(og.at[block(sib_other)], cores, 3, p.sibling)
    of_ff.finish()
    of_rest.finish()

    def feed_copy(seq, n, j):
        tile = rows_at(j * TILE, TILE)
        there = half_in.at[n, tile]
        return send(half_out.at[n, tile], there, cores, 8 + seq * 4 + n * 2 + j, p.sibling)

    def feed_sum(seq, j):
        tile = rows_at(j * TILE, TILE)
        return send(sum_out.at[seq, tile], sum_in.at[seq, tile], group, 6 + seq * 2 + j, p.across)

    def feed_gone(seq):
        for n in range(2):
            for j in range(HALF // TILE):
                feed_copy(seq, n, j).wait_send()

    def feed(seq):
        arrived(normed_mlp.at[block(2 * seq + 1 - p.core)], cores, 6 + seq, p.sibling)
        if seq == 0:
            for n in range(2):
                gone(("half", n))
        else:
            feed_gone(0)
        gone(("sum", seq))
        pl.semaphore_wait(credits.at[seq], 1)

        @pl.loop(0, tiles)
        def _(step):
            j = lax.rem(step, HALF // TILE)
            others = step < HALF // TILE
            h = jnp.where(others, 1 - p.core, p.core)
            here = rows_at(h * HALF + j * TILE, TILE)
            rows = rows_at(seq * SEQ_LEN + h * HALF + j * TILE, TILE)
            tile = rows_at(j * TILE, TILE)
            for n in range(wide // 256):
                lanes = [slice(m * wide + n * 256, m * wide + (n + 1) * 256) for m in range(3)]
                gate = dot_nn(normed_mlp[rows, :], ff_w[:, lanes[0]])
                up = dot_nn(normed_mlp[rows, :], ff_w[:, lanes[1]])
                grad_act = dot_nn(og[rows, :], ff_w[:, lanes[2]])
                sig = 1.0 / (1.0 + jnp.exp(-gate))
                swish = gate * sig
                units[here, lanes[0]] = (
                    grad_act * up * sig * (1.0 + gate * (1.0 - sig))
                ).astype(BF16)
                units[here, lanes[1]] = (grad_act * swish).astype(BF16)
                units[here, lanes[2]] = (swish * up).astype(BF16)
            down = dot_nt(units[here, 2 * wide :], ff_w[:, 2 * wide :])
            back = dot_nt(units[here, : 2 * wide], ff_w[:, : 2 * wide])

            @pl.when(others)
            def _():
                half_out[0, tile, :] = back.astype(BF16)
                half_out[1, tile, :] = down.astype(BF16)
                for n in range(2):
                    feed_copy(seq, n, j).start()

            @pl.when(jnp.logical_not(others))
            def _():
                for n in range(2):
                    feed_copy(seq, n, j).wait_recv()
                sum_out[seq, tile, :] = (back + half_in[0, tile, :].astype(F32)).astype(BF16)
                m_sum[seq, tile, :] = (down + half_in[1, tile, :].astype(F32)).astype(BF16)
                feed_sum(seq, j).start()

    def ff_weights(seq, n):
        rows = pl.ds(seq * SEQ_LEN, SEQ_LEN)
        left = og if n == 2 else normed_mlp
        lanes = slice(n * wide, (n + 1) * wide)

        @pl.loop(0, width // TILE)
        def _(j):
            cols = rows_at(j * TILE, TILE)
            part = dot_tn(left[rows, cols], units[:, lanes])
            if seq > 0:
                part = part + ff_grad[cols, lanes].astype(F32)
            ff_grad[cols, lanes] = part.astype(BF16)

    def pull(seq):
        for j in range(HALF // TILE):
            feed_sum(seq, j).wait_recv()

        @pl.loop(0, HALF // TILE)
        def _(j):
            tile = rows_at(j * TILE, TILE)
            rows = rows_at((2 * seq + p.core) * HALF + j * TILE, TILE)
            grad = sum_out[seq, tile, :].astype(F32) + sum_in[seq, tile, :].astype(F32)
            back, gain_rows = norm_pull(grad, hidden[seq, tile, :], gain_mlp)
            whole = og[rows, :].astype(F32) + back
            normed_mlp[rows, :] = whole.astype(BF16)

            @pl.when(p.chip == seq)
            def _():
                grad_hidden[tile, :] = whole
                gain_acc[1:2, :] += jnp.sum(gain_rows, axis=0, keepdims=True)

        mine = normed_mlp.at[block(2 * seq + p.core)]
        pl.semaphore_wait(credits.at[2 + seq], 1)
        go(("low", seq), send(mine, mine, cores, 16 + seq, p.sibling))

        @pl.when(p.chip == seq)
        def _():
            tell(credits.at[4], p.across)

    def release(sems):
        for who, n in [(p.pair, 0)] + [(p.behind(n), n) for n in range(1, p.line)]:
            tell(sems.at[n], who)

    def free_rows(seq):
        gone(("mlp", seq))
        tell(credits.at[2 + seq], p.sibling)

    feed(0)
    ff_weights(0, 0)
    ff_weights(0, 1)
    finish_branch(1)
    ff_weights(0, 2)
    free_rows(0)
    feed(1)
    of_ff.drain()
    of_rest.drain()
    of_gate.drain()
    release(ff_free)
    gain_acc[...] = jnp.zeros_like(gain_acc)
    scatters = [
        Scatter(
            p,
            ff_grad,
            ff_w,
            pl.ds(n * wide, wide),
            (pair_out.at[5 + n], pair_in.at[5 + n]),
            (line_out.at[n], line_in.at[n]),
            ff_free if n == 0 else None,
        )
        for n in range(3)
    ]
    scatters_attn = [
        Scatter(
            p,
            attn_grad,
            og,
            pl.ds(n * hw, hw),
            (pair_out.at[8 + n], pair_in.at[8 + n]),
            (line_out.at[3 + n], line_in.at[3 + n]),
            attn_free if n == 0 else None,
        )
        for n in range(4)
    ]
    away = far_first(p.line)
    for n in range(3):
        ff_weights(1, n)
        scatters[n].start(away or [0])
    if away:
        for n in range(2):
            scatters[n].start([0])
    relays = [(scatters[n], k) for n in range(3) for k in away]
    if len(away) == 3:
        relays = [relays[n] for n in (0, 1, 3, 2, 4, 6, 5, 7, 8)]

    def relay_grad():
        if relays:
            scatter, k = relays.pop(0)
            scatter.relay(k)

    pull(0)
    free_rows(1)

    dqkv = units

    def grad_att(i, heads):
        return units[pl.ds(i * TILE, TILE), rows_at(3 * hw + heads * 128, 128)]

    def turn(seq):
        @pl.loop(0, tiles)
        def _(j):
            rows = rows_at(seq * SEQ_LEN + j * TILE, TILE)
            turned[:, rows_at(j * TILE, TILE)] = k[rows, :].astype(F32).T.astype(BF16)

    def prepare(seq):
        arrived(normed_mlp.at[block(2 * seq + 1 - p.core)], cores, 16 + seq, p.sibling)

        @pl.loop(0, tiles)
        def _(j):
            here = rows_at(j * TILE, TILE)
            rows = rows_at(seq * SEQ_LEN + j * TILE, TILE)
            units[here, out_lanes] = dot_nn(normed_mlp[rows, :], attn_w[:, out_lanes]).astype(BF16)

    def grad_store(seq, heads):
        rows = pl.ds(seq * SEQ_LEN, SEQ_LEN)
        return local(6, dv, value_first_grad.at[rows, rows_at(heads * 128, 128)])

    def m_copy():
        return send(m_sum.at[1 - p.chip], xb.at[p.chip], group, 4, p.across)

    def attend_back(seq, jobs):
        if seq > 0:
            grad_store(0, hw // 128 - 1).wait()

        @pl.loop(0, hw // 128)
        def _(heads):
            @pl.when(heads > 0)
            def _():
                grad_store(seq, heads - 1).wait()

            for i in reversed(range(tiles)):
                for when, job in jobs:
                    if when[1] == i:

                        @pl.when(heads == when[0])
                        def _():
                            job()

                attention_rows_back(
                    seq,
                    heads,
                    i,
                    q,
                    k,
                    v,
                    turned,
                    segments,
                    lse,
                    attended,
                    grad_att,
                    dk,
                    dv,
                    cos,
                    sin,
                    dqkv,
                )

            @pl.loop(0, tiles)
            def _(j):
                here = rows_at(j * TILE, TILE)
                rows = rows_at(seq * SEQ_LEN + j * TILE, TILE)
                u = dk[here, :]
                dqkv[here, rows_at(hw + heads * 128, 128)] = (
                    u * cos[rows, :] - swap_halves(u) * sin[rows, :]
                ).astype(BF16)
                half = 0.5 * dv[here, :]
                dqkv[here, rows_at(2 * hw + heads * 128, 128)] = half.astype(BF16)
                dv[here, :] = half

            grad_store(seq, heads).start()

    def attn_weights(seq, part):
        rows = pl.ds(seq * SEQ_LEN, SEQ_LEN)
        pieces = [(normed, units[:, qkv], qkv)]
        if part == 3:
            pieces = [(normed_mlp, attended[rows, :], out_lanes)]
        elif seq > 0:
            lanes = slice(part * hw, (part + 1) * hw)
            pieces = [(normed, units[:, lanes], lanes)]

        @pl.loop(0, width // TILE)
        def _(j):
            cols = rows_at(j * TILE, TILE)
            for left, right, lanes in pieces:
                made = dot_tn(left[rows, cols], right)
                if seq > 0:
                    made = made + attn_grad[cols, lanes].astype(F32)
                attn_grad[cols, lanes] = made.astype(BF16)

    def back_other(seq):
        if seq == 0:
            feed_gone(1)

        @pl.loop(0, HALF // TILE)
        def _(j):
            here = rows_at((1 - p.core) * HALF + j * TILE, TILE)
            half_out[seq, rows_at(j * TILE, TILE), :] = dot_nt(
                dqkv[here, qkv], attn_w[:, qkv]
            ).astype(BF16)

        go(("half", seq), send(half_out.at[seq], half_in.at[seq], cores, 18 + seq, p.sibling))

    gain_sems = (gain_out_sems, gain_in_sems)

    def exchange(partners, first):
        copies = []
        for n, who in enumerate(partners):
            copy = send(gain_acc, gain_in.at[first + n], gain_sems, first + n, who)
            copy.start()
            copies.append(copy)

        def rest():
            for copy in copies:
                copy.wait()
            whole = gain_acc[...]
            for n in range(len(partners)):
                whole = whole + gain_in[first + n]
            gain_acc[...] = whole

        return rest

    def back_own(seq):
        arrived(half_in.at[seq], cores, 18 + seq, p.sibling)
        for j in range(HALF // TILE):
            feed_sum(seq, j).wait_send()

        @pl.loop(0, HALF // TILE)
        def _(j):
            here = rows_at(p.core * HALF + j * TILE, TILE)
            tile = rows_at(j * TILE, TILE)
            rows = rows_at((2 * seq + p.core) * HALF + j * TILE, TILE)
            part = dot_nt(dqkv[here, qkv], attn_w[:, qkv]) + half_in[seq, tile, :].astype(F32)
            sum_out[seq, tile, :] = part.astype(BF16)
            gain_acc[0:1, :] += jnp.sum(part * normed[rows, :].astype(F32), axis=0, keepdims=True)

        rest = None
        if seq == SEQS - 1:
            rest = exchange([p.sibling], 0)

        @pl.when(p.chip != seq)
        def _():
            pl.semaphore_wait(credits.at[4], 1)
            send(sum_out.at[seq], sum_in.at[seq], group, 5, p.across).start()

        return rest

    turn(0)
    relay_grad()
    prepare(0)
    attend_back(0, [((1, 3), m_copy().start), ((0, 1), relay_grad), ((1, 1), relay_grad)])
    relay_grad()
    back_other(0)
    turn(1)
    attn_weights(0, 0)
    attn_weights(0, 3)
    relay_grad()
    pull(1)
    for name in ("og_x", "og_c", "og_f"):
        gone(name)
    release(attn_free)
    back_own(0)
    prepare(1)
    attend_back(1, [((0, 1), relay_grad), ((0, 1), relay_grad), ((1, 3), relay_grad)])
    back_other(1)
    while relays:
        relay_grad()
    for n in range(3):
        attn_weights(1, n)
        scatters_attn[n].start(away or [0])
    rest = back_own(1)
    attn_weights(1, 3)
    rest()
    farther = [p.ahead(n) for n in away] + [p.beyond(n) for n in away]
    rest = exchange([p.pair] + farther, 2)
    scatters_attn[3].start(away or [0])
    if away:
        for scatter in (scatters[2], *scatters_attn):
            scatter.start([0])

    arrived(xb.at[1 - p.chip], group, 4, p.across)

    @pl.loop(0, HALF // TILE)
    def _(j):
        tile = rows_at(j * TILE, TILE)
        both = m_sum[p.chip, tile, :].astype(F32) + xb[1 - p.chip, tile, :].astype(F32)
        m_sum[p.chip, tile, :] = (hidden[p.chip, tile, :] + both).astype(BF16)

    stores = [fetch(8, m_sum.at[p.chip], block_output)]
    for n in range(4):
        for k in away[:-1]:
            scatters_attn[n].relay(k)
        for m in [n - 1] * (n > 0) + [n] * (n == 3):
            for k in away[-1:]:
                scatters_attn[m].relay(k)
        if n < 2:
            scatters[n].finish()
            (gate_sum, up_sum)[n][...] = scatters[n].total().T[:ff, :]
    rest()
    rest = exchange([p.across], 1)
    arrived(sum_in.at[p.chip], group, 5, p.across)

    @pl.loop(0, HALF // TILE)
    def _(j):
        tile = rows_at(j * TILE, TILE)
        grad = sum_out[p.chip, tile, :].astype(F32) + sum_in[p.chip, tile, :].astype(F32)
        back, _ = norm_pull(grad, xb[p.chip, tile, :].astype(F32), gain_attn)
        grad_hidden[tile, :] = grad_hidden[tile, :] + back

    stores.append(fetch(9, grad_hidden, input_grad))
    rest()
    gain_attn_grad[...] = gain_acc[0:1, :] / gain_attn
    gain_mlp_grad[...] = gain_acc[1:2, :]
    scatters[2].finish()
    down_sum[...] = scatters[2].total().T[:ff, :]
    for n, out in enumerate((query_sum, key_sum, value_sum)):
        scatters_attn[n].finish()
        out[...] = scatters_attn[n].total()
    scatters_attn[3].finish()
    out_sum[...] = scatters_attn[3].total().T
    send(sum_out.at[1 - p.chip], sum_in.at[1 - p.chip], group, 5, p.across).wait_send()
    m_copy().wait_send()
    grad_store(SEQS - 1, hw // 128 - 1).wait()
    for name in list(sent):
        gone(name)
    of_attn.drain()
    of_out.drain()
    for scatter in (*scatters, *scatters_attn):
        scatter.drain()
    for copy in stores:
        copy.wait()


def layer(dp, x, og, vf, segments, positions, gains, wq, wk, wv, wo, wg, wu, wd):
    rows, width = 4 * x.shape[0], x.shape[1]
    hw, ff, r = vf.shape[1], wg.shape[0], wq.shape[0]
    wide = -(-ff // 256) * 256
    line = dp // 2
    hops = max(line - 1, 1)
    vmem = pl.BlockSpec(memory_space=pltpu.VMEM)
    far = pl.BlockSpec(memory_space=pl.ANY)
    shapes = [
        ((HALF, width), BF16, far),
        ((HALF, width), F32, far),
        ((rows, hw), F32, far),
        ((1, width), F32, vmem),
        ((r, hw), F32, vmem),
        ((r, hw), F32, vmem),
        ((r, hw), F32, vmem),
        ((hw, r), F32, vmem),
        ((1, width), F32, vmem),
        ((ff, r), F32, vmem),
        ((ff, r), F32, vmem),
        ((ff, r), F32, vmem),
    ]
    dma = pltpu.SemaphoreType.DMA
    flag = pltpu.SemaphoreType.REGULAR

    def bf(*shape):
        return pltpu.VMEM(shape, BF16)

    def fl(*shape):
        return pltpu.VMEM(shape, F32)

    scratch = [
        bf(2, HALF, width),
        bf(rows, width),
        bf(rows, width),
        bf(rows, width),
        bf(width, 4 * hw),
        bf(width, 3 * wide),
        bf(rows, hw),
        bf(rows, hw),
        bf(rows, hw),
        bf(rows, hw),
        fl(8, 1, SEQ_LEN),
        fl(2, HALF, width),
        fl(HALF, width),
        bf(SEQ_LEN, 3 * wide),
        bf(width, 3 * wide),
        bf(width, 4 * hw),
        bf(2, HALF, width),
        bf(2, HALF, width),
        bf(2, HALF, width),
        bf(2, HALF, width),
        bf(2, HALF, width),
        bf(hw, SEQ_LEN),
        fl(SEQ_LEN, 128),
        fl(SEQ_LEN, 128),
        fl(rows, 128),
        fl(rows, 128),
        fl(2, width),
        fl(4 + 2 * hops, 2, width),
        dma((10,)),
        dma((10,)),
        dma((10,)),
        dma((20,)),
        dma((20,)),
        dma((5, hops)),
        dma((5, hops)),
        dma((5, hops)),
        dma((5, hops)),
        dma((12, line)),
        dma((12, line)),
        dma((7, line)),
        dma((7, line)),
        dma((4 + 2 * hops,)),
        dma((4 + 2 * hops,)),
        flag((5,)),
        flag((line,)),
        flag((line,)),
    ]
    in_specs = [far] * 3 + [vmem] * 3 + [far] * 3 + [vmem] * 4
    return pl.pallas_call(
        functools.partial(layer_kernel, dp),
        out_shape=[jax.ShapeDtypeStruct(s, t) for s, t, _ in shapes],
        in_specs=in_specs,
        out_specs=[space for _, _, space in shapes],
        scratch_shapes=scratch,
        compiler_params=pltpu.CompilerParams(
            collective_id=0, has_side_effects=True, vmem_limit_bytes=VMEM_LIMIT
        ),
        name="layer",
    )(x, og, vf, segments, positions, gains, wq, wk, wv, wo, wg, wu, wd)


def settle_kernel(count, *refs):
    ins, outs, held, sems = refs[:count], refs[count : 2 * count], refs[2 * count : -1], refs[-1]
    first = [pltpu.make_async_copy(ins[n], held[n], sems.at[n]) for n in range(count)]
    second = [pltpu.make_async_copy(held[n], outs[n], sems.at[count + n]) for n in range(count)]
    for copy in first:
        copy.start()
    for n in range(count):
        first[n].wait()
        second[n].start()
    for copy in second:
        copy.wait()


def settle(arrays):
    count = len(arrays)
    far = pl.BlockSpec(memory_space=pl.ANY)
    return pl.pallas_call(
        functools.partial(settle_kernel, count),
        out_shape=[jax.ShapeDtypeStruct(a.shape, a.dtype) for a in arrays],
        in_specs=[far] * count,
        out_specs=[far] * count,
        scratch_shapes=[pltpu.VMEM(a.shape, a.dtype) for a in arrays]
        + [pltpu.SemaphoreType.DMA((2 * count,))],
        compiler_params=pltpu.CompilerParams(vmem_limit_bytes=VMEM_LIMIT),
        name="settle",
    )(*arrays)


def on_device(
    dp,
    block_input,
    value_first,
    segment_ids,
    positions,
    gain_attn,
    query_weight,
    key_weight,
    value_weight,
    out_weight,
    gain_mlp,
    gate_weight,
    up_weight,
    down_weight,
    output_grad,
):
    first = lax.broadcasted_iota(jnp.int32, (2, gain_attn.shape[0]), 0) == 0
    outs = layer(
        dp,
        block_input,
        output_grad,
        value_first,
        segment_ids[None, :],
        positions[None, :],
        jnp.where(first, gain_attn.astype(F32)[None], gain_mlp.astype(F32)[None]),
        query_weight,
        key_weight,
        value_weight,
        out_weight,
        gate_weight.T,
        up_weight.T,
        down_weight,
    )
    (
        block_output,
        input_grad,
        value_first_grad,
        gain_attn_grad,
        query_sum,
        key_sum,
        value_sum,
        out_sum,
        gain_mlp_grad,
        gate_sum,
        up_sum,
        down_sum,
    ) = settle(outs)
    return (
        block_output,
        input_grad,
        value_first_grad,
        gain_attn_grad[0],
        query_sum,
        key_sum,
        value_sum,
        out_sum,
        gain_mlp_grad[0],
        gate_sum.T,
        up_sum.T,
        down_sum,
    )


def solution(mesh):
    rows = P(("dp", "tensor"), None)
    weight = P("dp", "tensor")
    across = P("tensor", "dp")
    return jax.shard_map(
        functools.partial(on_device, mesh.shape["dp"]),
        mesh=mesh,
        in_specs=(
            rows,
            weight,
            P("dp"),
            P("dp"),
            P(),
            weight,
            weight,
            weight,
            across,
            P(),
            weight,
            weight,
            across,
            rows,
        ),
        out_specs=(
            rows,
            rows,
            weight,
            P(),
            weight,
            weight,
            weight,
            across,
            P(),
            weight,
            weight,
            across,
        ),
        check_vma=False,
    )
```

```python
import functools
import math

import jax
import jax.numpy as jnp
from jax import lax
from jax.experimental import pallas as pl
from jax.experimental.pallas import tpu as pltpu
from jax.sharding import PartitionSpec as P

HEAD_DIM = 64
SEQ_LEN = 1024
SEQS = 2
PIECE = 256
HALF = 512
TILE = 256
EPSILON = 1e-06
ROPE_BASE = 10000.0
MASKED = -1e30
MESH = pl.DeviceIdType.MESH
F32 = jnp.float32
BF16 = jnp.bfloat16
VMEM_LIMIT = 639 * 2**20 // 10


def dot_nn(a, b):
    return lax.dot_general(a, b, (((1,), (0,)), ((), ())), preferred_element_type=F32)


def dot_nt(a, b):
    return lax.dot_general(a, b, (((1,), (1,)), ((), ())), preferred_element_type=F32)


def dot_tn(a, b):
    return lax.dot_general(a, b, (((0,), (0,)), ((), ())), preferred_element_type=F32)


def rows_at(start, size):
    return pl.ds(pl.multiple_of(start, size), size)


def block(b):
    return rows_at(b * HALF, HALF)


class Place:
    def __init__(self, dp):
        self.d = lax.axis_index("dp")
        self.t = lax.axis_index("tensor")
        self.core = lax.rem(self.t, 2)
        self.chip = self.t // 2
        self.line = dp // 2
        self.y = lax.rem(self.d, 2)
        self.z = self.d // 2
        self.sibling = (self.d, self.t + 1 - 2 * self.core)
        self.across = (self.d, lax.rem(self.t + 2, 4))
        self.pair = (self.d + 1 - 2 * self.y, self.t)
        self.up = (self.d + 2, self.t)
        self.down = (self.d - 2, self.t)

    def ahead(self, k):
        return (2 * lax.rem(self.z + k, self.line) + self.y, self.t)

    def beyond(self, k):
        return (2 * lax.rem(self.z + k, self.line) + 1 - self.y, self.t)

    def behind(self, k):
        return (2 * lax.rem(self.z + self.line - k, self.line) + self.y, self.t)

    def greet(self):
        barrier = pltpu.get_barrier_semaphore()
        partners = [self.sibling, self.across, self.pair]
        partners.extend(self.ahead(k) for k in range(1, self.line))
        partners.extend(self.beyond(k) for k in range(1, self.line))
        for who in partners:
            tell(barrier, who)
        self.greeted = len(partners)

    def met(self):
        pl.semaphore_wait(pltpu.get_barrier_semaphore(), self.greeted)


def tell(sem, who):
    pl.semaphore_signal(sem, inc=1, device_id=who, device_id_type=MESH)


def send(src, dst, sems, k, who):
    return pltpu.make_async_remote_copy(
        src_ref=src,
        dst_ref=dst,
        send_sem=sems[0].at[k],
        recv_sem=sems[1].at[k],
        device_id=who,
        device_id_type=MESH,
    )


class Gather:
    def __init__(self, place, full, lanes, rows, spread, up_sems, down_sems, pair_sems):
        self.p, self.full, self.lanes, self.r, self.spread = place, full, lanes, rows, spread
        self.up_sems, self.down_sems, self.pair_sems = up_sems, down_sems, pair_sems

    def shard(self, z, y):
        return self.full.at[rows_at((2 * z + y) * self.r, self.r), self.lanes]

    def load(self, z):
        if self.spread:
            return self.shard(z, self.p.y)
        return self.full.at[rows_at(2 * z * self.r, 2 * self.r), self.lanes]

    def sides(self, k):
        p = self.p
        return (
            (p.z - k, p.z >= k, self.up_sems, p.z + 1 < p.line, p.up),
            (p.z + k, p.z + k < p.line, self.down_sems, p.z >= 1, p.down),
        )

    def start_pair(self):
        p = self.p
        here = self.shard(p.z, p.y)
        send(here, here, self.pair_sems, p.z, p.pair).start()

    def start_line(self):
        p = self.p
        if not self.spread:
            there = self.shard(p.z, 1 - p.y)
            send(there, there, self.pair_sems, p.z, p.pair).wait_recv()
        here = self.load(p.z)
        for _, _, sems, onward, to in self.sides(0):

            @pl.when(onward)
            def _():
                send(here, here, sems, 0, to).start()

    def relay(self, k):
        p = self.p
        for z, exists, sems, onward, to in self.sides(k):

            @pl.when(exists)
            def _():
                here = self.load(z)
                send(here, here, sems, k - 1, to).wait_recv()

                @pl.when(onward)
                def _():
                    send(here, here, sems, k, to).start()

                if self.spread:
                    send(here, here, self.pair_sems, z, p.pair).start()

    def finish(self):
        p = self.p
        if self.spread:
            for z in range(p.line):
                there = self.shard(z, 1 - p.y)
                send(there, there, self.pair_sems, z, p.pair).wait_recv()

    def drain(self):
        p = self.p
        for z in range(p.line) if self.spread else (p.z,):
            here = self.shard(z, p.y)
            send(here, here, self.pair_sems, z, p.pair).wait_send()
        for k in range(p.line - 1):
            for z, exists, sems, onward, to in self.sides(k):

                @pl.when(jnp.logical_and(exists, onward))
                def _():
                    here = self.load(z)
                    send(here, here, sems, k, to).wait_send()


def far_first(n):
    if n < 4:
        return list(range(1, n))
    last = [2, n - 2] if n > 4 else [2]
    return [1, n - 1, *range(3, n - 2), *last]


class Scatter:
    def __init__(self, place, full, into, lanes, pair_sems, line_sems, free):
        self.p, self.full, self.into, self.lanes = place, full, into, lanes
        self.pair_sems, self.line_sems = pair_sems, line_sems
        self.free = free
        self.r = full.shape[0] // (2 * place.line)

    def rows(self, k, y):
        z = lax.rem(self.p.z + k, self.p.line)
        return rows_at((2 * z + y) * self.r, self.r)

    def pair_in(self, k):
        return self.into.at[pl.ds(k * self.r, self.r), self.lanes]

    def line_in(self, k):
        return self.into.at[pl.ds((self.p.line + k - 1) * self.r, self.r), self.lanes]

    def swap(self, k):
        theirs = self.full.at[self.rows(k, 1 - self.p.y), self.lanes]
        return send(theirs, self.pair_in(k), self.pair_sems, k, self.p.pair)

    def start(self, steps):
        if self.free is not None and (steps[0] == 1 or self.p.line == 1):
            pl.semaphore_wait(self.free.at[0], 1)
        for k in steps:
            self.swap(k).start()

    def relay(self, k):
        p = self.p
        n = p.line
        there = self.pair_in(k)
        send(there, there, self.pair_sems, k, p.pair).wait_recv()
        self.join(k, there)
        if self.free is not None and k == 1:
            for m in range(1, n):
                pl.semaphore_wait(self.free.at[m], 1)
        if n >= 4 and k in (2, n - 2):
            helping = jnp.logical_or(
                jnp.logical_and(p.z == 1, k == n - 2), jnp.logical_and(p.z == n - 2, k == 2)
            )

            @pl.when(helping)
            def _():
                self.helped().wait_recv()
                self.join(k, self.line_in(n))

        if n >= 4 and k in (1, n - 1):
            from_end = p.z == (0 if k == n - 1 else n - 1)

            @pl.when(from_end)
            def _():
                self.helped(k).start()

            @pl.when(jnp.logical_not(from_end))
            def _():
                self.onward(k).start()
        else:
            self.onward(k).start()

    def join(self, k, came):
        mine = self.full.at[self.rows(k, self.p.y), self.lanes]
        step = min(self.r, 32)

        @pl.loop(0, self.r // step)
        def _(j):
            rows = rows_at(j * step, step)
            mine[rows, :] = (mine[rows, :].astype(F32) + came[rows, :].astype(F32)).astype(BF16)

    def helped(self, k=1):
        p = self.p
        near = jnp.where(p.z == 0, 1, p.line - 2)
        mine = self.full.at[self.rows(k, p.y), self.lanes]
        return pltpu.make_async_remote_copy(
            src_ref=mine,
            dst_ref=self.line_in(p.line),
            send_sem=self.line_sems[0].at[k - 1],
            recv_sem=self.line_sems[1].at[p.line - 1],
            device_id=(2 * near + p.y, p.t),
            device_id_type=MESH,
        )

    def onward(self, k):
        p = self.p
        mine = self.full.at[self.rows(k, p.y), self.lanes]
        return send(mine, self.line_in(k), self.line_sems, k - 1, p.ahead(k))

    def merged(self, k):
        n = self.p.line
        if n < 4 or k not in (1, n - 1):
            return None
        return self.p.z == (n - 1 if k == n - 1 else 0)

    def finish(self):
        p = self.p
        there = self.pair_in(0)
        send(there, there, self.pair_sems, 0, p.pair).wait_recv()
        for k in range(1, p.line):
            there = self.line_in(k)
            merged = self.merged(k)
            if merged is None:
                send(there, there, self.line_sems, k - 1, p.pair).wait_recv()
            else:

                @pl.when(jnp.logical_not(merged))
                def _():
                    send(there, there, self.line_sems, k - 1, p.pair).wait_recv()

    def total(self):
        whole = self.full[self.rows(0, self.p.y), self.lanes].astype(F32)
        whole = whole + self.pair_in(0)[...].astype(F32)
        for k in range(1, self.p.line):
            came = self.line_in(k)[...].astype(F32)
            merged = self.merged(k)
            if merged is not None:
                came = jnp.where(merged, jnp.zeros_like(came), came)
            whole = whole + came
        return whole

    def drain(self):
        for k in range(self.p.line):
            self.swap(k).wait_send()
        for k in range(1, self.p.line):
            self.onward(k).wait_send()


def swap_halves(u):
    lane = lax.broadcasted_iota(jnp.int32, u.shape, 1)
    low = lax.rem(lane, HEAD_DIM) < HEAD_DIM // 2
    return jnp.where(low, pltpu.roll(u, 96, 1), pltpu.roll(u, 32, 1))


def norm_factor(u):
    return lax.rsqrt(jnp.mean(u * u, axis=-1, keepdims=True) + EPSILON)


def norm_pull(grad, u, gain):
    r = norm_factor(u)
    scaled = grad * gain
    back = r * scaled - u * (r * r * r) * jnp.mean(scaled * u, axis=-1, keepdims=True)
    return back, grad * u * r


def visible(segments):
    key = lax.broadcasted_iota(jnp.int32, (TILE, TILE), 0)
    query = lax.broadcasted_iota(jnp.int32, (TILE, TILE), 1)
    return jnp.logical_or(key <= query, segments > 0)


def attention_rows(seq, heads, i, q, k, vt, segments, attended, lse):
    lane = lax.broadcasted_iota(jnp.int32, (TILE, 128), 1)
    lanes = rows_at(heads * 128, 128)
    rows = pl.ds(seq * SEQ_LEN + i * TILE, TILE)
    q2 = q[rows, lanes]
    shown = visible(segments[:, rows])
    sides = []
    for a in range(2):
        qa = jnp.where((lane < HEAD_DIM) == (a == 0), q2, jnp.zeros_like(q2))
        vta = rows_at((heads * 2 + a) * HEAD_DIM, HEAD_DIM)
        score = jnp.where(shown, dot_nt(k[rows, lanes], qa), MASKED)
        top = jnp.max(score, axis=0, keepdims=True)
        if i > 0:
            before = dot_nt(k[pl.ds(seq * SEQ_LEN, i * TILE), lanes], qa)
            top = jnp.maximum(top, jnp.max(before, axis=0, keepdims=True))
        weight = jnp.exp(score - top)
        total = jnp.sum(weight, axis=0, keepdims=True)
        out = dot_nn(vt[vta, pl.ds(i * TILE, TILE)], weight.astype(BF16))
        if i > 0:
            weight = jnp.exp(before - top)
            total = total + jnp.sum(weight, axis=0, keepdims=True)
            out = out + dot_nn(vt[vta, pl.ds(0, i * TILE)], weight.astype(BF16))
        sides.append(out * (1.0 / total))
        lse[seq * 4 + heads * 2 + a, :, pl.ds(i * TILE, TILE)] = top + jnp.log(total)
    attended[rows, lanes] = jnp.concatenate(sides, axis=0).T.astype(BF16)


def attention_rows_back(
    seq, heads, i, q, k, v, kt, segments, lse, attended, grad_att, dk, dv, cos, sin, dqkv
):
    lane = lax.broadcasted_iota(jnp.int32, (TILE, 128), 1)
    lanes = rows_at(heads * 128, 128)
    local = pl.ds(i * TILE, TILE)
    rows = pl.ds(seq * SEQ_LEN + i * TILE, TILE)
    first = i == SEQ_LEN // TILE - 1
    q2, g2 = q[rows, lanes], grad_att(i, heads)
    shown = visible(segments[:, rows])
    products = (g2.astype(F32) * attended[rows, lanes].astype(F32)).T
    parts = [(i * TILE, TILE, True)]
    if i > 0:
        parts.append((0, i * TILE, False))
    sides = [None, None]
    for start, size, diagonal in parts:
        keys = pl.ds(seq * SEQ_LEN + start, size)
        here = pl.ds(start, size)
        dk_part, dv_part = 0.0, 0.0
        for a in range(2):
            mine = (lane < HEAD_DIM) == (a == 0)
            qa = jnp.where(mine, q2, jnp.zeros_like(q2))
            ga = jnp.where(mine, g2, jnp.zeros_like(g2))
            delta = jnp.sum(products[a * HEAD_DIM : (a + 1) * HEAD_DIM], axis=0, keepdims=True)
            stat = lse[seq * 4 + heads * 2 + a, :, local]
            score = dot_nt(k[keys, lanes], qa)
            if diagonal:
                score = jnp.where(shown, score, MASKED)
            prob = jnp.exp(score - stat)
            grad_prob = dot_nt(v[keys, lanes], ga)
            grad_score = (prob * (grad_prob - delta)).astype(BF16)
            dv_part = dv_part + dot_nn(prob.astype(BF16), ga)
            dk_part = dk_part + dot_nn(grad_score, qa)
            side = dot_nn(kt[rows_at((heads * 2 + a) * HEAD_DIM, HEAD_DIM), here], grad_score)
            sides[a] = side if sides[a] is None else sides[a] + side
        if first:
            dk[here, :] = dk_part
            dv[here, :] = dv_part
        else:
            dk[here, :] += dk_part
            dv[here, :] += dv_part
    dq = jnp.concatenate(sides, axis=0).T * HEAD_DIM**-0.5
    dqkv[local, lanes] = (dq * cos[rows, :] - swap_halves(dq) * sin[rows, :]).astype(BF16)


def layer_kernel(
    dp,
    x_in,
    og_in,
    value_first,
    segments,
    positions,
    gains,
    query_shard,
    key_shard,
    value_shard,
    out_shard,
    gate_shard,
    up_shard,
    down_shard,
    block_output,
    input_grad,
    value_first_grad,
    gain_attn_grad,
    query_sum,
    key_sum,
    value_sum,
    out_sum,
    gain_mlp_grad,
    gate_sum,
    up_sum,
    down_sum,
    xb,
    normed,
    normed_mlp,
    og,
    attn_w,
    ff_w,
    q,
    k,
    v,
    attended,
    lse,
    hidden,
    grad_hidden,
    units,
    ff_grad,
    attn_grad,
    half_out,
    half_in,
    sum_out,
    sum_in,
    m_sum,
    turned,
    dk,
    dv,
    cos,
    sin,
    gain_acc,
    gain_in,
    local_sems,
    group_out,
    group_in,
    core_out,
    core_in,
    up_out,
    up_in,
    down_out,
    down_in,
    pair_out,
    pair_in,
    line_out,
    line_in,
    gain_out_sems,
    gain_in_sems,
    credits,
    ff_free,
    attn_free,
):
    p = Place(dp)
    group, cores = (group_out, group_in), (core_out, core_in)
    rows_r, hw = query_shard.shape
    ff = gate_shard.shape[0]
    wide = ff_w.shape[1] // 3
    width = x_in.shape[1]
    tiles = SEQ_LEN // TILE
    slot = rows_at(p.d * rows_r, rows_r)
    qkv, out_lanes = slice(0, 3 * hw), slice(3 * hw, 4 * hw)
    middle = wide + 5 * wide // 6 // 128 * 128
    sent = {}

    def go(name, copy):
        copy.start()
        sent[name] = copy

    def gone(name):
        sent.pop(name).wait_send()

    def arrived(there, sems, n, who):
        send(there, there, sems, n, who).wait_recv()

    def local(n, src, dst):
        return pltpu.make_async_copy(src, dst, local_sems.at[n])

    def fetch(n, src, dst):
        copy = local(n, src, dst)
        copy.start()
        return copy

    p.greet()
    x_copy = fetch(0, x_in, xb.at[p.chip])
    qkv_copies = [
        fetch(1 + n, shard, attn_w.at[slot, pl.ds(n * hw, hw)])
        for n, shard in enumerate((query_shard, key_shard, value_shard))
    ]
    og_copy = fetch(4, og_in, og.at[block(p.t)])
    vf_copy = fetch(5, value_first, attended)
    attn_w[slot, out_lanes] = out_shard[...].astype(F32).T.astype(BF16)
    p.met()
    x_copy.wait()
    go("x", send(xb.at[p.chip], xb.at[p.chip], group, 0, p.across))
    gathers = [
        Gather(
            p,
            full,
            pl.ds(first, lanes),
            rows_r,
            spread,
            (up_out.at[n], up_in.at[n]),
            (down_out.at[n], down_in.at[n]),
            (pair_out.at[n], pair_in.at[n]),
        )
        for n, (full, first, lanes, spread) in enumerate(
            (
                (attn_w, 0, 3 * hw, True),
                (attn_w, 3 * hw, hw, True),
                (ff_w, wide // 2, middle - wide // 2, True),
                (ff_w, middle, 3 * wide - middle, True),
                (ff_w, 0, wide // 2, False),
            )
        )
    ]
    of_attn, of_out, of_ff, of_rest, of_gate = gathers
    for copy in qkv_copies:
        copy.wait()
    of_attn.start_line()
    of_attn.start_pair()
    of_out.start_line()
    of_out.start_pair()
    gain_attn, gain_mlp = gains[0:1, :], gains[1:2, :]
    other = lax.rem(p.t + 2, 4)
    sib = p.t + 1 - 2 * p.core
    sib_other = lax.rem(sib + 2, 4)

    def norm_block(b, chip, n):
        @pl.loop(0, HALF // TILE)
        def _(j):
            u = xb[chip, rows_at(j * TILE, TILE), :].astype(F32)
            normed[rows_at(b * HALF + j * TILE, TILE), :] = (
                u * norm_factor(u) * gain_attn
            ).astype(BF16)

        here = normed.at[block(b)]
        go(("normed", n), send(here, here, cores, n, p.sibling))

    norm_block(p.t, p.chip, 0)
    for n, shard in enumerate((gate_shard, up_shard, down_shard)):
        flat = shard[...].astype(F32)
        if wide > ff:
            flat = jnp.concatenate([flat, jnp.zeros((wide - ff, rows_r), F32)], axis=0)
        ff_w[slot, n * wide : (n + 1) * wide] = flat.T.astype(BF16)
    of_gate.start_pair()
    if p.line > 1:
        of_attn.relay(1)
        of_out.relay(1)

    @pl.loop(0, SEQS * tiles)
    def _(j):
        rows = rows_at(j * TILE, TILE)
        lane = lax.broadcasted_iota(jnp.int32, (TILE, 128), 1)
        half = HEAD_DIM // 2
        power = lax.rem(lane[0:1, :], half).astype(F32) * (-2.0 / HEAD_DIM)
        frequency = jnp.exp(power * math.log(ROPE_BASE))
        place = jnp.broadcast_to(positions[:, rows].astype(F32), (128, TILE)).T
        angle = place * frequency
        cos[rows, :] = jnp.cos(angle)
        sine = jnp.sin(angle)
        sin[rows, :] = jnp.where(lax.rem(lane, HEAD_DIM) < half, -sine, sine)

    og_copy.wait()
    own_rows = og.at[block(p.t)]
    go("og_c", send(own_rows, own_rows, cores, 2, p.sibling))
    for n in range(2, p.line):
        of_attn.relay(n)
        of_out.relay(n)
        if n == 2:
            go("og_x", send(own_rows, own_rows, group, 1, p.across))
    if p.line < 3:
        go("og_x", send(own_rows, own_rows, group, 1, p.across))
    of_ff.start_line()
    of_rest.start_line()
    of_gate.start_line()
    arrived(xb.at[1 - p.chip], group, 0, p.across)
    norm_block(other, 1 - p.chip, 1)
    of_ff.start_pair()
    of_rest.start_pair()
    of_attn.finish()
    arrived(normed.at[block(sib)], cores, 0, p.sibling)
    arrived(normed.at[block(sib_other)], cores, 1, p.sibling)
    vf_copy.wait()

    def project(seq):
        @pl.loop(0, tiles)
        def _(j):
            rows = rows_at(seq * SEQ_LEN + j * TILE, TILE)
            made = dot_nn(normed[rows, :], attn_w[:, qkv])
            c, s = cos[rows, :], sin[rows, :]
            for n in range(hw // 128):
                lanes = slice(n * 128, (n + 1) * 128)
                u = made[:, n * 128 : (n + 1) * 128]
                q[rows, lanes] = ((u * c + swap_halves(u) * s) * HEAD_DIM**-0.5).astype(BF16)
                u = made[:, hw + n * 128 : hw + (n + 1) * 128]
                k[rows, lanes] = (u * c + swap_halves(u) * s).astype(BF16)
            mixed = 0.5 * made[:, 2 * hw :] + 0.5 * attended[rows, :].astype(F32)
            v[rows, :] = mixed.astype(BF16)
            turned[:, rows_at(j * TILE, TILE)] = mixed.T.astype(BF16)

    def attend(seq, between):
        @pl.loop(0, hw // 128)
        def _(heads):
            @pl.when(heads == hw // 128 - 1)
            def _():
                for relay in between:
                    relay()

            for i in range(tiles):
                attention_rows(seq, heads, i, q, k, turned, segments, attended, lse)

    def branch_other(seq):
        @pl.loop(0, HALF // TILE)
        def _(j):
            rows = rows_at(seq * SEQ_LEN + (1 - p.core) * HALF + j * TILE, TILE)
            half_out[seq, rows_at(j * TILE, TILE), :] = dot_nt(
                attended[rows, :], attn_w[:, out_lanes]
            ).astype(BF16)

        go(("half", seq), send(half_out.at[seq], half_in.at[seq], cores, 4 + seq, p.sibling))

    def branch_own(seq):
        arrived(half_in.at[seq], cores, 4 + seq, p.sibling)

        @pl.loop(0, HALF // TILE)
        def _(j):
            rows = rows_at(seq * SEQ_LEN + p.core * HALF + j * TILE, TILE)
            tile = rows_at(j * TILE, TILE)
            part = dot_nt(attended[rows, :], attn_w[:, out_lanes])
            sum_out[seq, tile, :] = (part + half_in[seq, tile, :].astype(F32)).astype(BF16)

        go(("sum", seq), send(sum_out.at[seq], sum_in.at[seq], group, 2 + seq, p.across))

    def finish_branch(seq):
        arrived(sum_in.at[seq], group, 2 + seq, p.across)

        @pl.loop(0, HALF // TILE)
        def _(j):
            tile = rows_at(j * TILE, TILE)
            both = sum_out[seq, tile, :].astype(F32) + sum_in[seq, tile, :].astype(F32)
            u = xb[seq, tile, :].astype(F32) + both
            hidden[seq, tile, :] = u
            normed_mlp[rows_at((2 * seq + p.core) * HALF + j * TILE, TILE), :] = (
                u * norm_factor(u) * gain_mlp
            ).astype(BF16)

        mine = normed_mlp.at[block(2 * seq + p.core)]
        go(("mlp", seq), send(mine, mine, cores, 6 + seq, p.sibling))
        tell(credits.at[seq], p.across)

    def in_steps(gather):
        steps = list(range(1, p.line))

        def relay():
            if steps:
                gather.relay(steps.pop(0))

        return relay, steps

    relay_ff, steps = in_steps(of_ff)
    relay_rest, _ = in_steps(of_rest)
    relay_gate, left = in_steps(of_gate)
    project(0)
    attend(0, [relay_ff])
    relay_rest()
    of_out.finish()
    branch_other(0)
    project(1)
    branch_own(0)
    relay_gate()
    relay_ff()
    attend(1, [relay_rest])
    relay_gate()
    branch_other(1)
    branch_own(1)
    relay_ff()
    relay_rest()
    arrived(og.at[block(other)], group, 1, p.across)
    there = og.at[block(other)]
    go("og_f", send(there, there, cores, 3, p.sibling))
    while steps or left:
        relay_ff()
        relay_rest()
        relay_gate()
    finish_branch(0)
    arrived(og.at[block(sib)], cores, 2, p.sibling)
    arrived(og.at[block(sib_other)], cores, 3, p.sibling)
    of_ff.finish()
    of_rest.finish()

    def feed_copy(seq, n, j):
        tile = rows_at(j * TILE, TILE)
        there = half_in.at[n, tile]
        return send(half_out.at[n, tile], there, cores, 8 + seq * 4 + n * 2 + j, p.sibling)

    def feed_sum(seq, j):
        tile = rows_at(j * TILE, TILE)
        return send(sum_out.at[seq, tile], sum_in.at[seq, tile], group, 6 + seq * 2 + j, p.across)

    def feed_gone(seq):
        for n in range(2):
            for j in range(HALF // TILE):
                feed_copy(seq, n, j).wait_send()

    def feed(seq):
        arrived(normed_mlp.at[block(2 * seq + 1 - p.core)], cores, 6 + seq, p.sibling)
        if seq == 0:
            for n in range(2):
                gone(("half", n))
        else:
            feed_gone(0)
        gone(("sum", seq))
        pl.semaphore_wait(credits.at[seq], 1)

        @pl.loop(0, tiles)
        def _(step):
            j = lax.rem(step, HALF // TILE)
            others = step < HALF // TILE
            h = jnp.where(others, 1 - p.core, p.core)
            here = rows_at(h * HALF + j * TILE, TILE)
            rows = rows_at(seq * SEQ_LEN + h * HALF + j * TILE, TILE)
            tile = rows_at(j * TILE, TILE)
            for n in range(wide // 256):
                lanes = [slice(m * wide + n * 256, m * wide + (n + 1) * 256) for m in range(3)]
                gate = dot_nn(normed_mlp[rows, :], ff_w[:, lanes[0]])
                up = dot_nn(normed_mlp[rows, :], ff_w[:, lanes[1]])
                grad_act = dot_nn(og[rows, :], ff_w[:, lanes[2]])
                sig = 1.0 / (1.0 + jnp.exp(-gate))
                swish = gate * sig
                units[here, lanes[0]] = (
                    grad_act * up * sig * (1.0 + gate * (1.0 - sig))
                ).astype(BF16)
                units[here, lanes[1]] = (grad_act * swish).astype(BF16)
                units[here, lanes[2]] = (swish * up).astype(BF16)
            down = dot_nt(units[here, 2 * wide :], ff_w[:, 2 * wide :])
            back = dot_nt(units[here, : 2 * wide], ff_w[:, : 2 * wide])

            @pl.when(others)
            def _():
                half_out[0, tile, :] = back.astype(BF16)
                half_out[1, tile, :] = down.astype(BF16)
                for n in range(2):
                    feed_copy(seq, n, j).start()

            @pl.when(jnp.logical_not(others))
            def _():
                for n in range(2):
                    feed_copy(seq, n, j).wait_recv()
                sum_out[seq, tile, :] = (back + half_in[0, tile, :].astype(F32)).astype(BF16)
                m_sum[seq, tile, :] = (down + half_in[1, tile, :].astype(F32)).astype(BF16)
                feed_sum(seq, j).start()

    def ff_weights(seq, n):
        rows = pl.ds(seq * SEQ_LEN, SEQ_LEN)
        left = og if isinstance(n, int) else normed_mlp
        lanes = pl.ds(pl.multiple_of(n * wide, 128), wide)

        @pl.loop(0, width // TILE)
        def _(j):
            cols = rows_at(j * TILE, TILE)
            part = dot_tn(left[rows, cols], units[:, lanes])
            if seq > 0:
                part = part + ff_grad[cols, lanes].astype(F32)
            ff_grad[cols, lanes] = part.astype(BF16)

    def both_ff_weights(seq, then=()):
        @pl.loop(0, 2)
        def _(n):
            ff_weights(seq, n)
            for m, start in enumerate(then):
                pl.when(n == m)(start)

    def pull(seq):
        for j in range(HALF // TILE):
            feed_sum(seq, j).wait_recv()

        @pl.loop(0, HALF // TILE)
        def _(j):
            tile = rows_at(j * TILE, TILE)
            rows = rows_at((2 * seq + p.core) * HALF + j * TILE, TILE)
            grad = sum_out[seq, tile, :].astype(F32) + sum_in[seq, tile, :].astype(F32)
            back, gain_rows = norm_pull(grad, hidden[seq, tile, :], gain_mlp)
            whole = og[rows, :].astype(F32) + back
            normed_mlp[rows, :] = whole.astype(BF16)

            @pl.when(p.chip == seq)
            def _():
                grad_hidden[tile, :] = whole
                gain_acc[1:2, :] += jnp.sum(gain_rows, axis=0, keepdims=True)

        mine = normed_mlp.at[block(2 * seq + p.core)]
        pl.semaphore_wait(credits.at[2 + seq], 1)
        go(("low", seq), send(mine, mine, cores, 16 + seq, p.sibling))

        @pl.when(p.chip == seq)
        def _():
            tell(credits.at[4], p.across)

    def release(sems):
        for who, n in [(p.pair, 0)] + [(p.behind(n), n) for n in range(1, p.line)]:
            tell(sems.at[n], who)

    def free_rows(seq):
        gone(("mlp", seq))
        tell(credits.at[2 + seq], p.sibling)

    feed(0)
    both_ff_weights(0)
    finish_branch(1)
    ff_weights(0, 2)
    free_rows(0)
    feed(1)
    of_ff.drain()
    of_rest.drain()
    of_gate.drain()
    release(ff_free)
    gain_acc[...] = jnp.zeros_like(gain_acc)
    scatters = [
        Scatter(
            p,
            ff_grad,
            ff_w,
            pl.ds(n * wide, wide),
            (pair_out.at[5 + n], pair_in.at[5 + n]),
            (line_out.at[n], line_in.at[n]),
            ff_free if n == 0 else None,
        )
        for n in range(3)
    ]
    scatters_attn = [
        Scatter(
            p,
            attn_grad,
            og,
            pl.ds(n * hw, hw),
            (pair_out.at[8 + n], pair_in.at[8 + n]),
            (line_out.at[3 + n], line_in.at[3 + n]),
            attn_free if n == 0 else None,
        )
        for n in range(4)
    ]
    away = far_first(p.line)
    firsts = away or [0]
    both_ff_weights(1, [functools.partial(scatters[n].start, firsts) for n in range(2)])
    ff_weights(1, 2)
    scatters[2].start(firsts)
    if away:
        for n in range(2):
            scatters[n].start([0])
    relays = [(scatters[n], k) for n in range(3) for k in away]
    if len(away) == 3:
        relays = [relays[n] for n in (0, 1, 3, 2, 4, 6, 5, 7, 8)]

    def relay_grad():
        if relays:
            scatter, k = relays.pop(0)
            scatter.relay(k)

    pull(0)
    free_rows(1)

    dqkv = units

    def grad_att(i, heads):
        return units[pl.ds(i * TILE, TILE), rows_at(3 * hw + heads * 128, 128)]

    def turn(seq):
        @pl.loop(0, tiles)
        def _(j):
            rows = rows_at(seq * SEQ_LEN + j * TILE, TILE)
            turned[:, rows_at(j * TILE, TILE)] = k[rows, :].astype(F32).T.astype(BF16)

    def prepare(seq):
        arrived(normed_mlp.at[block(2 * seq + 1 - p.core)], cores, 16 + seq, p.sibling)

        @pl.loop(0, tiles)
        def _(j):
            here = rows_at(j * TILE, TILE)
            rows = rows_at(seq * SEQ_LEN + j * TILE, TILE)
            units[here, out_lanes] = dot_nn(normed_mlp[rows, :], attn_w[:, out_lanes]).astype(BF16)

    def grad_store(seq, heads):
        rows = pl.ds(seq * SEQ_LEN, SEQ_LEN)
        return local(6, dv, value_first_grad.at[rows, rows_at(heads * 128, 128)])

    def m_copy():
        return send(m_sum.at[1 - p.chip], xb.at[p.chip], group, 4, p.across)

    def attend_back(seq, jobs):
        if seq > 0:
            grad_store(0, hw // 128 - 1).wait()

        @pl.loop(0, hw // 128)
        def _(heads):
            @pl.when(heads > 0)
            def _():
                grad_store(seq, heads - 1).wait()

            for i in reversed(range(tiles)):
                for when, job in jobs:
                    if when[1] == i:

                        @pl.when(heads == when[0])
                        def _():
                            job()

                attention_rows_back(
                    seq,
                    heads,
                    i,
                    q,
                    k,
                    v,
                    turned,
                    segments,
                    lse,
                    attended,
                    grad_att,
                    dk,
                    dv,
                    cos,
                    sin,
                    dqkv,
                )

            @pl.loop(0, tiles)
            def _(j):
                here = rows_at(j * TILE, TILE)
                rows = rows_at(seq * SEQ_LEN + j * TILE, TILE)
                u = dk[here, :]
                dqkv[here, rows_at(hw + heads * 128, 128)] = (
                    u * cos[rows, :] - swap_halves(u) * sin[rows, :]
                ).astype(BF16)
                half = 0.5 * dv[here, :]
                dqkv[here, rows_at(2 * hw + heads * 128, 128)] = half.astype(BF16)
                dv[here, :] = half

            grad_store(seq, heads).start()

    def attn_weights(seq, part):
        rows = pl.ds(seq * SEQ_LEN, SEQ_LEN)
        pieces = [(normed, units[:, qkv], qkv)]
        if isinstance(part, int) and part == 3:
            pieces = [(normed_mlp, attended[rows, :], out_lanes)]
        elif seq > 0:
            lanes = rows_at(part * hw, hw)
            pieces = [(normed, units[:, lanes], lanes)]

        @pl.loop(0, width // TILE)
        def _(j):
            cols = rows_at(j * TILE, TILE)
            for left, right, lanes in pieces:
                made = dot_tn(left[rows, cols], right)
                if seq > 0:
                    made = made + attn_grad[cols, lanes].astype(F32)
                attn_grad[cols, lanes] = made.astype(BF16)

    def back_other(seq):
        if seq == 0:
            feed_gone(1)

        @pl.loop(0, HALF // TILE)
        def _(j):
            here = rows_at((1 - p.core) * HALF + j * TILE, TILE)
            half_out[seq, rows_at(j * TILE, TILE), :] = dot_nt(
                dqkv[here, qkv], attn_w[:, qkv]
            ).astype(BF16)

        go(("half", seq), send(half_out.at[seq], half_in.at[seq], cores, 18 + seq, p.sibling))

    gain_sems = (gain_out_sems, gain_in_sems)

    def exchange(partners, first):
        copies = []
        for n, who in enumerate(partners):
            copy = send(gain_acc, gain_in.at[first + n], gain_sems, first + n, who)
            copy.start()
            copies.append(copy)

        def rest():
            for copy in copies:
                copy.wait()
            whole = gain_acc[...]
            for n in range(len(partners)):
                whole = whole + gain_in[first + n]
            gain_acc[...] = whole

        return rest

    def back_own(seq):
        arrived(half_in.at[seq], cores, 18 + seq, p.sibling)
        for j in range(HALF // TILE):
            feed_sum(seq, j).wait_send()

        @pl.loop(0, HALF // TILE)
        def _(j):
            here = rows_at(p.core * HALF + j * TILE, TILE)
            tile = rows_at(j * TILE, TILE)
            rows = rows_at((2 * seq + p.core) * HALF + j * TILE, TILE)
            part = dot_nt(dqkv[here, qkv], attn_w[:, qkv]) + half_in[seq, tile, :].astype(F32)
            sum_out[seq, tile, :] = part.astype(BF16)
            gain_acc[0:1, :] += jnp.sum(part * normed[rows, :].astype(F32), axis=0, keepdims=True)

        rest = None
        if seq == SEQS - 1:
            rest = exchange([p.sibling], 0)

        @pl.when(p.chip != seq)
        def _():
            pl.semaphore_wait(credits.at[4], 1)
            send(sum_out.at[seq], sum_in.at[seq], group, 5, p.across).start()

        return rest

    turn(0)
    relay_grad()
    prepare(0)
    attend_back(0, [((1, 3), m_copy().start), ((0, 1), relay_grad), ((1, 1), relay_grad)])
    relay_grad()
    back_other(0)
    turn(1)
    attn_weights(0, 0)
    attn_weights(0, 3)
    relay_grad()
    pull(1)
    for name in ("og_x", "og_c", "og_f"):
        gone(name)
    release(attn_free)
    back_own(0)
    prepare(1)
    attend_back(1, [((0, 1), relay_grad), ((0, 1), relay_grad), ((1, 3), relay_grad)])
    back_other(1)
    while relays:
        relay_grad()

    @pl.loop(0, 3)
    def _(n):
        attn_weights(1, n)
        for m in range(3):
            pl.when(n == m)(functools.partial(scatters_attn[m].start, firsts))

    rest = back_own(1)
    attn_weights(1, 3)
    rest()
    farther = [p.ahead(n) for n in away] + [p.beyond(n) for n in away]
    rest = exchange([p.pair] + farther, 2)
    scatters_attn[3].start(firsts)
    if away:
        for scatter in (scatters[2], *scatters_attn):
            scatter.start([0])

    arrived(xb.at[1 - p.chip], group, 4, p.across)

    @pl.loop(0, HALF // TILE)
    def _(j):
        tile = rows_at(j * TILE, TILE)
        both = m_sum[p.chip, tile, :].astype(F32) + xb[1 - p.chip, tile, :].astype(F32)
        m_sum[p.chip, tile, :] = (hidden[p.chip, tile, :] + both).astype(BF16)

    stores = [fetch(8, m_sum.at[p.chip], block_output)]
    for n in range(4):
        for k in away[:-1]:
            scatters_attn[n].relay(k)
        for m in [n - 1] * (n > 0) + [n] * (n == 3):
            for k in away[-1:]:
                scatters_attn[m].relay(k)
        if n < 2:
            scatters[n].finish()
            (gate_sum, up_sum)[n][...] = scatters[n].total().T[:ff, :]
    rest()
    rest = exchange([p.across], 1)
    arrived(sum_in.at[p.chip], group, 5, p.across)

    @pl.loop(0, HALF // TILE)
    def _(j):
        tile = rows_at(j * TILE, TILE)
        grad = sum_out[p.chip, tile, :].astype(F32) + sum_in[p.chip, tile, :].astype(F32)
        back, _ = norm_pull(grad, xb[p.chip, tile, :].astype(F32), gain_attn)
        grad_hidden[tile, :] = grad_hidden[tile, :] + back

    stores.append(fetch(9, grad_hidden, input_grad))
    rest()
    gain_attn_grad[...] = gain_acc[0:1, :] / gain_attn
    gain_mlp_grad[...] = gain_acc[1:2, :]
    scatters[2].finish()
    down_sum[...] = scatters[2].total().T[:ff, :]
    for n, out in enumerate((query_sum, key_sum, value_sum)):
        scatters_attn[n].finish()
        out[...] = scatters_attn[n].total()
    scatters_attn[3].finish()
    out_sum[...] = scatters_attn[3].total().T
    send(sum_out.at[1 - p.chip], sum_in.at[1 - p.chip], group, 5, p.across).wait_send()
    m_copy().wait_send()
    grad_store(SEQS - 1, hw // 128 - 1).wait()
    for name in list(sent):
        gone(name)
    of_attn.drain()
    of_out.drain()
    for scatter in (*scatters, *scatters_attn):
        scatter.drain()
    for copy in stores:
        copy.wait()


def layer(dp, x, og, vf, segments, positions, gains, wq, wk, wv, wo, wg, wu, wd):
    rows, width = 4 * x.shape[0], x.shape[1]
    hw, ff, r = vf.shape[1], wg.shape[0], wq.shape[0]
    wide = -(-ff // 256) * 256
    line = dp // 2
    hops = max(line - 1, 1)
    vmem = pl.BlockSpec(memory_space=pltpu.VMEM)
    far = pl.BlockSpec(memory_space=pl.ANY)
    shapes = [
        ((HALF, width), BF16, far),
        ((HALF, width), F32, far),
        ((rows, hw), F32, far),
        ((1, width), F32, vmem),
        ((r, hw), F32, vmem),
        ((r, hw), F32, vmem),
        ((r, hw), F32, vmem),
        ((hw, r), F32, vmem),
        ((1, width), F32, vmem),
        ((ff, r), F32, vmem),
        ((ff, r), F32, vmem),
        ((ff, r), F32, vmem),
    ]
    dma = pltpu.SemaphoreType.DMA
    flag = pltpu.SemaphoreType.REGULAR

    def bf(*shape):
        return pltpu.VMEM(shape, BF16)

    def fl(*shape):
        return pltpu.VMEM(shape, F32)

    scratch = [
        bf(2, HALF, width),
        bf(rows, width),
        bf(rows, width),
        bf(rows, width),
        bf(width, 4 * hw),
        bf(width, 3 * wide),
        bf(rows, hw),
        bf(rows, hw),
        bf(rows, hw),
        bf(rows, hw),
        fl(8, 1, SEQ_LEN),
        fl(2, HALF, width),
        fl(HALF, width),
        bf(SEQ_LEN, 3 * wide),
        bf(width, 3 * wide),
        bf(width, 4 * hw),
        bf(2, HALF, width),
        bf(2, HALF, width),
        bf(2, HALF, width),
        bf(2, HALF, width),
        bf(2, HALF, width),
        bf(hw, SEQ_LEN),
        fl(SEQ_LEN, 128),
        fl(SEQ_LEN, 128),
        fl(rows, 128),
        fl(rows, 128),
        fl(2, width),
        fl(4 + 2 * hops, 2, width),
        dma((10,)),
        dma((10,)),
        dma((10,)),
        dma((20,)),
        dma((20,)),
        dma((5, hops)),
        dma((5, hops)),
        dma((5, hops)),
        dma((5, hops)),
        dma((12, line)),
        dma((12, line)),
        dma((7, line)),
        dma((7, line)),
        dma((4 + 2 * hops,)),
        dma((4 + 2 * hops,)),
        flag((5,)),
        flag((line,)),
        flag((line,)),
    ]
    in_specs = [far] * 3 + [vmem] * 3 + [far] * 3 + [vmem] * 4
    return pl.pallas_call(
        functools.partial(layer_kernel, dp),
        out_shape=[jax.ShapeDtypeStruct(s, t) for s, t, _ in shapes],
        in_specs=in_specs,
        out_specs=[space for _, _, space in shapes],
        scratch_shapes=scratch,
        compiler_params=pltpu.CompilerParams(
            collective_id=0, has_side_effects=True, vmem_limit_bytes=VMEM_LIMIT
        ),
        name="layer",
    )(x, og, vf, segments, positions, gains, wq, wk, wv, wo, wg, wu, wd)


def settle_kernel(count, *refs):
    ins, outs, held, sems = refs[:count], refs[count : 2 * count], refs[2 * count : -1], refs[-1]
    first = [pltpu.make_async_copy(ins[n], held[n], sems.at[n]) for n in range(count)]
    second = [pltpu.make_async_copy(held[n], outs[n], sems.at[count + n]) for n in range(count)]
    for copy in first:
        copy.start()
    for n in range(count):
        first[n].wait()
        second[n].start()
    for copy in second:
        copy.wait()


def settle(arrays):
    count = len(arrays)
    far = pl.BlockSpec(memory_space=pl.ANY)
    return pl.pallas_call(
        functools.partial(settle_kernel, count),
        out_shape=[jax.ShapeDtypeStruct(a.shape, a.dtype) for a in arrays],
        in_specs=[far] * count,
        out_specs=[far] * count,
        scratch_shapes=[pltpu.VMEM(a.shape, a.dtype) for a in arrays]
        + [pltpu.SemaphoreType.DMA((2 * count,))],
        compiler_params=pltpu.CompilerParams(vmem_limit_bytes=VMEM_LIMIT),
        name="settle",
    )(*arrays)


def on_device(
    dp,
    block_input,
    value_first,
    segment_ids,
    positions,
    gain_attn,
    query_weight,
    key_weight,
    value_weight,
    out_weight,
    gain_mlp,
    gate_weight,
    up_weight,
    down_weight,
    output_grad,
):
    first = lax.broadcasted_iota(jnp.int32, (2, gain_attn.shape[0]), 0) == 0
    outs = layer(
        dp,
        block_input,
        output_grad,
        value_first,
        segment_ids[None, :],
        positions[None, :],
        jnp.where(first, gain_attn.astype(F32)[None], gain_mlp.astype(F32)[None]),
        query_weight,
        key_weight,
        value_weight,
        out_weight,
        gate_weight.T,
        up_weight.T,
        down_weight,
    )
    (
        block_output,
        input_grad,
        value_first_grad,
        gain_attn_grad,
        query_sum,
        key_sum,
        value_sum,
        out_sum,
        gain_mlp_grad,
        gate_sum,
        up_sum,
        down_sum,
    ) = settle(outs)
    return (
        block_output,
        input_grad,
        value_first_grad,
        gain_attn_grad[0],
        query_sum,
        key_sum,
        value_sum,
        out_sum,
        gain_mlp_grad[0],
        gate_sum.T,
        up_sum.T,
        down_sum,
    )


def solution(mesh):
    rows = P(("dp", "tensor"), None)
    weight = P("dp", "tensor")
    across = P("tensor", "dp")
    return jax.shard_map(
        functools.partial(on_device, mesh.shape["dp"]),
        mesh=mesh,
        in_specs=(
            rows,
            weight,
            P("dp"),
            P("dp"),
            P(),
            weight,
            weight,
            weight,
            across,
            P(),
            weight,
            weight,
            across,
            rows,
        ),
        out_specs=(
            rows,
            rows,
            weight,
            P(),
            weight,
            weight,
            weight,
            across,
            P(),
            weight,
            weight,
            across,
        ),
        check_vma=False,
    )
```

```python
import functools
import math

import jax
import jax.numpy as jnp
from jax import lax
from jax.experimental import pallas as pl
from jax.experimental.pallas import tpu as pltpu
from jax.sharding import PartitionSpec as P

HEAD_DIM = 64
SEQ_LEN = 1024
SEQS = 2
PIECE = 256
HALF = 512
TILE = 256
EPSILON = 1e-06
ROPE_BASE = 10000.0
MASKED = -1e30
MESH = pl.DeviceIdType.MESH
F32 = jnp.float32
BF16 = jnp.bfloat16
VMEM_LIMIT = 639 * 2**20 // 10


def dot_nn(a, b):
    return lax.dot_general(a, b, (((1,), (0,)), ((), ())), preferred_element_type=F32)


def dot_nt(a, b):
    return lax.dot_general(a, b, (((1,), (1,)), ((), ())), preferred_element_type=F32)


def dot_tn(a, b):
    return lax.dot_general(a, b, (((0,), (0,)), ((), ())), preferred_element_type=F32)


def rows_at(start, size):
    return pl.ds(pl.multiple_of(start, size), size)


def block(b):
    return rows_at(b * HALF, HALF)


class Place:
    def __init__(self, dp):
        self.d = lax.axis_index("dp")
        self.t = lax.axis_index("tensor")
        self.core = lax.rem(self.t, 2)
        self.chip = self.t // 2
        self.line = dp // 2
        self.y = lax.rem(self.d, 2)
        self.z = self.d // 2
        self.sibling = (self.d, self.t + 1 - 2 * self.core)
        self.across = (self.d, lax.rem(self.t + 2, 4))
        self.pair = (self.d + 1 - 2 * self.y, self.t)
        self.up = (self.d + 2, self.t)
        self.down = (self.d - 2, self.t)

    def ahead(self, k):
        return (2 * lax.rem(self.z + k, self.line) + self.y, self.t)

    def beyond(self, k):
        return (2 * lax.rem(self.z + k, self.line) + 1 - self.y, self.t)

    def behind(self, k):
        return (2 * lax.rem(self.z + self.line - k, self.line) + self.y, self.t)

    def greet(self):
        barrier = pltpu.get_barrier_semaphore()
        partners = [self.sibling, self.across, self.pair]
        partners.extend(self.ahead(k) for k in range(1, self.line))
        partners.extend(self.beyond(k) for k in range(1, self.line))
        for who in partners:
            tell(barrier, who)
        self.greeted = len(partners)

    def met(self):
        pl.semaphore_wait(pltpu.get_barrier_semaphore(), self.greeted)


def tell(sem, who):
    pl.semaphore_signal(sem, inc=1, device_id=who, device_id_type=MESH)


def send(src, dst, sems, k, who):
    return pltpu.make_async_remote_copy(
        src_ref=src,
        dst_ref=dst,
        send_sem=sems[0].at[k],
        recv_sem=sems[1].at[k],
        device_id=who,
        device_id_type=MESH,
    )


class Gather:
    def __init__(self, place, full, lanes, rows, spread, up_sems, down_sems, pair_sems):
        self.p, self.full, self.lanes, self.r, self.spread = place, full, lanes, rows, spread
        self.up_sems, self.down_sems, self.pair_sems = up_sems, down_sems, pair_sems

    def shard(self, z, y):
        return self.full.at[rows_at((2 * z + y) * self.r, self.r), self.lanes]

    def load(self, z):
        if self.spread:
            return self.shard(z, self.p.y)
        return self.full.at[rows_at(2 * z * self.r, 2 * self.r), self.lanes]

    def sides(self, k):
        p = self.p
        return (
            (p.z - k, p.z >= k, self.up_sems, p.z + 1 < p.line, p.up),
            (p.z + k, p.z + k < p.line, self.down_sems, p.z >= 1, p.down),
        )

    def start_pair(self):
        p = self.p
        here = self.shard(p.z, p.y)
        send(here, here, self.pair_sems, p.z, p.pair).start()

    def start_line(self):
        p = self.p
        if not self.spread:
            there = self.shard(p.z, 1 - p.y)
            send(there, there, self.pair_sems, p.z, p.pair).wait_recv()
        here = self.load(p.z)
        for _, _, sems, onward, to in self.sides(0):

            @pl.when(onward)
            def _():
                send(here, here, sems, 0, to).start()

    def relay(self, k):
        p = self.p
        for z, exists, sems, onward, to in self.sides(k):

            @pl.when(exists)
            def _():
                here = self.load(z)
                send(here, here, sems, k - 1, to).wait_recv()

                @pl.when(onward)
                def _():
                    send(here, here, sems, k, to).start()

                if self.spread:
                    send(here, here, self.pair_sems, z, p.pair).start()

    def finish(self):
        p = self.p
        if self.spread:
            for z in range(p.line):
                there = self.shard(z, 1 - p.y)
                send(there, there, self.pair_sems, z, p.pair).wait_recv()

    def drain(self):
        p = self.p
        for z in range(p.line) if self.spread else (p.z,):
            here = self.shard(z, p.y)
            send(here, here, self.pair_sems, z, p.pair).wait_send()
        for k in range(p.line - 1):
            for z, exists, sems, onward, to in self.sides(k):

                @pl.when(jnp.logical_and(exists, onward))
                def _():
                    here = self.load(z)
                    send(here, here, sems, k, to).wait_send()


def far_first(n):
    if n < 4:
        return list(range(1, n))
    last = [2, n - 2] if n > 4 else [2]
    return [1, n - 1, *range(3, n - 2), *last]


class Scatter:
    def __init__(self, place, full, into, lanes, pair_sems, line_sems, free):
        self.p, self.full, self.into, self.lanes = place, full, into, lanes
        self.pair_sems, self.line_sems = pair_sems, line_sems
        self.free = free
        self.r = full.shape[0] // (2 * place.line)

    def rows(self, k, y):
        z = lax.rem(self.p.z + k, self.p.line)
        return rows_at((2 * z + y) * self.r, self.r)

    def pair_in(self, k):
        return self.into.at[pl.ds(k * self.r, self.r), self.lanes]

    def line_in(self, k):
        return self.into.at[pl.ds((self.p.line + k - 1) * self.r, self.r), self.lanes]

    def swap(self, k):
        theirs = self.full.at[self.rows(k, 1 - self.p.y), self.lanes]
        return send(theirs, self.pair_in(k), self.pair_sems, k, self.p.pair)

    def start(self, steps):
        if self.free is not None and (steps[0] == 1 or self.p.line == 1):
            pl.semaphore_wait(self.free.at[0], 1)
        for k in steps:
            self.swap(k).start()

    def relay(self, k):
        p = self.p
        n = p.line
        there = self.pair_in(k)
        send(there, there, self.pair_sems, k, p.pair).wait_recv()
        self.join(k, there)
        if self.free is not None and k == 1:
            for m in range(1, n):
                pl.semaphore_wait(self.free.at[m], 1)
        if n >= 4 and k in (2, n - 2):
            helping = jnp.logical_or(
                jnp.logical_and(p.z == 1, k == n - 2), jnp.logical_and(p.z == n - 2, k == 2)
            )

            @pl.when(helping)
            def _():
                self.helped().wait_recv()
                self.join(k, self.line_in(n))

        if n >= 4 and k in (1, n - 1):
            from_end = p.z == (0 if k == n - 1 else n - 1)

            @pl.when(from_end)
            def _():
                self.helped(k).start()

            @pl.when(jnp.logical_not(from_end))
            def _():
                self.onward(k).start()
        else:
            self.onward(k).start()

    def join(self, k, came):
        mine = self.full.at[self.rows(k, self.p.y), self.lanes]
        step = min(self.r, 32)

        @pl.loop(0, self.r // step)
        def _(j):
            rows = rows_at(j * step, step)
            mine[rows, :] = (mine[rows, :].astype(F32) + came[rows, :].astype(F32)).astype(BF16)

    def helped(self, k=1):
        p = self.p
        near = jnp.where(p.z == 0, 1, p.line - 2)
        mine = self.full.at[self.rows(k, p.y), self.lanes]
        return pltpu.make_async_remote_copy(
            src_ref=mine,
            dst_ref=self.line_in(p.line),
            send_sem=self.line_sems[0].at[k - 1],
            recv_sem=self.line_sems[1].at[p.line - 1],
            device_id=(2 * near + p.y, p.t),
            device_id_type=MESH,
        )

    def onward(self, k):
        p = self.p
        mine = self.full.at[self.rows(k, p.y), self.lanes]
        return send(mine, self.line_in(k), self.line_sems, k - 1, p.ahead(k))

    def merged(self, k):
        n = self.p.line
        if n < 4 or k not in (1, n - 1):
            return None
        return self.p.z == (n - 1 if k == n - 1 else 0)

    def finish(self):
        p = self.p
        there = self.pair_in(0)
        send(there, there, self.pair_sems, 0, p.pair).wait_recv()
        for k in range(1, p.line):
            there = self.line_in(k)
            merged = self.merged(k)
            if merged is None:
                send(there, there, self.line_sems, k - 1, p.pair).wait_recv()
            else:

                @pl.when(jnp.logical_not(merged))
                def _():
                    send(there, there, self.line_sems, k - 1, p.pair).wait_recv()

    def total(self):
        whole = self.full[self.rows(0, self.p.y), self.lanes].astype(F32)
        whole = whole + self.pair_in(0)[...].astype(F32)
        for k in range(1, self.p.line):
            came = self.line_in(k)[...].astype(F32)
            merged = self.merged(k)
            if merged is not None:
                came = jnp.where(merged, jnp.zeros_like(came), came)
            whole = whole + came
        return whole

    def drain(self):
        for k in range(self.p.line):
            self.swap(k).wait_send()
        for k in range(1, self.p.line):
            self.onward(k).wait_send()


def swap_halves(u):
    lane = lax.broadcasted_iota(jnp.int32, u.shape, 1)
    low = lax.rem(lane, HEAD_DIM) < HEAD_DIM // 2
    return jnp.where(low, pltpu.roll(u, 96, 1), pltpu.roll(u, 32, 1))


def norm_factor(u):
    return lax.rsqrt(jnp.mean(u * u, axis=-1, keepdims=True) + EPSILON)


def norm_pull(grad, u, gain):
    r = norm_factor(u)
    scaled = grad * gain
    back = r * scaled - u * (r * r * r) * jnp.mean(scaled * u, axis=-1, keepdims=True)
    return back, grad * u * r


def visible(segments):
    key = lax.broadcasted_iota(jnp.int32, (TILE, TILE), 0)
    query = lax.broadcasted_iota(jnp.int32, (TILE, TILE), 1)
    return jnp.logical_or(key <= query, segments > 0)


def attention_rows(seq, heads, i, q, k, vt, segments, attended, lse):
    lane = lax.broadcasted_iota(jnp.int32, (TILE, 128), 1)
    lanes = rows_at(heads * 128, 128)
    rows = pl.ds(seq * SEQ_LEN + i * TILE, TILE)
    q2 = q[rows, lanes]
    shown = visible(segments[:, rows])
    sides = []
    for a in range(2):
        qa = jnp.where((lane < HEAD_DIM) == (a == 0), q2, jnp.zeros_like(q2))
        vta = rows_at((heads * 2 + a) * HEAD_DIM, HEAD_DIM)
        score = jnp.where(shown, dot_nt(k[rows, lanes], qa), MASKED)
        top = jnp.max(score, axis=0, keepdims=True)
        if i > 0:
            before = dot_nt(k[pl.ds(seq * SEQ_LEN, i * TILE), lanes], qa)
            top = jnp.maximum(top, jnp.max(before, axis=0, keepdims=True))
        weight = jnp.exp(score - top)
        total = jnp.sum(weight, axis=0, keepdims=True)
        out = dot_nn(vt[vta, pl.ds(i * TILE, TILE)], weight.astype(BF16))
        if i > 0:
            weight = jnp.exp(before - top)
            total = total + jnp.sum(weight, axis=0, keepdims=True)
            out = out + dot_nn(vt[vta, pl.ds(0, i * TILE)], weight.astype(BF16))
        sides.append(out * (1.0 / total))
        lse[seq * 4 + heads * 2 + a, :, pl.ds(i * TILE, TILE)] = top + jnp.log(total)
    attended[rows, lanes] = jnp.concatenate(sides, axis=0).T.astype(BF16)


def attention_rows_back(
    seq, heads, i, q, k, v, kt, segments, lse, attended, grad_att, dk, dv, cos, sin, dqkv
):
    lane = lax.broadcasted_iota(jnp.int32, (TILE, 128), 1)
    lanes = rows_at(heads * 128, 128)
    local = pl.ds(i * TILE, TILE)
    rows = pl.ds(seq * SEQ_LEN + i * TILE, TILE)
    first = i == SEQ_LEN // TILE - 1
    q2, g2 = q[rows, lanes], grad_att(i, heads)
    shown = visible(segments[:, rows])
    products = (g2.astype(F32) * attended[rows, lanes].astype(F32)).T
    parts = [(i * TILE, TILE, True)]
    if i > 0:
        parts.append((0, i * TILE, False))
    sides = [None, None]
    for start, size, diagonal in parts:
        keys = pl.ds(seq * SEQ_LEN + start, size)
        here = pl.ds(start, size)
        dk_part, dv_part = 0.0, 0.0
        for a in range(2):
            mine = (lane < HEAD_DIM) == (a == 0)
            qa = jnp.where(mine, q2, jnp.zeros_like(q2))
            ga = jnp.where(mine, g2, jnp.zeros_like(g2))
            delta = jnp.sum(products[a * HEAD_DIM : (a + 1) * HEAD_DIM], axis=0, keepdims=True)
            stat = lse[seq * 4 + heads * 2 + a, :, local]
            score = dot_nt(k[keys, lanes], qa)
            if diagonal:
                score = jnp.where(shown, score, MASKED)
            prob = jnp.exp(score - stat)
            grad_prob = dot_nt(v[keys, lanes], ga)
            grad_score = (prob * (grad_prob - delta)).astype(BF16)
            dv_part = dv_part + dot_nn(prob.astype(BF16), ga)
            dk_part = dk_part + dot_nn(grad_score, qa)
            side = dot_nn(kt[rows_at((heads * 2 + a) * HEAD_DIM, HEAD_DIM), here], grad_score)
            sides[a] = side if sides[a] is None else sides[a] + side
        if first:
            dk[here, :] = dk_part
            dv[here, :] = dv_part
        else:
            dk[here, :] += dk_part
            dv[here, :] += dv_part
    dq = jnp.concatenate(sides, axis=0).T * HEAD_DIM**-0.5
    dqkv[local, lanes] = (dq * cos[rows, :] - swap_halves(dq) * sin[rows, :]).astype(BF16)


def layer_kernel(
    dp,
    x_in,
    og_in,
    value_first,
    segments,
    positions,
    gain_attn_in,
    gain_mlp_in,
    query_shard,
    key_shard,
    value_shard,
    out_shard,
    gate_shard,
    up_shard,
    down_shard,
    block_output,
    input_grad,
    value_first_grad,
    gain_attn_out,
    query_out,
    key_out,
    value_out,
    out_out,
    gain_mlp_out,
    gate_out,
    up_out_sum,
    down_out_sum,
    gain_attn_grad,
    query_sum,
    key_sum,
    value_sum,
    out_sum,
    gain_mlp_grad,
    gate_sum,
    up_sum,
    down_sum,
    xb,
    normed,
    normed_mlp,
    og,
    attn_w,
    ff_w,
    q,
    k,
    v,
    attended,
    lse,
    hidden,
    grad_hidden,
    units,
    ff_grad,
    attn_grad,
    half_out,
    half_in,
    sum_out,
    sum_in,
    m_sum,
    turned,
    dk,
    dv,
    cos,
    sin,
    gain_acc,
    gain_in,
    local_sems,
    group_out,
    group_in,
    core_out,
    core_in,
    up_out,
    up_in,
    down_out,
    down_in,
    pair_out,
    pair_in,
    line_out,
    line_in,
    gain_out_sems,
    gain_in_sems,
    credits,
    ff_free,
    attn_free,
):
    p = Place(dp)
    group, cores = (group_out, group_in), (core_out, core_in)
    rows_r, hw = query_shard.shape
    ff = gate_shard.shape[0]
    wide = ff_w.shape[1] // 3
    width = x_in.shape[1]
    tiles = SEQ_LEN // TILE
    slot = rows_at(p.d * rows_r, rows_r)
    qkv, out_lanes = slice(0, 3 * hw), slice(3 * hw, 4 * hw)
    middle = wide + 5 * wide // 6 // 128 * 128
    sent = {}

    def go(name, copy):
        copy.start()
        sent[name] = copy

    def gone(name):
        sent.pop(name).wait_send()

    def arrived(there, sems, n, who):
        send(there, there, sems, n, who).wait_recv()

    def local(n, src, dst):
        return pltpu.make_async_copy(src, dst, local_sems.at[n])

    def fetch(n, src, dst):
        copy = local(n, src, dst)
        copy.start()
        return copy

    p.greet()
    x_copy = fetch(0, x_in, xb.at[p.chip])
    qkv_copies = [
        fetch(1 + n, shard, attn_w.at[slot, pl.ds(n * hw, hw)])
        for n, shard in enumerate((query_shard, key_shard, value_shard))
    ]
    og_copy = fetch(4, og_in, og.at[block(p.t)])
    vf_copy = fetch(5, value_first, attended)
    attn_w[slot, out_lanes] = out_shard[...].astype(F32).T.astype(BF16)
    p.met()
    x_copy.wait()
    go("x", send(xb.at[p.chip], xb.at[p.chip], group, 0, p.across))
    gathers = [
        Gather(
            p,
            full,
            pl.ds(first, lanes),
            rows_r,
            spread,
            (up_out.at[n], up_in.at[n]),
            (down_out.at[n], down_in.at[n]),
            (pair_out.at[n], pair_in.at[n]),
        )
        for n, (full, first, lanes, spread) in enumerate(
            (
                (attn_w, 0, 3 * hw, True),
                (attn_w, 3 * hw, hw, True),
                (ff_w, wide // 2, middle - wide // 2, True),
                (ff_w, middle, 3 * wide - middle, True),
                (ff_w, 0, wide // 2, False),
            )
        )
    ]
    of_attn, of_out, of_ff, of_rest, of_gate = gathers
    for copy in qkv_copies:
        copy.wait()
    of_attn.start_line()
    of_attn.start_pair()
    of_out.start_line()
    of_out.start_pair()
    gain_attn = gain_attn_in[...].astype(F32).reshape(1, width)
    gain_mlp = gain_mlp_in[...].astype(F32).reshape(1, width)
    other = lax.rem(p.t + 2, 4)
    sib = p.t + 1 - 2 * p.core
    sib_other = lax.rem(sib + 2, 4)

    def norm_block(b, chip, n):
        @pl.loop(0, HALF // TILE)
        def _(j):
            u = xb[chip, rows_at(j * TILE, TILE), :].astype(F32)
            normed[rows_at(b * HALF + j * TILE, TILE), :] = (
                u * norm_factor(u) * gain_attn
            ).astype(BF16)

        here = normed.at[block(b)]
        go(("normed", n), send(here, here, cores, n, p.sibling))

    norm_block(p.t, p.chip, 0)
    for n, shard in enumerate((gate_shard, up_shard, down_shard)):
        flat = shard[...].astype(F32)
        if wide > ff:
            flat = jnp.concatenate([flat, jnp.zeros((wide - ff, rows_r), F32)], axis=0)
        ff_w[slot, n * wide : (n + 1) * wide] = flat.T.astype(BF16)
    of_gate.start_pair()
    if p.line > 1:
        of_attn.relay(1)
        of_out.relay(1)

    @pl.loop(0, SEQS * tiles)
    def _(j):
        rows = rows_at(j * TILE, TILE)
        lane = lax.broadcasted_iota(jnp.int32, (TILE, 128), 1)
        half = HEAD_DIM // 2
        power = lax.rem(lane[0:1, :], half).astype(F32) * (-2.0 / HEAD_DIM)
        frequency = jnp.exp(power * math.log(ROPE_BASE))
        place = jnp.broadcast_to(positions[:, rows].astype(F32), (128, TILE)).T
        angle = place * frequency
        cos[rows, :] = jnp.cos(angle)
        sine = jnp.sin(angle)
        sin[rows, :] = jnp.where(lax.rem(lane, HEAD_DIM) < half, -sine, sine)

    og_copy.wait()
    own_rows = og.at[block(p.t)]
    go("og_c", send(own_rows, own_rows, cores, 2, p.sibling))
    for n in range(2, p.line):
        of_attn.relay(n)
        of_out.relay(n)
        if n == 2:
            go("og_x", send(own_rows, own_rows, group, 1, p.across))
    if p.line < 3:
        go("og_x", send(own_rows, own_rows, group, 1, p.across))
    of_ff.start_line()
    of_rest.start_line()
    of_gate.start_line()
    arrived(xb.at[1 - p.chip], group, 0, p.across)
    norm_block(other, 1 - p.chip, 1)
    of_ff.start_pair()
    of_rest.start_pair()
    of_attn.finish()
    arrived(normed.at[block(sib)], cores, 0, p.sibling)
    arrived(normed.at[block(sib_other)], cores, 1, p.sibling)
    vf_copy.wait()

    def project(seq):
        @pl.loop(0, tiles)
        def _(j):
            rows = rows_at(seq * SEQ_LEN + j * TILE, TILE)
            made = dot_nn(normed[rows, :], attn_w[:, qkv])
            c, s = cos[rows, :], sin[rows, :]
            for n in range(hw // 128):
                lanes = slice(n * 128, (n + 1) * 128)
                u = made[:, n * 128 : (n + 1) * 128]
                q[rows, lanes] = ((u * c + swap_halves(u) * s) * HEAD_DIM**-0.5).astype(BF16)
                u = made[:, hw + n * 128 : hw + (n + 1) * 128]
                k[rows, lanes] = (u * c + swap_halves(u) * s).astype(BF16)
            mixed = 0.5 * made[:, 2 * hw :] + 0.5 * attended[rows, :].astype(F32)
            v[rows, :] = mixed.astype(BF16)
            turned[:, rows_at(j * TILE, TILE)] = mixed.T.astype(BF16)

    def attend(seq, between):
        @pl.loop(0, hw // 128)
        def _(heads):
            @pl.when(heads == hw // 128 - 1)
            def _():
                for relay in between:
                    relay()

            for i in range(tiles):
                attention_rows(seq, heads, i, q, k, turned, segments, attended, lse)

    def branch_other(seq):
        @pl.loop(0, HALF // TILE)
        def _(j):
            rows = rows_at(seq * SEQ_LEN + (1 - p.core) * HALF + j * TILE, TILE)
            half_out[seq, rows_at(j * TILE, TILE), :] = dot_nt(
                attended[rows, :], attn_w[:, out_lanes]
            ).astype(BF16)

        go(("half", seq), send(half_out.at[seq], half_in.at[seq], cores, 4 + seq, p.sibling))

    def branch_own(seq):
        arrived(half_in.at[seq], cores, 4 + seq, p.sibling)

        @pl.loop(0, HALF // TILE)
        def _(j):
            rows = rows_at(seq * SEQ_LEN + p.core * HALF + j * TILE, TILE)
            tile = rows_at(j * TILE, TILE)
            part = dot_nt(attended[rows, :], attn_w[:, out_lanes])
            sum_out[seq, tile, :] = (part + half_in[seq, tile, :].astype(F32)).astype(BF16)

        go(("sum", seq), send(sum_out.at[seq], sum_in.at[seq], group, 2 + seq, p.across))

    def finish_branch(seq):
        arrived(sum_in.at[seq], group, 2 + seq, p.across)

        @pl.loop(0, HALF // TILE)
        def _(j):
            tile = rows_at(j * TILE, TILE)
            both = sum_out[seq, tile, :].astype(F32) + sum_in[seq, tile, :].astype(F32)
            u = xb[seq, tile, :].astype(F32) + both
            hidden[seq, tile, :] = u
            normed_mlp[rows_at((2 * seq + p.core) * HALF + j * TILE, TILE), :] = (
                u * norm_factor(u) * gain_mlp
            ).astype(BF16)

        mine = normed_mlp.at[block(2 * seq + p.core)]
        go(("mlp", seq), send(mine, mine, cores, 6 + seq, p.sibling))
        tell(credits.at[seq], p.across)

    def in_steps(gather):
        steps = list(range(1, p.line))

        def relay():
            if steps:
                gather.relay(steps.pop(0))

        return relay, steps

    relay_ff, steps = in_steps(of_ff)
    relay_rest, _ = in_steps(of_rest)
    relay_gate, left = in_steps(of_gate)
    project(0)
    attend(0, [relay_ff])
    relay_rest()
    of_out.finish()
    branch_other(0)
    project(1)
    branch_own(0)
    relay_gate()
    relay_ff()
    attend(1, [relay_rest])
    relay_gate()
    branch_other(1)
    branch_own(1)
    relay_ff()
    relay_rest()
    arrived(og.at[block(other)], group, 1, p.across)
    there = og.at[block(other)]
    go("og_f", send(there, there, cores, 3, p.sibling))
    while steps or left:
        relay_ff()
        relay_rest()
        relay_gate()
    finish_branch(0)
    arrived(og.at[block(sib)], cores, 2, p.sibling)
    arrived(og.at[block(sib_other)], cores, 3, p.sibling)
    of_ff.finish()
    of_rest.finish()

    def feed_copy(seq, n, j):
        tile = rows_at(j * TILE, TILE)
        there = half_in.at[n, tile]
        return send(half_out.at[n, tile], there, cores, 8 + seq * 4 + n * 2 + j, p.sibling)

    def feed_sum(seq, j):
        tile = rows_at(j * TILE, TILE)
        return send(sum_out.at[seq, tile], sum_in.at[seq, tile], group, 6 + seq * 2 + j, p.across)

    def feed_gone(seq):
        for n in range(2):
            for j in range(HALF // TILE):
                feed_copy(seq, n, j).wait_send()

    def feed(seq):
        arrived(normed_mlp.at[block(2 * seq + 1 - p.core)], cores, 6 + seq, p.sibling)
        if seq == 0:
            for n in range(2):
                gone(("half", n))
        else:
            feed_gone(0)
        gone(("sum", seq))
        pl.semaphore_wait(credits.at[seq], 1)

        @pl.loop(0, tiles)
        def _(step):
            j = lax.rem(step, HALF // TILE)
            others = step < HALF // TILE
            h = jnp.where(others, 1 - p.core, p.core)
            here = rows_at(h * HALF + j * TILE, TILE)
            rows = rows_at(seq * SEQ_LEN + h * HALF + j * TILE, TILE)
            tile = rows_at(j * TILE, TILE)
            for n in range(wide // 256):
                lanes = [slice(m * wide + n * 256, m * wide + (n + 1) * 256) for m in range(3)]
                gate = dot_nn(normed_mlp[rows, :], ff_w[:, lanes[0]])
                up = dot_nn(normed_mlp[rows, :], ff_w[:, lanes[1]])
                grad_act = dot_nn(og[rows, :], ff_w[:, lanes[2]])
                sig = 1.0 / (1.0 + jnp.exp(-gate))
                swish = gate * sig
                units[here, lanes[0]] = (
                    grad_act * up * sig * (1.0 + gate * (1.0 - sig))
                ).astype(BF16)
                units[here, lanes[1]] = (grad_act * swish).astype(BF16)
                units[here, lanes[2]] = (swish * up).astype(BF16)
            down = dot_nt(units[here, 2 * wide :], ff_w[:, 2 * wide :])
            back = dot_nt(units[here, : 2 * wide], ff_w[:, : 2 * wide])

            @pl.when(others)
            def _():
                half_out[0, tile, :] = back.astype(BF16)
                half_out[1, tile, :] = down.astype(BF16)
                for n in range(2):
                    feed_copy(seq, n, j).start()

            @pl.when(jnp.logical_not(others))
            def _():
                for n in range(2):
                    feed_copy(seq, n, j).wait_recv()
                sum_out[seq, tile, :] = (back + half_in[0, tile, :].astype(F32)).astype(BF16)
                m_sum[seq, tile, :] = (down + half_in[1, tile, :].astype(F32)).astype(BF16)
                feed_sum(seq, j).start()

    def ff_weights(seq, n):
        rows = pl.ds(seq * SEQ_LEN, SEQ_LEN)
        left = og if isinstance(n, int) else normed_mlp
        lanes = pl.ds(pl.multiple_of(n * wide, 128), wide)

        @pl.loop(0, width // TILE)
        def _(j):
            cols = rows_at(j * TILE, TILE)
            part = dot_tn(left[rows, cols], units[:, lanes])
            if seq > 0:
                part = part + ff_grad[cols, lanes].astype(F32)
            ff_grad[cols, lanes] = part.astype(BF16)

    def both_ff_weights(seq, then=()):
        @pl.loop(0, 2)
        def _(n):
            ff_weights(seq, n)
            for m, start in enumerate(then):
                pl.when(n == m)(start)

    def pull(seq):
        for j in range(HALF // TILE):
            feed_sum(seq, j).wait_recv()

        @pl.loop(0, HALF // TILE)
        def _(j):
            tile = rows_at(j * TILE, TILE)
            rows = rows_at((2 * seq + p.core) * HALF + j * TILE, TILE)
            grad = sum_out[seq, tile, :].astype(F32) + sum_in[seq, tile, :].astype(F32)
            back, gain_rows = norm_pull(grad, hidden[seq, tile, :], gain_mlp)
            whole = og[rows, :].astype(F32) + back
            normed_mlp[rows, :] = whole.astype(BF16)

            @pl.when(p.chip == seq)
            def _():
                grad_hidden[tile, :] = whole
                gain_acc[1:2, :] += jnp.sum(gain_rows, axis=0, keepdims=True)

        mine = normed_mlp.at[block(2 * seq + p.core)]
        pl.semaphore_wait(credits.at[2 + seq], 1)
        go(("low", seq), send(mine, mine, cores, 16 + seq, p.sibling))

        @pl.when(p.chip == seq)
        def _():
            tell(credits.at[4], p.across)

    def release(sems):
        for who, n in [(p.pair, 0)] + [(p.behind(n), n) for n in range(1, p.line)]:
            tell(sems.at[n], who)

    def free_rows(seq):
        gone(("mlp", seq))
        tell(credits.at[2 + seq], p.sibling)

    feed(0)
    both_ff_weights(0)
    ff_weights(0, 2)
    finish_branch(1)
    free_rows(0)
    feed(1)
    of_ff.drain()
    of_rest.drain()
    of_gate.drain()
    release(ff_free)
    gain_acc[...] = jnp.zeros_like(gain_acc)
    scatters = [
        Scatter(
            p,
            ff_grad,
            ff_w,
            pl.ds(n * wide, wide),
            (pair_out.at[5 + n], pair_in.at[5 + n]),
            (line_out.at[n], line_in.at[n]),
            ff_free if n == 0 else None,
        )
        for n in range(3)
    ]
    scatters_attn = [
        Scatter(
            p,
            attn_grad,
            og,
            pl.ds(n * hw, hw),
            (pair_out.at[8 + n], pair_in.at[8 + n]),
            (line_out.at[3 + n], line_in.at[3 + n]),
            attn_free if n == 0 else None,
        )
        for n in range(4)
    ]
    away = far_first(p.line)
    firsts = away or [0]
    both_ff_weights(1, [functools.partial(scatters[n].start, firsts) for n in range(2)])
    ff_weights(1, 2)
    scatters[2].start(firsts)
    if away:
        for n in range(2):
            scatters[n].start([0])
    relays = [(scatters[n], k) for n in range(3) for k in away]
    if len(away) == 3:
        relays = [relays[n] for n in (0, 1, 3, 2, 4, 6, 5, 7, 8)]

    def relay_grad():
        if relays:
            scatter, k = relays.pop(0)
            scatter.relay(k)

    pull(0)
    free_rows(1)

    dqkv = units

    def grad_att(i, heads):
        return units[pl.ds(i * TILE, TILE), rows_at(3 * hw + heads * 128, 128)]

    def turn(seq):
        @pl.loop(0, tiles)
        def _(j):
            rows = rows_at(seq * SEQ_LEN + j * TILE, TILE)
            turned[:, rows_at(j * TILE, TILE)] = k[rows, :].astype(F32).T.astype(BF16)

    def prepare(seq):
        arrived(normed_mlp.at[block(2 * seq + 1 - p.core)], cores, 16 + seq, p.sibling)

        @pl.loop(0, tiles)
        def _(j):
            here = rows_at(j * TILE, TILE)
            rows = rows_at(seq * SEQ_LEN + j * TILE, TILE)
            units[here, out_lanes] = dot_nn(normed_mlp[rows, :], attn_w[:, out_lanes]).astype(BF16)

    def grad_store(seq, heads):
        rows = pl.ds(seq * SEQ_LEN, SEQ_LEN)
        return local(6, dv, value_first_grad.at[rows, rows_at(heads * 128, 128)])

    def m_copy():
        return send(m_sum.at[1 - p.chip], xb.at[p.chip], group, 4, p.across)

    def attend_back(seq, jobs):
        if seq > 0:
            grad_store(0, hw // 128 - 1).wait()

        @pl.loop(0, hw // 128)
        def _(heads):
            @pl.when(heads > 0)
            def _():
                grad_store(seq, heads - 1).wait()

            for i in reversed(range(tiles)):
                for when, job in jobs:
                    if when[1] == i:

                        @pl.when(heads == when[0])
                        def _():
                            job()

                attention_rows_back(
                    seq,
                    heads,
                    i,
                    q,
                    k,
                    v,
                    turned,
                    segments,
                    lse,
                    attended,
                    grad_att,
                    dk,
                    dv,
                    cos,
                    sin,
                    dqkv,
                )

            @pl.loop(0, tiles)
            def _(j):
                here = rows_at(j * TILE, TILE)
                rows = rows_at(seq * SEQ_LEN + j * TILE, TILE)
                u = dk[here, :]
                dqkv[here, rows_at(hw + heads * 128, 128)] = (
                    u * cos[rows, :] - swap_halves(u) * sin[rows, :]
                ).astype(BF16)
                half = 0.5 * dv[here, :]
                dqkv[here, rows_at(2 * hw + heads * 128, 128)] = half.astype(BF16)
                dv[here, :] = half

            grad_store(seq, heads).start()

    def attn_weights(seq, part):
        rows = pl.ds(seq * SEQ_LEN, SEQ_LEN)
        lanes = qkv if seq == 0 else rows_at(part * hw, hw)

        @pl.loop(0, width // TILE)
        def _(j):
            cols = rows_at(j * TILE, TILE)
            made = dot_tn(normed[rows, cols], units[:, lanes])
            if seq > 0:
                made = made + attn_grad[cols, lanes].astype(F32)
            attn_grad[cols, lanes] = made.astype(BF16)

    def out_weights():
        @pl.loop(0, width // TILE)
        def _(j):
            cols = rows_at(j * TILE, TILE)
            attn_grad[cols, out_lanes] = dot_tn(normed_mlp[:, cols], attended[...]).astype(BF16)

    def back_other(seq):
        if seq == 0:
            feed_gone(1)

        @pl.loop(0, HALF // TILE)
        def _(j):
            here = rows_at((1 - p.core) * HALF + j * TILE, TILE)
            half_out[seq, rows_at(j * TILE, TILE), :] = dot_nt(
                dqkv[here, qkv], attn_w[:, qkv]
            ).astype(BF16)

        go(("half", seq), send(half_out.at[seq], half_in.at[seq], cores, 18 + seq, p.sibling))

    gain_sems = (gain_out_sems, gain_in_sems)

    def gain_copies(partners, first):
        return [
            send(gain_acc, gain_in.at[first + n], gain_sems, first + n, who)
            for n, who in enumerate(partners)
        ]

    def exchange(partners, first):
        for copy in gain_copies(partners, first):
            copy.start()

    def add_gains(partners, first):
        for copy in gain_copies(partners, first):
            copy.wait()
        whole = gain_acc[...]
        for n in range(len(partners)):
            whole = whole + gain_in[first + n]
        gain_acc[...] = whole

    def back_own(seq):
        arrived(half_in.at[seq], cores, 18 + seq, p.sibling)
        for j in range(HALF // TILE):
            feed_sum(seq, j).wait_send()

        @pl.loop(0, HALF // TILE)
        def _(j):
            here = rows_at(p.core * HALF + j * TILE, TILE)
            tile = rows_at(j * TILE, TILE)
            rows = rows_at((2 * seq + p.core) * HALF + j * TILE, TILE)
            part = dot_nt(dqkv[here, qkv], attn_w[:, qkv]) + half_in[seq, tile, :].astype(F32)
            sum_out[seq, tile, :] = part.astype(BF16)
            gain_acc[0:1, :] += jnp.sum(part * normed[rows, :].astype(F32), axis=0, keepdims=True)

        if seq == SEQS - 1:
            exchange([p.sibling], 0)

        @pl.when(p.chip != seq)
        def _():
            pl.semaphore_wait(credits.at[4], 1)
            send(sum_out.at[seq], sum_in.at[seq], group, 5, p.across).start()

    turn(0)
    relay_grad()
    prepare(0)
    attend_back(0, [((1, 3), m_copy().start), ((0, 1), relay_grad), ((1, 1), relay_grad)])
    relay_grad()
    back_other(0)
    turn(1)
    attn_weights(0, 0)
    relay_grad()
    pull(1)
    for name in ("og_x", "og_c", "og_f"):
        gone(name)
    release(attn_free)
    back_own(0)
    prepare(1)
    attend_back(1, [((0, 1), relay_grad), ((0, 1), relay_grad), ((1, 3), relay_grad)])
    back_other(1)
    while relays:
        relay_grad()

    @pl.loop(0, 3)
    def _(n):
        attn_weights(1, n)
        for m in range(3):
            pl.when(n == m)(functools.partial(scatters_attn[m].start, firsts))
        pl.when(n == 0)(lambda: back_own(1))

    out_weights()
    add_gains([p.sibling], 0)
    farther = [p.pair] + [p.ahead(n) for n in away] + [p.beyond(n) for n in away]
    exchange(farther, 2)
    scatters_attn[3].start(firsts)
    if away:
        for scatter in (scatters[2], *scatters_attn):
            scatter.start([0])

    arrived(xb.at[1 - p.chip], group, 4, p.across)

    @pl.loop(0, HALF // TILE)
    def _(j):
        tile = rows_at(j * TILE, TILE)
        both = m_sum[p.chip, tile, :].astype(F32) + xb[1 - p.chip, tile, :].astype(F32)
        m_sum[p.chip, tile, :] = (hidden[p.chip, tile, :] + both).astype(BF16)

    stores = []

    def store(src, dst):
        stores.append(fetch(7 + len(stores), src, dst))

    store(m_sum.at[p.chip], block_output)
    for n in range(4):
        for k in away[:-1]:
            scatters_attn[n].relay(k)
        for m in [n - 1] * (n > 0) + [n] * (n == 3):
            for k in away[-1:]:
                scatters_attn[m].relay(k)
        if n < 2:
            scatters[n].finish()
            (gate_sum, up_sum)[n][...] = scatters[n].total().T[:ff, :]
            store((gate_sum, up_sum)[n], (gate_out, up_out_sum)[n])
    add_gains(farther, 2)
    exchange([p.across], 1)
    arrived(sum_in.at[p.chip], group, 5, p.across)

    @pl.loop(0, HALF // TILE)
    def _(j):
        tile = rows_at(j * TILE, TILE)
        grad = sum_out[p.chip, tile, :].astype(F32) + sum_in[p.chip, tile, :].astype(F32)
        back, _ = norm_pull(grad, xb[p.chip, tile, :].astype(F32), gain_attn)
        grad_hidden[tile, :] = grad_hidden[tile, :] + back

    store(grad_hidden, input_grad)
    scatters[2].finish()
    down_sum[...] = scatters[2].total().T[:ff, :]
    store(down_sum, down_out_sum)
    for n, (held, out) in enumerate(
        ((query_sum, query_out), (key_sum, key_out), (value_sum, value_out))
    ):
        scatters_attn[n].finish()
        held[...] = scatters_attn[n].total()
        store(held, out)
    scatters_attn[3].finish()
    out_sum[...] = scatters_attn[3].total().T
    store(out_sum, out_out)
    add_gains([p.across], 1)
    gain_attn_grad[...] = gain_acc[0:1, :] / gain_attn
    gain_mlp_grad[...] = gain_acc[1:2, :]
    store(gain_attn_grad, gain_attn_out)
    store(gain_mlp_grad, gain_mlp_out)
    send(sum_out.at[1 - p.chip], sum_in.at[1 - p.chip], group, 5, p.across).wait_send()
    m_copy().wait_send()
    grad_store(SEQS - 1, hw // 128 - 1).wait()
    for name in list(sent):
        gone(name)
    of_attn.drain()
    of_out.drain()
    for scatter in (*scatters, *scatters_attn):
        scatter.drain()
    for copy in stores:
        copy.wait()


def layer(dp, x, og, vf, segments, positions, gain_a, gain_m, wq, wk, wv, wo, wg, wu, wd):
    rows, width = 4 * x.shape[0], x.shape[1]
    hw, ff, r = vf.shape[1], wg.shape[0], wq.shape[0]
    wide = -(-ff // 256) * 256
    line = dp // 2
    hops = max(line - 1, 1)
    vmem = pl.BlockSpec(memory_space=pltpu.VMEM)
    far = pl.BlockSpec(memory_space=pl.ANY)
    shapes = [
        ((HALF, width), BF16, far),
        ((HALF, width), F32, far),
        ((rows, hw), F32, far),
        ((1, width), F32, far),
        ((r, hw), F32, far),
        ((r, hw), F32, far),
        ((r, hw), F32, far),
        ((hw, r), F32, far),
        ((1, width), F32, far),
        ((ff, r), F32, far),
        ((ff, r), F32, far),
        ((ff, r), F32, far),
    ]
    dma = pltpu.SemaphoreType.DMA
    flag = pltpu.SemaphoreType.REGULAR

    def bf(*shape):
        return pltpu.VMEM(shape, BF16)

    def fl(*shape):
        return pltpu.VMEM(shape, F32)

    scratch = [pltpu.VMEM(shape, kind) for shape, kind, _ in shapes[3:]] + [
        bf(2, HALF, width),
        bf(rows, width),
        bf(rows, width),
        bf(rows, width),
        bf(width, 4 * hw),
        bf(width, 3 * wide),
        bf(rows, hw),
        bf(rows, hw),
        bf(rows, hw),
        bf(rows, hw),
        fl(8, 1, SEQ_LEN),
        fl(2, HALF, width),
        fl(HALF, width),
        bf(SEQ_LEN, 3 * wide),
        bf(width, 3 * wide),
        bf(width, 4 * hw),
        bf(2, HALF, width),
        bf(2, HALF, width),
        bf(2, HALF, width),
        bf(2, HALF, width),
        bf(2, HALF, width),
        bf(hw, SEQ_LEN),
        fl(SEQ_LEN, 128),
        fl(SEQ_LEN, 128),
        fl(rows, 128),
        fl(rows, 128),
        fl(2, width),
        fl(4 + 2 * hops, 2, width),
        dma((18,)),
        dma((10,)),
        dma((10,)),
        dma((20,)),
        dma((20,)),
        dma((5, hops)),
        dma((5, hops)),
        dma((5, hops)),
        dma((5, hops)),
        dma((12, line)),
        dma((12, line)),
        dma((7, line)),
        dma((7, line)),
        dma((4 + 2 * hops,)),
        dma((4 + 2 * hops,)),
        flag((5,)),
        flag((line,)),
        flag((line,)),
    ]
    in_specs = [far] * 3 + [vmem] * 4 + [far] * 3 + [vmem] * 4
    return pl.pallas_call(
        functools.partial(layer_kernel, dp),
        out_shape=[jax.ShapeDtypeStruct(s, t) for s, t, _ in shapes],
        in_specs=in_specs,
        out_specs=[space for _, _, space in shapes],
        scratch_shapes=scratch,
        compiler_params=pltpu.CompilerParams(
            collective_id=0, has_side_effects=True, vmem_limit_bytes=VMEM_LIMIT
        ),
        name="layer",
    )(x, og, vf, segments, positions, gain_a, gain_m, wq, wk, wv, wo, wg, wu, wd)


def chunks(shape):
    parts = 4 if shape[0] % 512 == 0 else 1
    size = shape[0] // parts
    return [pl.ds(n * size, size) for n in range(parts)]


def settle_kernel(count, *refs):
    ins, outs, held, sems = refs[:count], refs[count : 2 * count], refs[2 * count : -1], refs[-1]
    pieces = [(n, rows) for n in range(count) for rows in chunks(ins[n].shape)]
    first, second = [], []
    for m, (n, rows) in enumerate(pieces):
        there = held[n].at[rows]
        first.append(pltpu.make_async_copy(ins[n].at[rows], there, sems.at[2 * m]))
        second.append(pltpu.make_async_copy(there, outs[n].at[rows], sems.at[2 * m + 1]))
    for copy in first:
        copy.start()
    for came, goes in zip(first, second):
        came.wait()
        goes.start()
    for copy in second:
        copy.wait()


def settle(arrays):
    count = len(arrays)
    far = pl.BlockSpec(memory_space=pl.ANY)
    return pl.pallas_call(
        functools.partial(settle_kernel, count),
        out_shape=[jax.ShapeDtypeStruct(a.shape, a.dtype) for a in arrays],
        in_specs=[far] * count,
        out_specs=[far] * count,
        scratch_shapes=[pltpu.VMEM(a.shape, a.dtype) for a in arrays]
        + [pltpu.SemaphoreType.DMA((2 * sum(len(chunks(a.shape)) for a in arrays),))],
        compiler_params=pltpu.CompilerParams(vmem_limit_bytes=VMEM_LIMIT),
        name="settle",
    )(*arrays)


def on_device(
    dp,
    block_input,
    value_first,
    segment_ids,
    positions,
    gain_attn,
    query_weight,
    key_weight,
    value_weight,
    out_weight,
    gain_mlp,
    gate_weight,
    up_weight,
    down_weight,
    output_grad,
):
    outs = layer(
        dp,
        block_input,
        output_grad,
        value_first,
        segment_ids[None, :],
        positions[None, :],
        gain_attn,
        gain_mlp,
        query_weight,
        key_weight,
        value_weight,
        out_weight,
        gate_weight.T,
        up_weight.T,
        down_weight,
    )
    (
        block_output,
        input_grad,
        value_first_grad,
        gain_attn_grad,
        query_sum,
        key_sum,
        value_sum,
        out_sum,
        gain_mlp_grad,
        gate_sum,
        up_sum,
        down_sum,
    ) = settle(outs)
    return (
        block_output,
        input_grad,
        value_first_grad,
        gain_attn_grad[0],
        query_sum,
        key_sum,
        value_sum,
        out_sum,
        gain_mlp_grad[0],
        gate_sum.T,
        up_sum.T,
        down_sum,
    )


def solution(mesh):
    rows = P(("dp", "tensor"), None)
    weight = P("dp", "tensor")
    across = P("tensor", "dp")
    return jax.shard_map(
        functools.partial(on_device, mesh.shape["dp"]),
        mesh=mesh,
        in_specs=(
            rows,
            weight,
            P("dp"),
            P("dp"),
            P(),
            weight,
            weight,
            weight,
            across,
            P(),
            weight,
            weight,
            across,
            rows,
        ),
        out_specs=(
            rows,
            rows,
            weight,
            P(),
            weight,
            weight,
            weight,
            across,
            P(),
            weight,
            weight,
            across,
        ),
        check_vma=False,
    )
```

```python
import functools
import math

import jax
import jax.numpy as jnp
from jax import lax
from jax.experimental import pallas as pl
from jax.experimental.pallas import tpu as pltpu
from jax.sharding import PartitionSpec as P

HEAD_DIM = 64
SEQ_LEN = 1024
SEQS = 2
PIECE = 256
HALF = 512
TILE = 256
EPSILON = 1e-06
ROPE_BASE = 10000.0
MASKED = -1e30
MESH = pl.DeviceIdType.MESH
F32 = jnp.float32
BF16 = jnp.bfloat16
VMEM_LIMIT = 639 * 2**20 // 10


def dot_nn(a, b):
    return lax.dot_general(a, b, (((1,), (0,)), ((), ())), preferred_element_type=F32)


def dot_nt(a, b):
    return lax.dot_general(a, b, (((1,), (1,)), ((), ())), preferred_element_type=F32)


def dot_tn(a, b):
    return lax.dot_general(a, b, (((0,), (0,)), ((), ())), preferred_element_type=F32)


def rows_at(start, size):
    return pl.ds(pl.multiple_of(start, size), size)


def block(b):
    return rows_at(b * HALF, HALF)


class Place:
    def __init__(self, dp):
        self.d = lax.axis_index("dp")
        self.t = lax.axis_index("tensor")
        self.core = lax.rem(self.t, 2)
        self.chip = self.t // 2
        self.line = dp // 2
        self.y = lax.rem(self.d, 2)
        self.z = self.d // 2
        self.sibling = (self.d, self.t + 1 - 2 * self.core)
        self.across = (self.d, lax.rem(self.t + 2, 4))
        self.pair = (self.d + 1 - 2 * self.y, self.t)
        self.up = (self.d + 2, self.t)
        self.down = (self.d - 2, self.t)

    def ahead(self, k):
        return (2 * lax.rem(self.z + k, self.line) + self.y, self.t)

    def beyond(self, k):
        return (2 * lax.rem(self.z + k, self.line) + 1 - self.y, self.t)

    def behind(self, k):
        return (2 * lax.rem(self.z + self.line - k, self.line) + self.y, self.t)

    def greet(self):
        barrier = pltpu.get_barrier_semaphore()
        partners = [self.sibling, self.across, self.pair]
        partners.extend(self.ahead(k) for k in range(1, self.line))
        partners.extend(self.beyond(k) for k in range(1, self.line))
        for who in partners:
            tell(barrier, who)
        self.greeted = len(partners)

    def met(self):
        pl.semaphore_wait(pltpu.get_barrier_semaphore(), self.greeted)


def tell(sem, who):
    pl.semaphore_signal(sem, inc=1, device_id=who, device_id_type=MESH)


def send(src, dst, sems, k, who):
    return pltpu.make_async_remote_copy(
        src_ref=src,
        dst_ref=dst,
        send_sem=sems[0].at[k],
        recv_sem=sems[1].at[k],
        device_id=who,
        device_id_type=MESH,
    )


class Gather:
    def __init__(self, place, full, lanes, rows, spread, up_sems, down_sems, pair_sems):
        self.p, self.full, self.lanes, self.r, self.spread = place, full, lanes, rows, spread
        self.up_sems, self.down_sems, self.pair_sems = up_sems, down_sems, pair_sems

    def shard(self, z, y):
        return self.full.at[rows_at((2 * z + y) * self.r, self.r), self.lanes]

    def load(self, z):
        if self.spread:
            return self.shard(z, self.p.y)
        return self.full.at[rows_at(2 * z * self.r, 2 * self.r), self.lanes]

    def sides(self, k):
        p = self.p
        return (
            (p.z - k, p.z >= k, self.up_sems, p.z + 1 < p.line, p.up),
            (p.z + k, p.z + k < p.line, self.down_sems, p.z >= 1, p.down),
        )

    def start_pair(self):
        p = self.p
        here = self.shard(p.z, p.y)
        send(here, here, self.pair_sems, p.z, p.pair).start()

    def start_line(self):
        p = self.p
        if not self.spread:
            there = self.shard(p.z, 1 - p.y)
            send(there, there, self.pair_sems, p.z, p.pair).wait_recv()
        here = self.load(p.z)
        for _, _, sems, onward, to in self.sides(0):

            @pl.when(onward)
            def _():
                send(here, here, sems, 0, to).start()

    def relay(self, k):
        p = self.p
        for z, exists, sems, onward, to in self.sides(k):

            @pl.when(exists)
            def _():
                here = self.load(z)
                send(here, here, sems, k - 1, to).wait_recv()

                @pl.when(onward)
                def _():
                    send(here, here, sems, k, to).start()

                if self.spread:
                    send(here, here, self.pair_sems, z, p.pair).start()

    def finish(self):
        p = self.p
        if self.spread:
            for z in range(p.line):
                there = self.shard(z, 1 - p.y)
                send(there, there, self.pair_sems, z, p.pair).wait_recv()

    def drain(self):
        p = self.p
        for z in range(p.line) if self.spread else (p.z,):
            here = self.shard(z, p.y)
            send(here, here, self.pair_sems, z, p.pair).wait_send()
        for k in range(p.line - 1):
            for z, exists, sems, onward, to in self.sides(k):

                @pl.when(jnp.logical_and(exists, onward))
                def _():
                    here = self.load(z)
                    send(here, here, sems, k, to).wait_send()


def far_first(n):
    if n < 4:
        return list(range(1, n))
    last = [2, n - 2] if n > 4 else [2]
    return [1, n - 1, *range(3, n - 2), *last]


class Scatter:
    def __init__(self, place, full, into, lanes, pair_sems, line_sems, free):
        self.p, self.full, self.into, self.lanes = place, full, into, lanes
        self.pair_sems, self.line_sems = pair_sems, line_sems
        self.free = free
        self.r = full.shape[0] // (2 * place.line)

    def rows(self, k, y):
        z = lax.rem(self.p.z + k, self.p.line)
        return rows_at((2 * z + y) * self.r, self.r)

    def pair_in(self, k):
        return self.into.at[pl.ds(k * self.r, self.r), self.lanes]

    def line_in(self, k):
        return self.into.at[pl.ds((self.p.line + k - 1) * self.r, self.r), self.lanes]

    def swap(self, k):
        theirs = self.full.at[self.rows(k, 1 - self.p.y), self.lanes]
        return send(theirs, self.pair_in(k), self.pair_sems, k, self.p.pair)

    def start(self, steps):
        if self.free is not None and (steps[0] == 1 or self.p.line == 1):
            pl.semaphore_wait(self.free.at[0], 1)
        for k in steps:
            self.swap(k).start()

    def relay(self, k):
        p = self.p
        n = p.line
        there = self.pair_in(k)
        send(there, there, self.pair_sems, k, p.pair).wait_recv()
        self.join(k, there)
        if self.free is not None and k == 1:
            for m in range(1, n):
                pl.semaphore_wait(self.free.at[m], 1)
        if n >= 4 and k in (2, n - 2):
            helping = jnp.logical_or(
                jnp.logical_and(p.z == 1, k == n - 2), jnp.logical_and(p.z == n - 2, k == 2)
            )

            @pl.when(helping)
            def _():
                self.helped().wait_recv()
                self.join(k, self.line_in(n))

        if n >= 4 and k in (1, n - 1):
            from_end = p.z == (0 if k == n - 1 else n - 1)

            @pl.when(from_end)
            def _():
                self.helped(k).start()

            @pl.when(jnp.logical_not(from_end))
            def _():
                self.onward(k).start()
        else:
            self.onward(k).start()

    def join(self, k, came):
        mine = self.full.at[self.rows(k, self.p.y), self.lanes]
        step = min(self.r, 32)

        @pl.loop(0, self.r // step)
        def _(j):
            rows = rows_at(j * step, step)
            mine[rows, :] = (mine[rows, :].astype(F32) + came[rows, :].astype(F32)).astype(BF16)

    def helped(self, k=1):
        p = self.p
        near = jnp.where(p.z == 0, 1, p.line - 2)
        mine = self.full.at[self.rows(k, p.y), self.lanes]
        return pltpu.make_async_remote_copy(
            src_ref=mine,
            dst_ref=self.line_in(p.line),
            send_sem=self.line_sems[0].at[k - 1],
            recv_sem=self.line_sems[1].at[p.line - 1],
            device_id=(2 * near + p.y, p.t),
            device_id_type=MESH,
        )

    def onward(self, k):
        p = self.p
        mine = self.full.at[self.rows(k, p.y), self.lanes]
        return send(mine, self.line_in(k), self.line_sems, k - 1, p.ahead(k))

    def merged(self, k):
        n = self.p.line
        if n < 4 or k not in (1, n - 1):
            return None
        return self.p.z == (n - 1 if k == n - 1 else 0)

    def finish(self):
        p = self.p
        there = self.pair_in(0)
        send(there, there, self.pair_sems, 0, p.pair).wait_recv()
        for k in range(1, p.line):
            there = self.line_in(k)
            merged = self.merged(k)
            if merged is None:
                send(there, there, self.line_sems, k - 1, p.pair).wait_recv()
            else:

                @pl.when(jnp.logical_not(merged))
                def _():
                    send(there, there, self.line_sems, k - 1, p.pair).wait_recv()

    def total(self):
        whole = self.full[self.rows(0, self.p.y), self.lanes].astype(F32)
        whole = whole + self.pair_in(0)[...].astype(F32)
        for k in range(1, self.p.line):
            came = self.line_in(k)[...].astype(F32)
            merged = self.merged(k)
            if merged is not None:
                came = jnp.where(merged, jnp.zeros_like(came), came)
            whole = whole + came
        return whole

    def drain(self):
        for k in range(self.p.line):
            self.swap(k).wait_send()
        for k in range(1, self.p.line):
            self.onward(k).wait_send()


def swap_halves(u):
    lane = lax.broadcasted_iota(jnp.int32, u.shape, 1)
    low = lax.rem(lane, HEAD_DIM) < HEAD_DIM // 2
    return jnp.where(low, pltpu.roll(u, 96, 1), pltpu.roll(u, 32, 1))


def norm_factor(u):
    return lax.rsqrt(jnp.mean(u * u, axis=-1, keepdims=True) + EPSILON)


def norm_pull(grad, u, gain):
    r = norm_factor(u)
    scaled = grad * gain
    back = r * scaled - u * (r * r * r) * jnp.mean(scaled * u, axis=-1, keepdims=True)
    return back, grad * u * r


def visible(segments):
    key = lax.broadcasted_iota(jnp.int32, (TILE, TILE), 0)
    query = lax.broadcasted_iota(jnp.int32, (TILE, TILE), 1)
    return jnp.logical_or(key <= query, segments > 0)


def attention_rows(seq, heads, i, q, k, vt, segments, attended, lse):
    lane = lax.broadcasted_iota(jnp.int32, (TILE, 128), 1)
    lanes = rows_at(heads * 128, 128)
    rows = pl.ds(seq * SEQ_LEN + i * TILE, TILE)
    q2 = q[rows, lanes]
    shown = visible(segments[:, rows])
    sides = []
    for a in range(2):
        qa = jnp.where((lane < HEAD_DIM) == (a == 0), q2, jnp.zeros_like(q2))
        vta = rows_at((heads * 2 + a) * HEAD_DIM, HEAD_DIM)
        score = jnp.where(shown, dot_nt(k[rows, lanes], qa), MASKED)
        top = jnp.max(score, axis=0, keepdims=True)
        if i > 0:
            before = dot_nt(k[pl.ds(seq * SEQ_LEN, i * TILE), lanes], qa)
            top = jnp.maximum(top, jnp.max(before, axis=0, keepdims=True))
        weight = jnp.exp(score - top)
        total = jnp.sum(weight, axis=0, keepdims=True)
        out = dot_nn(vt[vta, pl.ds(i * TILE, TILE)], weight.astype(BF16))
        if i > 0:
            weight = jnp.exp(before - top)
            total = total + jnp.sum(weight, axis=0, keepdims=True)
            out = out + dot_nn(vt[vta, pl.ds(0, i * TILE)], weight.astype(BF16))
        sides.append(out * (1.0 / total))
        lse[seq * 4 + heads * 2 + a, :, pl.ds(i * TILE, TILE)] = top + jnp.log(total)
    attended[rows, lanes] = jnp.concatenate(sides, axis=0).T.astype(BF16)


def attention_rows_back(
    seq, heads, i, q, k, v, kt, segments, lse, attended, grad_att, dk, dv, cos, sin, dqkv
):
    lane = lax.broadcasted_iota(jnp.int32, (TILE, 128), 1)
    lanes = rows_at(heads * 128, 128)
    local = pl.ds(i * TILE, TILE)
    rows = pl.ds(seq * SEQ_LEN + i * TILE, TILE)
    first = i == SEQ_LEN // TILE - 1
    q2, g2 = q[rows, lanes], grad_att(i, heads)
    shown = visible(segments[:, rows])
    products = (g2.astype(F32) * attended[rows, lanes].astype(F32)).T
    parts = [(i * TILE, TILE, True)]
    if i > 0:
        parts.append((0, i * TILE, False))
    sides = [None, None]
    for start, size, diagonal in parts:
        keys = pl.ds(seq * SEQ_LEN + start, size)
        here = pl.ds(start, size)
        dk_part, dv_part = 0.0, 0.0
        for a in range(2):
            mine = (lane < HEAD_DIM) == (a == 0)
            qa = jnp.where(mine, q2, jnp.zeros_like(q2))
            ga = jnp.where(mine, g2, jnp.zeros_like(g2))
            delta = jnp.sum(products[a * HEAD_DIM : (a + 1) * HEAD_DIM], axis=0, keepdims=True)
            stat = lse[seq * 4 + heads * 2 + a, :, local]
            score = dot_nt(k[keys, lanes], qa)
            if diagonal:
                score = jnp.where(shown, score, MASKED)
            prob = jnp.exp(score - stat)
            grad_prob = dot_nt(v[keys, lanes], ga)
            grad_score = (prob * (grad_prob - delta)).astype(BF16)
            dv_part = dv_part + dot_nn(prob.astype(BF16), ga)
            dk_part = dk_part + dot_nn(grad_score, qa)
            side = dot_nn(kt[rows_at((heads * 2 + a) * HEAD_DIM, HEAD_DIM), here], grad_score)
            sides[a] = side if sides[a] is None else sides[a] + side
        if first:
            dk[here, :] = dk_part
            dv[here, :] = dv_part
        else:
            dk[here, :] += dk_part
            dv[here, :] += dv_part
    dq = jnp.concatenate(sides, axis=0).T * HEAD_DIM**-0.5
    dqkv[local, lanes] = (dq * cos[rows, :] - swap_halves(dq) * sin[rows, :]).astype(BF16)


def layer_kernel(
    dp,
    x_in,
    og_in,
    value_first,
    segments,
    positions,
    gain_attn_in,
    gain_mlp_in,
    query_shard,
    key_shard,
    value_shard,
    out_shard,
    gate_shard,
    up_shard,
    down_shard,
    block_output,
    input_grad,
    value_first_grad,
    gain_attn_out,
    query_out,
    key_out,
    value_out,
    out_out,
    gain_mlp_out,
    gate_out,
    up_out_sum,
    down_out_sum,
    gain_attn_grad,
    query_sum,
    key_sum,
    value_sum,
    out_sum,
    gain_mlp_grad,
    gate_sum,
    up_sum,
    down_sum,
    xb,
    normed,
    normed_mlp,
    og,
    attn_w,
    ff_w,
    q,
    k,
    v,
    attended,
    lse,
    hidden,
    grad_hidden,
    units,
    ff_grad,
    attn_grad,
    half_out,
    half_in,
    sum_out,
    sum_in,
    m_sum,
    turned,
    dk,
    dv,
    cos,
    sin,
    gain_acc,
    gain_in,
    local_sems,
    group_out,
    group_in,
    core_out,
    core_in,
    up_out,
    up_in,
    down_out,
    down_in,
    pair_out,
    pair_in,
    line_out,
    line_in,
    gain_out_sems,
    gain_in_sems,
    credits,
    ff_free,
    attn_free,
):
    p = Place(dp)
    group, cores = (group_out, group_in), (core_out, core_in)
    rows_r, hw = query_shard.shape
    ff = gate_shard.shape[0]
    wide = ff_w.shape[1] // 3
    width = x_in.shape[1]
    tiles = SEQ_LEN // TILE
    slot = rows_at(p.d * rows_r, rows_r)
    qkv, out_lanes = slice(0, 3 * hw), slice(3 * hw, 4 * hw)
    middle = wide + 5 * wide // 6 // 128 * 128
    sent = {}

    def go(name, copy):
        copy.start()
        sent[name] = copy

    def gone(name):
        sent.pop(name).wait_send()

    def arrived(there, sems, n, who):
        send(there, there, sems, n, who).wait_recv()

    def local(n, src, dst):
        return pltpu.make_async_copy(src, dst, local_sems.at[n])

    def fetch(n, src, dst):
        copy = local(n, src, dst)
        copy.start()
        return copy

    p.greet()
    x_copy = fetch(0, x_in, xb.at[p.chip])
    qkv_copies = [
        fetch(1 + n, shard, attn_w.at[slot, pl.ds(n * hw, hw)])
        for n, shard in enumerate((query_shard, key_shard, value_shard))
    ]
    og_copy = fetch(4, og_in, og.at[block(p.t)])
    vf_copy = fetch(5, value_first, attended)
    attn_w[slot, out_lanes] = out_shard[...].astype(F32).T.astype(BF16)
    p.met()
    x_copy.wait()
    go("x", send(xb.at[p.chip], xb.at[p.chip], group, 0, p.across))
    gathers = [
        Gather(
            p,
            full,
            pl.ds(first, lanes),
            rows_r,
            spread,
            (up_out.at[n], up_in.at[n]),
            (down_out.at[n], down_in.at[n]),
            (pair_out.at[n], pair_in.at[n]),
        )
        for n, (full, first, lanes, spread) in enumerate(
            (
                (attn_w, 0, 3 * hw, True),
                (attn_w, 3 * hw, hw, True),
                (ff_w, wide // 2, middle - wide // 2, True),
                (ff_w, middle, 3 * wide - middle, True),
                (ff_w, 0, wide // 2, False),
            )
        )
    ]
    of_attn, of_out, of_ff, of_rest, of_gate = gathers
    for copy in qkv_copies:
        copy.wait()
    of_attn.start_line()
    of_attn.start_pair()
    of_out.start_line()
    of_out.start_pair()
    gain_attn = gain_attn_in[...].astype(F32).reshape(1, width)
    gain_mlp = gain_mlp_in[...].astype(F32).reshape(1, width)
    other = lax.rem(p.t + 2, 4)
    sib = p.t + 1 - 2 * p.core
    sib_other = lax.rem(sib + 2, 4)

    def norm_block(b, chip, n):
        @pl.loop(0, HALF // TILE)
        def _(j):
            u = xb[chip, rows_at(j * TILE, TILE), :].astype(F32)
            normed[rows_at(b * HALF + j * TILE, TILE), :] = (
                u * norm_factor(u) * gain_attn
            ).astype(BF16)

        here = normed.at[block(b)]
        go(("normed", n), send(here, here, cores, n, p.sibling))

    norm_block(p.t, p.chip, 0)
    for n, shard in enumerate((gate_shard, up_shard, down_shard)):
        flat = shard[...].astype(F32)
        if wide > ff:
            flat = jnp.concatenate([flat, jnp.zeros((wide - ff, rows_r), F32)], axis=0)
        ff_w[slot, n * wide : (n + 1) * wide] = flat.T.astype(BF16)
    of_gate.start_pair()
    if p.line > 1:
        of_attn.relay(1)
        of_out.relay(1)

    @pl.loop(0, SEQS * tiles)
    def _(j):
        rows = rows_at(j * TILE, TILE)
        lane = lax.broadcasted_iota(jnp.int32, (TILE, 128), 1)
        half = HEAD_DIM // 2
        power = lax.rem(lane[0:1, :], half).astype(F32) * (-2.0 / HEAD_DIM)
        frequency = jnp.exp(power * math.log(ROPE_BASE))
        place = jnp.broadcast_to(positions[:, rows].astype(F32), (128, TILE)).T
        angle = place * frequency
        cos[rows, :] = jnp.cos(angle)
        sine = jnp.sin(angle)
        sin[rows, :] = jnp.where(lax.rem(lane, HEAD_DIM) < half, -sine, sine)

    og_copy.wait()
    own_rows = og.at[block(p.t)]
    go("og_c", send(own_rows, own_rows, cores, 2, p.sibling))
    for n in range(2, p.line):
        of_attn.relay(n)
        of_out.relay(n)
        if n == 2:
            go("og_x", send(own_rows, own_rows, group, 1, p.across))
    if p.line < 3:
        go("og_x", send(own_rows, own_rows, group, 1, p.across))
    of_ff.start_line()
    of_rest.start_line()
    of_gate.start_line()
    arrived(xb.at[1 - p.chip], group, 0, p.across)
    norm_block(other, 1 - p.chip, 1)
    of_ff.start_pair()
    of_rest.start_pair()
    of_attn.finish()
    arrived(normed.at[block(sib)], cores, 0, p.sibling)
    arrived(normed.at[block(sib_other)], cores, 1, p.sibling)
    vf_copy.wait()

    def project(seq):
        @pl.loop(0, tiles)
        def _(j):
            rows = rows_at(seq * SEQ_LEN + j * TILE, TILE)
            made = dot_nn(normed[rows, :], attn_w[:, qkv])
            c, s = cos[rows, :], sin[rows, :]
            for n in range(hw // 128):
                lanes = slice(n * 128, (n + 1) * 128)
                u = made[:, n * 128 : (n + 1) * 128]
                q[rows, lanes] = ((u * c + swap_halves(u) * s) * HEAD_DIM**-0.5).astype(BF16)
                u = made[:, hw + n * 128 : hw + (n + 1) * 128]
                k[rows, lanes] = (u * c + swap_halves(u) * s).astype(BF16)
            mixed = 0.5 * made[:, 2 * hw :] + 0.5 * attended[rows, :].astype(F32)
            v[rows, :] = mixed.astype(BF16)
            turned[:, rows_at(j * TILE, TILE)] = mixed.T.astype(BF16)

    def attend(seq, between):
        @pl.loop(0, hw // 128)
        def _(heads):
            @pl.when(heads == hw // 128 - 1)
            def _():
                for relay in between:
                    relay()

            for i in range(tiles):
                attention_rows(seq, heads, i, q, k, turned, segments, attended, lse)

    def branch_other(seq):
        @pl.loop(0, HALF // TILE)
        def _(j):
            rows = rows_at(seq * SEQ_LEN + (1 - p.core) * HALF + j * TILE, TILE)
            half_out[seq, rows_at(j * TILE, TILE), :] = dot_nt(
                attended[rows, :], attn_w[:, out_lanes]
            ).astype(BF16)

        go(("half", seq), send(half_out.at[seq], half_in.at[seq], cores, 4 + seq, p.sibling))

    def branch_own(seq):
        arrived(half_in.at[seq], cores, 4 + seq, p.sibling)

        @pl.loop(0, HALF // TILE)
        def _(j):
            rows = rows_at(seq * SEQ_LEN + p.core * HALF + j * TILE, TILE)
            tile = rows_at(j * TILE, TILE)
            part = dot_nt(attended[rows, :], attn_w[:, out_lanes])
            sum_out[seq, tile, :] = (part + half_in[seq, tile, :].astype(F32)).astype(BF16)

        go(("sum", seq), send(sum_out.at[seq], sum_in.at[seq], group, 2 + seq, p.across))

    def finish_branch(seq):
        arrived(sum_in.at[seq], group, 2 + seq, p.across)

        @pl.loop(0, HALF // TILE)
        def _(j):
            tile = rows_at(j * TILE, TILE)
            both = sum_out[seq, tile, :].astype(F32) + sum_in[seq, tile, :].astype(F32)
            u = xb[seq, tile, :].astype(F32) + both
            hidden[seq, tile, :] = u
            normed_mlp[rows_at((2 * seq + p.core) * HALF + j * TILE, TILE), :] = (
                u * norm_factor(u) * gain_mlp
            ).astype(BF16)

        mine = normed_mlp.at[block(2 * seq + p.core)]
        go(("mlp", seq), send(mine, mine, cores, 6 + seq, p.sibling))
        tell(credits.at[seq], p.across)

    def in_steps(gather):
        steps = list(range(1, p.line))

        def relay():
            if steps:
                gather.relay(steps.pop(0))

        return relay, steps

    relay_ff, steps = in_steps(of_ff)
    relay_rest, _ = in_steps(of_rest)
    relay_gate, left = in_steps(of_gate)
    project(0)
    attend(0, [relay_ff])
    relay_rest()
    of_out.finish()
    branch_other(0)
    project(1)
    branch_own(0)
    relay_gate()
    relay_ff()
    attend(1, [relay_rest])
    relay_gate()
    branch_other(1)
    branch_own(1)
    relay_ff()
    relay_rest()
    arrived(og.at[block(other)], group, 1, p.across)
    there = og.at[block(other)]
    go("og_f", send(there, there, cores, 3, p.sibling))
    while steps or left:
        relay_ff()
        relay_rest()
        relay_gate()
    finish_branch(0)
    arrived(og.at[block(sib)], cores, 2, p.sibling)
    arrived(og.at[block(sib_other)], cores, 3, p.sibling)
    of_ff.finish()
    of_rest.finish()

    def feed_copy(seq, n, j):
        tile = rows_at(j * TILE, TILE)
        there = half_in.at[n, tile]
        return send(half_out.at[n, tile], there, cores, 8 + seq * 4 + n * 2 + j, p.sibling)

    def feed_sum(seq, j):
        tile = rows_at(j * TILE, TILE)
        return send(sum_out.at[seq, tile], sum_in.at[seq, tile], group, 6 + seq * 2 + j, p.across)

    def feed_gone(seq):
        for n in range(2):
            for j in range(HALF // TILE):
                feed_copy(seq, n, j).wait_send()

    def feed(seq):
        arrived(normed_mlp.at[block(2 * seq + 1 - p.core)], cores, 6 + seq, p.sibling)
        if seq == 0:
            for n in range(2):
                gone(("half", n))
        else:
            feed_gone(0)
        gone(("sum", seq))
        pl.semaphore_wait(credits.at[seq], 1)

        @pl.loop(0, tiles)
        def _(step):
            j = lax.rem(step, HALF // TILE)
            others = step < HALF // TILE
            h = jnp.where(others, 1 - p.core, p.core)
            here = rows_at(h * HALF + j * TILE, TILE)
            rows = rows_at(seq * SEQ_LEN + h * HALF + j * TILE, TILE)
            tile = rows_at(j * TILE, TILE)
            for n in range(wide // 256):
                lanes = [slice(m * wide + n * 256, m * wide + (n + 1) * 256) for m in range(3)]
                gate = dot_nn(normed_mlp[rows, :], ff_w[:, lanes[0]])
                up = dot_nn(normed_mlp[rows, :], ff_w[:, lanes[1]])
                grad_act = dot_nn(og[rows, :], ff_w[:, lanes[2]])
                sig = 1.0 / (1.0 + jnp.exp(-gate))
                swish = gate * sig
                units[here, lanes[0]] = (
                    grad_act * up * sig * (1.0 + gate * (1.0 - sig))
                ).astype(BF16)
                units[here, lanes[1]] = (grad_act * swish).astype(BF16)
                units[here, lanes[2]] = (swish * up).astype(BF16)
            down = dot_nt(units[here, 2 * wide :], ff_w[:, 2 * wide :])
            back = dot_nt(units[here, : 2 * wide], ff_w[:, : 2 * wide])

            @pl.when(others)
            def _():
                half_out[0, tile, :] = back.astype(BF16)
                half_out[1, tile, :] = down.astype(BF16)
                for n in range(2):
                    feed_copy(seq, n, j).start()

            @pl.when(jnp.logical_not(others))
            def _():
                for n in range(2):
                    feed_copy(seq, n, j).wait_recv()
                sum_out[seq, tile, :] = (back + half_in[0, tile, :].astype(F32)).astype(BF16)
                m_sum[seq, tile, :] = (down + half_in[1, tile, :].astype(F32)).astype(BF16)
                feed_sum(seq, j).start()

    def ff_weights(seq, n):
        rows = pl.ds(seq * SEQ_LEN, SEQ_LEN)
        left = og if isinstance(n, int) else normed_mlp
        lanes = pl.ds(pl.multiple_of(n * wide, 128), wide)

        @pl.loop(0, width // TILE)
        def _(j):
            cols = rows_at(j * TILE, TILE)
            part = dot_tn(left[rows, cols], units[:, lanes])
            if seq > 0:
                part = part + ff_grad[cols, lanes].astype(F32)
            ff_grad[cols, lanes] = part.astype(BF16)

    def both_ff_weights(seq, then=()):
        @pl.loop(0, 2)
        def _(n):
            ff_weights(seq, n)
            for m, start in enumerate(then):
                pl.when(n == m)(start)

    def pull(seq):
        for j in range(HALF // TILE):
            feed_sum(seq, j).wait_recv()

        @pl.loop(0, HALF // TILE)
        def _(j):
            tile = rows_at(j * TILE, TILE)
            rows = rows_at((2 * seq + p.core) * HALF + j * TILE, TILE)
            grad = sum_out[seq, tile, :].astype(F32) + sum_in[seq, tile, :].astype(F32)
            back, gain_rows = norm_pull(grad, hidden[seq, tile, :], gain_mlp)
            whole = og[rows, :].astype(F32) + back
            normed_mlp[rows, :] = whole.astype(BF16)

            @pl.when(p.chip == seq)
            def _():
                grad_hidden[tile, :] = whole
                gain_acc[1:2, :] += jnp.sum(gain_rows, axis=0, keepdims=True)

        mine = normed_mlp.at[block(2 * seq + p.core)]
        pl.semaphore_wait(credits.at[2 + seq], 1)
        go(("low", seq), send(mine, mine, cores, 16 + seq, p.sibling))

        @pl.when(p.chip == seq)
        def _():
            tell(credits.at[4], p.across)

    def release(sems):
        for who, n in [(p.pair, 0)] + [(p.behind(n), n) for n in range(1, p.line)]:
            tell(sems.at[n], who)

    def free_rows(seq):
        gone(("mlp", seq))
        tell(credits.at[2 + seq], p.sibling)

    feed(0)
    both_ff_weights(0)
    ff_weights(0, 2)
    finish_branch(1)
    free_rows(0)
    feed(1)
    of_ff.drain()
    of_rest.drain()
    of_gate.drain()
    release(ff_free)
    gain_acc[...] = jnp.zeros_like(gain_acc)
    scatters = [
        Scatter(
            p,
            ff_grad,
            ff_w,
            pl.ds(n * wide, wide),
            (pair_out.at[5 + n], pair_in.at[5 + n]),
            (line_out.at[n], line_in.at[n]),
            ff_free if n == 0 else None,
        )
        for n in range(3)
    ]
    scatters_attn = [
        Scatter(
            p,
            attn_grad,
            og,
            pl.ds(n * hw, hw),
            (pair_out.at[8 + n], pair_in.at[8 + n]),
            (line_out.at[3 + n], line_in.at[3 + n]),
            attn_free if n == 0 else None,
        )
        for n in range(4)
    ]
    away = far_first(p.line)
    firsts = away or [0]
    both_ff_weights(1, [functools.partial(scatters[n].start, firsts) for n in range(2)])
    ff_weights(1, 2)
    scatters[2].start(firsts)
    if away:
        for n in range(3):
            scatters[n].start([0])
    relays = [(scatters[n], k) for n in range(3) for k in away]
    if len(away) == 3:
        relays = [relays[n] for n in (0, 1, 3, 2, 4, 6, 5, 7, 8)]

    def relay_grad():
        if relays:
            scatter, k = relays.pop(0)
            scatter.relay(k)

    pull(0)
    free_rows(1)

    dqkv = units

    def grad_att(i, heads):
        return units[pl.ds(i * TILE, TILE), rows_at(3 * hw + heads * 128, 128)]

    def turn(seq):
        @pl.loop(0, tiles)
        def _(j):
            rows = rows_at(seq * SEQ_LEN + j * TILE, TILE)
            turned[:, rows_at(j * TILE, TILE)] = k[rows, :].astype(F32).T.astype(BF16)

    def prepare(seq):
        arrived(normed_mlp.at[block(2 * seq + 1 - p.core)], cores, 16 + seq, p.sibling)

        @pl.loop(0, tiles)
        def _(j):
            here = rows_at(j * TILE, TILE)
            rows = rows_at(seq * SEQ_LEN + j * TILE, TILE)
            units[here, out_lanes] = dot_nn(normed_mlp[rows, :], attn_w[:, out_lanes]).astype(BF16)

    def grad_store(seq, heads):
        rows = pl.ds(seq * SEQ_LEN, SEQ_LEN)
        return local(6, dv, value_first_grad.at[rows, rows_at(heads * 128, 128)])

    def m_copy():
        return send(m_sum.at[1 - p.chip], xb.at[p.chip], group, 4, p.across)

    def attend_back(seq, jobs):
        if seq > 0:
            grad_store(0, hw // 128 - 1).wait()

        @pl.loop(0, hw // 128)
        def _(heads):
            @pl.when(heads > 0)
            def _():
                grad_store(seq, heads - 1).wait()

            for i in reversed(range(tiles)):
                for when, job in jobs:
                    if when[1] == i:

                        @pl.when(heads == when[0])
                        def _():
                            job()

                attention_rows_back(
                    seq,
                    heads,
                    i,
                    q,
                    k,
                    v,
                    turned,
                    segments,
                    lse,
                    attended,
                    grad_att,
                    dk,
                    dv,
                    cos,
                    sin,
                    dqkv,
                )

            @pl.loop(0, tiles)
            def _(j):
                here = rows_at(j * TILE, TILE)
                rows = rows_at(seq * SEQ_LEN + j * TILE, TILE)
                u = dk[here, :]
                dqkv[here, rows_at(hw + heads * 128, 128)] = (
                    u * cos[rows, :] - swap_halves(u) * sin[rows, :]
                ).astype(BF16)
                half = 0.5 * dv[here, :]
                dqkv[here, rows_at(2 * hw + heads * 128, 128)] = half.astype(BF16)
                dv[here, :] = half

            grad_store(seq, heads).start()

    def attn_weights(seq, part):
        rows = pl.ds(seq * SEQ_LEN, SEQ_LEN)
        lanes = qkv if seq == 0 else rows_at(part * hw, hw)

        @pl.loop(0, width // TILE)
        def _(j):
            cols = rows_at(j * TILE, TILE)
            made = dot_tn(normed[rows, cols], units[:, lanes])
            if seq > 0:
                made = made + attn_grad[cols, lanes].astype(F32)
            attn_grad[cols, lanes] = made.astype(BF16)

    def out_weights():
        @pl.loop(0, width // TILE)
        def _(j):
            cols = rows_at(j * TILE, TILE)
            attn_grad[cols, out_lanes] = dot_tn(normed_mlp[:, cols], attended[...]).astype(BF16)

    def back_copy(seq, j):
        tile = rows_at(j * TILE, TILE)
        there = half_in.at[seq, tile]
        return send(half_out.at[seq, tile], there, cores, 18 + seq * 2 + j, p.sibling)

    def back_sum(seq, j):
        tile = rows_at(j * TILE, TILE)
        return send(sum_out.at[seq, tile], sum_in.at[seq, tile], group, 10 + j, p.across)

    def back_other(seq):
        if seq == 0:
            feed_gone(1)

        @pl.loop(0, HALF // TILE)
        def _(j):
            here = rows_at((1 - p.core) * HALF + j * TILE, TILE)
            half_out[seq, rows_at(j * TILE, TILE), :] = dot_nt(
                dqkv[here, qkv], attn_w[:, qkv]
            ).astype(BF16)
            back_copy(seq, j).start()

    gain_sems = (gain_out_sems, gain_in_sems)

    def gain_copies(partners, first):
        return [
            send(gain_acc, gain_in.at[first + n], gain_sems, first + n, who)
            for n, who in enumerate(partners)
        ]

    def exchange(partners, first):
        for copy in gain_copies(partners, first):
            copy.start()

    def add_gains(partners, first):
        for copy in gain_copies(partners, first):
            copy.wait()
        whole = gain_acc[...]
        for n in range(len(partners)):
            whole = whole + gain_in[first + n]
        gain_acc[...] = whole

    def back_own(seq):
        for j in range(HALF // TILE):
            feed_sum(seq, j).wait_send()

        @pl.when(p.chip != seq)
        def _():
            pl.semaphore_wait(credits.at[4], 1)

        @pl.loop(0, HALF // TILE)
        def _(j):
            here = rows_at(p.core * HALF + j * TILE, TILE)
            tile = rows_at(j * TILE, TILE)
            rows = rows_at((2 * seq + p.core) * HALF + j * TILE, TILE)
            part = dot_nt(dqkv[here, qkv], attn_w[:, qkv])
            back_copy(seq, j).wait_recv()
            part = part + half_in[seq, tile, :].astype(F32)
            sum_out[seq, tile, :] = part.astype(BF16)
            gain_acc[0:1, :] += jnp.sum(part * normed[rows, :].astype(F32), axis=0, keepdims=True)

            @pl.when(p.chip != seq)
            def _():
                back_sum(seq, j).start()

        if seq == SEQS - 1:
            exchange([p.sibling], 0)

    turn(0)
    relay_grad()
    prepare(0)
    attend_back(0, [((1, 3), m_copy().start), ((0, 1), relay_grad), ((1, 1), relay_grad)])
    relay_grad()
    back_other(0)
    turn(1)
    attn_weights(0, 0)
    relay_grad()
    pull(1)
    for name in ("og_x", "og_c", "og_f"):
        gone(name)
    release(attn_free)
    back_own(0)
    prepare(1)
    attend_back(1, [((0, 1), relay_grad), ((0, 1), relay_grad), ((1, 3), relay_grad)])
    back_other(1)
    while relays:
        relay_grad()

    @pl.loop(0, 3)
    def _(n):
        attn_weights(1, n)
        for m in range(3):
            pl.when(n == m)(functools.partial(scatters_attn[m].start, firsts))
        pl.when(n == 0)(lambda: back_own(1))

    out_weights()
    add_gains([p.sibling], 0)
    farther = [p.pair] + [p.ahead(n) for n in away] + [p.beyond(n) for n in away]
    exchange(farther, 2)
    scatters_attn[3].start(firsts)
    if away:
        for scatter in scatters_attn:
            scatter.start([0])

    arrived(xb.at[1 - p.chip], group, 4, p.across)

    @pl.loop(0, HALF // TILE)
    def _(j):
        tile = rows_at(j * TILE, TILE)
        both = m_sum[p.chip, tile, :].astype(F32) + xb[1 - p.chip, tile, :].astype(F32)
        m_sum[p.chip, tile, :] = (hidden[p.chip, tile, :] + both).astype(BF16)

    stores = []

    def store(src, dst):
        stores.append(fetch(7 + len(stores), src, dst))

    store(m_sum.at[p.chip], block_output)
    for n in range(4):
        for k in away[:-1]:
            scatters_attn[n].relay(k)
        for m in [n - 1] * (n > 0) + [n] * (n == 3):
            for k in away[-1:]:
                scatters_attn[m].relay(k)
        if n < 2:
            scatters[n].finish()
            (gate_sum, up_sum)[n][...] = scatters[n].total().T[:ff, :]
            store((gate_sum, up_sum)[n], (gate_out, up_out_sum)[n])
    add_gains(farther, 2)
    exchange([p.across], 1)
    of_attn.drain()
    of_out.drain()
    for n in range(3):
        scatters[n].drain()
    for j in range(HALF // TILE):
        for seq in range(SEQS):
            back_copy(seq, j).wait_send()
    m_copy().wait_send()
    for name in list(sent):
        gone(name)

    @pl.loop(0, HALF // TILE)
    def _(j):
        tile = rows_at(j * TILE, TILE)
        back_sum(p.chip, j).wait_recv()
        grad = sum_out[p.chip, tile, :].astype(F32) + sum_in[p.chip, tile, :].astype(F32)
        back, _ = norm_pull(grad, xb[p.chip, tile, :].astype(F32), gain_attn)
        grad_hidden[tile, :] = grad_hidden[tile, :] + back

    store(grad_hidden, input_grad)
    scatters[2].finish()
    down_sum[...] = scatters[2].total().T[:ff, :]
    store(down_sum, down_out_sum)
    for n, (held, out) in enumerate(
        ((query_sum, query_out), (key_sum, key_out), (value_sum, value_out))
    ):
        scatters_attn[n].finish()
        held[...] = scatters_attn[n].total()
        store(held, out)
    scatters_attn[3].finish()
    out_sum[...] = scatters_attn[3].total().T
    store(out_sum, out_out)
    add_gains([p.across], 1)
    gain_attn_grad[...] = gain_acc[0:1, :] / gain_attn
    gain_mlp_grad[...] = gain_acc[1:2, :]
    store(gain_attn_grad, gain_attn_out)
    store(gain_mlp_grad, gain_mlp_out)
    for j in range(HALF // TILE):
        back_sum(1 - p.chip, j).wait_send()
    grad_store(SEQS - 1, hw // 128 - 1).wait()
    for scatter in scatters_attn:
        scatter.drain()
    for copy in stores:
        copy.wait()


def layer(dp, x, og, vf, segments, positions, gain_a, gain_m, wq, wk, wv, wo, wg, wu, wd):
    rows, width = 4 * x.shape[0], x.shape[1]
    hw, ff, r = vf.shape[1], wg.shape[0], wq.shape[0]
    wide = -(-ff // 256) * 256
    line = dp // 2
    hops = max(line - 1, 1)
    vmem = pl.BlockSpec(memory_space=pltpu.VMEM)
    far = pl.BlockSpec(memory_space=pl.ANY)
    shapes = [
        ((HALF, width), BF16, far),
        ((HALF, width), F32, far),
        ((rows, hw), F32, far),
        ((1, width), F32, far),
        ((r, hw), F32, far),
        ((r, hw), F32, far),
        ((r, hw), F32, far),
        ((hw, r), F32, far),
        ((1, width), F32, far),
        ((ff, r), F32, far),
        ((ff, r), F32, far),
        ((ff, r), F32, far),
    ]
    dma = pltpu.SemaphoreType.DMA
    flag = pltpu.SemaphoreType.REGULAR

    def bf(*shape):
        return pltpu.VMEM(shape, BF16)

    def fl(*shape):
        return pltpu.VMEM(shape, F32)

    scratch = [pltpu.VMEM(shape, kind) for shape, kind, _ in shapes[3:]] + [
        bf(2, HALF, width),
        bf(rows, width),
        bf(rows, width),
        bf(rows, width),
        bf(width, 4 * hw),
        bf(width, 3 * wide),
        bf(rows, hw),
        bf(rows, hw),
        bf(rows, hw),
        bf(rows, hw),
        fl(8, 1, SEQ_LEN),
        fl(2, HALF, width),
        fl(HALF, width),
        bf(SEQ_LEN, 3 * wide),
        bf(width, 3 * wide),
        bf(width, 4 * hw),
        bf(2, HALF, width),
        bf(2, HALF, width),
        bf(2, HALF, width),
        bf(2, HALF, width),
        bf(2, HALF, width),
        bf(hw, SEQ_LEN),
        fl(SEQ_LEN, 128),
        fl(SEQ_LEN, 128),
        fl(rows, 128),
        fl(rows, 128),
        fl(2, width),
        fl(4 + 2 * hops, 2, width),
        dma((18,)),
        dma((12,)),
        dma((12,)),
        dma((22,)),
        dma((22,)),
        dma((5, hops)),
        dma((5, hops)),
        dma((5, hops)),
        dma((5, hops)),
        dma((12, line)),
        dma((12, line)),
        dma((7, line)),
        dma((7, line)),
        dma((4 + 2 * hops,)),
        dma((4 + 2 * hops,)),
        flag((5,)),
        flag((line,)),
        flag((line,)),
    ]
    in_specs = [far] * 3 + [vmem] * 4 + [far] * 3 + [vmem] * 4
    return pl.pallas_call(
        functools.partial(layer_kernel, dp),
        out_shape=[jax.ShapeDtypeStruct(s, t) for s, t, _ in shapes],
        in_specs=in_specs,
        out_specs=[space for _, _, space in shapes],
        scratch_shapes=scratch,
        compiler_params=pltpu.CompilerParams(
            collective_id=0, has_side_effects=True, vmem_limit_bytes=VMEM_LIMIT
        ),
        name="layer",
    )(x, og, vf, segments, positions, gain_a, gain_m, wq, wk, wv, wo, wg, wu, wd)


def chunks(shape):
    parts = 4 if shape[0] % 512 == 0 else 1
    size = shape[0] // parts
    return [pl.ds(n * size, size) for n in range(parts)]


def settle_kernel(count, *refs):
    ins, outs, held, sems = refs[:count], refs[count : 2 * count], refs[2 * count : -1], refs[-1]
    pieces = [(n, rows) for n in range(count) for rows in chunks(ins[n].shape)]
    first, second = [], []
    for m, (n, rows) in enumerate(pieces):
        there = held[n].at[rows]
        first.append(pltpu.make_async_copy(ins[n].at[rows], there, sems.at[2 * m]))
        second.append(pltpu.make_async_copy(there, outs[n].at[rows], sems.at[2 * m + 1]))
    for copy in first:
        copy.start()
    for came, goes in zip(first, second):
        came.wait()
        goes.start()
    for copy in second:
        copy.wait()


def settle(arrays):
    count = len(arrays)
    far = pl.BlockSpec(memory_space=pl.ANY)
    return pl.pallas_call(
        functools.partial(settle_kernel, count),
        out_shape=[jax.ShapeDtypeStruct(a.shape, a.dtype) for a in arrays],
        in_specs=[far] * count,
        out_specs=[far] * count,
        scratch_shapes=[pltpu.VMEM(a.shape, a.dtype) for a in arrays]
        + [pltpu.SemaphoreType.DMA((2 * sum(len(chunks(a.shape)) for a in arrays),))],
        compiler_params=pltpu.CompilerParams(vmem_limit_bytes=VMEM_LIMIT),
        name="settle",
    )(*arrays)


def on_device(
    dp,
    block_input,
    value_first,
    segment_ids,
    positions,
    gain_attn,
    query_weight,
    key_weight,
    value_weight,
    out_weight,
    gain_mlp,
    gate_weight,
    up_weight,
    down_weight,
    output_grad,
):
    outs = layer(
        dp,
        block_input,
        output_grad,
        value_first,
        segment_ids[None, :],
        positions[None, :],
        gain_attn,
        gain_mlp,
        query_weight,
        key_weight,
        value_weight,
        out_weight,
        gate_weight.T,
        up_weight.T,
        down_weight,
    )
    (
        block_output,
        input_grad,
        value_first_grad,
        gain_attn_grad,
        query_sum,
        key_sum,
        value_sum,
        out_sum,
        gain_mlp_grad,
        gate_sum,
        up_sum,
        down_sum,
    ) = settle(outs)
    return (
        block_output,
        input_grad,
        value_first_grad,
        gain_attn_grad[0],
        query_sum,
        key_sum,
        value_sum,
        out_sum,
        gain_mlp_grad[0],
        gate_sum.T,
        up_sum.T,
        down_sum,
    )


def solution(mesh):
    rows = P(("dp", "tensor"), None)
    weight = P("dp", "tensor")
    across = P("tensor", "dp")
    return jax.shard_map(
        functools.partial(on_device, mesh.shape["dp"]),
        mesh=mesh,
        in_specs=(
            rows,
            weight,
            P("dp"),
            P("dp"),
            P(),
            weight,
            weight,
            weight,
            across,
            P(),
            weight,
            weight,
            across,
            rows,
        ),
        out_specs=(
            rows,
            rows,
            weight,
            P(),
            weight,
            weight,
            weight,
            across,
            P(),
            weight,
            weight,
            across,
        ),
        check_vma=False,
    )
```

```python
import functools
import math

import jax
import jax.numpy as jnp
from jax import lax
from jax.experimental import pallas as pl
from jax.experimental.pallas import tpu as pltpu
from jax.sharding import PartitionSpec as P

HEAD_DIM = 64
SEQ_LEN = 1024
SEQS = 2
PIECE = 256
HALF = 512
TILE = 256
EPSILON = 1e-06
ROPE_BASE = 10000.0
MASKED = -1e30
MESH = pl.DeviceIdType.MESH
F32 = jnp.float32
BF16 = jnp.bfloat16
VMEM_LIMIT = 639 * 2**20 // 10


def dot_nn(a, b):
    return lax.dot_general(a, b, (((1,), (0,)), ((), ())), preferred_element_type=F32)


def dot_nt(a, b):
    return lax.dot_general(a, b, (((1,), (1,)), ((), ())), preferred_element_type=F32)


def dot_tn(a, b):
    return lax.dot_general(a, b, (((0,), (0,)), ((), ())), preferred_element_type=F32)


def rows_at(start, size):
    return pl.ds(pl.multiple_of(start, size), size)


def block(b):
    return rows_at(b * HALF, HALF)


class Place:
    def __init__(self, dp):
        self.d = lax.axis_index("dp")
        self.t = lax.axis_index("tensor")
        self.core = lax.rem(self.t, 2)
        self.chip = self.t // 2
        self.line = dp // 2
        self.y = lax.rem(self.d, 2)
        self.z = self.d // 2
        self.sibling = (self.d, self.t + 1 - 2 * self.core)
        self.across = (self.d, lax.rem(self.t + 2, 4))
        self.pair = (self.d + 1 - 2 * self.y, self.t)
        self.up = (self.d + 2, self.t)
        self.down = (self.d - 2, self.t)

    def ahead(self, k):
        return (2 * lax.rem(self.z + k, self.line) + self.y, self.t)

    def beyond(self, k):
        return (2 * lax.rem(self.z + k, self.line) + 1 - self.y, self.t)

    def behind(self, k):
        return (2 * lax.rem(self.z + self.line - k, self.line) + self.y, self.t)

    def greet(self):
        barrier = pltpu.get_barrier_semaphore()
        partners = [self.sibling, self.across, self.pair]
        partners.extend(self.ahead(k) for k in range(1, self.line))
        partners.extend(self.beyond(k) for k in range(1, self.line))
        for who in partners:
            tell(barrier, who)
        self.greeted = len(partners)

    def met(self):
        pl.semaphore_wait(pltpu.get_barrier_semaphore(), self.greeted)


def tell(sem, who):
    pl.semaphore_signal(sem, inc=1, device_id=who, device_id_type=MESH)


def send(src, dst, sems, k, who):
    return pltpu.make_async_remote_copy(
        src_ref=src,
        dst_ref=dst,
        send_sem=sems[0].at[k],
        recv_sem=sems[1].at[k],
        device_id=who,
        device_id_type=MESH,
    )


class Gather:
    def __init__(self, place, full, lanes, rows, spread, up_sems, down_sems, pair_sems):
        self.p, self.full, self.lanes, self.r, self.spread = place, full, lanes, rows, spread
        self.up_sems, self.down_sems, self.pair_sems = up_sems, down_sems, pair_sems

    def shard(self, z, y):
        return self.full.at[rows_at((2 * z + y) * self.r, self.r), self.lanes]

    def load(self, z):
        if self.spread:
            return self.shard(z, self.p.y)
        return self.full.at[rows_at(2 * z * self.r, 2 * self.r), self.lanes]

    def sides(self, k):
        p = self.p
        return (
            (p.z - k, p.z >= k, self.up_sems, p.z + 1 < p.line, p.up),
            (p.z + k, p.z + k < p.line, self.down_sems, p.z >= 1, p.down),
        )

    def start_pair(self):
        p = self.p
        here = self.shard(p.z, p.y)
        send(here, here, self.pair_sems, p.z, p.pair).start()

    def start_line(self):
        p = self.p
        if not self.spread:
            there = self.shard(p.z, 1 - p.y)
            send(there, there, self.pair_sems, p.z, p.pair).wait_recv()
        here = self.load(p.z)
        for _, _, sems, onward, to in self.sides(0):

            @pl.when(onward)
            def _():
                send(here, here, sems, 0, to).start()

    def relay(self, k):
        p = self.p
        for z, exists, sems, onward, to in self.sides(k):

            @pl.when(exists)
            def _():
                here = self.load(z)
                send(here, here, sems, k - 1, to).wait_recv()

                @pl.when(onward)
                def _():
                    send(here, here, sems, k, to).start()

                if self.spread:
                    send(here, here, self.pair_sems, z, p.pair).start()

    def finish(self):
        p = self.p
        if self.spread:
            for z in range(p.line):
                there = self.shard(z, 1 - p.y)
                send(there, there, self.pair_sems, z, p.pair).wait_recv()

    def drain(self):
        p = self.p
        for z in range(p.line) if self.spread else (p.z,):
            here = self.shard(z, p.y)
            send(here, here, self.pair_sems, z, p.pair).wait_send()
        for k in range(p.line - 1):
            for z, exists, sems, onward, to in self.sides(k):

                @pl.when(jnp.logical_and(exists, onward))
                def _():
                    here = self.load(z)
                    send(here, here, sems, k, to).wait_send()


def far_first(n):
    if n < 4:
        return list(range(1, n))
    last = [2, n - 2] if n > 4 else [2]
    return [1, n - 1, *range(3, n - 2), *last]


class Scatter:
    def __init__(self, place, full, into, lanes, pair_sems, line_sems, free):
        self.p, self.full, self.into, self.lanes = place, full, into, lanes
        self.pair_sems, self.line_sems = pair_sems, line_sems
        self.free = free
        self.r = full.shape[0] // (2 * place.line)

    def rows(self, k, y):
        z = lax.rem(self.p.z + k, self.p.line)
        return rows_at((2 * z + y) * self.r, self.r)

    def pair_in(self, k):
        return self.into.at[pl.ds(k * self.r, self.r), self.lanes]

    def line_in(self, k):
        return self.into.at[pl.ds((self.p.line + k - 1) * self.r, self.r), self.lanes]

    def swap(self, k):
        theirs = self.full.at[self.rows(k, 1 - self.p.y), self.lanes]
        return send(theirs, self.pair_in(k), self.pair_sems, k, self.p.pair)

    def start(self, steps):
        if self.free is not None and (steps[0] == 1 or self.p.line == 1):
            pl.semaphore_wait(self.free.at[0], 1)
        for k in steps:
            self.swap(k).start()

    def relay(self, k):
        p = self.p
        n = p.line
        there = self.pair_in(k)
        send(there, there, self.pair_sems, k, p.pair).wait_recv()
        self.join(k, there)
        if self.free is not None and k == 1:
            for m in range(1, n):
                pl.semaphore_wait(self.free.at[m], 1)
        if n >= 4 and k in (2, n - 2):
            helping = jnp.logical_or(
                jnp.logical_and(p.z == 1, k == n - 2), jnp.logical_and(p.z == n - 2, k == 2)
            )

            @pl.when(helping)
            def _():
                self.helped().wait_recv()
                self.join(k, self.line_in(n))

        if n >= 4 and k in (1, n - 1):
            from_end = p.z == (0 if k == n - 1 else n - 1)

            @pl.when(from_end)
            def _():
                self.helped(k).start()

            @pl.when(jnp.logical_not(from_end))
            def _():
                self.onward(k).start()
        else:
            self.onward(k).start()

    def join(self, k, came):
        mine = self.full.at[self.rows(k, self.p.y), self.lanes]
        step = min(self.r, 32)

        @pl.loop(0, self.r // step)
        def _(j):
            rows = rows_at(j * step, step)
            mine[rows, :] = (mine[rows, :].astype(F32) + came[rows, :].astype(F32)).astype(BF16)

    def helped(self, k=1):
        p = self.p
        near = jnp.where(p.z == 0, 1, p.line - 2)
        mine = self.full.at[self.rows(k, p.y), self.lanes]
        return pltpu.make_async_remote_copy(
            src_ref=mine,
            dst_ref=self.line_in(p.line),
            send_sem=self.line_sems[0].at[k - 1],
            recv_sem=self.line_sems[1].at[p.line - 1],
            device_id=(2 * near + p.y, p.t),
            device_id_type=MESH,
        )

    def onward(self, k):
        p = self.p
        mine = self.full.at[self.rows(k, p.y), self.lanes]
        return send(mine, self.line_in(k), self.line_sems, k - 1, p.ahead(k))

    def merged(self, k):
        n = self.p.line
        if n < 4 or k not in (1, n - 1):
            return None
        return self.p.z == (n - 1 if k == n - 1 else 0)

    def finish(self):
        p = self.p
        there = self.pair_in(0)
        send(there, there, self.pair_sems, 0, p.pair).wait_recv()
        for k in range(1, p.line):
            there = self.line_in(k)
            merged = self.merged(k)
            if merged is None:
                send(there, there, self.line_sems, k - 1, p.pair).wait_recv()
            else:

                @pl.when(jnp.logical_not(merged))
                def _():
                    send(there, there, self.line_sems, k - 1, p.pair).wait_recv()

    def total(self):
        whole = self.full[self.rows(0, self.p.y), self.lanes].astype(F32)
        whole = whole + self.pair_in(0)[...].astype(F32)
        for k in range(1, self.p.line):
            came = self.line_in(k)[...].astype(F32)
            merged = self.merged(k)
            if merged is not None:
                came = jnp.where(merged, jnp.zeros_like(came), came)
            whole = whole + came
        return whole

    def drain(self):
        for k in range(self.p.line):
            self.swap(k).wait_send()
        for k in range(1, self.p.line):
            self.onward(k).wait_send()


def swap_halves(u):
    lane = lax.broadcasted_iota(jnp.int32, u.shape, 1)
    low = lax.rem(lane, HEAD_DIM) < HEAD_DIM // 2
    return jnp.where(low, pltpu.roll(u, 96, 1), pltpu.roll(u, 32, 1))


def norm_factor(u):
    return lax.rsqrt(jnp.mean(u * u, axis=-1, keepdims=True) + EPSILON)


def norm_pull(grad, u, gain):
    r = norm_factor(u)
    scaled = grad * gain
    back = r * scaled - u * (r * r * r) * jnp.mean(scaled * u, axis=-1, keepdims=True)
    return back, grad * u * r


def visible(segments):
    key = lax.broadcasted_iota(jnp.int32, (TILE, TILE), 0)
    query = lax.broadcasted_iota(jnp.int32, (TILE, TILE), 1)
    return jnp.logical_or(key <= query, segments > 0)


def attention_rows(seq, heads, i, q, k, vt, segments, attended, lse):
    lane = lax.broadcasted_iota(jnp.int32, (TILE, 128), 1)
    lanes = rows_at(heads * 128, 128)
    rows = pl.ds(seq * SEQ_LEN + i * TILE, TILE)
    q2 = q[rows, lanes]
    shown = visible(segments[:, rows])
    sides = []
    for a in range(2):
        qa = jnp.where((lane < HEAD_DIM) == (a == 0), q2, jnp.zeros_like(q2))
        vta = rows_at((heads * 2 + a) * HEAD_DIM, HEAD_DIM)
        score = jnp.where(shown, dot_nt(k[rows, lanes], qa), MASKED)
        top = jnp.max(score, axis=0, keepdims=True)
        if i > 0:
            before = dot_nt(k[pl.ds(seq * SEQ_LEN, i * TILE), lanes], qa)
            top = jnp.maximum(top, jnp.max(before, axis=0, keepdims=True))
        weight = jnp.exp(score - top)
        total = jnp.sum(weight, axis=0, keepdims=True)
        out = dot_nn(vt[vta, pl.ds(i * TILE, TILE)], weight.astype(BF16))
        if i > 0:
            weight = jnp.exp(before - top)
            total = total + jnp.sum(weight, axis=0, keepdims=True)
            out = out + dot_nn(vt[vta, pl.ds(0, i * TILE)], weight.astype(BF16))
        sides.append(out * (1.0 / total))
        lse[seq * 4 + heads * 2 + a, :, pl.ds(i * TILE, TILE)] = top + jnp.log(total)
    attended[rows, lanes] = jnp.concatenate(sides, axis=0).T.astype(BF16)


def attention_rows_back(
    seq, heads, i, q, k, v, kt, segments, lse, attended, grad_att, dk, dv, cos, sin, dqkv
):
    lane = lax.broadcasted_iota(jnp.int32, (TILE, 128), 1)
    lanes = rows_at(heads * 128, 128)
    local = pl.ds(i * TILE, TILE)
    rows = pl.ds(seq * SEQ_LEN + i * TILE, TILE)
    first = i == SEQ_LEN // TILE - 1
    q2, g2 = q[rows, lanes], grad_att(i, heads)
    shown = visible(segments[:, rows])
    products = (g2.astype(F32) * attended[rows, lanes].astype(F32)).T
    parts = [(i * TILE, TILE, True)]
    if i > 0:
        parts.append((0, i * TILE, False))
    sides = [None, None]
    for start, size, diagonal in parts:
        keys = pl.ds(seq * SEQ_LEN + start, size)
        here = pl.ds(start, size)
        dk_part, dv_part = 0.0, 0.0
        for a in range(2):
            mine = (lane < HEAD_DIM) == (a == 0)
            qa = jnp.where(mine, q2, jnp.zeros_like(q2))
            ga = jnp.where(mine, g2, jnp.zeros_like(g2))
            delta = jnp.sum(products[a * HEAD_DIM : (a + 1) * HEAD_DIM], axis=0, keepdims=True)
            stat = lse[seq * 4 + heads * 2 + a, :, local]
            score = dot_nt(k[keys, lanes], qa)
            if diagonal:
                score = jnp.where(shown, score, MASKED)
            prob = jnp.exp(score - stat)
            grad_prob = dot_nt(v[keys, lanes], ga)
            grad_score = (prob * (grad_prob - delta)).astype(BF16)
            dv_part = dv_part + dot_nn(prob.astype(BF16), ga)
            dk_part = dk_part + dot_nn(grad_score, qa)
            side = dot_nn(kt[rows_at((heads * 2 + a) * HEAD_DIM, HEAD_DIM), here], grad_score)
            sides[a] = side if sides[a] is None else sides[a] + side
        if first:
            dk[here, :] = dk_part
            dv[here, :] = dv_part
        else:
            dk[here, :] += dk_part
            dv[here, :] += dv_part
    dq = jnp.concatenate(sides, axis=0).T * HEAD_DIM**-0.5
    dqkv[local, lanes] = (dq * cos[rows, :] - swap_halves(dq) * sin[rows, :]).astype(BF16)


def layer_kernel(
    dp,
    x_in,
    og_in,
    value_first,
    segments,
    positions,
    gain_attn_in,
    gain_mlp_in,
    query_shard,
    key_shard,
    value_shard,
    out_shard,
    gate_shard,
    up_shard,
    down_shard,
    block_output,
    input_grad,
    value_first_grad,
    gain_attn_out,
    query_out,
    key_out,
    value_out,
    out_out,
    gain_mlp_out,
    gate_out,
    up_out_sum,
    down_out_sum,
    gain_attn_grad,
    query_sum,
    key_sum,
    value_sum,
    out_sum,
    gain_mlp_grad,
    gate_sum,
    up_sum,
    down_sum,
    xb,
    normed,
    normed_mlp,
    og,
    attn_w,
    ff_w,
    q,
    k,
    v,
    attended,
    lse,
    hidden,
    grad_hidden,
    units,
    ff_grad,
    attn_grad,
    half_out,
    half_in,
    sum_out,
    sum_in,
    m_sum,
    turned,
    dk,
    dv,
    cos,
    sin,
    gain_acc,
    gain_in,
    local_sems,
    group_out,
    group_in,
    core_out,
    core_in,
    up_out,
    up_in,
    down_out,
    down_in,
    pair_out,
    pair_in,
    line_out,
    line_in,
    gain_out_sems,
    gain_in_sems,
    credits,
    ff_free,
    attn_free,
):
    p = Place(dp)
    group, cores = (group_out, group_in), (core_out, core_in)
    rows_r, hw = query_shard.shape
    ff = gate_shard.shape[0]
    wide = ff_w.shape[1] // 3
    width = x_in.shape[1]
    tiles = SEQ_LEN // TILE
    slot = rows_at(p.d * rows_r, rows_r)
    qkv, out_lanes = slice(0, 3 * hw), slice(3 * hw, 4 * hw)
    middle = wide + 5 * wide // 6 // 128 * 128
    sent = {}

    def go(name, copy):
        copy.start()
        sent[name] = copy

    def gone(name):
        sent.pop(name).wait_send()

    def arrived(there, sems, n, who):
        send(there, there, sems, n, who).wait_recv()

    def local(n, src, dst):
        return pltpu.make_async_copy(src, dst, local_sems.at[n])

    def fetch(n, src, dst):
        copy = local(n, src, dst)
        copy.start()
        return copy

    p.greet()
    x_copy = fetch(0, x_in, xb.at[p.chip])
    qkv_copies = [
        fetch(1 + n, shard, attn_w.at[slot, pl.ds(n * hw, hw)])
        for n, shard in enumerate((query_shard, key_shard, value_shard))
    ]
    og_copy = fetch(4, og_in, og.at[block(p.t)])
    vf_copy = fetch(5, value_first, attended)
    attn_w[slot, out_lanes] = out_shard[...].astype(F32).T.astype(BF16)
    p.met()
    x_copy.wait()
    go("x", send(xb.at[p.chip], xb.at[p.chip], group, 0, p.across))
    gathers = [
        Gather(
            p,
            full,
            pl.ds(first, lanes),
            rows_r,
            spread,
            (up_out.at[n], up_in.at[n]),
            (down_out.at[n], down_in.at[n]),
            (pair_out.at[n], pair_in.at[n]),
        )
        for n, (full, first, lanes, spread) in enumerate(
            (
                (attn_w, 0, 3 * hw, True),
                (attn_w, 3 * hw, hw, True),
                (ff_w, wide // 2, middle - wide // 2, True),
                (ff_w, middle, 3 * wide - middle, True),
                (ff_w, 0, wide // 2, False),
            )
        )
    ]
    of_attn, of_out, of_ff, of_rest, of_gate = gathers
    for copy in qkv_copies:
        copy.wait()
    of_attn.start_line()
    of_attn.start_pair()
    of_out.start_line()
    of_out.start_pair()
    gain_attn = gain_attn_in[...].astype(F32).reshape(1, width)
    gain_mlp = gain_mlp_in[...].astype(F32).reshape(1, width)
    other = lax.rem(p.t + 2, 4)
    sib = p.t + 1 - 2 * p.core
    sib_other = lax.rem(sib + 2, 4)

    def norm_block(b, chip, n):
        @pl.loop(0, HALF // TILE)
        def _(j):
            u = xb[chip, rows_at(j * TILE, TILE), :].astype(F32)
            normed[rows_at(b * HALF + j * TILE, TILE), :] = (
                u * norm_factor(u) * gain_attn
            ).astype(BF16)

        here = normed.at[block(b)]
        go(("normed", n), send(here, here, cores, n, p.sibling))

    norm_block(p.t, p.chip, 0)
    for n, shard in enumerate((gate_shard, up_shard, down_shard)):
        flat = shard[...].astype(F32)
        if wide > ff:
            flat = jnp.concatenate([flat, jnp.zeros((wide - ff, rows_r), F32)], axis=0)
        ff_w[slot, n * wide : (n + 1) * wide] = flat.T.astype(BF16)
    of_gate.start_pair()
    if p.line > 1:
        of_attn.relay(1)
        of_out.relay(1)

    @pl.loop(0, SEQS * tiles)
    def _(j):
        rows = rows_at(j * TILE, TILE)
        lane = lax.broadcasted_iota(jnp.int32, (TILE, 128), 1)
        half = HEAD_DIM // 2
        power = lax.rem(lane[0:1, :], half).astype(F32) * (-2.0 / HEAD_DIM)
        frequency = jnp.exp(power * math.log(ROPE_BASE))
        place = jnp.broadcast_to(positions[:, rows].astype(F32), (128, TILE)).T
        angle = place * frequency
        cos[rows, :] = jnp.cos(angle)
        sine = jnp.sin(angle)
        sin[rows, :] = jnp.where(lax.rem(lane, HEAD_DIM) < half, -sine, sine)

    og_copy.wait()
    own_rows = og.at[block(p.t)]
    go("og_c", send(own_rows, own_rows, cores, 2, p.sibling))
    for n in range(2, p.line):
        of_attn.relay(n)
        of_out.relay(n)
        if n == 2:
            go("og_x", send(own_rows, own_rows, group, 1, p.across))
    if p.line < 3:
        go("og_x", send(own_rows, own_rows, group, 1, p.across))
    of_ff.start_line()
    of_rest.start_line()
    of_gate.start_line()
    arrived(xb.at[1 - p.chip], group, 0, p.across)
    norm_block(other, 1 - p.chip, 1)
    of_ff.start_pair()
    of_rest.start_pair()
    of_attn.finish()
    arrived(normed.at[block(sib)], cores, 0, p.sibling)
    arrived(normed.at[block(sib_other)], cores, 1, p.sibling)
    vf_copy.wait()

    def project(seq):
        @pl.loop(0, tiles)
        def _(j):
            rows = rows_at(seq * SEQ_LEN + j * TILE, TILE)
            made = dot_nn(normed[rows, :], attn_w[:, qkv])
            c, s = cos[rows, :], sin[rows, :]
            for n in range(hw // 128):
                lanes = slice(n * 128, (n + 1) * 128)
                u = made[:, n * 128 : (n + 1) * 128]
                q[rows, lanes] = ((u * c + swap_halves(u) * s) * HEAD_DIM**-0.5).astype(BF16)
                u = made[:, hw + n * 128 : hw + (n + 1) * 128]
                k[rows, lanes] = (u * c + swap_halves(u) * s).astype(BF16)
            mixed = 0.5 * made[:, 2 * hw :] + 0.5 * attended[rows, :].astype(F32)
            v[rows, :] = mixed.astype(BF16)
            turned[:, rows_at(j * TILE, TILE)] = mixed.T.astype(BF16)

    def attend(seq, between):
        @pl.loop(0, hw // 128)
        def _(heads):
            @pl.when(heads == hw // 128 - 1)
            def _():
                for relay in between:
                    relay()

            for i in range(tiles):
                attention_rows(seq, heads, i, q, k, turned, segments, attended, lse)

    def branch_other(seq):
        @pl.loop(0, HALF // TILE)
        def _(j):
            rows = rows_at(seq * SEQ_LEN + (1 - p.core) * HALF + j * TILE, TILE)
            half_out[seq, rows_at(j * TILE, TILE), :] = dot_nt(
                attended[rows, :], attn_w[:, out_lanes]
            ).astype(BF16)

        go(("half", seq), send(half_out.at[seq], half_in.at[seq], cores, 4 + seq, p.sibling))

    def branch_own(seq):
        arrived(half_in.at[seq], cores, 4 + seq, p.sibling)

        @pl.loop(0, HALF // TILE)
        def _(j):
            rows = rows_at(seq * SEQ_LEN + p.core * HALF + j * TILE, TILE)
            tile = rows_at(j * TILE, TILE)
            part = dot_nt(attended[rows, :], attn_w[:, out_lanes])
            sum_out[seq, tile, :] = (part + half_in[seq, tile, :].astype(F32)).astype(BF16)

        go(("sum", seq), send(sum_out.at[seq], sum_in.at[seq], group, 2 + seq, p.across))

    def finish_branch(seq):
        arrived(sum_in.at[seq], group, 2 + seq, p.across)

        @pl.loop(0, HALF // TILE)
        def _(j):
            tile = rows_at(j * TILE, TILE)
            both = sum_out[seq, tile, :].astype(F32) + sum_in[seq, tile, :].astype(F32)
            u = xb[seq, tile, :].astype(F32) + both
            hidden[seq, tile, :] = u
            normed_mlp[rows_at((2 * seq + p.core) * HALF + j * TILE, TILE), :] = (
                u * norm_factor(u) * gain_mlp
            ).astype(BF16)

        mine = normed_mlp.at[block(2 * seq + p.core)]
        go(("mlp", seq), send(mine, mine, cores, 6 + seq, p.sibling))
        tell(credits.at[seq], p.across)

    def in_steps(gather):
        steps = list(range(1, p.line))

        def relay():
            if steps:
                gather.relay(steps.pop(0))

        return relay, steps

    relay_ff, steps = in_steps(of_ff)
    relay_rest, _ = in_steps(of_rest)
    relay_gate, left = in_steps(of_gate)
    project(0)
    attend(0, [relay_ff])
    relay_rest()
    of_out.finish()
    branch_other(0)
    project(1)
    branch_own(0)
    relay_gate()
    relay_ff()
    attend(1, [relay_rest])
    relay_gate()
    branch_other(1)
    branch_own(1)
    relay_ff()
    relay_rest()
    arrived(og.at[block(other)], group, 1, p.across)
    there = og.at[block(other)]
    go("og_f", send(there, there, cores, 3, p.sibling))
    while steps or left:
        relay_ff()
        relay_rest()
        relay_gate()
    finish_branch(0)
    arrived(og.at[block(sib)], cores, 2, p.sibling)
    arrived(og.at[block(sib_other)], cores, 3, p.sibling)
    of_ff.finish()
    of_rest.finish()

    def feed_copy(seq, n, j):
        tile = rows_at(j * TILE, TILE)
        there = half_in.at[n, tile]
        return send(half_out.at[n, tile], there, cores, 8 + seq * 4 + n * 2 + j, p.sibling)

    def feed_sum(seq, j):
        tile = rows_at(j * TILE, TILE)
        return send(sum_out.at[seq, tile], sum_in.at[seq, tile], group, 6 + seq * 2 + j, p.across)

    def feed_gone(seq):
        for n in range(2):
            for j in range(HALF // TILE):
                feed_copy(seq, n, j).wait_send()

    def feed(seq):
        arrived(normed_mlp.at[block(2 * seq + 1 - p.core)], cores, 6 + seq, p.sibling)
        if seq == 0:
            for n in range(2):
                gone(("half", n))
        else:
            feed_gone(0)
        gone(("sum", seq))
        pl.semaphore_wait(credits.at[seq], 1)

        @pl.loop(0, tiles)
        def _(step):
            j = lax.rem(step, HALF // TILE)
            others = step < HALF // TILE
            h = jnp.where(others, 1 - p.core, p.core)
            here = rows_at(h * HALF + j * TILE, TILE)
            rows = rows_at(seq * SEQ_LEN + h * HALF + j * TILE, TILE)
            tile = rows_at(j * TILE, TILE)
            for n in range(wide // 256):
                lanes = [slice(m * wide + n * 256, m * wide + (n + 1) * 256) for m in range(3)]
                gate = dot_nn(normed_mlp[rows, :], ff_w[:, lanes[0]])
                up = dot_nn(normed_mlp[rows, :], ff_w[:, lanes[1]])
                grad_act = dot_nn(og[rows, :], ff_w[:, lanes[2]])
                sig = 1.0 / (1.0 + jnp.exp(-gate))
                swish = gate * sig
                units[here, lanes[0]] = (
                    grad_act * up * sig * (1.0 + gate * (1.0 - sig))
                ).astype(BF16)
                units[here, lanes[1]] = (grad_act * swish).astype(BF16)
                units[here, lanes[2]] = (swish * up).astype(BF16)
            down = dot_nt(units[here, 2 * wide :], ff_w[:, 2 * wide :])
            back = dot_nt(units[here, : 2 * wide], ff_w[:, : 2 * wide])

            @pl.when(others)
            def _():
                half_out[0, tile, :] = back.astype(BF16)
                half_out[1, tile, :] = down.astype(BF16)
                for n in range(2):
                    feed_copy(seq, n, j).start()

            @pl.when(jnp.logical_not(others))
            def _():
                for n in range(2):
                    feed_copy(seq, n, j).wait_recv()
                sum_out[seq, tile, :] = (back + half_in[0, tile, :].astype(F32)).astype(BF16)
                m_sum[seq, tile, :] = (down + half_in[1, tile, :].astype(F32)).astype(BF16)
                feed_sum(seq, j).start()

    def ff_weights(seq, n):
        rows = pl.ds(seq * SEQ_LEN, SEQ_LEN)
        left = og if isinstance(n, int) else normed_mlp
        lanes = pl.ds(pl.multiple_of(n * wide, 128), wide)

        @pl.loop(0, width // TILE)
        def _(j):
            cols = rows_at(j * TILE, TILE)
            part = dot_tn(left[rows, cols], units[:, lanes])
            if seq > 0:
                part = part + ff_grad[cols, lanes].astype(F32)
            ff_grad[cols, lanes] = part.astype(BF16)

    def both_ff_weights(seq, then=()):
        @pl.loop(0, 2)
        def _(n):
            ff_weights(seq, n)
            for m, start in enumerate(then):
                pl.when(n == m)(start)

    def pull(seq):
        for j in range(HALF // TILE):
            feed_sum(seq, j).wait_recv()

        @pl.loop(0, HALF // TILE)
        def _(j):
            tile = rows_at(j * TILE, TILE)
            rows = rows_at((2 * seq + p.core) * HALF + j * TILE, TILE)
            grad = sum_out[seq, tile, :].astype(F32) + sum_in[seq, tile, :].astype(F32)
            back, gain_rows = norm_pull(grad, hidden[seq, tile, :], gain_mlp)
            whole = og[rows, :].astype(F32) + back
            normed_mlp[rows, :] = whole.astype(BF16)

            @pl.when(p.chip == seq)
            def _():
                grad_hidden[tile, :] = whole
                gain_acc[1:2, :] += jnp.sum(gain_rows, axis=0, keepdims=True)

        mine = normed_mlp.at[block(2 * seq + p.core)]
        pl.semaphore_wait(credits.at[2 + seq], 1)
        go(("low", seq), send(mine, mine, cores, 16 + seq, p.sibling))

        @pl.when(p.chip == seq)
        def _():
            tell(credits.at[4], p.across)

    def release(sems):
        for who, n in [(p.pair, 0)] + [(p.behind(n), n) for n in range(1, p.line)]:
            tell(sems.at[n], who)

    def free_rows(seq):
        gone(("mlp", seq))
        tell(credits.at[2 + seq], p.sibling)

    feed(0)
    both_ff_weights(0)
    ff_weights(0, 2)
    finish_branch(1)
    free_rows(0)
    feed(1)
    of_ff.drain()
    of_rest.drain()
    of_gate.drain()
    release(ff_free)
    gain_acc[...] = jnp.zeros_like(gain_acc)
    scatters = [
        Scatter(
            p,
            ff_grad,
            ff_w,
            pl.ds(n * wide, wide),
            (pair_out.at[5 + n], pair_in.at[5 + n]),
            (line_out.at[n], line_in.at[n]),
            ff_free if n == 0 else None,
        )
        for n in range(3)
    ]
    scatters_attn = [
        Scatter(
            p,
            attn_grad,
            og,
            pl.ds(n * hw, hw),
            (pair_out.at[8 + n], pair_in.at[8 + n]),
            (line_out.at[3 + n], line_in.at[3 + n]),
            attn_free if n == 0 else None,
        )
        for n in range(4)
    ]
    away = far_first(p.line)
    firsts = away or [0]
    both_ff_weights(1, [functools.partial(scatters[n].start, firsts) for n in range(2)])
    ff_weights(1, 2)
    scatters[2].start(firsts)
    relays = [(scatters[n], k) for n in range(3) for k in away]
    if len(away) == 3:
        relays = [relays[n] for n in (0, 1, 3, 2, 4, 6, 5, 7, 8)]

    def relay_grad():
        if relays:
            scatter, k = relays.pop(0)
            scatter.relay(k)

    pull(0)
    free_rows(1)

    dqkv = units

    def grad_att(i, heads):
        return units[pl.ds(i * TILE, TILE), rows_at(3 * hw + heads * 128, 128)]

    def turn(seq):
        @pl.loop(0, tiles)
        def _(j):
            rows = rows_at(seq * SEQ_LEN + j * TILE, TILE)
            turned[:, rows_at(j * TILE, TILE)] = k[rows, :].astype(F32).T.astype(BF16)

    def prepare(seq):
        arrived(normed_mlp.at[block(2 * seq + 1 - p.core)], cores, 16 + seq, p.sibling)

        @pl.loop(0, tiles)
        def _(j):
            here = rows_at(j * TILE, TILE)
            rows = rows_at(seq * SEQ_LEN + j * TILE, TILE)
            units[here, out_lanes] = dot_nn(normed_mlp[rows, :], attn_w[:, out_lanes]).astype(BF16)

    def grad_store(seq, heads):
        rows = pl.ds(seq * SEQ_LEN, SEQ_LEN)
        return local(6, dv, value_first_grad.at[rows, rows_at(heads * 128, 128)])

    def m_copy():
        return send(m_sum.at[1 - p.chip], xb.at[p.chip], group, 4, p.across)

    def attend_back(seq, jobs):
        if seq > 0:
            grad_store(0, hw // 128 - 1).wait()

        @pl.loop(0, hw // 128)
        def _(heads):
            @pl.when(heads > 0)
            def _():
                grad_store(seq, heads - 1).wait()

            for i in reversed(range(tiles)):
                for when, job in jobs:
                    if when[1] == i:

                        @pl.when(heads == when[0])
                        def _():
                            job()

                attention_rows_back(
                    seq,
                    heads,
                    i,
                    q,
                    k,
                    v,
                    turned,
                    segments,
                    lse,
                    attended,
                    grad_att,
                    dk,
                    dv,
                    cos,
                    sin,
                    dqkv,
                )

            @pl.loop(0, tiles)
            def _(j):
                here = rows_at(j * TILE, TILE)
                rows = rows_at(seq * SEQ_LEN + j * TILE, TILE)
                u = dk[here, :]
                dqkv[here, rows_at(hw + heads * 128, 128)] = (
                    u * cos[rows, :] - swap_halves(u) * sin[rows, :]
                ).astype(BF16)
                half = 0.5 * dv[here, :]
                dqkv[here, rows_at(2 * hw + heads * 128, 128)] = half.astype(BF16)
                dv[here, :] = half

            grad_store(seq, heads).start()

    def attn_weights(seq, part):
        rows = pl.ds(seq * SEQ_LEN, SEQ_LEN)
        lanes = qkv if seq == 0 else rows_at(part * hw, hw)

        @pl.loop(0, width // TILE)
        def _(j):
            cols = rows_at(j * TILE, TILE)
            made = dot_tn(normed[rows, cols], units[:, lanes])
            if seq > 0:
                made = made + attn_grad[cols, lanes].astype(F32)
            attn_grad[cols, lanes] = made.astype(BF16)

    def out_weights():
        @pl.loop(0, width // TILE)
        def _(j):
            cols = rows_at(j * TILE, TILE)
            attn_grad[cols, out_lanes] = dot_tn(normed_mlp[:, cols], attended[...]).astype(BF16)

    def back_copy(seq, j):
        tile = rows_at(j * TILE, TILE)
        there = half_in.at[seq, tile]
        return send(half_out.at[seq, tile], there, cores, 18 + seq * 2 + j, p.sibling)

    def back_sum(seq, j):
        tile = rows_at(j * TILE, TILE)
        return send(sum_out.at[seq, tile], sum_in.at[seq, tile], group, 10 + j, p.across)

    def back_other(seq):
        if seq == 0:
            feed_gone(1)

        @pl.loop(0, HALF // TILE)
        def _(j):
            here = rows_at((1 - p.core) * HALF + j * TILE, TILE)
            half_out[seq, rows_at(j * TILE, TILE), :] = dot_nt(
                dqkv[here, qkv], attn_w[:, qkv]
            ).astype(BF16)
            back_copy(seq, j).start()

    gain_sems = (gain_out_sems, gain_in_sems)

    def gain_copies(partners, first):
        return [
            send(gain_acc, gain_in.at[first + n], gain_sems, first + n, who)
            for n, who in enumerate(partners)
        ]

    def exchange(partners, first):
        for copy in gain_copies(partners, first):
            copy.start()

    def add_gains(partners, first):
        for copy in gain_copies(partners, first):
            copy.wait()
        whole = gain_acc[...]
        for n in range(len(partners)):
            whole = whole + gain_in[first + n]
        gain_acc[...] = whole

    def back_own(seq):
        for j in range(HALF // TILE):
            feed_sum(seq, j).wait_send()

        @pl.when(p.chip != seq)
        def _():
            pl.semaphore_wait(credits.at[4], 1)

        @pl.loop(0, HALF // TILE)
        def _(j):
            here = rows_at(p.core * HALF + j * TILE, TILE)
            tile = rows_at(j * TILE, TILE)
            rows = rows_at((2 * seq + p.core) * HALF + j * TILE, TILE)
            part = dot_nt(dqkv[here, qkv], attn_w[:, qkv])
            back_copy(seq, j).wait_recv()
            part = part + half_in[seq, tile, :].astype(F32)
            sum_out[seq, tile, :] = part.astype(BF16)
            gain_acc[0:1, :] += jnp.sum(part * normed[rows, :].astype(F32), axis=0, keepdims=True)

            @pl.when(p.chip != seq)
            def _():
                back_sum(seq, j).start()

        if seq == SEQS - 1:
            exchange([p.sibling], 0)

    turn(0)
    relay_grad()
    prepare(0)
    attend_back(0, [((1, 3), m_copy().start), ((0, 1), relay_grad), ((1, 1), relay_grad)])
    relay_grad()
    back_other(0)
    turn(1)
    attn_weights(0, 0)
    relay_grad()
    pull(1)
    for name in ("og_x", "og_c", "og_f"):
        gone(name)
    release(attn_free)
    back_own(0)
    if away:
        for n in range(3):
            scatters[n].start([0])
    prepare(1)
    attend_back(1, [((0, 1), relay_grad), ((0, 1), relay_grad), ((1, 3), relay_grad)])
    back_other(1)
    while relays:
        relay_grad()

    @pl.loop(0, 3)
    def _(n):
        attn_weights(1, n)
        for m in range(3):
            steps_now = firsts if m < 2 else firsts[:-1]
            pl.when(n == m)(functools.partial(scatters_attn[m].start, steps_now))
        pl.when(n == 0)(lambda: back_own(1))

    out_weights()
    add_gains([p.sibling], 0)
    farther = [p.pair] + [p.ahead(n) for n in away] + [p.beyond(n) for n in away]
    exchange(farther, 2)
    scatters_attn[3].start(firsts[:-1])
    for n in (2, 3):
        scatters_attn[n].start(firsts[-1:])
    if away:
        for scatter in scatters_attn:
            scatter.start([0])

    arrived(xb.at[1 - p.chip], group, 4, p.across)

    @pl.loop(0, HALF // TILE)
    def _(j):
        tile = rows_at(j * TILE, TILE)
        both = m_sum[p.chip, tile, :].astype(F32) + xb[1 - p.chip, tile, :].astype(F32)
        m_sum[p.chip, tile, :] = (hidden[p.chip, tile, :] + both).astype(BF16)

    stores = []

    def store(src, dst):
        stores.append(fetch(7 + len(stores), src, dst))

    store(m_sum.at[p.chip], block_output)
    for n in range(4):
        for k in away[:-1]:
            scatters_attn[n].relay(k)
        for m in [n - 1] * (n > 0) + [n] * (n == 3):
            for k in away[-1:]:
                scatters_attn[m].relay(k)
        if n < 2:
            scatters[n].finish()
            (gate_sum, up_sum)[n][...] = scatters[n].total().T[:ff, :]
            store((gate_sum, up_sum)[n], (gate_out, up_out_sum)[n])
    add_gains(farther, 2)
    exchange([p.across], 1)
    of_attn.drain()
    of_out.drain()
    for n in range(3):
        scatters[n].drain()
    for j in range(HALF // TILE):
        for seq in range(SEQS):
            back_copy(seq, j).wait_send()
    m_copy().wait_send()
    for name in list(sent):
        gone(name)

    @pl.loop(0, HALF // TILE)
    def _(j):
        tile = rows_at(j * TILE, TILE)
        back_sum(p.chip, j).wait_recv()
        grad = sum_out[p.chip, tile, :].astype(F32) + sum_in[p.chip, tile, :].astype(F32)
        back, _ = norm_pull(grad, xb[p.chip, tile, :].astype(F32), gain_attn)
        grad_hidden[tile, :] = grad_hidden[tile, :] + back

    store(grad_hidden, input_grad)
    scatters[2].finish()
    down_sum[...] = scatters[2].total().T[:ff, :]
    store(down_sum, down_out_sum)
    add_gains([p.across], 1)
    gain_attn_grad[...] = gain_acc[0:1, :] / gain_attn
    gain_mlp_grad[...] = gain_acc[1:2, :]
    store(gain_attn_grad, gain_attn_out)
    store(gain_mlp_grad, gain_mlp_out)
    for n, (held, out) in enumerate(
        ((query_sum, query_out), (key_sum, key_out), (value_sum, value_out))
    ):
        if n == 2:
            scatters_attn[0].drain()
            scatters_attn[1].drain()
            for j in range(HALF // TILE):
                back_sum(1 - p.chip, j).wait_send()
            grad_store(SEQS - 1, hw // 128 - 1).wait()
        scatters_attn[n].finish()
        held[...] = scatters_attn[n].total()
        store(held, out)
    scatters_attn[3].finish()
    out_sum[...] = scatters_attn[3].total().T
    store(out_sum, out_out)
    scatters_attn[2].drain()
    scatters_attn[3].drain()
    for copy in stores:
        copy.wait()


def layer(dp, x, og, vf, segments, positions, gain_a, gain_m, wq, wk, wv, wo, wg, wu, wd):
    rows, width = 4 * x.shape[0], x.shape[1]
    hw, ff, r = vf.shape[1], wg.shape[0], wq.shape[0]
    wide = -(-ff // 256) * 256
    line = dp // 2
    hops = max(line - 1, 1)
    vmem = pl.BlockSpec(memory_space=pltpu.VMEM)
    far = pl.BlockSpec(memory_space=pl.ANY)
    shapes = [
        ((HALF, width), BF16, far),
        ((HALF, width), F32, far),
        ((rows, hw), F32, far),
        ((1, width), F32, far),
        ((r, hw), F32, far),
        ((r, hw), F32, far),
        ((r, hw), F32, far),
        ((hw, r), F32, far),
        ((1, width), F32, far),
        ((ff, r), F32, far),
        ((ff, r), F32, far),
        ((ff, r), F32, far),
    ]
    dma = pltpu.SemaphoreType.DMA
    flag = pltpu.SemaphoreType.REGULAR

    def bf(*shape):
        return pltpu.VMEM(shape, BF16)

    def fl(*shape):
        return pltpu.VMEM(shape, F32)

    scratch = [pltpu.VMEM(shape, kind) for shape, kind, _ in shapes[3:]] + [
        bf(2, HALF, width),
        bf(rows, width),
        bf(rows, width),
        bf(rows, width),
        bf(width, 4 * hw),
        bf(width, 3 * wide),
        bf(rows, hw),
        bf(rows, hw),
        bf(rows, hw),
        bf(rows, hw),
        fl(8, 1, SEQ_LEN),
        fl(2, HALF, width),
        fl(HALF, width),
        bf(SEQ_LEN, 3 * wide),
        bf(width, 3 * wide),
        bf(width, 4 * hw),
        bf(2, HALF, width),
        bf(2, HALF, width),
        bf(2, HALF, width),
        bf(2, HALF, width),
        bf(2, HALF, width),
        bf(hw, SEQ_LEN),
        fl(SEQ_LEN, 128),
        fl(SEQ_LEN, 128),
        fl(rows, 128),
        fl(rows, 128),
        fl(2, width),
        fl(4 + 2 * hops, 2, width),
        dma((18,)),
        dma((12,)),
        dma((12,)),
        dma((22,)),
        dma((22,)),
        dma((5, hops)),
        dma((5, hops)),
        dma((5, hops)),
        dma((5, hops)),
        dma((12, line)),
        dma((12, line)),
        dma((7, line)),
        dma((7, line)),
        dma((4 + 2 * hops,)),
        dma((4 + 2 * hops,)),
        flag((5,)),
        flag((line,)),
        flag((line,)),
    ]
    in_specs = [far] * 3 + [vmem] * 4 + [far] * 3 + [vmem] * 4
    return pl.pallas_call(
        functools.partial(layer_kernel, dp),
        out_shape=[jax.ShapeDtypeStruct(s, t) for s, t, _ in shapes],
        in_specs=in_specs,
        out_specs=[space for _, _, space in shapes],
        scratch_shapes=scratch,
        compiler_params=pltpu.CompilerParams(
            collective_id=0, has_side_effects=True, vmem_limit_bytes=VMEM_LIMIT
        ),
        name="layer",
    )(x, og, vf, segments, positions, gain_a, gain_m, wq, wk, wv, wo, wg, wu, wd)


def chunks(shape):
    parts = 4 if shape[0] % 512 == 0 else 1
    size = shape[0] // parts
    return [pl.ds(n * size, size) for n in range(parts)]


def settle_kernel(count, *refs):
    ins, outs, held, sems = refs[:count], refs[count : 2 * count], refs[2 * count : -1], refs[-1]
    pieces = [(n, rows) for n in range(count) for rows in chunks(ins[n].shape)]
    first, second = [], []
    for m, (n, rows) in enumerate(pieces):
        there = held[n].at[rows]
        first.append(pltpu.make_async_copy(ins[n].at[rows], there, sems.at[2 * m]))
        second.append(pltpu.make_async_copy(there, outs[n].at[rows], sems.at[2 * m + 1]))
    for copy in first:
        copy.start()
    for came, goes in zip(first, second):
        came.wait()
        goes.start()
    for copy in second:
        copy.wait()


def settle(arrays):
    count = len(arrays)
    far = pl.BlockSpec(memory_space=pl.ANY)
    return pl.pallas_call(
        functools.partial(settle_kernel, count),
        out_shape=[jax.ShapeDtypeStruct(a.shape, a.dtype) for a in arrays],
        in_specs=[far] * count,
        out_specs=[far] * count,
        scratch_shapes=[pltpu.VMEM(a.shape, a.dtype) for a in arrays]
        + [pltpu.SemaphoreType.DMA((2 * sum(len(chunks(a.shape)) for a in arrays),))],
        compiler_params=pltpu.CompilerParams(vmem_limit_bytes=VMEM_LIMIT),
        name="settle",
    )(*arrays)


def on_device(
    dp,
    block_input,
    value_first,
    segment_ids,
    positions,
    gain_attn,
    query_weight,
    key_weight,
    value_weight,
    out_weight,
    gain_mlp,
    gate_weight,
    up_weight,
    down_weight,
    output_grad,
):
    outs = layer(
        dp,
        block_input,
        output_grad,
        value_first,
        segment_ids[None, :],
        positions[None, :],
        gain_attn,
        gain_mlp,
        query_weight,
        key_weight,
        value_weight,
        out_weight,
        gate_weight.T,
        up_weight.T,
        down_weight,
    )
    (
        block_output,
        input_grad,
        value_first_grad,
        gain_attn_grad,
        query_sum,
        key_sum,
        value_sum,
        out_sum,
        gain_mlp_grad,
        gate_sum,
        up_sum,
        down_sum,
    ) = settle(outs)
    return (
        block_output,
        input_grad,
        value_first_grad,
        gain_attn_grad[0],
        query_sum,
        key_sum,
        value_sum,
        out_sum,
        gain_mlp_grad[0],
        gate_sum.T,
        up_sum.T,
        down_sum,
    )


def solution(mesh):
    rows = P(("dp", "tensor"), None)
    weight = P("dp", "tensor")
    across = P("tensor", "dp")
    return jax.shard_map(
        functools.partial(on_device, mesh.shape["dp"]),
        mesh=mesh,
        in_specs=(
            rows,
            weight,
            P("dp"),
            P("dp"),
            P(),
            weight,
            weight,
            weight,
            across,
            P(),
            weight,
            weight,
            across,
            rows,
        ),
        out_specs=(
            rows,
            rows,
            weight,
            P(),
            weight,
            weight,
            weight,
            across,
            P(),
            weight,
            weight,
            across,
        ),
        check_vma=False,
    )
```

```python
import functools
import math

import jax
import jax.numpy as jnp
from jax import lax
from jax.experimental import pallas as pl
from jax.experimental.pallas import tpu as pltpu
from jax.sharding import PartitionSpec as P

HEAD_DIM = 64
SEQ_LEN = 1024
SEQS = 2
PIECE = 256
HALF = 512
TILE = 256
EPSILON = 1e-06
ROPE_BASE = 10000.0
MASKED = -1e30
MESH = pl.DeviceIdType.MESH
F32 = jnp.float32
BF16 = jnp.bfloat16
VMEM_LIMIT = 639 * 2**20 // 10


def dot_nn(a, b):
    return lax.dot_general(a, b, (((1,), (0,)), ((), ())), preferred_element_type=F32)


def dot_nt(a, b):
    return lax.dot_general(a, b, (((1,), (1,)), ((), ())), preferred_element_type=F32)


def dot_tn(a, b):
    return lax.dot_general(a, b, (((0,), (0,)), ((), ())), preferred_element_type=F32)


def rows_at(start, size):
    return pl.ds(pl.multiple_of(start, size), size)


def block(b):
    return rows_at(b * HALF, HALF)


class Place:
    def __init__(self, dp):
        self.d = lax.axis_index("dp")
        self.t = lax.axis_index("tensor")
        self.core = lax.rem(self.t, 2)
        self.chip = self.t // 2
        self.line = dp // 2
        self.y = lax.rem(self.d, 2)
        self.z = self.d // 2
        self.sibling = (self.d, self.t + 1 - 2 * self.core)
        self.across = (self.d, lax.rem(self.t + 2, 4))
        self.pair = (self.d + 1 - 2 * self.y, self.t)
        self.up = (self.d + 2, self.t)
        self.down = (self.d - 2, self.t)

    def ahead(self, k):
        return (2 * lax.rem(self.z + k, self.line) + self.y, self.t)

    def beyond(self, k):
        return (2 * lax.rem(self.z + k, self.line) + 1 - self.y, self.t)

    def behind(self, k):
        return (2 * lax.rem(self.z + self.line - k, self.line) + self.y, self.t)

    def greet(self):
        barrier = pltpu.get_barrier_semaphore()
        partners = [self.sibling, self.across, self.pair]
        partners.extend(self.ahead(k) for k in range(1, self.line))
        partners.extend(self.beyond(k) for k in range(1, self.line))
        for who in partners:
            tell(barrier, who)
        self.greeted = len(partners)

    def met(self):
        pl.semaphore_wait(pltpu.get_barrier_semaphore(), self.greeted)


def tell(sem, who):
    pl.semaphore_signal(sem, inc=1, device_id=who, device_id_type=MESH)


def send(src, dst, sems, k, who):
    return pltpu.make_async_remote_copy(
        src_ref=src,
        dst_ref=dst,
        send_sem=sems[0].at[k],
        recv_sem=sems[1].at[k],
        device_id=who,
        device_id_type=MESH,
    )


class Gather:
    def __init__(self, place, full, lanes, rows, spread, up_sems, down_sems, pair_sems):
        self.p, self.full, self.lanes, self.r, self.spread = place, full, lanes, rows, spread
        self.up_sems, self.down_sems, self.pair_sems = up_sems, down_sems, pair_sems

    def shard(self, z, y):
        return self.full.at[rows_at((2 * z + y) * self.r, self.r), self.lanes]

    def load(self, z):
        if self.spread:
            return self.shard(z, self.p.y)
        return self.full.at[rows_at(2 * z * self.r, 2 * self.r), self.lanes]

    def sides(self, k):
        p = self.p
        return (
            (p.z - k, p.z >= k, self.up_sems, p.z + 1 < p.line, p.up),
            (p.z + k, p.z + k < p.line, self.down_sems, p.z >= 1, p.down),
        )

    def start_pair(self):
        p = self.p
        here = self.shard(p.z, p.y)
        send(here, here, self.pair_sems, p.z, p.pair).start()

    def start_line(self):
        p = self.p
        if not self.spread:
            there = self.shard(p.z, 1 - p.y)
            send(there, there, self.pair_sems, p.z, p.pair).wait_recv()
        here = self.load(p.z)
        for _, _, sems, onward, to in self.sides(0):

            @pl.when(onward)
            def _():
                send(here, here, sems, 0, to).start()

    def relay(self, k):
        p = self.p
        for z, exists, sems, onward, to in self.sides(k):

            @pl.when(exists)
            def _():
                here = self.load(z)
                send(here, here, sems, k - 1, to).wait_recv()

                @pl.when(onward)
                def _():
                    send(here, here, sems, k, to).start()

                if self.spread:
                    send(here, here, self.pair_sems, z, p.pair).start()

    def finish(self):
        p = self.p
        if self.spread:
            for z in range(p.line):
                there = self.shard(z, 1 - p.y)
                send(there, there, self.pair_sems, z, p.pair).wait_recv()

    def drain(self):
        p = self.p
        for z in range(p.line) if self.spread else (p.z,):
            here = self.shard(z, p.y)
            send(here, here, self.pair_sems, z, p.pair).wait_send()
        for k in range(p.line - 1):
            for z, exists, sems, onward, to in self.sides(k):

                @pl.when(jnp.logical_and(exists, onward))
                def _():
                    here = self.load(z)
                    send(here, here, sems, k, to).wait_send()


def far_first(n):
    if n < 4:
        return list(range(1, n))
    last = [2, n - 2] if n > 4 else [2]
    return [1, n - 1, *range(3, n - 2), *last]


class Scatter:
    def __init__(self, place, full, into, lanes, pair_sems, line_sems, free):
        self.p, self.full, self.into, self.lanes = place, full, into, lanes
        self.pair_sems, self.line_sems = pair_sems, line_sems
        self.free = free
        self.r = full.shape[0] // (2 * place.line)

    def rows(self, k, y):
        z = lax.rem(self.p.z + k, self.p.line)
        return rows_at((2 * z + y) * self.r, self.r)

    def pair_in(self, k):
        return self.into.at[pl.ds(k * self.r, self.r), self.lanes]

    def line_in(self, k):
        return self.into.at[pl.ds((self.p.line + k - 1) * self.r, self.r), self.lanes]

    def swap(self, k):
        theirs = self.full.at[self.rows(k, 1 - self.p.y), self.lanes]
        return send(theirs, self.pair_in(k), self.pair_sems, k, self.p.pair)

    def start(self, steps):
        if self.free is not None and (steps[0] == 1 or self.p.line == 1):
            pl.semaphore_wait(self.free.at[0], 1)
        for k in steps:
            self.swap(k).start()

    def relay(self, k):
        p = self.p
        n = p.line
        there = self.pair_in(k)
        send(there, there, self.pair_sems, k, p.pair).wait_recv()
        self.join(k, there)
        if self.free is not None and k == 1:
            for m in range(1, n):
                pl.semaphore_wait(self.free.at[m], 1)
        if n >= 4 and k in (2, n - 2):
            helping = jnp.logical_or(
                jnp.logical_and(p.z == 1, k == n - 2), jnp.logical_and(p.z == n - 2, k == 2)
            )

            @pl.when(helping)
            def _():
                self.helped().wait_recv()
                self.join(k, self.line_in(n))

        if n >= 4 and k in (1, n - 1):
            from_end = p.z == (0 if k == n - 1 else n - 1)

            @pl.when(from_end)
            def _():
                self.helped(k).start()

            @pl.when(jnp.logical_not(from_end))
            def _():
                self.onward(k).start()
        else:
            self.onward(k).start()

    def join(self, k, came):
        mine = self.full.at[self.rows(k, self.p.y), self.lanes]
        step = min(self.r, 32)

        @pl.loop(0, self.r // step)
        def _(j):
            rows = rows_at(j * step, step)
            mine[rows, :] = (mine[rows, :].astype(F32) + came[rows, :].astype(F32)).astype(BF16)

    def helped(self, k=1):
        p = self.p
        near = jnp.where(p.z == 0, 1, p.line - 2)
        mine = self.full.at[self.rows(k, p.y), self.lanes]
        return pltpu.make_async_remote_copy(
            src_ref=mine,
            dst_ref=self.line_in(p.line),
            send_sem=self.line_sems[0].at[k - 1],
            recv_sem=self.line_sems[1].at[p.line - 1],
            device_id=(2 * near + p.y, p.t),
            device_id_type=MESH,
        )

    def onward(self, k):
        p = self.p
        mine = self.full.at[self.rows(k, p.y), self.lanes]
        return send(mine, self.line_in(k), self.line_sems, k - 1, p.ahead(k))

    def merged(self, k):
        n = self.p.line
        if n < 4 or k not in (1, n - 1):
            return None
        return self.p.z == (n - 1 if k == n - 1 else 0)

    def finish(self):
        p = self.p
        there = self.pair_in(0)
        send(there, there, self.pair_sems, 0, p.pair).wait_recv()
        for k in range(1, p.line):
            there = self.line_in(k)
            merged = self.merged(k)
            if merged is None:
                send(there, there, self.line_sems, k - 1, p.pair).wait_recv()
            else:

                @pl.when(jnp.logical_not(merged))
                def _():
                    send(there, there, self.line_sems, k - 1, p.pair).wait_recv()

    def total(self):
        whole = self.full[self.rows(0, self.p.y), self.lanes].astype(F32)
        whole = whole + self.pair_in(0)[...].astype(F32)
        for k in range(1, self.p.line):
            came = self.line_in(k)[...].astype(F32)
            merged = self.merged(k)
            if merged is not None:
                came = jnp.where(merged, jnp.zeros_like(came), came)
            whole = whole + came
        return whole

    def drain(self):
        for k in range(self.p.line):
            self.swap(k).wait_send()
        for k in range(1, self.p.line):
            self.onward(k).wait_send()


def swap_halves(u):
    lane = lax.broadcasted_iota(jnp.int32, u.shape, 1)
    low = lax.rem(lane, HEAD_DIM) < HEAD_DIM // 2
    return jnp.where(low, pltpu.roll(u, 96, 1), pltpu.roll(u, 32, 1))


def norm_factor(u):
    return lax.rsqrt(jnp.mean(u * u, axis=-1, keepdims=True) + EPSILON)


def norm_pull(grad, u, gain):
    r = norm_factor(u)
    scaled = grad * gain
    back = r * scaled - u * (r * r * r) * jnp.mean(scaled * u, axis=-1, keepdims=True)
    return back, grad * u * r


def visible(segments):
    key = lax.broadcasted_iota(jnp.int32, (TILE, TILE), 0)
    query = lax.broadcasted_iota(jnp.int32, (TILE, TILE), 1)
    return jnp.logical_or(key <= query, segments > 0)


def attention_rows(seq, heads, i, q, k, vt, segments, attended, lse):
    lane = lax.broadcasted_iota(jnp.int32, (TILE, 128), 1)
    lanes = rows_at(heads * 128, 128)
    rows = pl.ds(seq * SEQ_LEN + i * TILE, TILE)
    q2 = q[rows, lanes]
    shown = visible(segments[:, rows])
    sides = []
    for a in range(2):
        qa = jnp.where((lane < HEAD_DIM) == (a == 0), q2, jnp.zeros_like(q2))
        vta = rows_at((heads * 2 + a) * HEAD_DIM, HEAD_DIM)
        score = jnp.where(shown, dot_nt(k[rows, lanes], qa), MASKED)
        top = jnp.max(score, axis=0, keepdims=True)
        if i > 0:
            before = dot_nt(k[pl.ds(seq * SEQ_LEN, i * TILE), lanes], qa)
            top = jnp.maximum(top, jnp.max(before, axis=0, keepdims=True))
        weight = jnp.exp(score - top)
        total = jnp.sum(weight, axis=0, keepdims=True)
        out = dot_nn(vt[vta, pl.ds(i * TILE, TILE)], weight.astype(BF16))
        if i > 0:
            weight = jnp.exp(before - top)
            total = total + jnp.sum(weight, axis=0, keepdims=True)
            out = out + dot_nn(vt[vta, pl.ds(0, i * TILE)], weight.astype(BF16))
        sides.append(out * (1.0 / total))
        lse[seq * 4 + heads * 2 + a, :, pl.ds(i * TILE, TILE)] = top + jnp.log(total)
    attended[rows, lanes] = jnp.concatenate(sides, axis=0).T.astype(BF16)


def attention_rows_back(
    seq, heads, i, q, k, v, kt, segments, lse, attended, grad_att, dk, dv, cos, sin, dqkv
):
    lane = lax.broadcasted_iota(jnp.int32, (TILE, 128), 1)
    lanes = rows_at(heads * 128, 128)
    local = pl.ds(i * TILE, TILE)
    rows = pl.ds(seq * SEQ_LEN + i * TILE, TILE)
    first = i == SEQ_LEN // TILE - 1
    q2, g2 = q[rows, lanes], grad_att(i, heads)
    shown = visible(segments[:, rows])
    products = (g2.astype(F32) * attended[rows, lanes].astype(F32)).T
    parts = [(i * TILE, TILE, True)]
    if i > 0:
        parts.append((0, i * TILE, False))
    sides = [None, None]
    for start, size, diagonal in parts:
        keys = pl.ds(seq * SEQ_LEN + start, size)
        here = pl.ds(start, size)
        dk_part, dv_part = 0.0, 0.0
        for a in range(2):
            mine = (lane < HEAD_DIM) == (a == 0)
            qa = jnp.where(mine, q2, jnp.zeros_like(q2))
            ga = jnp.where(mine, g2, jnp.zeros_like(g2))
            delta = jnp.sum(products[a * HEAD_DIM : (a + 1) * HEAD_DIM], axis=0, keepdims=True)
            stat = lse[seq * 4 + heads * 2 + a, :, local]
            score = dot_nt(k[keys, lanes], qa)
            if diagonal:
                score = jnp.where(shown, score, MASKED)
            prob = jnp.exp(score - stat)
            grad_prob = dot_nt(v[keys, lanes], ga)
            grad_score = (prob * (grad_prob - delta)).astype(BF16)
            dv_part = dv_part + dot_nn(prob.astype(BF16), ga)
            dk_part = dk_part + dot_nn(grad_score, qa)
            side = dot_nn(kt[rows_at((heads * 2 + a) * HEAD_DIM, HEAD_DIM), here], grad_score)
            sides[a] = side if sides[a] is None else sides[a] + side
        if first:
            dk[here, :] = dk_part
            dv[here, :] = dv_part
        else:
            dk[here, :] += dk_part
            dv[here, :] += dv_part
    dq = jnp.concatenate(sides, axis=0).T * HEAD_DIM**-0.5
    dqkv[local, lanes] = (dq * cos[rows, :] - swap_halves(dq) * sin[rows, :]).astype(BF16)


def layer_kernel(
    dp,
    x_in,
    og_in,
    value_first,
    segments,
    positions,
    gain_attn_in,
    gain_mlp_in,
    query_shard,
    key_shard,
    value_shard,
    out_shard,
    gate_shard,
    up_shard,
    down_shard,
    block_output,
    input_grad,
    value_first_grad,
    gain_attn_out,
    query_out,
    key_out,
    value_out,
    out_out,
    gain_mlp_out,
    gate_out,
    up_out_sum,
    down_out_sum,
    gain_attn_grad,
    query_sum,
    key_sum,
    value_sum,
    out_sum,
    gain_mlp_grad,
    gate_sum,
    up_sum,
    down_sum,
    xb,
    normed,
    normed_mlp,
    og,
    attn_w,
    ff_w,
    q,
    k,
    v,
    attended,
    lse,
    hidden,
    grad_hidden,
    units,
    ff_grad,
    attn_grad,
    half_out,
    half_in,
    sum_out,
    sum_in,
    m_sum,
    turned,
    dk,
    dv,
    cos,
    sin,
    gain_acc,
    gain_in,
    local_sems,
    group_out,
    group_in,
    core_out,
    core_in,
    up_out,
    up_in,
    down_out,
    down_in,
    pair_out,
    pair_in,
    line_out,
    line_in,
    gain_out_sems,
    gain_in_sems,
    credits,
    ff_free,
    attn_free,
):
    p = Place(dp)
    group, cores = (group_out, group_in), (core_out, core_in)
    rows_r, hw = query_shard.shape
    ff = gate_shard.shape[0]
    wide = ff_w.shape[1] // 3
    width = x_in.shape[1]
    tiles = SEQ_LEN // TILE
    slot = rows_at(p.d * rows_r, rows_r)
    qkv, out_lanes = slice(0, 3 * hw), slice(3 * hw, 4 * hw)
    middle = wide + 5 * wide // 6 // 128 * 128
    sent = {}

    def go(name, copy):
        copy.start()
        sent[name] = copy

    def gone(name):
        sent.pop(name).wait_send()

    def arrived(there, sems, n, who):
        send(there, there, sems, n, who).wait_recv()

    def local(n, src, dst):
        return pltpu.make_async_copy(src, dst, local_sems.at[n])

    def fetch(n, src, dst):
        copy = local(n, src, dst)
        copy.start()
        return copy

    p.greet()
    x_copy = fetch(0, x_in, xb.at[p.chip])
    qkv_copies = [
        fetch(1 + n, shard, attn_w.at[slot, pl.ds(n * hw, hw)])
        for n, shard in enumerate((query_shard, key_shard, value_shard))
    ]
    og_copy = fetch(4, og_in, og.at[block(p.t)])
    vf_copy = fetch(5, value_first, attended)
    attn_w[slot, out_lanes] = out_shard[...].astype(F32).T.astype(BF16)
    p.met()
    x_copy.wait()
    go("x", send(xb.at[p.chip], xb.at[p.chip], group, 0, p.across))
    gathers = [
        Gather(
            p,
            full,
            pl.ds(first, lanes),
            rows_r,
            spread,
            (up_out.at[n], up_in.at[n]),
            (down_out.at[n], down_in.at[n]),
            (pair_out.at[n], pair_in.at[n]),
        )
        for n, (full, first, lanes, spread) in enumerate(
            (
                (attn_w, 0, 3 * hw, True),
                (attn_w, 3 * hw, hw, True),
                (ff_w, wide // 2, middle - wide // 2, True),
                (ff_w, middle, 3 * wide - middle, True),
                (ff_w, 0, wide // 2, False),
            )
        )
    ]
    of_attn, of_out, of_ff, of_rest, of_gate = gathers
    for copy in qkv_copies:
        copy.wait()
    of_attn.start_line()
    of_attn.start_pair()
    of_out.start_line()
    of_out.start_pair()
    gain_attn = gain_attn_in[...].astype(F32).reshape(1, width)
    gain_mlp = gain_mlp_in[...].astype(F32).reshape(1, width)
    other = lax.rem(p.t + 2, 4)
    sib = p.t + 1 - 2 * p.core
    sib_other = lax.rem(sib + 2, 4)

    def norm_block(b, chip, n):
        @pl.loop(0, HALF // TILE)
        def _(j):
            u = xb[chip, rows_at(j * TILE, TILE), :].astype(F32)
            normed[rows_at(b * HALF + j * TILE, TILE), :] = (
                u * norm_factor(u) * gain_attn
            ).astype(BF16)

        here = normed.at[block(b)]
        go(("normed", n), send(here, here, cores, n, p.sibling))

    norm_block(p.t, p.chip, 0)
    for n, shard in enumerate((gate_shard, up_shard, down_shard)):
        flat = shard[...].astype(F32)
        if wide > ff:
            flat = jnp.concatenate([flat, jnp.zeros((wide - ff, rows_r), F32)], axis=0)
        ff_w[slot, n * wide : (n + 1) * wide] = flat.T.astype(BF16)
    of_gate.start_pair()
    if p.line > 1:
        of_attn.relay(1)
        of_out.relay(1)

    @pl.loop(0, SEQS * tiles)
    def _(j):
        rows = rows_at(j * TILE, TILE)
        lane = lax.broadcasted_iota(jnp.int32, (TILE, 128), 1)
        half = HEAD_DIM // 2
        power = lax.rem(lane[0:1, :], half).astype(F32) * (-2.0 / HEAD_DIM)
        frequency = jnp.exp(power * math.log(ROPE_BASE))
        place = jnp.broadcast_to(positions[:, rows].astype(F32), (128, TILE)).T
        angle = place * frequency
        cos[rows, :] = jnp.cos(angle)
        sine = jnp.sin(angle)
        sin[rows, :] = jnp.where(lax.rem(lane, HEAD_DIM) < half, -sine, sine)

    og_copy.wait()
    own_rows = og.at[block(p.t)]
    go("og_c", send(own_rows, own_rows, cores, 2, p.sibling))
    for n in range(2, p.line):
        of_attn.relay(n)
        of_out.relay(n)
        if n == 2:
            go("og_x", send(own_rows, own_rows, group, 1, p.across))
    if p.line < 3:
        go("og_x", send(own_rows, own_rows, group, 1, p.across))
    of_ff.start_line()
    of_rest.start_line()
    of_gate.start_line()
    arrived(xb.at[1 - p.chip], group, 0, p.across)
    norm_block(other, 1 - p.chip, 1)
    of_ff.start_pair()
    of_rest.start_pair()
    of_attn.finish()
    arrived(normed.at[block(sib)], cores, 0, p.sibling)
    arrived(normed.at[block(sib_other)], cores, 1, p.sibling)
    vf_copy.wait()

    def project(seq):
        @pl.loop(0, tiles)
        def _(j):
            rows = rows_at(seq * SEQ_LEN + j * TILE, TILE)
            made = dot_nn(normed[rows, :], attn_w[:, qkv])
            c, s = cos[rows, :], sin[rows, :]
            for n in range(hw // 128):
                lanes = slice(n * 128, (n + 1) * 128)
                u = made[:, n * 128 : (n + 1) * 128]
                q[rows, lanes] = ((u * c + swap_halves(u) * s) * HEAD_DIM**-0.5).astype(BF16)
                u = made[:, hw + n * 128 : hw + (n + 1) * 128]
                k[rows, lanes] = (u * c + swap_halves(u) * s).astype(BF16)
            mixed = 0.5 * made[:, 2 * hw :] + 0.5 * attended[rows, :].astype(F32)
            v[rows, :] = mixed.astype(BF16)
            turned[:, rows_at(j * TILE, TILE)] = mixed.T.astype(BF16)

    def attend(seq, between):
        @pl.loop(0, hw // 128)
        def _(heads):
            @pl.when(heads == hw // 128 - 1)
            def _():
                for relay in between:
                    relay()

            for i in range(tiles):
                attention_rows(seq, heads, i, q, k, turned, segments, attended, lse)

    def branch_other(seq):
        @pl.loop(0, HALF // TILE)
        def _(j):
            rows = rows_at(seq * SEQ_LEN + (1 - p.core) * HALF + j * TILE, TILE)
            half_out[seq, rows_at(j * TILE, TILE), :] = dot_nt(
                attended[rows, :], attn_w[:, out_lanes]
            ).astype(BF16)

        go(("half", seq), send(half_out.at[seq], half_in.at[seq], cores, 4 + seq, p.sibling))

    def branch_own(seq):
        arrived(half_in.at[seq], cores, 4 + seq, p.sibling)

        @pl.loop(0, HALF // TILE)
        def _(j):
            rows = rows_at(seq * SEQ_LEN + p.core * HALF + j * TILE, TILE)
            tile = rows_at(j * TILE, TILE)
            part = dot_nt(attended[rows, :], attn_w[:, out_lanes])
            sum_out[seq, tile, :] = (part + half_in[seq, tile, :].astype(F32)).astype(BF16)

        go(("sum", seq), send(sum_out.at[seq], sum_in.at[seq], group, 2 + seq, p.across))

    def finish_branch(seq):
        arrived(sum_in.at[seq], group, 2 + seq, p.across)

        @pl.loop(0, HALF // TILE)
        def _(j):
            tile = rows_at(j * TILE, TILE)
            both = sum_out[seq, tile, :].astype(F32) + sum_in[seq, tile, :].astype(F32)
            u = xb[seq, tile, :].astype(F32) + both
            hidden[seq, tile, :] = u
            normed_mlp[rows_at((2 * seq + p.core) * HALF + j * TILE, TILE), :] = (
                u * norm_factor(u) * gain_mlp
            ).astype(BF16)

        mine = normed_mlp.at[block(2 * seq + p.core)]
        go(("mlp", seq), send(mine, mine, cores, 6 + seq, p.sibling))
        tell(credits.at[seq], p.across)

    def in_steps(gather):
        steps = list(range(1, p.line))

        def relay():
            if steps:
                gather.relay(steps.pop(0))

        return relay, steps

    relay_ff, steps = in_steps(of_ff)
    relay_rest, _ = in_steps(of_rest)
    relay_gate, left = in_steps(of_gate)
    project(0)
    attend(0, [relay_ff])
    relay_rest()
    of_out.finish()
    branch_other(0)
    project(1)
    branch_own(0)
    relay_gate()
    relay_ff()
    attend(1, [relay_rest])
    relay_gate()
    branch_other(1)
    branch_own(1)
    relay_ff()
    relay_rest()
    arrived(og.at[block(other)], group, 1, p.across)
    there = og.at[block(other)]
    go("og_f", send(there, there, cores, 3, p.sibling))
    while steps or left:
        relay_ff()
        relay_rest()
        relay_gate()
    finish_branch(0)
    arrived(og.at[block(sib)], cores, 2, p.sibling)
    arrived(og.at[block(sib_other)], cores, 3, p.sibling)
    of_ff.finish()
    of_rest.finish()

    def feed_copy(seq, n, j):
        tile = rows_at(j * TILE, TILE)
        there = half_in.at[n, tile]
        return send(half_out.at[n, tile], there, cores, 8 + seq * 4 + n * 2 + j, p.sibling)

    def feed_sum(seq, j):
        tile = rows_at(j * TILE, TILE)
        return send(sum_out.at[seq, tile], sum_in.at[seq, tile], group, 6 + seq * 2 + j, p.across)

    def feed_gone(seq):
        for n in range(2):
            for j in range(HALF // TILE):
                feed_copy(seq, n, j).wait_send()

    def feed(seq):
        arrived(normed_mlp.at[block(2 * seq + 1 - p.core)], cores, 6 + seq, p.sibling)
        if seq == 0:
            for n in range(2):
                gone(("half", n))
        else:
            feed_gone(0)
        gone(("sum", seq))
        pl.semaphore_wait(credits.at[seq], 1)

        @pl.loop(0, tiles)
        def _(step):
            j = lax.rem(step, HALF // TILE)
            others = step < HALF // TILE
            h = jnp.where(others, 1 - p.core, p.core)
            here = rows_at(h * HALF + j * TILE, TILE)
            rows = rows_at(seq * SEQ_LEN + h * HALF + j * TILE, TILE)
            tile = rows_at(j * TILE, TILE)
            for n in range(wide // 256):
                lanes = [slice(m * wide + n * 256, m * wide + (n + 1) * 256) for m in range(3)]
                gate = dot_nn(normed_mlp[rows, :], ff_w[:, lanes[0]])
                up = dot_nn(normed_mlp[rows, :], ff_w[:, lanes[1]])
                grad_act = dot_nn(og[rows, :], ff_w[:, lanes[2]])
                sig = 1.0 / (1.0 + jnp.exp(-gate))
                swish = gate * sig
                units[here, lanes[0]] = (
                    grad_act * up * sig * (1.0 + gate * (1.0 - sig))
                ).astype(BF16)
                units[here, lanes[1]] = (grad_act * swish).astype(BF16)
                units[here, lanes[2]] = (swish * up).astype(BF16)
            down = dot_nt(units[here, 2 * wide :], ff_w[:, 2 * wide :])
            back = dot_nt(units[here, : 2 * wide], ff_w[:, : 2 * wide])

            @pl.when(others)
            def _():
                half_out[0, tile, :] = back.astype(BF16)
                half_out[1, tile, :] = down.astype(BF16)
                for n in range(2):
                    feed_copy(seq, n, j).start()

            @pl.when(jnp.logical_not(others))
            def _():
                for n in range(2):
                    feed_copy(seq, n, j).wait_recv()
                sum_out[seq, tile, :] = (back + half_in[0, tile, :].astype(F32)).astype(BF16)
                m_sum[seq, tile, :] = (down + half_in[1, tile, :].astype(F32)).astype(BF16)
                feed_sum(seq, j).start()

    def ff_weights(seq, n):
        rows = pl.ds(seq * SEQ_LEN, SEQ_LEN)
        left = og if isinstance(n, int) else normed_mlp
        lanes = pl.ds(pl.multiple_of(n * wide, 128), wide)

        @pl.loop(0, width // TILE)
        def _(j):
            cols = rows_at(j * TILE, TILE)
            part = dot_tn(left[rows, cols], units[:, lanes])
            if seq > 0:
                part = part + ff_grad[cols, lanes].astype(F32)
            ff_grad[cols, lanes] = part.astype(BF16)

    def both_ff_weights(seq, then=()):
        @pl.loop(0, 2)
        def _(n):
            ff_weights(seq, n)
            for m, start in enumerate(then):
                pl.when(n == m)(start)

    def pull(seq):
        for j in range(HALF // TILE):
            feed_sum(seq, j).wait_recv()

        @pl.loop(0, HALF // TILE)
        def _(j):
            tile = rows_at(j * TILE, TILE)
            rows = rows_at((2 * seq + p.core) * HALF + j * TILE, TILE)
            grad = sum_out[seq, tile, :].astype(F32) + sum_in[seq, tile, :].astype(F32)
            back, gain_rows = norm_pull(grad, hidden[seq, tile, :], gain_mlp)
            whole = og[rows, :].astype(F32) + back
            normed_mlp[rows, :] = whole.astype(BF16)

            @pl.when(p.chip == seq)
            def _():
                grad_hidden[tile, :] = whole
                gain_acc[1:2, :] += jnp.sum(gain_rows, axis=0, keepdims=True)

        mine = normed_mlp.at[block(2 * seq + p.core)]
        pl.semaphore_wait(credits.at[2 + seq], 1)
        go(("low", seq), send(mine, mine, cores, 16 + seq, p.sibling))

        @pl.when(p.chip == seq)
        def _():
            tell(credits.at[4], p.across)

    def release(sems):
        for who, n in [(p.pair, 0)] + [(p.behind(n), n) for n in range(1, p.line)]:
            tell(sems.at[n], who)

    def free_rows(seq):
        gone(("mlp", seq))
        tell(credits.at[2 + seq], p.sibling)

    feed(0)
    both_ff_weights(0)
    ff_weights(0, 2)
    finish_branch(1)
    free_rows(0)
    feed(1)
    of_ff.drain()
    of_rest.drain()
    of_gate.drain()
    release(ff_free)
    gain_acc[...] = jnp.zeros_like(gain_acc)
    scatters = [
        Scatter(
            p,
            ff_grad,
            ff_w,
            pl.ds(n * wide, wide),
            (pair_out.at[5 + n], pair_in.at[5 + n]),
            (line_out.at[n], line_in.at[n]),
            ff_free if n == 0 else None,
        )
        for n in range(3)
    ]
    scatters_attn = [
        Scatter(
            p,
            attn_grad,
            og,
            pl.ds(n * hw, hw),
            (pair_out.at[8 + n], pair_in.at[8 + n]),
            (line_out.at[3 + n], line_in.at[3 + n]),
            attn_free if n == 0 else None,
        )
        for n in range(4)
    ]
    away = far_first(p.line)
    firsts = away or [0]
    both_ff_weights(1, [functools.partial(scatters[n].start, firsts) for n in range(2)])
    ff_weights(1, 2)
    scatters[2].start(firsts)
    if away:
        for n in range(3):
            scatters[n].start([0])
    relays = [(scatters[n], k) for n in range(3) for k in away]
    if len(away) == 3:
        relays = [relays[n] for n in (0, 1, 3, 2, 4, 6, 5, 7, 8)]

    def relay_grad():
        if relays:
            scatter, k = relays.pop(0)
            scatter.relay(k)

    pull(0)
    free_rows(1)

    dqkv = units

    def grad_att(i, heads):
        return units[pl.ds(i * TILE, TILE), rows_at(3 * hw + heads * 128, 128)]

    def turn(seq):
        @pl.loop(0, tiles)
        def _(j):
            rows = rows_at(seq * SEQ_LEN + j * TILE, TILE)
            turned[:, rows_at(j * TILE, TILE)] = k[rows, :].astype(F32).T.astype(BF16)

    def prepare(seq):
        arrived(normed_mlp.at[block(2 * seq + 1 - p.core)], cores, 16 + seq, p.sibling)

        @pl.loop(0, tiles)
        def _(j):
            here = rows_at(j * TILE, TILE)
            rows = rows_at(seq * SEQ_LEN + j * TILE, TILE)
            units[here, out_lanes] = dot_nn(normed_mlp[rows, :], attn_w[:, out_lanes]).astype(BF16)

    def grad_store(seq, heads):
        rows = pl.ds(seq * SEQ_LEN, SEQ_LEN)
        return local(6, dv, value_first_grad.at[rows, rows_at(heads * 128, 128)])

    def m_copy():
        return send(m_sum.at[1 - p.chip], xb.at[p.chip], group, 4, p.across)

    def attend_back(seq, jobs):
        if seq > 0:
            grad_store(0, hw // 128 - 1).wait()

        @pl.loop(0, hw // 128)
        def _(heads):
            @pl.when(heads > 0)
            def _():
                grad_store(seq, heads - 1).wait()

            for i in reversed(range(tiles)):
                for when, job in jobs:
                    if when[1] == i:

                        @pl.when(heads == when[0])
                        def _():
                            job()

                attention_rows_back(
                    seq,
                    heads,
                    i,
                    q,
                    k,
                    v,
                    turned,
                    segments,
                    lse,
                    attended,
                    grad_att,
                    dk,
                    dv,
                    cos,
                    sin,
                    dqkv,
                )

            @pl.loop(0, tiles)
            def _(j):
                here = rows_at(j * TILE, TILE)
                rows = rows_at(seq * SEQ_LEN + j * TILE, TILE)
                u = dk[here, :]
                dqkv[here, rows_at(hw + heads * 128, 128)] = (
                    u * cos[rows, :] - swap_halves(u) * sin[rows, :]
                ).astype(BF16)
                half = 0.5 * dv[here, :]
                dqkv[here, rows_at(2 * hw + heads * 128, 128)] = half.astype(BF16)
                dv[here, :] = half

            grad_store(seq, heads).start()

    def attn_weights(seq, part):
        rows = pl.ds(seq * SEQ_LEN, SEQ_LEN)
        lanes = qkv if seq == 0 else rows_at(part * hw, hw)

        @pl.loop(0, width // TILE)
        def _(j):
            cols = rows_at(j * TILE, TILE)
            made = dot_tn(normed[rows, cols], units[:, lanes])
            if seq > 0:
                made = made + attn_grad[cols, lanes].astype(F32)
            attn_grad[cols, lanes] = made.astype(BF16)

    def out_weights():
        @pl.loop(0, width // TILE)
        def _(j):
            cols = rows_at(j * TILE, TILE)
            attn_grad[cols, out_lanes] = dot_tn(normed_mlp[:, cols], attended[...]).astype(BF16)

    def back_copy(seq, j):
        tile = rows_at(j * TILE, TILE)
        there = half_in.at[seq, tile]
        return send(half_out.at[seq, tile], there, cores, 18 + seq * 2 + j, p.sibling)

    def back_sum(seq, j):
        tile = rows_at(j * TILE, TILE)
        return send(sum_out.at[seq, tile], sum_in.at[seq, tile], group, 10 + j, p.across)

    def back_other(seq):
        if seq == 0:
            feed_gone(1)

        @pl.loop(0, HALF // TILE)
        def _(j):
            here = rows_at((1 - p.core) * HALF + j * TILE, TILE)
            half_out[seq, rows_at(j * TILE, TILE), :] = dot_nt(
                dqkv[here, qkv], attn_w[:, qkv]
            ).astype(BF16)
            back_copy(seq, j).start()

    gain_sems = (gain_out_sems, gain_in_sems)

    def gain_copies(partners, first):
        return [
            send(gain_acc, gain_in.at[first + n], gain_sems, first + n, who)
            for n, who in enumerate(partners)
        ]

    def exchange(partners, first):
        for copy in gain_copies(partners, first):
            copy.start()

    def add_gains(partners, first):
        for copy in gain_copies(partners, first):
            copy.wait()
        whole = gain_acc[...]
        for n in range(len(partners)):
            whole = whole + gain_in[first + n]
        gain_acc[...] = whole

    def back_own(seq):
        for j in range(HALF // TILE):
            feed_sum(seq, j).wait_send()

        @pl.when(p.chip != seq)
        def _():
            pl.semaphore_wait(credits.at[4], 1)

        @pl.loop(0, HALF // TILE)
        def _(j):
            here = rows_at(p.core * HALF + j * TILE, TILE)
            tile = rows_at(j * TILE, TILE)
            rows = rows_at((2 * seq + p.core) * HALF + j * TILE, TILE)
            part = dot_nt(dqkv[here, qkv], attn_w[:, qkv])
            back_copy(seq, j).wait_recv()
            part = part + half_in[seq, tile, :].astype(F32)
            sum_out[seq, tile, :] = part.astype(BF16)
            gain_acc[0:1, :] += jnp.sum(part * normed[rows, :].astype(F32), axis=0, keepdims=True)

            @pl.when(p.chip != seq)
            def _():
                back_sum(seq, j).start()

        if seq == SEQS - 1:
            exchange([p.sibling], 0)

    turn(0)
    relay_grad()
    prepare(0)
    attend_back(0, [((1, 3), m_copy().start), ((0, 1), relay_grad), ((1, 1), relay_grad)])
    relay_grad()
    back_other(0)
    turn(1)
    attn_weights(0, 0)
    relay_grad()
    pull(1)
    for name in ("og_x", "og_c", "og_f"):
        gone(name)
    release(attn_free)
    back_own(0)
    prepare(1)
    attend_back(1, [((0, 1), relay_grad), ((0, 1), relay_grad), ((1, 3), relay_grad)])
    back_other(1)
    while relays:
        relay_grad()

    @pl.loop(0, 3)
    def _(n):
        attn_weights(1, n)
        for m in range(3):
            steps_now = firsts if m < 2 else firsts[:-1]
            pl.when(n == m)(functools.partial(scatters_attn[m].start, steps_now))
        pl.when(n == 0)(lambda: back_own(1))

    out_weights()
    add_gains([p.sibling], 0)
    farther = [p.pair] + [p.ahead(n) for n in away] + [p.beyond(n) for n in away]
    exchange(farther, 2)
    scatters_attn[3].start(firsts[:-1])
    for n in (2, 3):
        scatters_attn[n].start(firsts[-1:])
    if away:
        for scatter in scatters_attn:
            scatter.start([0])

    arrived(xb.at[1 - p.chip], group, 4, p.across)

    @pl.loop(0, HALF // TILE)
    def _(j):
        tile = rows_at(j * TILE, TILE)
        both = m_sum[p.chip, tile, :].astype(F32) + xb[1 - p.chip, tile, :].astype(F32)
        m_sum[p.chip, tile, :] = (hidden[p.chip, tile, :] + both).astype(BF16)

    stores = []

    def store(src, dst):
        stores.append(fetch(7 + len(stores), src, dst))

    store(m_sum.at[p.chip], block_output)
    for n in range(4):
        for k in away[:-1]:
            scatters_attn[n].relay(k)
        for m in [n - 1] * (n > 0) + [n] * (n == 3):
            for k in away[-1:]:
                scatters_attn[m].relay(k)
        if n < 2:
            scatters[n].finish()
            (gate_sum, up_sum)[n][...] = scatters[n].total().T[:ff, :]
            store((gate_sum, up_sum)[n], (gate_out, up_out_sum)[n])
    add_gains(farther, 2)
    exchange([p.across], 1)
    of_attn.drain()
    of_out.drain()
    for n in range(3):
        scatters[n].drain()
    for j in range(HALF // TILE):
        for seq in range(SEQS):
            back_copy(seq, j).wait_send()
    m_copy().wait_send()
    for name in list(sent):
        gone(name)

    @pl.loop(0, HALF // TILE)
    def _(j):
        tile = rows_at(j * TILE, TILE)
        back_sum(p.chip, j).wait_recv()
        grad = sum_out[p.chip, tile, :].astype(F32) + sum_in[p.chip, tile, :].astype(F32)
        back, _ = norm_pull(grad, xb[p.chip, tile, :].astype(F32), gain_attn)
        grad_hidden[tile, :] = grad_hidden[tile, :] + back

    store(grad_hidden, input_grad)
    scatters[2].finish()
    down_sum[...] = scatters[2].total().T[:ff, :]
    store(down_sum, down_out_sum)
    add_gains([p.across], 1)
    gain_attn_grad[...] = gain_acc[0:1, :] / gain_attn
    gain_mlp_grad[...] = gain_acc[1:2, :]
    store(gain_attn_grad, gain_attn_out)
    store(gain_mlp_grad, gain_mlp_out)
    for n, (held, out) in enumerate(
        ((query_sum, query_out), (key_sum, key_out), (value_sum, value_out))
    ):
        if n == 2:
            scatters_attn[0].drain()
            scatters_attn[1].drain()
            for j in range(HALF // TILE):
                back_sum(1 - p.chip, j).wait_send()
            grad_store(SEQS - 1, hw // 128 - 1).wait()
        scatters_attn[n].finish()
        held[...] = scatters_attn[n].total()
        store(held, out)
    scatters_attn[3].finish()
    out_sum[...] = scatters_attn[3].total().T
    store(out_sum, out_out)
    scatters_attn[2].drain()
    scatters_attn[3].drain()
    for copy in stores:
        copy.wait()


def layer(dp, x, og, vf, segments, positions, gain_a, gain_m, wq, wk, wv, wo, wg, wu, wd):
    rows, width = 4 * x.shape[0], x.shape[1]
    hw, ff, r = vf.shape[1], wg.shape[0], wq.shape[0]
    wide = -(-ff // 256) * 256
    line = dp // 2
    hops = max(line - 1, 1)
    vmem = pl.BlockSpec(memory_space=pltpu.VMEM)
    far = pl.BlockSpec(memory_space=pl.ANY)
    shapes = [
        ((HALF, width), BF16, far),
        ((HALF, width), F32, far),
        ((rows, hw), F32, far),
        ((1, width), F32, far),
        ((r, hw), F32, far),
        ((r, hw), F32, far),
        ((r, hw), F32, far),
        ((hw, r), F32, far),
        ((1, width), F32, far),
        ((ff, r), F32, far),
        ((ff, r), F32, far),
        ((ff, r), F32, far),
    ]
    dma = pltpu.SemaphoreType.DMA
    flag = pltpu.SemaphoreType.REGULAR

    def bf(*shape):
        return pltpu.VMEM(shape, BF16)

    def fl(*shape):
        return pltpu.VMEM(shape, F32)

    scratch = [pltpu.VMEM(shape, kind) for shape, kind, _ in shapes[3:]] + [
        bf(2, HALF, width),
        bf(rows, width),
        bf(rows, width),
        bf(rows, width),
        bf(width, 4 * hw),
        bf(width, 3 * wide),
        bf(rows, hw),
        bf(rows, hw),
        bf(rows, hw),
        bf(rows, hw),
        fl(8, 1, SEQ_LEN),
        fl(2, HALF, width),
        fl(HALF, width),
        bf(SEQ_LEN, 3 * wide),
        bf(width, 3 * wide),
        bf(width, 4 * hw),
        bf(2, HALF, width),
        bf(2, HALF, width),
        bf(2, HALF, width),
        bf(2, HALF, width),
        bf(2, HALF, width),
        bf(hw, SEQ_LEN),
        fl(SEQ_LEN, 128),
        fl(SEQ_LEN, 128),
        fl(rows, 128),
        fl(rows, 128),
        fl(2, width),
        fl(4 + 2 * hops, 2, width),
        dma((18,)),
        dma((12,)),
        dma((12,)),
        dma((22,)),
        dma((22,)),
        dma((5, hops)),
        dma((5, hops)),
        dma((5, hops)),
        dma((5, hops)),
        dma((12, line)),
        dma((12, line)),
        dma((7, line)),
        dma((7, line)),
        dma((4 + 2 * hops,)),
        dma((4 + 2 * hops,)),
        flag((5,)),
        flag((line,)),
        flag((line,)),
    ]
    in_specs = [far] * 3 + [vmem] * 4 + [far] * 3 + [vmem] * 4
    return pl.pallas_call(
        functools.partial(layer_kernel, dp),
        out_shape=[jax.ShapeDtypeStruct(s, t) for s, t, _ in shapes],
        in_specs=in_specs,
        out_specs=[space for _, _, space in shapes],
        scratch_shapes=scratch,
        compiler_params=pltpu.CompilerParams(
            collective_id=0, has_side_effects=True, vmem_limit_bytes=VMEM_LIMIT
        ),
        name="layer",
    )(x, og, vf, segments, positions, gain_a, gain_m, wq, wk, wv, wo, wg, wu, wd)


def chunks(shape):
    parts = 4 if shape[0] % 512 == 0 else 1
    size = shape[0] // parts
    return [pl.ds(n * size, size) for n in range(parts)]


def settle_kernel(count, *refs):
    ins, outs, held, sems = refs[:count], refs[count : 2 * count], refs[2 * count : -1], refs[-1]
    pieces = [(n, rows) for n in range(count) for rows in chunks(ins[n].shape)]
    first, second = [], []
    for m, (n, rows) in enumerate(pieces):
        there = held[n].at[rows]
        first.append(pltpu.make_async_copy(ins[n].at[rows], there, sems.at[2 * m]))
        second.append(pltpu.make_async_copy(there, outs[n].at[rows], sems.at[2 * m + 1]))
    for copy in first:
        copy.start()
    for came, goes in zip(first, second):
        came.wait()
        goes.start()
    for copy in second:
        copy.wait()


def settle(arrays):
    count = len(arrays)
    far = pl.BlockSpec(memory_space=pl.ANY)
    return pl.pallas_call(
        functools.partial(settle_kernel, count),
        out_shape=[jax.ShapeDtypeStruct(a.shape, a.dtype) for a in arrays],
        in_specs=[far] * count,
        out_specs=[far] * count,
        scratch_shapes=[pltpu.VMEM(a.shape, a.dtype) for a in arrays]
        + [pltpu.SemaphoreType.DMA((2 * sum(len(chunks(a.shape)) for a in arrays),))],
        compiler_params=pltpu.CompilerParams(vmem_limit_bytes=VMEM_LIMIT),
        name="settle",
    )(*arrays)


def on_device(
    dp,
    block_input,
    value_first,
    segment_ids,
    positions,
    gain_attn,
    query_weight,
    key_weight,
    value_weight,
    out_weight,
    gain_mlp,
    gate_weight,
    up_weight,
    down_weight,
    output_grad,
):
    outs = layer(
        dp,
        block_input,
        output_grad,
        value_first,
        segment_ids[None, :],
        positions[None, :],
        gain_attn,
        gain_mlp,
        query_weight,
        key_weight,
        value_weight,
        out_weight,
        gate_weight.T,
        up_weight.T,
        down_weight,
    )
    (
        block_output,
        input_grad,
        value_first_grad,
        gain_attn_grad,
        query_sum,
        key_sum,
        value_sum,
        out_sum,
        gain_mlp_grad,
        gate_sum,
        up_sum,
        down_sum,
    ) = settle(outs)
    return (
        block_output,
        input_grad,
        value_first_grad,
        gain_attn_grad[0],
        query_sum,
        key_sum,
        value_sum,
        out_sum,
        gain_mlp_grad[0],
        gate_sum.T,
        up_sum.T,
        down_sum,
    )


def solution(mesh):
    rows = P(("dp", "tensor"), None)
    weight = P("dp", "tensor")
    across = P("tensor", "dp")
    return jax.shard_map(
        functools.partial(on_device, mesh.shape["dp"]),
        mesh=mesh,
        in_specs=(
            rows,
            weight,
            P("dp"),
            P("dp"),
            P(),
            weight,
            weight,
            weight,
            across,
            P(),
            weight,
            weight,
            across,
            rows,
        ),
        out_specs=(
            rows,
            rows,
            weight,
            P(),
            weight,
            weight,
            weight,
            across,
            P(),
            weight,
            weight,
            across,
        ),
        check_vma=False,
    )
```
